32 devices in a mesh: dp: 16 (over z, x, core), tensor: 2 (over y).
Axes of the slice: x: 2, y: 2, z: 4, core: 2. Of those that a mesh axis runs over, the one named last changes fastest.
Arguments:
- tokens: bfloat16 [16, 1024, 1024], P('dp', 'tensor'), may hold values from -6 to 6
- segments: int32 [16, 1024], P('dp'), may hold values from 0 to 7, never falling along the last dimension, each value on 1 to 512 neighbouring positions
- qkv_weight: bfloat16 [1024, 3, 1024], P('dp', None, 'tensor'), may hold values from -0.1875 to 0.1875
- attn_out_weight: bfloat16 [1024, 1024], P('tensor', 'dp'), may hold values from -1 to 1
- in_weight: bfloat16 [1024, 2, 2624], P('dp', None, 'tensor'), may hold values from -0.1875 to 0.1875
- down_weight: bfloat16 [2624, 1024], P('tensor', 'dp'), may hold values from -0.15625 to 0.15625
- norm_attn: bfloat16 [1024], P('dp'), may hold values from 0.5 to 1.5
- norm_mlp: bfloat16 [1024], P('dp'), may hold values from 0.5 to 1.5
- cotangent: bfloat16 [16, 1024, 1024], P('dp', 'tensor'), may hold values from -6 to 6
Outputs:
- output: bfloat16 [16, 1024, 1024], P('dp', 'tensor')
- token_grad: float32 [16, 1024, 1024], P('dp', 'tensor')
- norm_attn_grad: float32 [1024], P('dp')
- norm_mlp_grad: float32 [1024], P('dp')
- qkv_weight_grad: float32 [1024, 3, 1024], P('dp', None, 'tensor')
- attn_out_weight_grad: float32 [1024, 1024], P('tensor', 'dp')
- in_weight_grad: float32 [1024, 2, 2624], P('dp', None, 'tensor')
- down_weight_grad: float32 [2624, 1024], P('tensor', 'dp')
The draws below stay inside these ranges and needn't reach their ends.
Inputs may be any that keep to these rules, and one draw needn't show every extreme that they name: `segments`: segment ids never fall along a sequence; each document holds 1 to 512 tokens, and in every sequence one holds exactly 512.
All inputs are finite; a program needn't handle non-finite values.
Results may differ from the reference program's by a relative error of at most 0.015.
Values may be sent and summed in bfloat16 or wider, within the bound.
A program may use at most 192 MiB of HBM per device.

```python
import math
import jax
import jax.numpy as jnp
import numpy as np
from jax import lax

D = 1024
H = 16
HD = 64
FF = 2624
LEN = 1024
DOCS = 8
SEQS = 16


def raised(values, key, source, target, parts, factor):
    def block_of(axis_at):
        return (jnp.arange(values.shape[axis_at]) // (values.shape[axis_at] // parts)).reshape((-1,) + (1,) * (values.ndim - 1 - axis_at))

    first = jax.random.permutation(key, parts)[block_of(target)]
    second = (block_of(target) + parts // 2) % parts
    return jnp.where((block_of(source) == first) | (block_of(source) == second), factor * values, values)


def block_levels(own_key, shape, split, smallest, largest):
    factor_of, own = 1.0, jax.random.fold_in(own_key, 6)
    for dim, blocks in split:
        steps = jnp.exp(jax.random.uniform(jax.random.fold_in(own, dim), (blocks,), jnp.float32, smallest / len(split), largest / len(split)))
        factor_of = factor_of * jnp.repeat(steps, shape[dim] // blocks).reshape([-1 if axis == dim else 1 for axis in range(len(shape))])
    return factor_of


def split_up(count, total, bound, slope):
    weights = [(1 << 20) // math.isqrt(rank ** slope) + 1 for rank in range(2, count + 1)]
    surplus, counts = total - bound - (count - 1), [1] * (count - 1)
    while surplus > 0:
        free = [i for i in range(count - 1) if counts[i] < bound]
        mass, remaining = sum([weights[i] for i in free]), surplus
        for i in free:
            more = min(bound - counts[i], max(1, remaining * weights[i] // mass), surplus)
            counts[i] = counts[i] + more
            surplus = surplus - more
    return np.array([bound] + counts)


def ragged_sizes(rng, amount, total, most, lean):
    if amount == 2:
        one = jax.random.randint(rng, (), max(1, total - most), min(most, total - 1) + 1)
        return jnp.stack([one, total - one])
    sizes = jnp.asarray(split_up(amount, total, most, lean), jnp.int32)
    twos = (amount - 1) // 2
    giver, taker = sizes[1:1 + 2 * twos:2], sizes[2:2 + 2 * twos:2]
    margin = jnp.minimum(giver - 1, most - taker)
    moved = jax.random.randint(jax.random.fold_in(rng, 1), (twos,), 0, 1 << 20) % (margin + 1)
    sizes = sizes.at[1:1 + 2 * twos:2].set(giver - moved).at[2:2 + 2 * twos:2].set(taker + moved)
    return sizes[jax.random.permutation(jax.random.fold_in(rng, 2), amount)]


def gaussian(own_key, extent, deviation, reach, shards=(), kind=jnp.bfloat16):
    entries = deviation * jax.random.normal(own_key, extent, jnp.float32)
    if shards:
        entries = entries * block_levels(own_key, extent, shards, -0.22, 0.18)
    return jnp.clip(entries, -reach, reach).astype(kind)


def noise_with(stream_key, dims, scale, limit, pieces, heavy, kind=jnp.bfloat16):
    entries = scale * jax.random.normal(stream_key, dims, jnp.float32)
    if pieces:
        entries = entries * block_levels(stream_key, dims, pieces, -0.22, 0.18)
    return jnp.clip(raised(entries, jax.random.fold_in(stream_key, 3), *heavy), -limit, limit).astype(kind)


def setup_inputs(seed: int = 0) -> dict:
    arg_keys = jax.random.split(jax.random.key(seed), 10)
    tokens = noise_with(arg_keys[0], (SEQS, LEN, D), 1.0, 6.0, ((0, 16), (1, 2)), (0, 2, 16, 2.0))
    segments = jax.vmap(lambda own: jnp.searchsorted(jnp.cumsum(ragged_sizes(own, DOCS, LEN, LEN // 2, 2)), jnp.arange(LEN), side="right"))(jax.random.split(arg_keys[1], SEQS)).reshape((SEQS, LEN)).astype(jnp.int32)
    qkv_weight = gaussian(arg_keys[2], (D, 3, H * HD), D ** -0.5, 0.1875, ((0, 16), (2, 2)))
    attn_out_weight = gaussian(arg_keys[3], (H * HD, D), (H * HD // 32) ** -0.5, 1.0, ((0, 2), (1, 16)))
    in_weight = gaussian(arg_keys[4], (D, 2, FF), D ** -0.5, 0.1875, ((0, 16), (2, 2)))
    down_weight = gaussian(arg_keys[5], (FF, D), (FF // 2) ** -0.5, 0.15625, ((0, 2), (1, 16)))
    norm_attn = jnp.clip(1.0 + 0.1 * jax.random.normal(arg_keys[6], (D,), jnp.float32), 0.5, 1.5).astype(jnp.bfloat16)
    norm_mlp = jnp.clip(1.0 + 0.1 * jax.random.normal(arg_keys[7], (D,), jnp.float32), 0.5, 1.5).astype(jnp.bfloat16)
    cotangent = noise_with(arg_keys[8], (SEQS, LEN, D), 1.0, 6.0, ((0, 16), (1, 2)), (0, 2, 16, 2.0))
    return dict(tokens=tokens, segments=segments, qkv_weight=qkv_weight, attn_out_weight=attn_out_weight, in_weight=in_weight, down_weight=down_weight, norm_attn=norm_attn, norm_mlp=norm_mlp, cotangent=cotangent)


@jax.custom_vjp
def low(v):
    return lax.optimization_barrier(v.astype(jnp.bfloat16)).astype(jnp.float32)

@jax.custom_vjp
def low_back(v):
    return v

def low_keep(v):
    return (low(v), None)

def low_pass(kept, grad):
    return (grad,)

def back_keep(v):
    return (v, None)

def back_low(kept, grad):
    return (low(grad),)
low.defvjp(low_keep, low_pass)
low_back.defvjp(back_keep, back_low)
highest = lax.Precision.HIGHEST
norm_epsilon = 1e-05
rotary_base = 160000.0

def level_normalize(values, gain):
    centre = lax.optimization_barrier(jnp.mean(values, axis=-1, keepdims=True))
    centred = values - centre
    spread = lax.optimization_barrier(jnp.mean(centred * centred, axis=-1, keepdims=True))
    return centred * lax.rsqrt(spread + norm_epsilon) * gain

def rotary_tables(length, head_size):
    half_size = head_size // 2
    inverse = 1.0 / rotary_base ** (jnp.arange(half_size).astype(jnp.float32) * (2.0 / head_size))
    angles = jnp.arange(length).astype(jnp.float32)[:, None] * inverse[None, :]
    angles = jnp.concatenate([angles, angles], axis=-1)
    return (jnp.cos(angles), jnp.sin(angles))

def rotate(values, cosine, sine):
    half_size = values.shape[-1] // 2
    turned = jnp.concatenate([-values[..., half_size:], values[..., :half_size]], axis=-1)
    return values * cosine + turned * sine

def attend(query_all, key_all, value_all, segment_ids):
    length = key_all.shape[0]
    block_rows = min(512, length)
    score_scale = 1.0 / math.sqrt(HD)

    def one_block(position):
        begin_at = position * block_rows
        asking_vectors = lax.dynamic_slice_in_dim(query_all, begin_at, block_rows, 0)
        query_segs = lax.dynamic_slice_in_dim(segment_ids, begin_at, block_rows, 0)
        raw_scores = low_back(jnp.dot(asking_vectors, key_all.T, precision=highest) * score_scale)
        masked = jnp.where(query_segs[:, None] == segment_ids[None, :], raw_scores, -1e+30)
        highest_score = lax.optimization_barrier(jnp.max(masked, axis=-1, keepdims=True))
        expvals = jnp.exp(masked - highest_score)
        probs = expvals / lax.optimization_barrier(jnp.sum(expvals, axis=-1, keepdims=True))
        return jnp.dot(low(probs), value_all, precision=highest)
    tile_outputs = lax.map(jax.checkpoint(one_block), jnp.arange(length // block_rows, dtype=jnp.int32))
    return tile_outputs.reshape(length, value_all.shape[-1])

def forward(inputs, segment_ids, wqkv, wmix, wgate, wdown, gain_one, gain_two):
    groups, length, width = inputs.shape
    heads = wmix.shape[0] // HD
    normed_one = low(level_normalize(inputs, gain_one))
    projected_rows = low_back(jnp.einsum('gld,dcf->glcf', normed_one, wqkv, precision=highest))
    cosine, sine = rotary_tables(length, HD)
    cos_heads = cosine[:, None, :]
    sin_heads = sine[:, None, :]

    def heads_of(values):
        return values.reshape(groups, length, heads, HD)
    queries = low(rotate(heads_of(projected_rows[:, :, 0]), cos_heads, sin_heads))
    keys_all = low(rotate(heads_of(projected_rows[:, :, 1]), cos_heads, sin_heads))
    values_all = low(heads_of(projected_rows[:, :, 2]))
    per_head = jax.vmap(attend, in_axes=(1, 1, 1, None), out_axes=1)

    def per_sequence(packed):
        return per_head(packed[0], packed[1], packed[2], packed[3])
    mixed = lax.map(per_sequence, (queries, keys_all, values_all, segment_ids))
    head_results = low(low_back(mixed.reshape(groups, length, heads * HD)))
    attn_branch = low_back(jnp.einsum('glf,fd->gld', head_results, wmix, precision=highest))
    resid = inputs + attn_branch
    normed_two = low(level_normalize(resid, gain_two))
    gates = low_back(jnp.einsum('gld,dcf->glcf', normed_two, wgate, precision=highest))
    hidden_state = low(low_back(jax.nn.gelu(gates[:, :, 0], approximate=False) * gates[:, :, 1]))
    mlp_branch = low_back(jnp.einsum('glf,fd->gld', hidden_state, wdown, precision=highest))
    return resid + mlp_branch

def reference(tokens, segments, qkv_weight, attn_out_weight, in_weight, down_weight, norm_attn, norm_mlp, cotangent):
    weights = tuple((w.astype(jnp.float32) for w in (qkv_weight, attn_out_weight, in_weight, down_weight, norm_attn, norm_mlp)))
    group_size = math.gcd(SEQS, max(1, 4096 // LEN))
    group_count = SEQS // group_size
    inputs = tokens.astype(jnp.float32).reshape(group_count, group_size, LEN, D)
    segment_groups = segments.reshape(group_count, group_size, LEN)
    grad_groups = cotangent.astype(jnp.float32).reshape(group_count, group_size, LEN, D)

    def one_group(totals, packed):
        input_part, document_portion, grad_part = packed

        def local_layer(x_arg, w_one, w_two, w_three, w_four, g_one, g_two):
            return forward(x_arg, document_portion, w_one, w_two, w_three, w_four, g_one, g_two)
        result, pullback = jax.vjp(local_layer, input_part, weights[0], weights[1], weights[2], weights[3], weights[4], weights[5])
        pulled = pullback(grad_part)
        totals = tuple((a + b for a, b in zip(totals, pulled[1:])))
        return (totals, (result.astype(jnp.bfloat16), pulled[0]))
    initial = tuple((jnp.zeros_like(w) for w in weights))
    totals, (results, input_grads) = lax.scan(one_group, initial, (inputs, segment_groups, grad_groups))
    return (results.reshape(SEQS, LEN, D), input_grads.reshape(SEQS, LEN, D), totals[4], totals[5], totals[0], totals[1], totals[2], totals[3])
```

```python
import math

import jax
import jax.numpy as jnp
from jax import lax
from jax.experimental import pallas as pl
from jax.experimental.pallas import tpu as pltpu
from jax.sharding import PartitionSpec as P

HD = 64
EPS = 1e-05
ROTARY_BASE = 160000.0
BF = jnp.bfloat16
F32 = jnp.float32


def dotf(a, b, dims):
    return lax.dot_general(a, b, (dims, ((), ())), preferred_element_type=F32)


NN = ((1,), (0,))
NT = ((1,), (1,))
TN = ((0,), (0,))


def rope_tables(positions):
    half = HD // 2
    inverse = 1.0 / ROTARY_BASE ** (jnp.arange(half).astype(F32) * (2.0 / HD))
    angles = positions.astype(F32)[:, None] * inverse[None, :]
    cos, sin = jnp.cos(angles), jnp.sin(angles)
    zero = jnp.zeros_like(sin)
    cosine = jnp.concatenate([cos] * 4, axis=-1)
    upper = jnp.concatenate([-sin, zero] * 2, axis=-1)
    lower = jnp.concatenate([zero, sin] * 2, axis=-1)
    return cosine, upper, lower


def turn(u, upper, lower):
    return pltpu.roll(u, 128 - HD // 2, 1) * upper + pltpu.roll(u, HD // 2, 1) * lower


def attn_fwd_kernel(xh, wq, wk, wv, cos, upper, lower, seg_col, seg_row, o, q, k, v, lse, kh):
    length = xh.shape[0]
    rows = min(256, length)
    lane = lax.broadcasted_iota(jnp.int32, (length, 128), 1)
    first = lane < HD
    tokens = xh[...]
    qf = dotf(tokens, wq[...], NN)
    qf = qf * cos[...] + turn(qf, upper[...], lower[...])
    q[...] = (qf * (1.0 / math.sqrt(HD))).astype(BF)
    kf = dotf(tokens, wk[...], NN)
    kf = (kf * cos[...] + turn(kf, upper[...], lower[...])).astype(BF)
    k[...] = kf
    kh[0] = jnp.where(first, kf, jnp.zeros_like(kf))
    kh[1] = jnp.where(first, jnp.zeros_like(kf), kf)
    v[...] = dotf(tokens, wv[...], NN).astype(BF)

    def block(i, carry):
        at = pl.multiple_of(i * rows, rows)
        q_rows = q[pl.ds(at, rows), :]
        same = seg_col[pl.ds(at, rows), :] == seg_row[...]
        outs = []
        for head in range(2):
            scores = dotf(q_rows, kh[head], NT)
            scores = jnp.where(same, scores, -1e30)
            top = jnp.max(scores, axis=-1, keepdims=True)
            expv = jnp.exp(scores - top)
            total = jnp.sum(expv, axis=-1, keepdims=True)
            low = (expv * (1.0 / total)).astype(BF)
            outs.append(dotf(low, v[...], NN))
            level = top + jnp.log(total)
            flat = jnp.transpose(jnp.broadcast_to(level, (rows, 128)))
            lse[0, pl.ds(head, 1), pl.ds(at, rows)] = flat[0:1, :]
        o[pl.ds(at, rows), :] = jnp.where(first[:rows], outs[0], outs[1]).astype(BF)
        return carry

    lax.fori_loop(0, length // rows, block, 0)


def attn_fwd(xh, w_qk, w_vo, tables, seg_col, seg_row):
    length, width = xh.shape
    pairs = w_qk.shape[1] // 256
    whole = lambda a: pl.BlockSpec(a.shape, lambda h: (0,) * a.ndim)
    col = lambda off: pl.BlockSpec((width, 128), lambda h: (0, h + off))
    out = pl.BlockSpec((length, 128), lambda h: (0, h))
    shape = jax.ShapeDtypeStruct((length, pairs * 128), BF)
    flops = 2 * length * width * pairs * 384 + 4 * pairs * 2 * length * length * 128
    return pl.pallas_call(
        attn_fwd_kernel,
        grid=(pairs,),
        in_specs=[whole(xh), col(0), col(pairs), col(0)]
        + [whole(t) for t in tables]
        + [whole(seg_col), whole(seg_row)],
        out_specs=[out] * 4 + [pl.BlockSpec((1, 2, length), lambda h: (h, 0, 0))],
        out_shape=[shape] * 4 + [jax.ShapeDtypeStruct((pairs, 2, length), F32)],
        scratch_shapes=[pltpu.VMEM((2, length, 128), BF)],
        cost_estimate=pl.CostEstimate(
            flops=flops, bytes_accessed=length * width * 8, transcendentals=pairs * 2 * length * length
        ),
        name="attn_fwd",
    )(xh, w_qk, w_qk, w_vo, *tables, seg_col, seg_row)


def attn_bwd_kernel(
    q, k, v, o, do, lse, cos, upper, lower, seg_col, seg_row, pg, kh, dk, dv
):
    length = q.shape[0]
    rows = min(256, length)
    lane = lax.broadcasted_iota(jnp.int32, (length, 128), 1)
    first = lane < HD
    kf = k[...]
    none = jnp.zeros_like(kf)
    kh[0] = jnp.where(first, kf, none)
    kh[1] = jnp.where(first, none, kf)
    dk[...] = jnp.zeros_like(dk)
    dv[...] = jnp.zeros_like(dv)

    def block(i, carry):
        at = pl.multiple_of(i * rows, rows)
        here = pl.ds(at, rows)
        q_rows = q[here, :]
        g_rows = do[here, :]
        seg_here = seg_row[:, here]
        same = seg_col[...] == seg_here
        prod = g_rows.astype(F32) * o[here, :].astype(F32)
        f = first[:rows]
        blank = jnp.zeros_like(q_rows)
        dq = jnp.zeros((rows, 128), F32)
        for head in range(2):
            mine = f if head == 0 else jnp.logical_not(f)
            q_head = jnp.where(mine, q_rows, blank)
            g_head = jnp.where(mine, g_rows, blank)
            delta = lax.dot_general(
                jnp.ones((8, 128), F32),
                jnp.where(mine, prod, 0.0),
                (NT, ((), ())),
                precision=lax.Precision.HIGHEST,
                preferred_element_type=F32,
            )[0:1, :]
            scores = dotf(k[...], q_head, NT)
            level = lse[0, pl.ds(head, 1), here]
            probs = jnp.where(same, jnp.exp(scores - level), 0.0)
            dv[...] += dotf(probs.astype(BF), g_head, NN)
            dp = dotf(v[...], g_head, NT)
            ds = (probs * (dp - delta)).astype(BF)
            dk[...] += dotf(ds, q_head, NN)
            dq = dq + dotf(ds, kh[head], TN)
        dq = dq * (1.0 / math.sqrt(HD))
        c, a, b = cos[here, :], upper[here, :], lower[here, :]
        pg[0, here, :] = (dq * c - turn(dq, a, b)).astype(BF)
        return carry

    lax.fori_loop(0, length // rows, block, 0)
    dkf = dk[...]
    pg[1] = (dkf * cos[...] - turn(dkf, upper[...], lower[...])).astype(BF)
    pg[2] = dv[...].astype(BF)


def attn_bwd(q, k, v, o, do, lse, tables, seg_col, seg_row):
    length, width = q.shape
    pairs = width // 128
    whole = lambda a: pl.BlockSpec(a.shape, lambda h: (0,) * a.ndim)
    col = pl.BlockSpec((length, 128), lambda h: (0, h))
    return pl.pallas_call(
        attn_bwd_kernel,
        grid=(pairs,),
        in_specs=[col] * 5
        + [pl.BlockSpec((1, 2, length), lambda h: (h, 0, 0))]
        + [whole(t) for t in tables]
        + [whole(seg_col), whole(seg_row)],
        out_specs=pl.BlockSpec((3, length, 128), lambda h: (0, 0, h)),
        out_shape=jax.ShapeDtypeStruct((3, length, width), BF),
        scratch_shapes=[
            pltpu.VMEM((2, length, 128), BF),
            pltpu.VMEM((length, 128), F32),
            pltpu.VMEM((length, 128), F32),
        ],
        cost_estimate=pl.CostEstimate(
            flops=10 * pairs * 2 * length * length * 128,
            bytes_accessed=length * width * 20,
            transcendentals=pairs * 2 * length * length,
        ),
        name="attn_bwd",
    )(q, k, v, o, do, lse, *tables, seg_col, seg_row)


class Chips:
    def __init__(self):
        self.axes = ("dp", "tensor")
        dp = lax.axis_index("dp")
        self.z, self.x, self.core = dp // 4, (dp // 2) % 2, dp % 2
        self.y = lax.axis_index("tensor")

    @staticmethod
    def place(z, x, c, y):
        return ((z * 2 + x) * 2 + c) * 2 + y

    def send(self, value, dz=0, dx=0, dy=0, dc=0):
        pairs = [
            (self.place(z, x, c, y), self.place(z ^ dz, x ^ dx, c ^ dc, y ^ dy))
            for z in range(4)
            for x in range(2)
            for c in range(2)
            for y in range(2)
        ]
        return lax.ppermute(value, self.axes, pairs)

    def swap(self, value):
        pairs = [
            (self.place(z, x, c, y), self.place(z, x, y, c))
            for z in range(4)
            for x in range(2)
            for c in range(2)
            for y in range(2)
        ]
        return lax.ppermute(value, self.axes, pairs)

    def flips(self, blocks):
        for axis, bit in ((1, self.y), (2, self.x), (3, self.z // 2), (4, self.z % 2)):
            blocks = jnp.where(bit == 1, jnp.flip(blocks, axis), blocks)
        return blocks

    def to_relative(self, value):
        rows, width = value.shape
        blocks = value.reshape(rows, 2, 2, 2, 2, width // 16).transpose(0, 4, 3, 1, 2, 5)
        return self.flips(blocks).reshape(rows, width)

    def from_relative(self, value):
        rows, width = value.shape
        blocks = self.flips(value.reshape(rows, 2, 2, 2, 2, width // 16))
        return blocks.transpose(0, 3, 4, 2, 1, 5).reshape(rows, width)

    def positions(self, half):
        near = jnp.arange(half, dtype=jnp.int32)
        return jnp.concatenate([near + self.core * half, near + (1 - self.core) * half])

    def turn_rows(self, value):
        half = value.shape[0] // 2
        return jnp.where(self.core == 0, value, jnp.concatenate([value[half:], value[:half]]))

    def gather_rows(self, value):
        return jnp.concatenate([value, self.send(value, dc=1)], axis=0)

    def scatter_rows(self, value):
        half = value.shape[0] // 2
        return value[:half] + self.send(value[half:].astype(BF), dc=1).astype(F32)

    def gather(self, a, b):
        parts = [(a, b)] + [(self.send(a, dz=k), self.send(b, dz=k)) for k in (1, 2, 3)]
        za = jnp.stack([p[0] for p in parts])
        zb = jnp.stack([p[1] for p in parts])
        xa = jnp.concatenate([za, self.send(za, dx=1)])
        ya = self.send(xa, dy=1)
        yb = self.send(zb, dy=1)
        xb = self.send(jnp.concatenate([zb, yb]), dx=1)
        full_a = jnp.concatenate([xa, ya])
        full_b = jnp.concatenate([zb, xb[:4], yb, xb[4:]])
        flat = lambda f: f.reshape((f.shape[0] * f.shape[1],) + f.shape[2:])
        return flat(full_a), flat(full_b)

    def reduce(self, a, b):
        a = a.astype(BF).reshape(16, a.shape[0] // 16, a.shape[1])
        b = b.astype(BF).reshape(16, b.shape[0] // 16, b.shape[1])
        add = lambda u, w: (u.astype(F32) + w.astype(F32)).astype(BF)
        a = add(a[:8], self.send(a[8:], dy=1))
        b = add(
            jnp.concatenate([b[:4], b[8:12]]),
            self.send(jnp.concatenate([b[4:8], b[12:]]), dx=1),
        )
        a = add(a[:4], self.send(a[4:], dx=1))
        b = add(b[:4], self.send(b[4:], dy=1))
        sum_a, sum_b = a[0].astype(F32), b[0].astype(F32)
        for k in (1, 2, 3):
            sum_a = sum_a + self.send(a[k], dz=k).astype(F32)
            sum_b = sum_b + self.send(b[k], dz=k).astype(F32)
        return self.swap(sum_a.astype(BF)).astype(F32), self.swap(sum_b.astype(BF)).astype(F32)

    def sum_tensor(self, value):
        return value + self.send(value, dy=1)


class Axes:
    def swap(self, value):
        return value

    to_relative = from_relative = swap

    def positions(self, half):
        return jnp.arange(half * lax.axis_size("tensor"), dtype=jnp.int32)

    def turn_rows(self, value):
        return value

    def gather_rows(self, value):
        return lax.all_gather(value, "tensor", axis=0, tiled=True)

    def scatter_rows(self, value):
        return lax.psum_scatter(value.astype(BF), "tensor", scatter_dimension=0, tiled=True).astype(F32)

    def gather(self, a, b):
        return tuple(lax.all_gather(w, "dp", axis=0, tiled=True) for w in (a, b))

    def reduce(self, a, b):
        return tuple(
            lax.psum_scatter(w.astype(BF), "dp", scatter_dimension=0, tiled=True).astype(F32)
            for w in (a, b)
        )

    def sum_tensor(self, value):
        return lax.psum(value, "tensor")


def normalize(values):
    centred = values - jnp.mean(values, axis=-1, keepdims=True)
    scale = lax.rsqrt(jnp.mean(centred * centred, axis=-1, keepdims=True) + EPS)
    return centred * scale, scale


def normalize_back(f, xhat, scale):
    return scale * (
        f
        - jnp.mean(f, axis=-1, keepdims=True)
        - xhat * jnp.mean(f * xhat, axis=-1, keepdims=True)
    )


def gelu_parts(gate):
    half_erf = 0.5 * (1.0 + lax.erf(gate * (1.0 / math.sqrt(2.0))))
    density = jnp.exp(-0.5 * gate * gate) * (1.0 / math.sqrt(2.0 * math.pi))
    return gate * half_erf, half_erf + gate * density


def make_local(comm_type):
    def local(tokens, segments, w_qkv, w_out, w_in, w_down, g_attn, g_mlp, cotangent):
        comm = comm_type()
        shard = w_qkv.shape[0]
        cols = w_qkv.shape[2]
        units = w_in.shape[2]
        low = 128 * (units // 256)
        pad = 128 * pl.cdiv(units, 128) - units
        gain_one = g_attn.astype(F32)[:, None]
        gain_two = g_mlp.astype(F32)[:, None]
        scaled = lambda w, g: (w.astype(F32) * g).astype(BF)
        padded = lambda w: jnp.pad(w, ((0, 0), (0, pad)))
        down_rows = w_down.T
        a_one = jnp.concatenate([scaled(w_qkv[:, 0], gain_one), scaled(w_qkv[:, 1], gain_one)], axis=1)
        b_one = jnp.concatenate([scaled(w_qkv[:, 2], gain_one), w_out.T], axis=1)
        a_two = jnp.concatenate([padded(scaled(w_in[:, 0], gain_two)), down_rows[:, :low]], axis=1)
        b_two = jnp.concatenate([padded(scaled(w_in[:, 1], gain_two)), down_rows[:, low:]], axis=1)
        w_qk, w_vo = comm.gather(comm.swap(a_one), comm.swap(b_one))
        w_gd, w_ud = comm.gather(comm.swap(a_two), comm.swap(b_two))
        w_o = w_vo[:, cols:]
        w_gate, w_up = w_gd[:, :units], w_ud[:, :units]
        w_dn = jnp.concatenate([w_gd[:, units + pad :], w_ud[:, units + pad :]], axis=1)

        x_in = comm.to_relative(comm.swap(tokens[0])).astype(F32)
        seg = comm.turn_rows(comm.swap(segments[0]))
        cot = comm.to_relative(comm.swap(cotangent[0]))
        cot_all = comm.gather_rows(cot)
        tables = rope_tables(comm.positions(x_in.shape[0]))
        seg_col, seg_row = seg[:, None], seg[None, :]

        xh_one, scale_one = normalize(x_in)
        xh = comm.gather_rows(xh_one.astype(BF))
        o, q, k, v, lse = attn_fwd(xh, w_qk, w_vo, tables, seg_col, seg_row)
        resid = x_in + comm.scatter_rows(dotf(o, w_o, NT))
        xh_two, scale_two = normalize(resid)
        xn = comm.gather_rows(xh_two.astype(BF))
        gate, up = dotf(xn, w_gate, NN), dotf(xn, w_up, NN)
        act, slope = gelu_parts(gate)
        hidden = (act * up).astype(BF)
        mlp = comm.scatter_rows(dotf(hidden, w_dn, NT))
        result = comm.swap(comm.from_relative((resid + mlp).astype(BF)))

        hidden_grad = dotf(cot_all, w_dn, NN).astype(BF).astype(F32)
        gate_grad = (hidden_grad * up * slope).astype(BF)
        up_grad = (hidden_grad * act).astype(BF)
        f_two = comm.scatter_rows(dotf(gate_grad, w_gate, NT) + dotf(up_grad, w_up, NT))
        resid_grad = cot.astype(F32) + normalize_back(f_two, xh_two, scale_two)
        attn_cot = comm.gather_rows(resid_grad.astype(BF))

        d_down = dotf(cot_all, hidden, TN)
        d_gate, d_up = dotf(xn, gate_grad, TN), dotf(xn, up_grad, TN)
        wide = lambda g, d: jnp.concatenate([padded(g), d], axis=1)
        two_a, two_b = comm.reduce(wide(d_gate, d_down[:, :low]), wide(d_up, d_down[:, low:]))

        heads_grad = dotf(attn_cot, w_o, NN).astype(BF)
        pg = attn_bwd(q, k, v, o, heads_grad, lse, tables, seg_col, seg_row)
        d_out = dotf(attn_cot, o, TN)
        d_q, d_k, d_v = (dotf(xh, pg[i], TN) for i in range(3))
        one_a, one_b = comm.reduce(
            jnp.concatenate([d_q, d_k], axis=1), jnp.concatenate([d_v, d_out], axis=1)
        )
        f_one = comm.scatter_rows(
            dotf(pg[0], w_qk[:, :cols], NT)
            + dotf(pg[1], w_qk[:, cols:], NT)
            + dotf(pg[2], w_vo[:, :cols], NT)
        )
        token_grad = resid_grad + normalize_back(f_one, xh_one, scale_one)
        token_grad = comm.swap(comm.from_relative(token_grad.astype(BF))).astype(F32)

        qkv_raw = jnp.stack([one_a[:, :cols], one_a[:, cols:], one_b[:, :cols]], axis=1)
        in_raw = jnp.stack([two_a[:, :units], two_b[:, :units]], axis=1)
        down_sum = jnp.concatenate([two_a[:, units + pad :], two_b[:, units + pad :]], axis=1).T
        gains = jnp.stack(
            [
                jnp.sum(qkv_raw * w_qkv.astype(F32), axis=(1, 2)),
                jnp.sum(in_raw * w_in.astype(F32), axis=(1, 2)),
            ]
        )
        gains = comm.sum_tensor(gains)
        return (
            result[None],
            token_grad[None],
            gains[0],
            gains[1],
            qkv_raw * gain_one[:, :, None],
            one_b[:, cols:].T,
            in_raw * gain_two[:, :, None],
            down_sum,
        )

    return local


def solution(mesh):
    paired = mesh.shape["dp"] == 16 and mesh.shape["tensor"] == 2
    return jax.shard_map(
        make_local(Chips if paired else Axes),
        mesh=mesh,
        in_specs=(
            P("dp", "tensor", None),
            P("dp", None),
            P("dp", None, "tensor"),
            P("tensor", "dp"),
            P("dp", None, "tensor"),
            P("tensor", "dp"),
            P("dp"),
            P("dp"),
            P("dp", "tensor", None),
        ),
        out_specs=(
            P("dp", "tensor", None),
            P("dp", "tensor", None),
            P("dp"),
            P("dp"),
            P("dp", None, "tensor"),
            P("tensor", "dp"),
            P("dp", None, "tensor"),
            P("tensor", "dp"),
        ),
        check_vma=False,
    )
```

```python
import math

import jax
import jax.numpy as jnp
from jax import lax
from jax.experimental import pallas as pl
from jax.experimental.pallas import tpu as pltpu
from jax.sharding import PartitionSpec as P

HD = 64
EPS = 1e-05
ROTARY_BASE = 160000.0
BF = jnp.bfloat16
F32 = jnp.float32


def dotf(a, b, dims):
    return lax.dot_general(a, b, (dims, ((), ())), preferred_element_type=F32)


NN = ((1,), (0,))
NT = ((1,), (1,))
TN = ((0,), (0,))


def rope_tables(positions):
    half = HD // 2
    inverse = 1.0 / ROTARY_BASE ** (jnp.arange(half).astype(F32) * (2.0 / HD))
    angles = positions.astype(F32)[:, None] * inverse[None, :]
    cos, sin = jnp.cos(angles), jnp.sin(angles)
    zero = jnp.zeros_like(sin)
    cosine = jnp.concatenate([cos] * 4, axis=-1)
    upper = jnp.concatenate([-sin, zero] * 2, axis=-1)
    lower = jnp.concatenate([zero, sin] * 2, axis=-1)
    return cosine, upper, lower


def turn(u, upper, lower):
    return pltpu.roll(u, 128 - HD // 2, 1) * upper + pltpu.roll(u, HD // 2, 1) * lower


def attn_fwd_kernel(xh, wq, wk, wv, cos, upper, lower, seg_col, seg_row, o, q, k, v, lse, kh):
    length = xh.shape[0]
    rows = min(256, length)
    lane = lax.broadcasted_iota(jnp.int32, (length, 128), 1)
    first = lane < HD
    tokens = xh[...]
    qf = dotf(tokens, wq[...], NN)
    qf = qf * cos[...] + turn(qf, upper[...], lower[...])
    q[...] = (qf * (1.0 / math.sqrt(HD))).astype(BF)
    kf = dotf(tokens, wk[...], NN)
    kf = (kf * cos[...] + turn(kf, upper[...], lower[...])).astype(BF)
    k[...] = kf
    kh[0] = jnp.where(first, kf, jnp.zeros_like(kf))
    kh[1] = jnp.where(first, jnp.zeros_like(kf), kf)
    v[...] = dotf(tokens, wv[...], NN).astype(BF)

    def block(i, carry):
        at = pl.multiple_of(i * rows, rows)
        q_rows = q[pl.ds(at, rows), :]
        same = seg_col[pl.ds(at, rows), :] == seg_row[...]
        outs = []
        for head in range(2):
            scores = dotf(q_rows, kh[head], NT)
            scores = jnp.where(same, scores, -1e30)
            top = jnp.max(scores, axis=-1, keepdims=True)
            expv = jnp.exp(scores - top)
            total = jnp.sum(expv, axis=-1, keepdims=True)
            low = (expv * (1.0 / total)).astype(BF)
            outs.append(dotf(low, v[...], NN))
            level = top + jnp.log(total)
            flat = jnp.transpose(jnp.broadcast_to(level, (rows, 128)))
            lse[0, pl.ds(head, 1), pl.ds(at, rows)] = flat[0:1, :]
        o[pl.ds(at, rows), :] = jnp.where(first[:rows], outs[0], outs[1]).astype(BF)
        return carry

    lax.fori_loop(0, length // rows, block, 0)


def attn_fwd(xh, w_qk, w_vo, tables, seg_col, seg_row):
    length, width = xh.shape
    pairs = w_qk.shape[1] // 256
    whole = lambda a: pl.BlockSpec(a.shape, lambda h: (0,) * a.ndim)
    col = lambda off: pl.BlockSpec((width, 128), lambda h: (0, h + off))
    out = pl.BlockSpec((length, 128), lambda h: (0, h))
    shape = jax.ShapeDtypeStruct((length, pairs * 128), BF)
    flops = 2 * length * width * pairs * 384 + 4 * pairs * 2 * length * length * 128
    return pl.pallas_call(
        attn_fwd_kernel,
        grid=(pairs,),
        in_specs=[whole(xh), col(0), col(pairs), col(0)]
        + [whole(t) for t in tables]
        + [whole(seg_col), whole(seg_row)],
        out_specs=[out] * 4 + [pl.BlockSpec((1, 2, length), lambda h: (h, 0, 0))],
        out_shape=[shape] * 4 + [jax.ShapeDtypeStruct((pairs, 2, length), F32)],
        scratch_shapes=[pltpu.VMEM((2, length, 128), BF)],
        cost_estimate=pl.CostEstimate(
            flops=flops, bytes_accessed=length * width * 8, transcendentals=pairs * 2 * length * length
        ),
        name="attn_fwd",
    )(xh, w_qk, w_qk, w_vo, *tables, seg_col, seg_row)


def attn_bwd_kernel(
    q, k, v, o, do, lse, cos, upper, lower, seg_col, seg_row, pg, kh, dk, dv
):
    length = q.shape[0]
    rows = min(256, length)
    lane = lax.broadcasted_iota(jnp.int32, (length, 128), 1)
    first = lane < HD
    kf = k[...]
    none = jnp.zeros_like(kf)
    kh[0] = jnp.where(first, kf, none)
    kh[1] = jnp.where(first, none, kf)
    dk[...] = jnp.zeros_like(dk)
    dv[...] = jnp.zeros_like(dv)

    def block(i, carry):
        at = pl.multiple_of(i * rows, rows)
        here = pl.ds(at, rows)
        q_rows = q[here, :]
        g_rows = do[here, :]
        seg_here = seg_row[:, here]
        same = seg_col[...] == seg_here
        prod = g_rows.astype(F32) * o[here, :].astype(F32)
        f = first[:rows]
        blank = jnp.zeros_like(q_rows)
        dq = jnp.zeros((rows, 128), F32)
        for head in range(2):
            mine = f if head == 0 else jnp.logical_not(f)
            q_head = jnp.where(mine, q_rows, blank)
            g_head = jnp.where(mine, g_rows, blank)
            delta = lax.dot_general(
                jnp.ones((8, 128), F32),
                jnp.where(mine, prod, 0.0),
                (NT, ((), ())),
                precision=lax.Precision.HIGHEST,
                preferred_element_type=F32,
            )[0:1, :]
            scores = dotf(k[...], q_head, NT)
            level = lse[0, pl.ds(head, 1), here]
            probs = jnp.where(same, jnp.exp(scores - level), 0.0)
            dv[...] += dotf(probs.astype(BF), g_head, NN)
            dp = dotf(v[...], g_head, NT)
            ds = (probs * (dp - delta)).astype(BF)
            dk[...] += dotf(ds, q_head, NN)
            dq = dq + dotf(ds, kh[head], TN)
        dq = dq * (1.0 / math.sqrt(HD))
        c, a, b = cos[here, :], upper[here, :], lower[here, :]
        pg[0, here, :] = (dq * c - turn(dq, a, b)).astype(BF)
        return carry

    lax.fori_loop(0, length // rows, block, 0)
    dkf = dk[...]
    pg[1] = (dkf * cos[...] - turn(dkf, upper[...], lower[...])).astype(BF)
    pg[2] = dv[...].astype(BF)


def attn_bwd(q, k, v, o, do, lse, tables, seg_col, seg_row):
    length, width = q.shape
    pairs = width // 128
    whole = lambda a: pl.BlockSpec(a.shape, lambda h: (0,) * a.ndim)
    col = pl.BlockSpec((length, 128), lambda h: (0, h))
    return pl.pallas_call(
        attn_bwd_kernel,
        grid=(pairs,),
        in_specs=[col] * 5
        + [pl.BlockSpec((1, 2, length), lambda h: (h, 0, 0))]
        + [whole(t) for t in tables]
        + [whole(seg_col), whole(seg_row)],
        out_specs=pl.BlockSpec((3, length, 128), lambda h: (0, 0, h)),
        out_shape=jax.ShapeDtypeStruct((3, length, width), BF),
        scratch_shapes=[
            pltpu.VMEM((2, length, 128), BF),
            pltpu.VMEM((length, 128), F32),
            pltpu.VMEM((length, 128), F32),
        ],
        cost_estimate=pl.CostEstimate(
            flops=10 * pairs * 2 * length * length * 128,
            bytes_accessed=length * width * 20,
            transcendentals=pairs * 2 * length * length,
        ),
        name="attn_bwd",
    )(q, k, v, o, do, lse, *tables, seg_col, seg_row)


SHARD = (4, 2, 2)


def place():
    dp = lax.axis_index("dp")
    return dp // 4, (dp // 2) % 2, dp % 2, lax.axis_index("tensor")


def partners():
    z, x, c, y = place()
    at = lambda z, x, c, y: ((z * 2 + x) * 2 + c, y)
    return {
        "z1": at(z + 1 - 2 * (z % 2), x, c, y),
        "z2": at(z + 2 - 4 * (z // 2), x, c, y),
        "z3": at(3 - z, x, c, y),
        "x": at(z, 1 - x, c, y),
        "y": at(z, x, c, 1 - y),
        "c": at(z, x, 1 - c, y),
    }


def meet(peers):
    barrier = pltpu.get_barrier_semaphore()
    for peer in peers.values():
        pl.semaphore_signal(barrier, inc=1, device_id=peer, device_id_type=pl.DeviceIdType.MESH)
    pl.semaphore_wait(barrier, len(peers))


def remote(src, dst, send_sem, recv_sem, peer):
    return pltpu.make_async_remote_copy(
        src_ref=src,
        dst_ref=dst,
        send_sem=send_sem,
        recv_sem=recv_sem,
        device_id=peer,
        device_id_type=pl.DeviceIdType.MESH,
    )


def to_place(values, inverse=False):
    z, x, _, y = place()
    tiles = [values[:, j * 128 : (j + 1) * 128] for j in range(8)]
    tiles = [jnp.where(y == 1, pltpu.roll(t, 64, 1), t) for t in tiles]
    for bit, step in ((x, 1), (z % 2, 2), (z // 2, 4)):
        tiles = [jnp.where(bit == 1, tiles[j ^ step], tiles[j]) for j in range(8)]
    return jnp.concatenate(tiles, axis=1)


class Gather:
    MESSAGES = 15

    def __init__(self, own, buf, rows, axes, peers, sems, base):
        self.buf, self.rows, self.axes, self.peers = buf, rows, axes, peers
        self.own = own.at[rows]
        self.send_sem, self.recv_sem = sems
        self.base = base

    def slot(self, z, first, second):
        x, y = (first, second) if self.axes[0] == "x" else (second, first)
        return self.buf.at[z, x, y, self.rows]

    def copy(self, i):
        if i < 3:
            src, dst, peer = self.own, self.slot(i + 1, 0, 0), "z%d" % (i + 1)
        elif i < 7:
            src, dst, peer = self.slot(i - 3, 0, 0), self.slot(i - 3, 1, 0), self.axes[0]
        else:
            f, z = divmod(i - 7, 4)
            src, dst, peer = self.slot(z, f, 0), self.slot(z, f, 1), self.axes[1]
        if i in (3, 7):
            src = self.own
        n = self.base + i
        return remote(src, dst, self.send_sem.at[n], self.recv_sem.at[n], self.peers[peer])

    def start_z(self):
        for i in range(3):
            self.copy(i).start()

    def relay_z(self, z):
        if z:
            self.copy(z - 1).wait_recv()
        self.copy(3 + z).start()
        self.copy(7 + z).start()

    def relay_first(self, z):
        self.copy(3 + z).wait_recv()
        self.copy(11 + z).start()

    def finish(self):
        for i in range(7, 15):
            self.copy(i).wait_recv()
        for i in range(15):
            self.copy(i).wait_send()


def forward_kernel(
    a_own, b_own, g_own, u_own, d_own, x_half, cos, upper, lower, seg_col, seg_row,
    q, k, v, o, lse, xh, w_qk, w_vo, resid, xn, w_gate, w_up, w_down,
    kh, x_rel, part, sent, got, send_sem, recv_sem, pair_send, pair_recv, own_sem,
):
    length = xh.shape[0]
    half = length // 2
    width = xh.shape[1]
    pairs = q.shape[1] // 128
    rows = 256
    peers = partners()
    sems = (send_sem, recv_sem)
    n = Gather.MESSAGES
    whole, low, high = pl.ds(0, 64), pl.ds(0, 32), pl.ds(32, 32)
    one = [
        Gather(a_own, w_qk, whole, "xy", peers, sems, 0),
        Gather(b_own, w_vo, whole, "yx", peers, sems, n),
    ]
    two = [
        Gather(g_own, w_gate, whole, "xy", peers, sems, 2 * n),
        Gather(u_own, w_up, whole, "yx", peers, sems, 3 * n),
    ]
    three = [
        Gather(d_own, w_down, low, "xy", peers, sems, 4 * n),
        Gather(d_own, w_down, high, "yx", peers, sems, 5 * n),
    ]
    owns = [
        pltpu.make_async_copy(src, dst.at[0, 0, 0], own_sem.at[i])
        for i, (src, dst) in enumerate(
            ((a_own, w_qk), (b_own, w_vo), (g_own, w_gate), (u_own, w_up), (d_own, w_down))
        )
    ]
    for copy in owns:
        copy.start()
    meet(peers)
    for gather in one:
        gather.start_z()
    for gather in one:
        gather.relay_z(0)

    def first_norm(i, carry):
        here = pl.ds(pl.multiple_of(i * 128, 128), 128)
        values = to_place(x_half[here, :].astype(F32))
        x_rel[here, :] = values.astype(BF)
        xh[here, :] = normalize(values)[0].astype(BF)
        return carry

    lax.fori_loop(0, half // 128, first_norm, 0)
    for z in (1, 2, 3):
        for gather in one:
            gather.relay_z(z)
    swap_xh = remote(
        xh.at[pl.ds(0, half)], xh.at[pl.ds(half, half)], pair_send.at[0], pair_recv.at[0], peers["c"]
    )
    swap_xh.start()
    for gather in two:
        gather.start_z()
    for z in range(4):
        for gather in one:
            gather.relay_first(z)
    for gather in three:
        gather.start_z()
    swap_xh.wait()
    for gather in one:
        gather.finish()
    for copy in owns:
        copy.wait()

    events = {}
    for z in range(4):
        events.setdefault(1 + z, []).extend((g.relay_z, z) for g in two)
        events.setdefault(6 + z, []).extend((g.relay_first, z) for g in two)
        events.setdefault(9 + z, []).extend((g.relay_z, z) for g in three)
    first = lax.broadcasted_iota(jnp.int32, (length, 128), 1) < HD

    def pair(h, carry):
        lanes = pl.ds(pl.multiple_of(h * 128, 128), 128)
        lanes_k = pl.ds(pl.multiple_of((h + pairs) * 128, 128), 128)
        weight = lambda ref, cols: ref[:, :, :, :, cols].reshape(width, 128)
        tokens = xh[...]
        qf = dotf(tokens, weight(w_qk, lanes), NN)
        qf = qf * cos[...] + turn(qf, upper[...], lower[...])
        q[:, lanes] = (qf * (1.0 / math.sqrt(HD))).astype(BF)
        kf = dotf(tokens, weight(w_qk, lanes_k), NN)
        kf = (kf * cos[...] + turn(kf, upper[...], lower[...])).astype(BF)
        k[:, lanes] = kf
        kh[0] = jnp.where(first, kf, jnp.zeros_like(kf))
        kh[1] = jnp.where(first, jnp.zeros_like(kf), kf)
        v[:, lanes] = dotf(tokens, weight(w_vo, lanes), NN).astype(BF)

        def block(i, carry):
            for step, calls in events.items():

                @pl.when(h * (length // rows) + i == step)
                def _():
                    for call, z in calls:
                        call(z)

            at = pl.multiple_of(i * rows, rows)
            q_rows = q[pl.ds(at, rows), lanes]
            same = seg_col[pl.ds(at, rows), :] == seg_row[...]
            outs = []
            for head in range(2):
                scores = dotf(q_rows, kh[head], NT)
                scores = jnp.where(same, scores, -1e30)
                top = jnp.max(scores, axis=-1, keepdims=True)
                expv = jnp.exp(scores - top)
                total = jnp.sum(expv, axis=-1, keepdims=True)
                low_probs = (expv * (1.0 / total)).astype(BF)
                outs.append(dotf(low_probs, v[:, lanes], NN))
                level = top + jnp.log(total)
                flat = jnp.transpose(jnp.broadcast_to(level, (rows, 128)))
                lse[h, pl.ds(head, 1), pl.ds(at, rows)] = flat[0:1, :]
            o[pl.ds(at, rows), lanes] = jnp.where(first[:rows], outs[0], outs[1]).astype(BF)
            return carry

        return lax.fori_loop(0, length // rows, block, carry)

    lax.fori_loop(0, pairs, pair, 0)
    w_o = w_vo[:, :, :, :, pairs * 128 :].reshape(width, pairs * 128)

    def project(i, carry):
        at = pl.multiple_of(half + i * rows, rows)
        sent[pl.ds(pl.multiple_of(i * rows, rows), rows), :] = dotf(
            o[pl.ds(at, rows), :], w_o, NT
        ).astype(BF)
        return carry

    lax.fori_loop(0, half // rows, project, 0)

    def project_own(i, carry):
        here = pl.ds(pl.multiple_of(i * rows, rows), rows)
        part[here, :] = dotf(o[here, :], w_o, NT)
        return carry

    give = remote(sent, got, pair_send.at[1], pair_recv.at[1], peers["c"])
    lax.fori_loop(0, half // rows, project_own, 0)
    give.start()
    for gather in two + three:
        for z in range(4):
            if gather in three:
                gather.relay_first(z)
    give.wait()

    def second_norm(i, carry):
        here = pl.ds(pl.multiple_of(i * 128, 128), 128)
        values = x_rel[here, :].astype(F32) + (part[here, :] + got[here, :].astype(F32))
        resid[here, :] = values
        xn[here, :] = normalize(values)[0].astype(BF)
        return carry

    lax.fori_loop(0, half // 128, second_norm, 0)
    swap_xn = remote(
        xn.at[pl.ds(0, half)], xn.at[pl.ds(half, half)], pair_send.at[2], pair_recv.at[2], peers["c"]
    )
    swap_xn.start()
    for gather in two + three:
        gather.finish()
    swap_xn.wait()


def forward_block(owned, x_half, tables, seg_col, seg_row):
    half, width = x_half.shape
    length = 2 * half
    cols = owned[0].shape[1] // 2
    pairs = cols // 128
    units = owned[2].shape[1]
    vmem = pl.BlockSpec(memory_space=pltpu.VMEM)
    any_ = pl.BlockSpec(memory_space=pl.ANY)
    gathered = lambda n: jax.ShapeDtypeStruct(SHARD + (width // 16, n), BF)
    heads = jax.ShapeDtypeStruct((length, cols), BF)
    return pl.pallas_call(
        forward_kernel,
        in_specs=[any_] * 5 + [vmem] * 6,
        out_specs=[vmem] * 10 + [any_] * 3,
        out_shape=[heads] * 4
        + [
            jax.ShapeDtypeStruct((pairs, 2, length), F32),
            jax.ShapeDtypeStruct((length, width), BF),
            gathered(2 * cols),
            gathered(2 * cols),
            jax.ShapeDtypeStruct((half, width), F32),
            jax.ShapeDtypeStruct((length, width), BF),
        ]
        + [gathered(units)] * 3,
        scratch_shapes=[
            pltpu.VMEM((2, length, 128), BF),
            pltpu.VMEM((half, width), BF),
            pltpu.VMEM((half, width), F32),
            pltpu.VMEM((half, width), BF),
            pltpu.VMEM((half, width), BF),
            pltpu.SemaphoreType.DMA((6 * Gather.MESSAGES,)),
            pltpu.SemaphoreType.DMA((6 * Gather.MESSAGES,)),
            pltpu.SemaphoreType.DMA((3,)),
            pltpu.SemaphoreType.DMA((3,)),
            pltpu.SemaphoreType.DMA((5,)),
        ],
        compiler_params=pltpu.CompilerParams(collective_id=0, has_side_effects=True),
        name="forward_block",
    )(*owned, x_half, *tables, seg_col, seg_row)


class Chips:
    def __init__(self):
        self.axes = ("dp", "tensor")
        dp = lax.axis_index("dp")
        self.z, self.x, self.core = dp // 4, (dp // 2) % 2, dp % 2
        self.y = lax.axis_index("tensor")

    @staticmethod
    def place(z, x, c, y):
        return ((z * 2 + x) * 2 + c) * 2 + y

    def send(self, value, dz=0, dx=0, dy=0, dc=0):
        pairs = [
            (self.place(z, x, c, y), self.place(z ^ dz, x ^ dx, c ^ dc, y ^ dy))
            for z in range(4)
            for x in range(2)
            for c in range(2)
            for y in range(2)
        ]
        return lax.ppermute(value, self.axes, pairs)

    def swap(self, value):
        pairs = [
            (self.place(z, x, c, y), self.place(z, x, y, c))
            for z in range(4)
            for x in range(2)
            for c in range(2)
            for y in range(2)
        ]
        return lax.ppermute(value, self.axes, pairs)

    def to_relative(self, value):
        rows, width = value.shape
        blocks = value.reshape(rows, 2, 2, 2, 2, width // 16)
        for axis, bit in ((4, self.y), (3, self.x), (2, self.z % 2), (1, self.z // 2)):
            blocks = jnp.where(bit == 1, jnp.flip(blocks, axis), blocks)
        return blocks.reshape(rows, width)

    from_relative = to_relative

    def positions(self, half):
        near = jnp.arange(half, dtype=jnp.int32)
        return jnp.concatenate([near + self.core * half, near + (1 - self.core) * half])

    def turn_rows(self, value):
        half = value.shape[0] // 2
        return jnp.where(self.core == 0, value, jnp.concatenate([value[half:], value[:half]]))

    def gather_rows(self, value):
        return jnp.concatenate([value, self.send(value, dc=1)], axis=0)

    def scatter_rows(self, value):
        half = value.shape[0] // 2
        return value[:half] + self.send(value[half:].astype(BF), dc=1).astype(F32)

    def reduce(self, a, b):
        order = lambda w: w.astype(BF).reshape(4, 2, 2, -1, w.shape[1]).swapaxes(0, 2)
        a, b = (order(w).reshape(16, -1, w.shape[1]) for w in (a, b))
        add = lambda u, w: (u.astype(F32) + w.astype(F32)).astype(BF)
        a = add(a[:8], self.send(a[8:], dy=1))
        b = add(
            jnp.concatenate([b[:4], b[8:12]]),
            self.send(jnp.concatenate([b[4:8], b[12:]]), dx=1),
        )
        a = add(a[:4], self.send(a[4:], dx=1))
        b = add(b[:4], self.send(b[4:], dy=1))
        sum_a, sum_b = a[0].astype(F32), b[0].astype(F32)
        for k in (1, 2, 3):
            sum_a = sum_a + self.send(a[k], dz=k).astype(F32)
            sum_b = sum_b + self.send(b[k], dz=k).astype(F32)
        return self.swap(sum_a.astype(BF)).astype(F32), self.swap(sum_b.astype(BF)).astype(F32)

    def sum_tensor(self, value):
        return value + self.send(value, dy=1)


class Axes:
    def swap(self, value):
        return value

    to_relative = from_relative = swap

    def positions(self, half):
        return jnp.arange(half * lax.axis_size("tensor"), dtype=jnp.int32)

    def turn_rows(self, value):
        return value

    def gather_rows(self, value):
        return lax.all_gather(value, "tensor", axis=0, tiled=True)

    def scatter_rows(self, value):
        return lax.psum_scatter(value.astype(BF), "tensor", scatter_dimension=0, tiled=True).astype(F32)

    def gather(self, a, b):
        return tuple(lax.all_gather(w, "dp", axis=0, tiled=True) for w in (a, b))

    def reduce(self, a, b):
        return tuple(
            lax.psum_scatter(w.astype(BF), "dp", scatter_dimension=0, tiled=True).astype(F32)
            for w in (a, b)
        )

    def sum_tensor(self, value):
        return lax.psum(value, "tensor")


def normalize(values):
    centred = values - jnp.mean(values, axis=-1, keepdims=True)
    scale = lax.rsqrt(jnp.mean(centred * centred, axis=-1, keepdims=True) + EPS)
    return centred * scale, scale


def normalize_back(f, xhat, scale):
    return scale * (
        f
        - jnp.mean(f, axis=-1, keepdims=True)
        - xhat * jnp.mean(f * xhat, axis=-1, keepdims=True)
    )


def gelu_parts(gate):
    half_erf = 0.5 * (1.0 + lax.erf(gate * (1.0 / math.sqrt(2.0))))
    density = jnp.exp(-0.5 * gate * gate) * (1.0 / math.sqrt(2.0 * math.pi))
    return gate * half_erf, half_erf + gate * density


def make_local(comm_type):
    def local(tokens, segments, w_qkv, w_out, w_in, w_down, g_attn, g_mlp, cotangent):
        comm = comm_type()
        paired = comm_type is Chips
        shard = w_qkv.shape[0]
        cols = w_qkv.shape[2]
        units = w_in.shape[2]
        low = 128 * (units // 256)
        pad = 128 * pl.cdiv(units, 128) - units
        gain_one = g_attn.astype(F32)[:, None]
        gain_two = g_mlp.astype(F32)[:, None]
        scaled = lambda w, g: (w.astype(F32) * g).astype(BF)
        padded = lambda w: jnp.pad(w, ((0, 0), (0, pad)))
        down_rows = w_down.T
        a_one = jnp.concatenate([scaled(w_qkv[:, 0], gain_one), scaled(w_qkv[:, 1], gain_one)], axis=1)
        b_one = jnp.concatenate([scaled(w_qkv[:, 2], gain_one), w_out.T], axis=1)
        own_gate, own_up = scaled(w_in[:, 0], gain_two), scaled(w_in[:, 1], gain_two)

        seg = comm.turn_rows(comm.swap(segments[0]))
        cot = comm.to_relative(comm.swap(cotangent[0]))
        cot_all = comm.gather_rows(cot)
        tables = rope_tables(comm.positions(tokens.shape[1]))
        seg_col, seg_row = seg[:, None], seg[None, :]
        owned = (a_one, b_one, own_gate, own_up, down_rows)
        if paired:
            owned = [comm.swap(w) for w in owned]
            x_half = comm.swap(tokens[0])
            q, k, v, o, lse, xh, w_qk, w_vo, resid, xn, w_gate, w_up, w_dn = forward_block(
                owned, x_half, tables, seg_col, seg_row
            )
            w_qk, w_vo, w_gate, w_up, w_dn = (
                w.reshape(-1, w.shape[-1]) for w in (w_qk, w_vo, w_gate, w_up, w_dn)
            )
            xh_one, scale_one = normalize(comm.to_relative(x_half).astype(F32))
            xh_two, scale_two = normalize(resid)
            w_o = w_vo[:, cols:]
        else:
            w_qk, w_vo, w_gate, w_up, w_dn = (
                lax.all_gather(w, "dp", axis=0, tiled=True) for w in owned
            )
            w_o = w_vo[:, cols:]
            x_in = tokens[0].astype(F32)
            xh_one, scale_one = normalize(x_in)
            xh = comm.gather_rows(xh_one.astype(BF))
            o, q, k, v, lse = attn_fwd(xh, w_qk, w_vo, tables, seg_col, seg_row)
            resid = x_in + comm.scatter_rows(dotf(o, w_o, NT))
            xh_two, scale_two = normalize(resid)
            xn = comm.gather_rows(xh_two.astype(BF))
        gate, up = dotf(xn, w_gate, NN), dotf(xn, w_up, NN)
        act, slope = gelu_parts(gate)
        hidden = (act * up).astype(BF)
        mlp = comm.scatter_rows(dotf(hidden, w_dn, NT))
        result = comm.swap(comm.from_relative((resid + mlp).astype(BF)))

        hidden_grad = dotf(cot_all, w_dn, NN).astype(BF).astype(F32)
        gate_grad = (hidden_grad * up * slope).astype(BF)
        up_grad = (hidden_grad * act).astype(BF)
        f_two = comm.scatter_rows(dotf(gate_grad, w_gate, NT) + dotf(up_grad, w_up, NT))
        resid_grad = cot.astype(F32) + normalize_back(f_two, xh_two, scale_two)
        attn_cot = comm.gather_rows(resid_grad.astype(BF))

        d_down = dotf(cot_all, hidden, TN)
        d_gate, d_up = dotf(xn, gate_grad, TN), dotf(xn, up_grad, TN)
        wide = lambda g, d: jnp.concatenate([padded(g), d], axis=1)
        two_a, two_b = comm.reduce(wide(d_gate, d_down[:, :low]), wide(d_up, d_down[:, low:]))

        heads_grad = dotf(attn_cot, w_o, NN).astype(BF)
        pg = attn_bwd(q, k, v, o, heads_grad, lse, tables, seg_col, seg_row)
        d_out = dotf(attn_cot, o, TN)
        d_q, d_k, d_v = (dotf(xh, pg[i], TN) for i in range(3))
        one_a, one_b = comm.reduce(
            jnp.concatenate([d_q, d_k], axis=1), jnp.concatenate([d_v, d_out], axis=1)
        )
        f_one = comm.scatter_rows(
            dotf(pg[0], w_qk[:, :cols], NT)
            + dotf(pg[1], w_qk[:, cols:], NT)
            + dotf(pg[2], w_vo[:, :cols], NT)
        )
        token_grad = resid_grad + normalize_back(f_one, xh_one, scale_one)
        token_grad = comm.swap(comm.from_relative(token_grad.astype(BF))).astype(F32)

        qkv_raw = jnp.stack([one_a[:, :cols], one_a[:, cols:], one_b[:, :cols]], axis=1)
        in_raw = jnp.stack([two_a[:, :units], two_b[:, :units]], axis=1)
        down_sum = jnp.concatenate([two_a[:, units + pad :], two_b[:, units + pad :]], axis=1).T
        gains = jnp.stack(
            [
                jnp.sum(qkv_raw * w_qkv.astype(F32), axis=(1, 2)),
                jnp.sum(in_raw * w_in.astype(F32), axis=(1, 2)),
            ]
        )
        gains = comm.sum_tensor(gains)
        return (
            result[None],
            token_grad[None],
            gains[0],
            gains[1],
            qkv_raw * gain_one[:, :, None],
            one_b[:, cols:].T,
            in_raw * gain_two[:, :, None],
            down_sum,
        )

    return local


def solution(mesh):
    paired = mesh.shape["dp"] == 16 and mesh.shape["tensor"] == 2
    return jax.shard_map(
        make_local(Chips if paired else Axes),
        mesh=mesh,
        in_specs=(
            P("dp", "tensor", None),
            P("dp", None),
            P("dp", None, "tensor"),
            P("tensor", "dp"),
            P("dp", None, "tensor"),
            P("tensor", "dp"),
            P("dp"),
            P("dp"),
            P("dp", "tensor", None),
        ),
        out_specs=(
            P("dp", "tensor", None),
            P("dp", "tensor", None),
            P("dp"),
            P("dp"),
            P("dp", None, "tensor"),
            P("tensor", "dp"),
            P("dp", None, "tensor"),
            P("tensor", "dp"),
        ),
        check_vma=False,
    )
```

```python
import math

import jax
import jax.numpy as jnp
from jax import lax
from jax.experimental import pallas as pl
from jax.experimental.pallas import tpu as pltpu
from jax.sharding import PartitionSpec as P

HD = 64
EPS = 1e-05
ROTARY_BASE = 160000.0
BF = jnp.bfloat16
F32 = jnp.float32


def dotf(a, b, dims):
    return lax.dot_general(a, b, (dims, ((), ())), preferred_element_type=F32)


NN = ((1,), (0,))
NT = ((1,), (1,))
TN = ((0,), (0,))


def rope_tables(positions):
    half = HD // 2
    inverse = 1.0 / ROTARY_BASE ** (jnp.arange(half).astype(F32) * (2.0 / HD))
    angles = positions.astype(F32)[:, None] * inverse[None, :]
    cos, sin = jnp.cos(angles), jnp.sin(angles)
    zero = jnp.zeros_like(sin)
    cosine = jnp.concatenate([cos] * 4, axis=-1)
    upper = jnp.concatenate([-sin, zero] * 2, axis=-1)
    lower = jnp.concatenate([zero, sin] * 2, axis=-1)
    return cosine, upper, lower


def turn(u, upper, lower):
    return pltpu.roll(u, 128 - HD // 2, 1) * upper + pltpu.roll(u, HD // 2, 1) * lower


def attn_fwd_kernel(xh, wq, wk, wv, cos, upper, lower, seg_col, seg_row, o, q, k, v, lse, kh):
    length = xh.shape[0]
    rows = min(256, length)
    lane = lax.broadcasted_iota(jnp.int32, (length, 128), 1)
    first = lane < HD
    tokens = xh[...]
    qf = dotf(tokens, wq[...], NN)
    qf = qf * cos[...] + turn(qf, upper[...], lower[...])
    q[...] = (qf * (1.0 / math.sqrt(HD))).astype(BF)
    kf = dotf(tokens, wk[...], NN)
    kf = (kf * cos[...] + turn(kf, upper[...], lower[...])).astype(BF)
    k[...] = kf
    kh[0] = jnp.where(first, kf, jnp.zeros_like(kf))
    kh[1] = jnp.where(first, jnp.zeros_like(kf), kf)
    v[...] = dotf(tokens, wv[...], NN).astype(BF)

    def block(i, carry):
        at = pl.multiple_of(i * rows, rows)
        q_rows = q[pl.ds(at, rows), :]
        same = seg_col[pl.ds(at, rows), :] == seg_row[...]
        outs = []
        for head in range(2):
            scores = dotf(q_rows, kh[head], NT)
            scores = jnp.where(same, scores, -1e30)
            top = jnp.max(scores, axis=-1, keepdims=True)
            expv = jnp.exp(scores - top)
            total = jnp.sum(expv, axis=-1, keepdims=True)
            low = (expv * (1.0 / total)).astype(BF)
            outs.append(dotf(low, v[...], NN))
            level = top + jnp.log(total)
            flat = jnp.transpose(jnp.broadcast_to(level, (rows, 128)))
            lse[0, pl.ds(head, 1), pl.ds(at, rows)] = flat[0:1, :]
        o[pl.ds(at, rows), :] = jnp.where(first[:rows], outs[0], outs[1]).astype(BF)
        return carry

    lax.fori_loop(0, length // rows, block, 0)


def attn_fwd(xh, w_qk, w_vo, tables, seg_col, seg_row):
    length, width = xh.shape
    pairs = w_qk.shape[1] // 256
    whole = lambda a: pl.BlockSpec(a.shape, lambda h: (0,) * a.ndim)
    col = lambda off: pl.BlockSpec((width, 128), lambda h: (0, h + off))
    out = pl.BlockSpec((length, 128), lambda h: (0, h))
    shape = jax.ShapeDtypeStruct((length, pairs * 128), BF)
    flops = 2 * length * width * pairs * 384 + 4 * pairs * 2 * length * length * 128
    return pl.pallas_call(
        attn_fwd_kernel,
        grid=(pairs,),
        in_specs=[whole(xh), col(0), col(pairs), col(0)]
        + [whole(t) for t in tables]
        + [whole(seg_col), whole(seg_row)],
        out_specs=[out] * 4 + [pl.BlockSpec((1, 2, length), lambda h: (h, 0, 0))],
        out_shape=[shape] * 4 + [jax.ShapeDtypeStruct((pairs, 2, length), F32)],
        scratch_shapes=[pltpu.VMEM((2, length, 128), BF)],
        cost_estimate=pl.CostEstimate(
            flops=flops, bytes_accessed=length * width * 8, transcendentals=pairs * 2 * length * length
        ),
        name="attn_fwd",
    )(xh, w_qk, w_qk, w_vo, *tables, seg_col, seg_row)


def attn_bwd_kernel(
    q, k, v, o, do, lse, cos, upper, lower, seg_col, seg_row, pg, kh, dk, dv
):
    length = q.shape[0]
    rows = min(256, length)
    lane = lax.broadcasted_iota(jnp.int32, (length, 128), 1)
    first = lane < HD
    kf = k[...]
    none = jnp.zeros_like(kf)
    kh[0] = jnp.where(first, kf, none)
    kh[1] = jnp.where(first, none, kf)
    dk[...] = jnp.zeros_like(dk)
    dv[...] = jnp.zeros_like(dv)

    def block(i, carry):
        at = pl.multiple_of(i * rows, rows)
        here = pl.ds(at, rows)
        q_rows = q[here, :]
        g_rows = do[here, :]
        seg_here = seg_row[:, here]
        same = seg_col[...] == seg_here
        prod = g_rows.astype(F32) * o[here, :].astype(F32)
        f = first[:rows]
        blank = jnp.zeros_like(q_rows)
        dq = jnp.zeros((rows, 128), F32)
        for head in range(2):
            mine = f if head == 0 else jnp.logical_not(f)
            q_head = jnp.where(mine, q_rows, blank)
            g_head = jnp.where(mine, g_rows, blank)
            delta = lax.dot_general(
                jnp.ones((8, 128), F32),
                jnp.where(mine, prod, 0.0),
                (NT, ((), ())),
                precision=lax.Precision.HIGHEST,
                preferred_element_type=F32,
            )[0:1, :]
            scores = dotf(k[...], q_head, NT)
            level = lse[0, pl.ds(head, 1), here]
            probs = jnp.where(same, jnp.exp(scores - level), 0.0)
            dv[...] += dotf(probs.astype(BF), g_head, NN)
            dp = dotf(v[...], g_head, NT)
            ds = (probs * (dp - delta)).astype(BF)
            dk[...] += dotf(ds, q_head, NN)
            dq = dq + dotf(ds, kh[head], TN)
        dq = dq * (1.0 / math.sqrt(HD))
        c, a, b = cos[here, :], upper[here, :], lower[here, :]
        pg[0, here, :] = (dq * c - turn(dq, a, b)).astype(BF)
        return carry

    lax.fori_loop(0, length // rows, block, 0)
    dkf = dk[...]
    pg[1] = (dkf * cos[...] - turn(dkf, upper[...], lower[...])).astype(BF)
    pg[2] = dv[...].astype(BF)


def attn_bwd(q, k, v, o, do, lse, tables, seg_col, seg_row):
    length, width = q.shape
    pairs = width // 128
    whole = lambda a: pl.BlockSpec(a.shape, lambda h: (0,) * a.ndim)
    col = pl.BlockSpec((length, 128), lambda h: (0, h))
    return pl.pallas_call(
        attn_bwd_kernel,
        grid=(pairs,),
        in_specs=[col] * 5
        + [pl.BlockSpec((1, 2, length), lambda h: (h, 0, 0))]
        + [whole(t) for t in tables]
        + [whole(seg_col), whole(seg_row)],
        out_specs=pl.BlockSpec((3, length, 128), lambda h: (0, 0, h)),
        out_shape=jax.ShapeDtypeStruct((3, length, width), BF),
        scratch_shapes=[
            pltpu.VMEM((2, length, 128), BF),
            pltpu.VMEM((length, 128), F32),
            pltpu.VMEM((length, 128), F32),
        ],
        cost_estimate=pl.CostEstimate(
            flops=10 * pairs * 2 * length * length * 128,
            bytes_accessed=length * width * 20,
            transcendentals=pairs * 2 * length * length,
        ),
        name="attn_bwd",
    )(q, k, v, o, do, lse, *tables, seg_col, seg_row)


SHARD = (4, 2, 2)


def place():
    dp = lax.axis_index("dp")
    return dp // 4, (dp // 2) % 2, dp % 2, lax.axis_index("tensor")


def partners():
    z, x, c, y = place()
    at = lambda z, x, c, y: ((z * 2 + x) * 2 + c, y)
    return {
        "z1": at(z + 1 - 2 * (z % 2), x, c, y),
        "z2": at(z + 2 - 4 * (z // 2), x, c, y),
        "z3": at(3 - z, x, c, y),
        "x": at(z, 1 - x, c, y),
        "y": at(z, x, c, 1 - y),
        "c": at(z, x, 1 - c, y),
    }


def meet(peers):
    barrier = pltpu.get_barrier_semaphore()
    for peer in peers.values():
        pl.semaphore_signal(barrier, inc=1, device_id=peer, device_id_type=pl.DeviceIdType.MESH)
    pl.semaphore_wait(barrier, len(peers))


def remote(src, dst, send_sem, recv_sem, peer):
    return pltpu.make_async_remote_copy(
        src_ref=src,
        dst_ref=dst,
        send_sem=send_sem,
        recv_sem=recv_sem,
        device_id=peer,
        device_id_type=pl.DeviceIdType.MESH,
    )


def to_place(values, inverse=False):
    z, x, _, y = place()
    tiles = [values[:, j * 128 : (j + 1) * 128] for j in range(8)]
    tiles = [jnp.where(y == 1, pltpu.roll(t, 64, 1), t) for t in tiles]
    for bit, step in ((x, 1), (z % 2, 2), (z // 2, 4)):
        tiles = [jnp.where(bit == 1, tiles[j ^ step], tiles[j]) for j in range(8)]
    return jnp.concatenate(tiles, axis=1)


class Gather:
    MESSAGES = 15

    def __init__(self, own, buf, rows, axes, peers, sems, base):
        self.buf, self.rows, self.axes, self.peers = buf, rows, axes, peers
        self.own = own.at[rows]
        self.send_sem, self.recv_sem = sems
        self.base = base

    def slot(self, z, first, second):
        x, y = (first, second) if self.axes[0] == "x" else (second, first)
        return self.buf.at[z, x, y, self.rows]

    def copy(self, i):
        if i < 3:
            src, dst, peer = self.own, self.slot(i + 1, 0, 0), "z%d" % (i + 1)
        elif i < 7:
            src, dst, peer = self.slot(i - 3, 0, 0), self.slot(i - 3, 1, 0), self.axes[0]
        else:
            f, z = divmod(i - 7, 4)
            src, dst, peer = self.slot(z, f, 0), self.slot(z, f, 1), self.axes[1]
        if i in (3, 7):
            src = self.own
        n = self.base + i
        return remote(src, dst, self.send_sem.at[n], self.recv_sem.at[n], self.peers[peer])

    def start_z(self):
        for i in range(3):
            self.copy(i).start()

    def relay_z(self, z):
        if z:
            self.copy(z - 1).wait_recv()
        self.copy(3 + z).start()
        self.copy(7 + z).start()

    def relay_first(self, z):
        self.copy(3 + z).wait_recv()
        self.copy(11 + z).start()

    def finish(self):
        for i in range(7, 15):
            self.copy(i).wait_recv()
        for i in range(15):
            self.copy(i).wait_send()


def forward_kernel(
    a_own, b_own, g_own, u_own, d_own, x_half, cos, upper, lower, seg_col, seg_row,
    q, k, v, o, lse, xh, w_qk, w_vo, resid, xn, w_gate, w_up, w_down,
    kh, x_rel, part, sent, got, send_sem, recv_sem, pair_send, pair_recv, own_sem,
):
    length = xh.shape[0]
    half = length // 2
    width = xh.shape[1]
    pairs = q.shape[1] // 128
    rows = 256
    peers = partners()
    sems = (send_sem, recv_sem)
    n = Gather.MESSAGES
    whole, low, high = pl.ds(0, 64), pl.ds(0, 32), pl.ds(32, 32)
    one = [
        Gather(a_own, w_qk, whole, "xy", peers, sems, 0),
        Gather(b_own, w_vo, whole, "yx", peers, sems, n),
    ]
    two = [
        Gather(g_own, w_gate, whole, "xy", peers, sems, 2 * n),
        Gather(u_own, w_up, whole, "yx", peers, sems, 3 * n),
    ]
    three = [
        Gather(d_own, w_down, low, "xy", peers, sems, 4 * n),
        Gather(d_own, w_down, high, "yx", peers, sems, 5 * n),
    ]
    owns = [
        pltpu.make_async_copy(src, dst.at[0, 0, 0], own_sem.at[i])
        for i, (src, dst) in enumerate(
            ((a_own, w_qk), (b_own, w_vo), (g_own, w_gate), (u_own, w_up), (d_own, w_down))
        )
    ]
    for copy in owns:
        copy.start()
    meet(peers)
    for gather in one:
        gather.start_z()
    for gather in one:
        gather.relay_z(0)

    def first_norm(i, carry):
        here = pl.ds(pl.multiple_of(i * 128, 128), 128)
        values = to_place(x_half[here, :].astype(F32))
        x_rel[here, :] = values.astype(BF)
        xh[here, :] = normalize(values)[0].astype(BF)
        return carry

    lax.fori_loop(0, half // 128, first_norm, 0)
    for z in (1, 2, 3):
        for gather in one:
            gather.relay_z(z)
    swap_xh = remote(
        xh.at[pl.ds(0, half)], xh.at[pl.ds(half, half)], pair_send.at[0], pair_recv.at[0], peers["c"]
    )
    swap_xh.start()
    for gather in two:
        gather.start_z()
    for z in range(4):
        for gather in one:
            gather.relay_first(z)
    for gather in three:
        gather.start_z()
    swap_xh.wait()
    for gather in one:
        gather.finish()
    for copy in owns:
        copy.wait()

    events = {}
    for z in range(4):
        events.setdefault(1 + z, []).extend((g.relay_z, z) for g in two)
        events.setdefault(6 + z, []).extend((g.relay_first, z) for g in two)
        events.setdefault(9 + z, []).extend((g.relay_z, z) for g in three)
    first = lax.broadcasted_iota(jnp.int32, (length, 128), 1) < HD

    def pair(h, carry):
        lanes = pl.ds(pl.multiple_of(h * 128, 128), 128)
        lanes_k = pl.ds(pl.multiple_of((h + pairs) * 128, 128), 128)
        weight = lambda ref, cols: ref[:, :, :, :, cols].reshape(width, 128)
        tokens = xh[...]
        qf = dotf(tokens, weight(w_qk, lanes), NN)
        qf = qf * cos[...] + turn(qf, upper[...], lower[...])
        q[:, lanes] = (qf * (1.0 / math.sqrt(HD))).astype(BF)
        kf = dotf(tokens, weight(w_qk, lanes_k), NN)
        kf = (kf * cos[...] + turn(kf, upper[...], lower[...])).astype(BF)
        k[:, lanes] = kf
        kh[0] = jnp.where(first, kf, jnp.zeros_like(kf))
        kh[1] = jnp.where(first, jnp.zeros_like(kf), kf)
        v[:, lanes] = dotf(tokens, weight(w_vo, lanes), NN).astype(BF)

        def block(i, carry):
            for step, calls in events.items():

                @pl.when(h * (length // rows) + i == step)
                def _():
                    for call, z in calls:
                        call(z)

            at = pl.multiple_of(i * rows, rows)
            q_rows = q[pl.ds(at, rows), lanes]
            same = seg_col[pl.ds(at, rows), :] == seg_row[...]
            outs = []
            for head in range(2):
                scores = dotf(q_rows, kh[head], NT)
                scores = jnp.where(same, scores, -1e30)
                top = jnp.max(scores, axis=-1, keepdims=True)
                expv = jnp.exp(scores - top)
                total = jnp.sum(expv, axis=-1, keepdims=True)
                low_probs = (expv * (1.0 / total)).astype(BF)
                outs.append(dotf(low_probs, v[:, lanes], NN))
                level = top + jnp.log(total)
                flat = jnp.transpose(jnp.broadcast_to(level, (rows, 128)))
                lse[h, pl.ds(head, 1), pl.ds(at, rows)] = flat[0:1, :]
            o[pl.ds(at, rows), lanes] = jnp.where(first[:rows], outs[0], outs[1]).astype(BF)
            return carry

        return lax.fori_loop(0, length // rows, block, carry)

    lax.fori_loop(0, pairs, pair, 0)
    w_o = w_vo[:, :, :, :, pairs * 128 :].reshape(width, pairs * 128)

    def project(i, carry):
        at = pl.multiple_of(half + i * rows, rows)
        sent[pl.ds(pl.multiple_of(i * rows, rows), rows), :] = dotf(
            o[pl.ds(at, rows), :], w_o, NT
        ).astype(BF)
        return carry

    lax.fori_loop(0, half // rows, project, 0)

    def project_own(i, carry):
        here = pl.ds(pl.multiple_of(i * rows, rows), rows)
        part[here, :] = dotf(o[here, :], w_o, NT)
        return carry

    give = remote(sent, got, pair_send.at[1], pair_recv.at[1], peers["c"])
    lax.fori_loop(0, half // rows, project_own, 0)
    give.start()
    for gather in two + three:
        for z in range(4):
            if gather in three:
                gather.relay_first(z)
    give.wait()

    def second_norm(i, carry):
        here = pl.ds(pl.multiple_of(i * 128, 128), 128)
        values = x_rel[here, :].astype(F32) + (part[here, :] + got[here, :].astype(F32))
        resid[here, :] = values
        xn[here, :] = normalize(values)[0].astype(BF)
        return carry

    lax.fori_loop(0, half // 128, second_norm, 0)
    swap_xn = remote(
        xn.at[pl.ds(0, half)], xn.at[pl.ds(half, half)], pair_send.at[2], pair_recv.at[2], peers["c"]
    )
    swap_xn.start()
    for gather in two + three:
        gather.finish()
    swap_xn.wait()


def forward_block(owned, x_half, tables, seg_col, seg_row):
    half, width = x_half.shape
    length = 2 * half
    cols = owned[0].shape[1] // 2
    pairs = cols // 128
    units = owned[2].shape[1]
    vmem = pl.BlockSpec(memory_space=pltpu.VMEM)
    any_ = pl.BlockSpec(memory_space=pl.ANY)
    gathered = lambda n: jax.ShapeDtypeStruct(SHARD + (width // 16, n), BF)
    heads = jax.ShapeDtypeStruct((length, cols), BF)
    return pl.pallas_call(
        forward_kernel,
        in_specs=[any_] * 5 + [vmem] * 6,
        out_specs=[vmem] * 10 + [any_] * 3,
        out_shape=[heads] * 4
        + [
            jax.ShapeDtypeStruct((pairs, 2, length), F32),
            jax.ShapeDtypeStruct((length, width), BF),
            gathered(2 * cols),
            gathered(2 * cols),
            jax.ShapeDtypeStruct((half, width), F32),
            jax.ShapeDtypeStruct((length, width), BF),
        ]
        + [gathered(units)] * 3,
        scratch_shapes=[
            pltpu.VMEM((2, length, 128), BF),
            pltpu.VMEM((half, width), BF),
            pltpu.VMEM((half, width), F32),
            pltpu.VMEM((half, width), BF),
            pltpu.VMEM((half, width), BF),
            pltpu.SemaphoreType.DMA((6 * Gather.MESSAGES,)),
            pltpu.SemaphoreType.DMA((6 * Gather.MESSAGES,)),
            pltpu.SemaphoreType.DMA((3,)),
            pltpu.SemaphoreType.DMA((3,)),
            pltpu.SemaphoreType.DMA((5,)),
        ],
        compiler_params=pltpu.CompilerParams(collective_id=0, has_side_effects=True),
        name="forward_block",
    )(*owned, x_half, *tables, seg_col, seg_row)


def in_chunks(total, size, body):
    def step(j, carry):
        body(pl.ds(pl.multiple_of(j * size, size), size))
        return carry

    lax.fori_loop(0, total // size, step, 0)
    if total % size:
        body(pl.ds(total - total % size, total % size))


def mlp_kernel(
    xn, cot, w_gate, w_up, w_down, resid,
    result, resid_grad, attn_cot, d_gate, d_up, d_down,
    hidden, gate_grad, up_grad, own, sent, got, send_sem, recv_sem,
):
    length, width = xn.shape
    half = length // 2
    units = w_gate.shape[1]
    peer = partners()["c"]
    meet({"c": peer})

    def units_of(rows, cols):
        gate = dotf(xn[rows, :], w_gate[:, cols], NN)
        up = dotf(xn[rows, :], w_up[:, cols], NN)
        grad = dotf(cot[rows, :], w_down[:, cols], NN).astype(BF).astype(F32)
        act, slope = gelu_parts(gate)
        hidden[rows, cols] = (act * up).astype(BF)
        gate_grad[rows, cols] = (grad * up * slope).astype(BF)
        up_grad[rows, cols] = (grad * act).astype(BF)

    def phase(rows, put):
        in_chunks(units, 256, lambda cols: units_of(rows, cols))

        def sums(here):
            put[0, :, here] = dotf(hidden[rows, :], w_down[here, :], NT).astype(put.dtype)
            both = dotf(gate_grad[rows, :], w_gate[here, :], NT)
            both = both + dotf(up_grad[rows, :], w_up[here, :], NT)
            put[1, :, here] = both.astype(put.dtype)

        in_chunks(width, 256, sums)

    phase(pl.ds(half, half), sent)
    give = remote(sent, got, send_sem.at[0], recv_sem.at[0], peer)
    give.start()
    phase(pl.ds(0, half), own)
    give.wait()

    def finish(here):
        values = resid[here, :]
        mlp = own[0, here, :] + got[0, here, :].astype(F32)
        result[here, :] = to_place(values + mlp).astype(BF)
        xhat, scale = normalize(values)
        back = normalize_back(own[1, here, :] + got[1, here, :].astype(F32), xhat, scale)
        grad = cot[here, :].astype(F32) + back
        resid_grad[here, :] = grad
        attn_cot[here, :] = grad.astype(BF)

    in_chunks(half, 64, finish)
    swap = remote(
        attn_cot.at[pl.ds(0, half)], attn_cot.at[pl.ds(half, half)], send_sem.at[1], recv_sem.at[1], peer
    )
    swap.start()

    def weights(here):
        left = jnp.transpose(cot[:, here])
        d_down[here, :] = dotf(left, hidden[...], NN).astype(BF)
        left = jnp.transpose(xn[:, here])
        d_gate[here, :] = dotf(left, gate_grad[...], NN).astype(BF)
        d_up[here, :] = dotf(left, up_grad[...], NN).astype(BF)

    in_chunks(width, 256, weights)
    swap.wait()


def mlp_block(xn, cot, w_gate, w_up, w_down, resid):
    length, width = xn.shape
    half = length // 2
    units = w_gate.shape[1]
    vmem = pl.BlockSpec(memory_space=pltpu.VMEM)
    grads = jax.ShapeDtypeStruct((width, units), BF)
    return pl.pallas_call(
        mlp_kernel,
        in_specs=[vmem] * 6,
        out_specs=[vmem] * 6,
        out_shape=[
            jax.ShapeDtypeStruct((half, width), BF),
            jax.ShapeDtypeStruct((half, width), F32),
            jax.ShapeDtypeStruct((length, width), BF),
            grads,
            grads,
            grads,
        ],
        scratch_shapes=[pltpu.VMEM((length, units), BF)] * 3
        + [
            pltpu.VMEM((2, half, width), F32),
            pltpu.VMEM((2, half, width), BF),
            pltpu.VMEM((2, half, width), BF),
            pltpu.SemaphoreType.DMA((2,)),
            pltpu.SemaphoreType.DMA((2,)),
        ],
        compiler_params=pltpu.CompilerParams(
            collective_id=1, has_side_effects=True, vmem_limit_bytes=60 << 20
        ),
        name="mlp_block",
    )(xn, cot, w_gate, w_up, w_down, resid)


class Chips:
    def __init__(self):
        self.axes = ("dp", "tensor")
        dp = lax.axis_index("dp")
        self.z, self.x, self.core = dp // 4, (dp // 2) % 2, dp % 2
        self.y = lax.axis_index("tensor")

    @staticmethod
    def place(z, x, c, y):
        return ((z * 2 + x) * 2 + c) * 2 + y

    def send(self, value, dz=0, dx=0, dy=0, dc=0):
        pairs = [
            (self.place(z, x, c, y), self.place(z ^ dz, x ^ dx, c ^ dc, y ^ dy))
            for z in range(4)
            for x in range(2)
            for c in range(2)
            for y in range(2)
        ]
        return lax.ppermute(value, self.axes, pairs)

    def swap(self, value):
        pairs = [
            (self.place(z, x, c, y), self.place(z, x, y, c))
            for z in range(4)
            for x in range(2)
            for c in range(2)
            for y in range(2)
        ]
        return lax.ppermute(value, self.axes, pairs)

    def to_relative(self, value):
        rows, width = value.shape
        blocks = value.reshape(rows, 2, 2, 2, 2, width // 16)
        for axis, bit in ((4, self.y), (3, self.x), (2, self.z % 2), (1, self.z // 2)):
            blocks = jnp.where(bit == 1, jnp.flip(blocks, axis), blocks)
        return blocks.reshape(rows, width)

    from_relative = to_relative

    def positions(self, half):
        near = jnp.arange(half, dtype=jnp.int32)
        return jnp.concatenate([near + self.core * half, near + (1 - self.core) * half])

    def turn_rows(self, value):
        half = value.shape[0] // 2
        return jnp.where(self.core == 0, value, jnp.concatenate([value[half:], value[:half]]))

    def gather_rows(self, value):
        return jnp.concatenate([value, self.send(value, dc=1)], axis=0)

    def scatter_rows(self, value):
        half = value.shape[0] // 2
        return value[:half] + self.send(value[half:].astype(BF), dc=1).astype(F32)

    def reduce(self, a, b):
        order = lambda w: w.astype(BF).reshape(4, 2, 2, -1, w.shape[1]).swapaxes(0, 2)
        a, b = (order(w).reshape(16, -1, w.shape[1]) for w in (a, b))
        add = lambda u, w: (u.astype(F32) + w.astype(F32)).astype(BF)
        a = add(a[:8], self.send(a[8:], dy=1))
        b = add(
            jnp.concatenate([b[:4], b[8:12]]),
            self.send(jnp.concatenate([b[4:8], b[12:]]), dx=1),
        )
        a = add(a[:4], self.send(a[4:], dx=1))
        b = add(b[:4], self.send(b[4:], dy=1))
        sum_a, sum_b = a[0].astype(F32), b[0].astype(F32)
        for k in (1, 2, 3):
            sum_a = sum_a + self.send(a[k], dz=k).astype(F32)
            sum_b = sum_b + self.send(b[k], dz=k).astype(F32)
        return self.swap(sum_a.astype(BF)).astype(F32), self.swap(sum_b.astype(BF)).astype(F32)

    def sum_tensor(self, value):
        return value + self.send(value, dy=1)


class Axes:
    def swap(self, value):
        return value

    to_relative = from_relative = swap

    def positions(self, half):
        return jnp.arange(half * lax.axis_size("tensor"), dtype=jnp.int32)

    def turn_rows(self, value):
        return value

    def gather_rows(self, value):
        return lax.all_gather(value, "tensor", axis=0, tiled=True)

    def scatter_rows(self, value):
        return lax.psum_scatter(value.astype(BF), "tensor", scatter_dimension=0, tiled=True).astype(F32)

    def gather(self, a, b):
        return tuple(lax.all_gather(w, "dp", axis=0, tiled=True) for w in (a, b))

    def reduce(self, a, b):
        return tuple(
            lax.psum_scatter(w.astype(BF), "dp", scatter_dimension=0, tiled=True).astype(F32)
            for w in (a, b)
        )

    def sum_tensor(self, value):
        return lax.psum(value, "tensor")


def normalize(values):
    centred = values - jnp.mean(values, axis=-1, keepdims=True)
    scale = lax.rsqrt(jnp.mean(centred * centred, axis=-1, keepdims=True) + EPS)
    return centred * scale, scale


def normalize_back(f, xhat, scale):
    return scale * (
        f
        - jnp.mean(f, axis=-1, keepdims=True)
        - xhat * jnp.mean(f * xhat, axis=-1, keepdims=True)
    )


def gelu_parts(gate):
    half_erf = 0.5 * (1.0 + lax.erf(gate * (1.0 / math.sqrt(2.0))))
    density = jnp.exp(-0.5 * gate * gate) * (1.0 / math.sqrt(2.0 * math.pi))
    return gate * half_erf, half_erf + gate * density


def make_local(comm_type):
    def local(tokens, segments, w_qkv, w_out, w_in, w_down, g_attn, g_mlp, cotangent):
        comm = comm_type()
        paired = comm_type is Chips
        shard = w_qkv.shape[0]
        cols = w_qkv.shape[2]
        units = w_in.shape[2]
        low = 128 * (units // 256)
        pad = 128 * pl.cdiv(units, 128) - units
        gain_one = g_attn.astype(F32)[:, None]
        gain_two = g_mlp.astype(F32)[:, None]
        scaled = lambda w, g: (w.astype(F32) * g).astype(BF)
        padded = lambda w: jnp.pad(w, ((0, 0), (0, pad)))
        down_rows = w_down.T
        a_one = jnp.concatenate([scaled(w_qkv[:, 0], gain_one), scaled(w_qkv[:, 1], gain_one)], axis=1)
        b_one = jnp.concatenate([scaled(w_qkv[:, 2], gain_one), w_out.T], axis=1)
        own_gate, own_up = scaled(w_in[:, 0], gain_two), scaled(w_in[:, 1], gain_two)

        seg = comm.turn_rows(comm.swap(segments[0]))
        cot = comm.to_relative(comm.swap(cotangent[0]))
        cot_all = comm.gather_rows(cot)
        tables = rope_tables(comm.positions(tokens.shape[1]))
        seg_col, seg_row = seg[:, None], seg[None, :]
        owned = (a_one, b_one, own_gate, own_up, down_rows)
        if paired:
            owned = [comm.swap(w) for w in owned[:2] + tuple(padded(w) for w in owned[2:])]
            x_half = comm.swap(tokens[0])
            q, k, v, o, lse, xh, w_qk, w_vo, resid, xn, w_gate, w_up, w_dn = forward_block(
                owned, x_half, tables, seg_col, seg_row
            )
            w_qk, w_vo, w_gate, w_up, w_dn = (
                w.reshape(-1, w.shape[-1]) for w in (w_qk, w_vo, w_gate, w_up, w_dn)
            )
            xh_one, scale_one = normalize(comm.to_relative(x_half).astype(F32))
            w_o = w_vo[:, cols:]
        else:
            w_qk, w_vo, w_gate, w_up, w_dn = (
                lax.all_gather(w, "dp", axis=0, tiled=True) for w in owned
            )
            w_o = w_vo[:, cols:]
            x_in = tokens[0].astype(F32)
            xh_one, scale_one = normalize(x_in)
            xh = comm.gather_rows(xh_one.astype(BF))
            o, q, k, v, lse = attn_fwd(xh, w_qk, w_vo, tables, seg_col, seg_row)
            resid = x_in + comm.scatter_rows(dotf(o, w_o, NT))
            xh_two, scale_two = normalize(resid)
            xn = comm.gather_rows(xh_two.astype(BF))
        if paired:
            placed, resid_grad, attn_cot, d_gate, d_up, d_down = mlp_block(
                xn, cot_all, w_gate, w_up, w_dn, resid
            )
            result = comm.swap(placed)
        else:
            gate, up = dotf(xn, w_gate, NN), dotf(xn, w_up, NN)
            act, slope = gelu_parts(gate)
            hidden = (act * up).astype(BF)
            mlp = comm.scatter_rows(dotf(hidden, w_dn, NT))
            result = comm.swap(comm.from_relative((resid + mlp).astype(BF)))
            hidden_grad = dotf(cot_all, w_dn, NN).astype(BF).astype(F32)
            gate_grad = (hidden_grad * up * slope).astype(BF)
            up_grad = (hidden_grad * act).astype(BF)
            f_two = comm.scatter_rows(dotf(gate_grad, w_gate, NT) + dotf(up_grad, w_up, NT))
            resid_grad = cot.astype(F32) + normalize_back(f_two, xh_two, scale_two)
            attn_cot = comm.gather_rows(resid_grad.astype(BF))
            d_down = dotf(cot_all, hidden, TN)
            d_gate, d_up = dotf(xn, gate_grad, TN), dotf(xn, up_grad, TN)

        wide = lambda g, d: jnp.concatenate([g if paired else padded(g), d], axis=1)
        two_a, two_b = comm.reduce(wide(d_gate, d_down[:, :low]), wide(d_up, d_down[:, low:units]))

        heads_grad = dotf(attn_cot, w_o, NN).astype(BF)
        pg = attn_bwd(q, k, v, o, heads_grad, lse, tables, seg_col, seg_row)
        d_out = dotf(attn_cot, o, TN)
        d_q, d_k, d_v = (dotf(xh, pg[i], TN) for i in range(3))
        one_a, one_b = comm.reduce(
            jnp.concatenate([d_q, d_k], axis=1), jnp.concatenate([d_v, d_out], axis=1)
        )
        f_one = comm.scatter_rows(
            dotf(pg[0], w_qk[:, :cols], NT)
            + dotf(pg[1], w_qk[:, cols:], NT)
            + dotf(pg[2], w_vo[:, :cols], NT)
        )
        token_grad = resid_grad + normalize_back(f_one, xh_one, scale_one)
        token_grad = comm.swap(comm.from_relative(token_grad.astype(BF))).astype(F32)

        qkv_raw = jnp.stack([one_a[:, :cols], one_a[:, cols:], one_b[:, :cols]], axis=1)
        in_raw = jnp.stack([two_a[:, :units], two_b[:, :units]], axis=1)
        down_sum = jnp.concatenate([two_a[:, units + pad :], two_b[:, units + pad :]], axis=1).T
        gains = jnp.stack(
            [
                jnp.sum(qkv_raw * w_qkv.astype(F32), axis=(1, 2)),
                jnp.sum(in_raw * w_in.astype(F32), axis=(1, 2)),
            ]
        )
        gains = comm.sum_tensor(gains)
        return (
            result[None],
            token_grad[None],
            gains[0],
            gains[1],
            qkv_raw * gain_one[:, :, None],
            one_b[:, cols:].T,
            in_raw * gain_two[:, :, None],
            down_sum,
        )

    return local


def solution(mesh):
    paired = mesh.shape["dp"] == 16 and mesh.shape["tensor"] == 2
    return jax.shard_map(
        make_local(Chips if paired else Axes),
        mesh=mesh,
        in_specs=(
            P("dp", "tensor", None),
            P("dp", None),
            P("dp", None, "tensor"),
            P("tensor", "dp"),
            P("dp", None, "tensor"),
            P("tensor", "dp"),
            P("dp"),
            P("dp"),
            P("dp", "tensor", None),
        ),
        out_specs=(
            P("dp", "tensor", None),
            P("dp", "tensor", None),
            P("dp"),
            P("dp"),
            P("dp", None, "tensor"),
            P("tensor", "dp"),
            P("dp", None, "tensor"),
            P("tensor", "dp"),
        ),
        check_vma=False,
    )
```

```python
import math

import jax
import jax.numpy as jnp
from jax import lax
from jax.experimental import pallas as pl
from jax.experimental.pallas import tpu as pltpu
from jax.sharding import PartitionSpec as P

HD = 64
EPS = 1e-05
ROTARY_BASE = 160000.0
BF = jnp.bfloat16
F32 = jnp.float32


def dotf(a, b, dims):
    return lax.dot_general(a, b, (dims, ((), ())), preferred_element_type=F32)


NN = ((1,), (0,))
NT = ((1,), (1,))
TN = ((0,), (0,))


def rope_tables(positions):
    half = HD // 2
    inverse = 1.0 / ROTARY_BASE ** (jnp.arange(half).astype(F32) * (2.0 / HD))
    angles = positions.astype(F32)[:, None] * inverse[None, :]
    cos, sin = jnp.cos(angles), jnp.sin(angles)
    zero = jnp.zeros_like(sin)
    cosine = jnp.concatenate([cos] * 4, axis=-1)
    upper = jnp.concatenate([-sin, zero] * 2, axis=-1)
    lower = jnp.concatenate([zero, sin] * 2, axis=-1)
    return cosine, upper, lower


def turn(u, upper, lower):
    return pltpu.roll(u, 128 - HD // 2, 1) * upper + pltpu.roll(u, HD // 2, 1) * lower


def attn_fwd_kernel(xh, wq, wk, wv, cos, upper, lower, seg_col, seg_row, o, q, k, v, lse, kh):
    length = xh.shape[0]
    rows = min(256, length)
    lane = lax.broadcasted_iota(jnp.int32, (length, 128), 1)
    first = lane < HD
    tokens = xh[...]
    qf = dotf(tokens, wq[...], NN)
    qf = qf * cos[...] + turn(qf, upper[...], lower[...])
    q[...] = (qf * (1.0 / math.sqrt(HD))).astype(BF)
    kf = dotf(tokens, wk[...], NN)
    kf = (kf * cos[...] + turn(kf, upper[...], lower[...])).astype(BF)
    k[...] = kf
    kh[0] = jnp.where(first, kf, jnp.zeros_like(kf))
    kh[1] = jnp.where(first, jnp.zeros_like(kf), kf)
    v[...] = dotf(tokens, wv[...], NN).astype(BF)

    def block(i, carry):
        at = pl.multiple_of(i * rows, rows)
        q_rows = q[pl.ds(at, rows), :]
        same = seg_col[pl.ds(at, rows), :] == seg_row[...]
        outs = []
        for head in range(2):
            scores = dotf(q_rows, kh[head], NT)
            scores = jnp.where(same, scores, -1e30)
            top = jnp.max(scores, axis=-1, keepdims=True)
            expv = jnp.exp(scores - top)
            total = jnp.sum(expv, axis=-1, keepdims=True)
            low = (expv * (1.0 / total)).astype(BF)
            outs.append(dotf(low, v[...], NN))
            level = top + jnp.log(total)
            flat = jnp.transpose(jnp.broadcast_to(level, (rows, 128)))
            lse[0, pl.ds(head, 1), pl.ds(at, rows)] = flat[0:1, :]
        o[pl.ds(at, rows), :] = jnp.where(first[:rows], outs[0], outs[1]).astype(BF)
        return carry

    lax.fori_loop(0, length // rows, block, 0)


def attn_fwd(xh, w_qk, w_vo, tables, seg_col, seg_row):
    length, width = xh.shape
    pairs = w_qk.shape[1] // 256
    whole = lambda a: pl.BlockSpec(a.shape, lambda h: (0,) * a.ndim)
    col = lambda off: pl.BlockSpec((width, 128), lambda h: (0, h + off))
    out = pl.BlockSpec((length, 128), lambda h: (0, h))
    shape = jax.ShapeDtypeStruct((length, pairs * 128), BF)
    flops = 2 * length * width * pairs * 384 + 4 * pairs * 2 * length * length * 128
    return pl.pallas_call(
        attn_fwd_kernel,
        grid=(pairs,),
        in_specs=[whole(xh), col(0), col(pairs), col(0)]
        + [whole(t) for t in tables]
        + [whole(seg_col), whole(seg_row)],
        out_specs=[out] * 4 + [pl.BlockSpec((1, 2, length), lambda h: (h, 0, 0))],
        out_shape=[shape] * 4 + [jax.ShapeDtypeStruct((pairs, 2, length), F32)],
        scratch_shapes=[pltpu.VMEM((2, length, 128), BF)],
        cost_estimate=pl.CostEstimate(
            flops=flops, bytes_accessed=length * width * 8, transcendentals=pairs * 2 * length * length
        ),
        name="attn_fwd",
    )(xh, w_qk, w_qk, w_vo, *tables, seg_col, seg_row)


def attn_bwd_kernel(
    q, k, v, o, do, lse, cos, upper, lower, seg_col, seg_row, pg, kh, dk, dv
):
    length = q.shape[0]
    rows = min(256, length)
    lane = lax.broadcasted_iota(jnp.int32, (length, 128), 1)
    first = lane < HD
    kf = k[...]
    none = jnp.zeros_like(kf)
    kh[0] = jnp.where(first, kf, none)
    kh[1] = jnp.where(first, none, kf)
    dk[...] = jnp.zeros_like(dk)
    dv[...] = jnp.zeros_like(dv)

    def block(i, carry):
        at = pl.multiple_of(i * rows, rows)
        here = pl.ds(at, rows)
        q_rows = q[here, :]
        g_rows = do[here, :]
        seg_here = seg_row[:, here]
        same = seg_col[...] == seg_here
        prod = g_rows.astype(F32) * o[here, :].astype(F32)
        f = first[:rows]
        blank = jnp.zeros_like(q_rows)
        dq = jnp.zeros((rows, 128), F32)
        for head in range(2):
            mine = f if head == 0 else jnp.logical_not(f)
            q_head = jnp.where(mine, q_rows, blank)
            g_head = jnp.where(mine, g_rows, blank)
            delta = lax.dot_general(
                jnp.ones((8, 128), F32),
                jnp.where(mine, prod, 0.0),
                (NT, ((), ())),
                precision=lax.Precision.HIGHEST,
                preferred_element_type=F32,
            )[0:1, :]
            scores = dotf(k[...], q_head, NT)
            level = lse[0, pl.ds(head, 1), here]
            probs = jnp.where(same, jnp.exp(scores - level), 0.0)
            dv[...] += dotf(probs.astype(BF), g_head, NN)
            dp = dotf(v[...], g_head, NT)
            ds = (probs * (dp - delta)).astype(BF)
            dk[...] += dotf(ds, q_head, NN)
            dq = dq + dotf(ds, kh[head], TN)
        dq = dq * (1.0 / math.sqrt(HD))
        c, a, b = cos[here, :], upper[here, :], lower[here, :]
        pg[0, here, :] = (dq * c - turn(dq, a, b)).astype(BF)
        return carry

    lax.fori_loop(0, length // rows, block, 0)
    dkf = dk[...]
    pg[1] = (dkf * cos[...] - turn(dkf, upper[...], lower[...])).astype(BF)
    pg[2] = dv[...].astype(BF)


def attn_bwd(q, k, v, o, do, lse, tables, seg_col, seg_row):
    length, width = q.shape
    pairs = width // 128
    whole = lambda a: pl.BlockSpec(a.shape, lambda h: (0,) * a.ndim)
    col = pl.BlockSpec((length, 128), lambda h: (0, h))
    return pl.pallas_call(
        attn_bwd_kernel,
        grid=(pairs,),
        in_specs=[col] * 5
        + [pl.BlockSpec((1, 2, length), lambda h: (h, 0, 0))]
        + [whole(t) for t in tables]
        + [whole(seg_col), whole(seg_row)],
        out_specs=pl.BlockSpec((3, length, 128), lambda h: (0, 0, h)),
        out_shape=jax.ShapeDtypeStruct((3, length, width), BF),
        scratch_shapes=[
            pltpu.VMEM((2, length, 128), BF),
            pltpu.VMEM((length, 128), F32),
            pltpu.VMEM((length, 128), F32),
        ],
        cost_estimate=pl.CostEstimate(
            flops=10 * pairs * 2 * length * length * 128,
            bytes_accessed=length * width * 20,
            transcendentals=pairs * 2 * length * length,
        ),
        name="attn_bwd",
    )(q, k, v, o, do, lse, *tables, seg_col, seg_row)


SHARD = (4, 2, 2)


def place():
    dp = lax.axis_index("dp")
    return dp // 4, (dp // 2) % 2, dp % 2, lax.axis_index("tensor")


def partners():
    z, x, c, y = place()
    at = lambda z, x, c, y: ((z * 2 + x) * 2 + c, y)
    return {
        "z1": at(z + 1 - 2 * (z % 2), x, c, y),
        "z2": at(z + 2 - 4 * (z // 2), x, c, y),
        "z3": at(3 - z, x, c, y),
        "x": at(z, 1 - x, c, y),
        "y": at(z, x, c, 1 - y),
        "c": at(z, x, 1 - c, y),
    }


def meet(peers, other=None):
    barrier = pltpu.get_barrier_semaphore()
    greet = lambda peer: pl.semaphore_signal(
        barrier, inc=1, device_id=peer, device_id_type=pl.DeviceIdType.MESH
    )
    for peer in peers.values():
        greet(peer)
    if other is None:
        pl.semaphore_wait(barrier, len(peers))
    else:
        moved, peer = other

        @pl.when(moved)
        def _():
            greet(peer)

        pl.semaphore_wait(barrier, len(peers) + jnp.where(moved, 1, 0))


def exchanged():
    z, x, c, y = place()
    return c != y, ((z * 2 + x) * 2 + y, c)


def remote(src, dst, send_sem, recv_sem, peer):
    return pltpu.make_async_remote_copy(
        src_ref=src,
        dst_ref=dst,
        send_sem=send_sem,
        recv_sem=recv_sem,
        device_id=peer,
        device_id_type=pl.DeviceIdType.MESH,
    )


def to_place(values, inverse=False):
    z, x, _, y = place()
    tiles = [values[:, j * 128 : (j + 1) * 128] for j in range(8)]
    tiles = [jnp.where(y == 1, pltpu.roll(t, 64, 1), t) for t in tiles]
    for bit, step in ((x, 1), (z % 2, 2), (z // 2, 4)):
        tiles = [jnp.where(bit == 1, tiles[j ^ step], tiles[j]) for j in range(8)]
    return jnp.concatenate(tiles, axis=1)


class Gather:
    MESSAGES = 15

    def __init__(self, own, buf, rows, axes, peers, sems, base):
        self.buf, self.rows, self.axes, self.peers = buf, rows, axes, peers
        self.own = own.at[rows]
        self.send_sem, self.recv_sem = sems
        self.base = base

    def slot(self, z, first, second):
        x, y = (first, second) if self.axes[0] == "x" else (second, first)
        return self.buf.at[z, x, y, self.rows]

    def copy(self, i):
        if i < 3:
            src, dst, peer = self.own, self.slot(i + 1, 0, 0), "z%d" % (i + 1)
        elif i < 7:
            src, dst, peer = self.slot(i - 3, 0, 0), self.slot(i - 3, 1, 0), self.axes[0]
        else:
            f, z = divmod(i - 7, 4)
            src, dst, peer = self.slot(z, f, 0), self.slot(z, f, 1), self.axes[1]
        if i in (3, 7):
            src = self.own
        n = self.base + i
        return remote(src, dst, self.send_sem.at[n], self.recv_sem.at[n], self.peers[peer])

    def start_z(self):
        for i in range(3):
            self.copy(i).start()

    def relay_z(self, z):
        if z:
            self.copy(z - 1).wait_recv()
        self.copy(3 + z).start()
        self.copy(7 + z).start()

    def relay_first(self, z):
        self.copy(3 + z).wait_recv()
        self.copy(11 + z).start()

    def finish(self):
        for i in range(7, 15):
            self.copy(i).wait_recv()
        for i in range(15):
            self.copy(i).wait_send()


def forward_kernel(
    a_own, b_own, g_own, u_own, d_own, x_half, cos, upper, lower, seg_col, seg_row,
    q, k, v, o, lse, xh, w_qk, w_vo, resid, xn, w_gate, w_up, w_down,
    kh, x_rel, part, sent, got, send_sem, recv_sem, pair_send, pair_recv, own_sem,
):
    length = xh.shape[0]
    half = length // 2
    width = xh.shape[1]
    pairs = q.shape[1] // 128
    rows = 256
    peers = partners()
    sems = (send_sem, recv_sem)
    n = Gather.MESSAGES
    whole, low, high = pl.ds(0, 64), pl.ds(0, 32), pl.ds(32, 32)
    one = [
        Gather(a_own, w_qk, whole, "xy", peers, sems, 0),
        Gather(b_own, w_vo, whole, "yx", peers, sems, n),
    ]
    two = [
        Gather(g_own, w_gate, whole, "xy", peers, sems, 2 * n),
        Gather(u_own, w_up, whole, "yx", peers, sems, 3 * n),
    ]
    three = [
        Gather(d_own, w_down, low, "xy", peers, sems, 4 * n),
        Gather(d_own, w_down, high, "yx", peers, sems, 5 * n),
    ]
    owns = [
        pltpu.make_async_copy(src, dst.at[0, 0, 0], own_sem.at[i])
        for i, (src, dst) in enumerate(
            ((a_own, w_qk), (b_own, w_vo), (g_own, w_gate), (u_own, w_up), (d_own, w_down))
        )
    ]
    for copy in owns:
        copy.start()
    meet(peers)
    for gather in one:
        gather.start_z()
    for gather in one:
        gather.relay_z(0)

    def first_norm(i, carry):
        here = pl.ds(pl.multiple_of(i * 128, 128), 128)
        values = to_place(x_half[here, :].astype(F32))
        x_rel[here, :] = values.astype(BF)
        xh[here, :] = normalize(values)[0].astype(BF)
        return carry

    lax.fori_loop(0, half // 128, first_norm, 0)
    for z in (1, 2, 3):
        for gather in one:
            gather.relay_z(z)
    swap_xh = remote(
        xh.at[pl.ds(0, half)], xh.at[pl.ds(half, half)], pair_send.at[0], pair_recv.at[0], peers["c"]
    )
    swap_xh.start()
    for gather in two:
        gather.start_z()
    for z in range(4):
        for gather in one:
            gather.relay_first(z)
    for gather in three:
        gather.start_z()
    swap_xh.wait()
    for gather in one:
        gather.finish()
    for copy in owns:
        copy.wait()

    events = {}
    for z in range(4):
        events.setdefault(1 + z, []).extend((g.relay_z, z) for g in two)
        events.setdefault(6 + z, []).extend((g.relay_first, z) for g in two)
        events.setdefault(9 + z, []).extend((g.relay_z, z) for g in three)
    first = lax.broadcasted_iota(jnp.int32, (length, 128), 1) < HD

    def pair(h, carry):
        lanes = pl.ds(pl.multiple_of(h * 128, 128), 128)
        lanes_k = pl.ds(pl.multiple_of((h + pairs) * 128, 128), 128)
        weight = lambda ref, cols: ref[:, :, :, :, cols].reshape(width, 128)
        tokens = xh[...]
        qf = dotf(tokens, weight(w_qk, lanes), NN)
        qf = qf * cos[...] + turn(qf, upper[...], lower[...])
        q[:, lanes] = (qf * (1.0 / math.sqrt(HD))).astype(BF)
        kf = dotf(tokens, weight(w_qk, lanes_k), NN)
        kf = (kf * cos[...] + turn(kf, upper[...], lower[...])).astype(BF)
        k[:, lanes] = kf
        kh[0] = jnp.where(first, kf, jnp.zeros_like(kf))
        kh[1] = jnp.where(first, jnp.zeros_like(kf), kf)
        v[:, lanes] = dotf(tokens, weight(w_vo, lanes), NN).astype(BF)

        def block(i, carry):
            for step, calls in events.items():

                @pl.when(h * (length // rows) + i == step)
                def _():
                    for call, z in calls:
                        call(z)

            at = pl.multiple_of(i * rows, rows)
            q_rows = q[pl.ds(at, rows), lanes]
            same = seg_col[pl.ds(at, rows), :] == seg_row[...]
            outs = []
            for head in range(2):
                scores = dotf(q_rows, kh[head], NT)
                scores = jnp.where(same, scores, -1e30)
                top = jnp.max(scores, axis=-1, keepdims=True)
                expv = jnp.exp(scores - top)
                total = jnp.sum(expv, axis=-1, keepdims=True)
                low_probs = (expv * (1.0 / total)).astype(BF)
                outs.append(dotf(low_probs, v[:, lanes], NN))
                level = top + jnp.log(total)
                flat = jnp.transpose(jnp.broadcast_to(level, (rows, 128)))
                lse[h, pl.ds(head, 1), pl.ds(at, rows)] = flat[0:1, :]
            o[pl.ds(at, rows), lanes] = jnp.where(first[:rows], outs[0], outs[1]).astype(BF)
            return carry

        return lax.fori_loop(0, length // rows, block, carry)

    lax.fori_loop(0, pairs, pair, 0)
    w_o = w_vo[:, :, :, :, pairs * 128 :].reshape(width, pairs * 128)

    def project(i, carry):
        at = pl.multiple_of(half + i * rows, rows)
        sent[pl.ds(pl.multiple_of(i * rows, rows), rows), :] = dotf(
            o[pl.ds(at, rows), :], w_o, NT
        ).astype(BF)
        return carry

    lax.fori_loop(0, half // rows, project, 0)

    def project_own(i, carry):
        here = pl.ds(pl.multiple_of(i * rows, rows), rows)
        part[here, :] = dotf(o[here, :], w_o, NT)
        return carry

    give = remote(sent, got, pair_send.at[1], pair_recv.at[1], peers["c"])
    lax.fori_loop(0, half // rows, project_own, 0)
    give.start()
    for gather in two + three:
        for z in range(4):
            if gather in three:
                gather.relay_first(z)
    give.wait()

    def second_norm(i, carry):
        here = pl.ds(pl.multiple_of(i * 128, 128), 128)
        values = x_rel[here, :].astype(F32) + (part[here, :] + got[here, :].astype(F32))
        resid[here, :] = values
        xn[here, :] = normalize(values)[0].astype(BF)
        return carry

    lax.fori_loop(0, half // 128, second_norm, 0)
    swap_xn = remote(
        xn.at[pl.ds(0, half)], xn.at[pl.ds(half, half)], pair_send.at[2], pair_recv.at[2], peers["c"]
    )
    swap_xn.start()
    for gather in two + three:
        gather.finish()
    swap_xn.wait()


def forward_block(owned, x_half, tables, seg_col, seg_row):
    half, width = x_half.shape
    length = 2 * half
    cols = owned[0].shape[1] // 2
    pairs = cols // 128
    units = owned[2].shape[1]
    vmem = pl.BlockSpec(memory_space=pltpu.VMEM)
    any_ = pl.BlockSpec(memory_space=pl.ANY)
    gathered = lambda n: jax.ShapeDtypeStruct(SHARD + (width // 16, n), BF)
    heads = jax.ShapeDtypeStruct((length, cols), BF)
    return pl.pallas_call(
        forward_kernel,
        in_specs=[any_] * 5 + [vmem] * 6,
        out_specs=[vmem] * 10 + [any_] * 3,
        out_shape=[heads] * 4
        + [
            jax.ShapeDtypeStruct((pairs, 2, length), F32),
            jax.ShapeDtypeStruct((length, width), BF),
            gathered(2 * cols),
            gathered(2 * cols),
            jax.ShapeDtypeStruct((half, width), F32),
            jax.ShapeDtypeStruct((length, width), BF),
        ]
        + [gathered(units)] * 3,
        scratch_shapes=[
            pltpu.VMEM((2, length, 128), BF),
            pltpu.VMEM((half, width), BF),
            pltpu.VMEM((half, width), F32),
            pltpu.VMEM((half, width), BF),
            pltpu.VMEM((half, width), BF),
            pltpu.SemaphoreType.DMA((6 * Gather.MESSAGES,)),
            pltpu.SemaphoreType.DMA((6 * Gather.MESSAGES,)),
            pltpu.SemaphoreType.DMA((3,)),
            pltpu.SemaphoreType.DMA((3,)),
            pltpu.SemaphoreType.DMA((5,)),
        ],
        compiler_params=pltpu.CompilerParams(collective_id=0, has_side_effects=True),
        name="forward_block",
    )(*owned, x_half, *tables, seg_col, seg_row)


def in_chunks(total, size, body):
    def step(j, carry):
        body(pl.ds(pl.multiple_of(j * size, size), size))
        return carry

    lax.fori_loop(0, total // size, step, 0)
    if total % size:
        body(pl.ds(total - total % size, total % size))


def mlp_kernel(
    xn, cot, w_gate, w_up, w_down, resid,
    result, resid_grad, attn_cot, d_gate, d_up, d_down,
    hidden, gate_grad, up_grad, own, sent, got, send_sem, recv_sem,
):
    length, width = xn.shape
    half = length // 2
    units = w_gate.shape[1]
    peer = partners()["c"]
    meet({"c": peer})

    def units_of(rows, cols):
        gate = dotf(xn[rows, :], w_gate[:, cols], NN)
        up = dotf(xn[rows, :], w_up[:, cols], NN)
        grad = dotf(cot[rows, :], w_down[:, cols], NN).astype(BF).astype(F32)
        act, slope = gelu_parts(gate)
        hidden[rows, cols] = (act * up).astype(BF)
        gate_grad[rows, cols] = (grad * up * slope).astype(BF)
        up_grad[rows, cols] = (grad * act).astype(BF)

    def phase(rows, put):
        in_chunks(units, 256, lambda cols: units_of(rows, cols))

        def sums(here):
            put[0, :, here] = dotf(hidden[rows, :], w_down[here, :], NT).astype(put.dtype)
            both = dotf(gate_grad[rows, :], w_gate[here, :], NT)
            both = both + dotf(up_grad[rows, :], w_up[here, :], NT)
            put[1, :, here] = both.astype(put.dtype)

        in_chunks(width, 256, sums)

    phase(pl.ds(half, half), sent)
    give = remote(sent, got, send_sem.at[0], recv_sem.at[0], peer)
    give.start()
    phase(pl.ds(0, half), own)
    give.wait()

    def finish(here):
        values = resid[here, :]
        mlp = own[0, here, :] + got[0, here, :].astype(F32)
        result[here, :] = to_place(values + mlp).astype(BF)
        xhat, scale = normalize(values)
        back = normalize_back(own[1, here, :] + got[1, here, :].astype(F32), xhat, scale)
        grad = cot[here, :].astype(F32) + back
        resid_grad[here, :] = grad
        attn_cot[here, :] = grad.astype(BF)

    in_chunks(half, 64, finish)
    swap = remote(
        attn_cot.at[pl.ds(0, half)], attn_cot.at[pl.ds(half, half)], send_sem.at[1], recv_sem.at[1], peer
    )
    swap.start()

    def weights(here):
        left = jnp.transpose(cot[:, here])
        d_down[here, :] = dotf(left, hidden[...], NN).astype(BF)
        left = jnp.transpose(xn[:, here])
        d_gate[here, :] = dotf(left, gate_grad[...], NN).astype(BF)
        d_up[here, :] = dotf(left, up_grad[...], NN).astype(BF)

    in_chunks(width, 256, weights)
    swap.wait()


def mlp_block(xn, cot, w_gate, w_up, w_down, resid):
    length, width = xn.shape
    half = length // 2
    units = w_gate.shape[1]
    vmem = pl.BlockSpec(memory_space=pltpu.VMEM)
    grads = jax.ShapeDtypeStruct((width, units), BF)
    return pl.pallas_call(
        mlp_kernel,
        in_specs=[vmem] * 6,
        out_specs=[vmem] * 6,
        out_shape=[
            jax.ShapeDtypeStruct((half, width), BF),
            jax.ShapeDtypeStruct((half, width), F32),
            jax.ShapeDtypeStruct((length, width), BF),
            grads,
            grads,
            grads,
        ],
        scratch_shapes=[pltpu.VMEM((length, units), BF)] * 3
        + [
            pltpu.VMEM((2, half, width), F32),
            pltpu.VMEM((2, half, width), BF),
            pltpu.VMEM((2, half, width), BF),
            pltpu.SemaphoreType.DMA((2,)),
            pltpu.SemaphoreType.DMA((2,)),
        ],
        compiler_params=pltpu.CompilerParams(
            collective_id=1, has_side_effects=True, vmem_limit_bytes=60 << 20
        ),
        name="mlp_block",
    )(xn, cot, w_gate, w_up, w_down, resid)


class Reduce:
    MESSAGES = 12
    ORDER = (2, 3, 1, 0)

    def __init__(self, parts, near, rows, axes, peers, sems, base, bufs, out):
        self.parts, self.near, self.rows, self.axes, self.peers = parts, near, rows, axes, peers
        self.send_sem, self.recv_sem = sems
        self.base = base
        self.one, self.two, self.three, self.sum = bufs
        self.out = out

    def link(self, i, src, dst, peer):
        n = self.base + i
        return remote(src, dst, self.send_sem.at[n], self.recv_sem.at[n], peer)

    def first(self, z):
        if self.axes == "xy":
            src = self.parts.at[z, :, 1, self.rows]
        else:
            src = self.parts.at[z, 1, :, self.rows]
        return self.link(z, src, self.one.at[z], self.peers[self.axes[1]])

    def second(self, z):
        return self.link(4 + z, self.one.at[z, 1], self.two.at[z], self.peers[self.axes[0]])

    def third(self, z):
        return self.link(7 + z, self.two.at[z], self.three.at[z - 1], self.peers["z%d" % z])

    def start(self):
        for z in self.ORDER:
            self.first(z).start()

    def relay_first(self, z):
        self.first(z).wait_recv()
        self.one[z] = (self.one[z].astype(F32) + self.near(z).astype(F32)).astype(BF)
        self.second(z).start()

    def relay_second(self, z):
        self.second(z).wait_recv()
        self.two[z] = (self.two[z].astype(F32) + self.one[z, 0].astype(F32)).astype(BF)
        if z:
            self.third(z).start()

    def last(self):
        moved, peer = exchanged()
        return moved, self.link(11, self.sum, self.out, peer)

    def finish(self):
        total = self.two[0].astype(F32)
        for z in (1, 2, 3):
            self.third(z).wait_recv()
            total = total + self.three[z - 1].astype(F32)
        self.sum[...] = total.astype(BF)
        moved, copy = self.last()

        @pl.when(moved)
        def _():
            copy.start()

        @pl.when(jnp.logical_not(moved))
        def _():
            self.out[...] = self.sum[...]

    def close(self):
        for z in range(4):
            self.first(z).wait_send()
            self.second(z).wait_send()
            if z:
                self.third(z).wait_send()
        moved, copy = self.last()

        @pl.when(moved)
        def _():
            copy.wait()


def backward_kernel(
    d_gate, d_up, d_down, q, k, v, o, lse, attn_cot, w_qk, w_vo, xh, x_half, resid_grad,
    cos, upper, lower, seg_col, seg_row,
    token_grad, s_gate, s_up, s_down_low, s_down_high, s_qk, s_vo,
    d_qk, d_vo, pg, heads_grad, kh, dk, dv, own, sent, got, near_gate, near_up, near_low, near_high,
    *rest,
):
    bufs = [rest[4 * i : 4 * i + 4] for i in range(6)]
    send_sem, recv_sem, pair_send, pair_recv, near_sem = rest[24:]
    length, width = xh.shape
    half = length // 2
    cols = q.shape[1]
    pairs = cols // 128
    rows = 256
    peers = partners()
    sems = (send_sem, recv_sem)
    n = Reduce.MESSAGES
    whole, low, high = pl.ds(0, 64), pl.ds(0, 32), pl.ds(32, 32)
    held = lambda ref: (lambda z: ref[z])
    gate = Reduce(d_gate, held(near_gate), whole, "xy", peers, sems, 0, bufs[0], s_gate)
    up = Reduce(d_up, held(near_up), whole, "yx", peers, sems, n, bufs[1], s_up)
    down = [
        Reduce(d_down, held(near_low), low, "xy", peers, sems, 2 * n, bufs[2], s_down_low),
        Reduce(d_down, held(near_high), high, "yx", peers, sems, 3 * n, bufs[3], s_down_high),
    ]
    one = [gate, up]
    last = [
        Reduce(d_qk, lambda z: d_qk[z, :, 0], whole, "xy", peers, sems, 4 * n, bufs[4], s_qk),
        Reduce(d_vo, lambda z: d_vo[z, 0], whole, "yx", peers, sems, 5 * n, bufs[5], s_vo),
    ]
    nears = [
        pltpu.make_async_copy(src, dst, near_sem.at[i])
        for i, (src, dst) in enumerate(
            (
                (d_gate.at[:, :, 0], near_gate),
                (d_up.at[:, 0], near_up),
                (d_down.at[:, :, 0, low], near_low),
                (d_down.at[:, 0, :, high], near_high),
            )
        )
    ]
    for copy in nears:
        copy.start()
    meet(peers, exchanged())
    for part in one:
        part.start()

    def heads(here):
        heads_grad[here, :] = dotf(attn_cot[here, :], w_vo[:, cols:], NN).astype(BF)

    in_chunks(length, 256, heads)

    def out_weights(z, carry):
        here = pl.ds(pl.multiple_of(z * 256, 256), 256)
        value = dotf(jnp.transpose(attn_cot[:, here]), o[...], NN).astype(BF)
        d_vo[z, :, :, :, cols:] = value.reshape(2, 2, 64, cols)
        return carry

    lax.fori_loop(0, width // 256, out_weights, 0)
    for copy in nears:
        copy.wait()

    events = {}
    for i, z in enumerate(Reduce.ORDER):
        events.setdefault(2 + 4 * i, []).extend((lambda r=r, z=z: r.relay_first(z)) for r in one)
    events.setdefault(11, []).extend(r.start for r in down)
    lane = lax.broadcasted_iota(jnp.int32, (length, 128), 1)
    first = lane < HD

    def pair(h, carry):
        lanes = pl.ds(pl.multiple_of(h * 128, 128), 128)
        kf = k[:, lanes]
        none = jnp.zeros_like(kf)
        kh[0] = jnp.where(first, kf, none)
        kh[1] = jnp.where(first, none, kf)
        dk[...] = jnp.zeros_like(dk)
        dv[...] = jnp.zeros_like(dv)

        def block(i, carry):
            for step, calls in events.items():

                @pl.when(h * (length // rows) + i == step)
                def _():
                    for call in calls:
                        call()

            at = pl.multiple_of(i * rows, rows)
            here = pl.ds(at, rows)
            q_rows = q[here, lanes]
            g_rows = heads_grad[here, lanes]
            same = seg_col[...] == seg_row[:, here]
            prod = g_rows.astype(F32) * o[here, lanes].astype(F32)
            f = first[:rows]
            blank = jnp.zeros_like(q_rows)
            dq = jnp.zeros((rows, 128), F32)
            for head in range(2):
                mine = f if head == 0 else jnp.logical_not(f)
                q_head = jnp.where(mine, q_rows, blank)
                g_head = jnp.where(mine, g_rows, blank)
                delta = lax.dot_general(
                    jnp.ones((8, 128), F32),
                    jnp.where(mine, prod, 0.0),
                    (NT, ((), ())),
                    precision=lax.Precision.HIGHEST,
                    preferred_element_type=F32,
                )[0:1, :]
                scores = dotf(k[:, lanes], q_head, NT)
                level = lse[h, pl.ds(head, 1), here]
                probs = jnp.where(same, jnp.exp(scores - level), 0.0)
                dv[...] += dotf(probs.astype(BF), g_head, NN)
                dp = dotf(v[:, lanes], g_head, NT)
                ds = (probs * (dp - delta)).astype(BF)
                dk[...] += dotf(ds, q_head, NN)
                dq = dq + dotf(ds, kh[head], TN)
            dq = dq * (1.0 / math.sqrt(HD))
            c, a, b = cos[here, :], upper[here, :], lower[here, :]
            pg[0, here, lanes] = (dq * c - turn(dq, a, b)).astype(BF)
            return carry

        lax.fori_loop(0, length // rows, block, 0)
        dkf = dk[...]
        pg[1, :, lanes] = (dkf * cos[...] - turn(dkf, upper[...], lower[...])).astype(BF)
        pg[2, :, lanes] = dv[...].astype(BF)
        return carry

    lax.fori_loop(0, pairs, pair, 0)

    def weights(z, carry):
        left = jnp.transpose(xh[:, pl.ds(pl.multiple_of(z * 256, 256), 256)])
        for i, (ref, at) in enumerate(((d_qk, 0), (d_qk, cols), (d_vo, 0))):
            value = dotf(left, pg[i], NN).astype(BF)
            ref[z, :, :, :, at : at + cols] = value.reshape(2, 2, 64, cols)
        return carry

    lax.fori_loop(0, width // 256, weights, 0)

    def back(tokens, put):
        def step(here):
            total = dotf(pg[0, tokens, :], w_qk[here, :cols], NT)
            total = total + dotf(pg[1, tokens, :], w_qk[here, cols:], NT)
            put[:, here] = (total + dotf(pg[2, tokens, :], w_vo[here, :cols], NT)).astype(put.dtype)

        in_chunks(width, 256, step)

    back(pl.ds(half, half), sent)
    for part in last:
        part.start()
    give = remote(sent, got, pair_send.at[0], pair_recv.at[0], peers["c"])
    give.start()
    back(pl.ds(0, half), own)
    for z in Reduce.ORDER:
        for part in one:
            part.relay_second(z)
    give.wait()

    def finish(here):
        xhat, scale = normalize(to_place(x_half[here, :].astype(F32)))
        f = own[here, :] + got[here, :].astype(F32)
        value = resid_grad[here, :] + normalize_back(f, xhat, scale)
        token_grad[here, :] = to_place(value).astype(BF)

    in_chunks(half, 64, finish)
    for z in Reduce.ORDER:
        for part in down:
            part.relay_first(z)
    for part in one:
        part.finish()
    for z in Reduce.ORDER:
        for part in down:
            part.relay_second(z)
        for part in last:
            part.relay_first(z)
    for part in down:
        part.finish()
    for z in Reduce.ORDER:
        for part in last:
            part.relay_second(z)
    for part in last:
        part.finish()
    for part in one + down + last:
        part.close()


def backward_block(grads, heads, lse, attn_cot, w_qk, w_vo, xh, x_half, resid_grad, tables, seg_col, seg_row):
    length, width = xh.shape
    half = length // 2
    cols = heads[0].shape[1]
    units = grads[0].shape[1]
    shard = width // 16
    vmem = pl.BlockSpec(memory_space=pltpu.VMEM)
    any_ = pl.BlockSpec(memory_space=pl.ANY)
    sizes = [(shard, units), (shard, units), (shard // 2, units), (shard // 2, units)]
    sizes += [(shard, 2 * cols)] * 2
    bufs = []
    for size in sizes:
        bufs += [
            pltpu.VMEM((4, 2) + size, BF),
            pltpu.VMEM((4,) + size, BF),
            pltpu.VMEM((3,) + size, BF),
            pltpu.VMEM(size, BF),
        ]
    messages = 6 * Reduce.MESSAGES
    return pl.pallas_call(
        backward_kernel,
        in_specs=[any_] * 3 + [vmem] * 16,
        out_specs=[vmem] * 7,
        out_shape=[jax.ShapeDtypeStruct((half, width), BF)]
        + [jax.ShapeDtypeStruct(size, BF) for size in sizes],
        scratch_shapes=[pltpu.VMEM(SHARD + (shard, 2 * cols), BF)] * 2
        + [
            pltpu.VMEM((3, length, cols), BF),
            pltpu.VMEM((length, cols), BF),
            pltpu.VMEM((2, length, 128), BF),
            pltpu.VMEM((length, 128), F32),
            pltpu.VMEM((length, 128), F32),
            pltpu.VMEM((half, width), F32),
            pltpu.VMEM((half, width), BF),
            pltpu.VMEM((half, width), BF),
        ]
        + [pltpu.VMEM((4, 2) + size, BF) for size in sizes[:4]]
        + bufs
        + [
            pltpu.SemaphoreType.DMA((messages,)),
            pltpu.SemaphoreType.DMA((messages,)),
            pltpu.SemaphoreType.DMA((1,)),
            pltpu.SemaphoreType.DMA((1,)),
            pltpu.SemaphoreType.DMA((4,)),
        ],
        compiler_params=pltpu.CompilerParams(
            collective_id=2, has_side_effects=True, vmem_limit_bytes=60 << 20
        ),
        name="backward_block",
    )(
        *(g.reshape(SHARD + (shard, units)) for g in grads),
        *heads, lse, attn_cot, w_qk, w_vo, xh, x_half, resid_grad, *tables, seg_col, seg_row,
    )


class Chips:
    def __init__(self):
        self.axes = ("dp", "tensor")
        dp = lax.axis_index("dp")
        self.z, self.x, self.core = dp // 4, (dp // 2) % 2, dp % 2
        self.y = lax.axis_index("tensor")

    @staticmethod
    def place(z, x, c, y):
        return ((z * 2 + x) * 2 + c) * 2 + y

    def send(self, value, dz=0, dx=0, dy=0, dc=0):
        pairs = [
            (self.place(z, x, c, y), self.place(z ^ dz, x ^ dx, c ^ dc, y ^ dy))
            for z in range(4)
            for x in range(2)
            for c in range(2)
            for y in range(2)
        ]
        return lax.ppermute(value, self.axes, pairs)

    def swap(self, value):
        pairs = [
            (self.place(z, x, c, y), self.place(z, x, y, c))
            for z in range(4)
            for x in range(2)
            for c in range(2)
            for y in range(2)
        ]
        return lax.ppermute(value, self.axes, pairs)

    def to_relative(self, value):
        rows, width = value.shape
        blocks = value.reshape(rows, 2, 2, 2, 2, width // 16)
        for axis, bit in ((4, self.y), (3, self.x), (2, self.z % 2), (1, self.z // 2)):
            blocks = jnp.where(bit == 1, jnp.flip(blocks, axis), blocks)
        return blocks.reshape(rows, width)

    from_relative = to_relative

    def positions(self, half):
        near = jnp.arange(half, dtype=jnp.int32)
        return jnp.concatenate([near + self.core * half, near + (1 - self.core) * half])

    def turn_rows(self, value):
        half = value.shape[0] // 2
        return jnp.where(self.core == 0, value, jnp.concatenate([value[half:], value[:half]]))

    def gather_rows(self, value):
        return jnp.concatenate([value, self.send(value, dc=1)], axis=0)

    def sum_tensor(self, value):
        return value + self.send(value, dy=1)


class Axes:
    def swap(self, value):
        return value

    to_relative = from_relative = swap

    def positions(self, half):
        return jnp.arange(half * lax.axis_size("tensor"), dtype=jnp.int32)

    def turn_rows(self, value):
        return value

    def gather_rows(self, value):
        return lax.all_gather(value, "tensor", axis=0, tiled=True)

    def scatter_rows(self, value):
        return lax.psum_scatter(value.astype(BF), "tensor", scatter_dimension=0, tiled=True).astype(F32)

    def gather(self, a, b):
        return tuple(lax.all_gather(w, "dp", axis=0, tiled=True) for w in (a, b))

    def reduce(self, a, b):
        return tuple(
            lax.psum_scatter(w.astype(BF), "dp", scatter_dimension=0, tiled=True).astype(F32)
            for w in (a, b)
        )

    def sum_tensor(self, value):
        return lax.psum(value, "tensor")


def normalize(values):
    centred = values - jnp.mean(values, axis=-1, keepdims=True)
    scale = lax.rsqrt(jnp.mean(centred * centred, axis=-1, keepdims=True) + EPS)
    return centred * scale, scale


def normalize_back(f, xhat, scale):
    return scale * (
        f
        - jnp.mean(f, axis=-1, keepdims=True)
        - xhat * jnp.mean(f * xhat, axis=-1, keepdims=True)
    )


def gelu_parts(gate):
    half_erf = 0.5 * (1.0 + lax.erf(gate * (1.0 / math.sqrt(2.0))))
    density = jnp.exp(-0.5 * gate * gate) * (1.0 / math.sqrt(2.0 * math.pi))
    return gate * half_erf, half_erf + gate * density


def make_local(comm_type):
    def local(tokens, segments, w_qkv, w_out, w_in, w_down, g_attn, g_mlp, cotangent):
        comm = comm_type()
        paired = comm_type is Chips
        shard = w_qkv.shape[0]
        cols = w_qkv.shape[2]
        units = w_in.shape[2]
        low = 128 * (units // 256)
        pad = 128 * pl.cdiv(units, 128) - units
        gain_one = g_attn.astype(F32)[:, None]
        gain_two = g_mlp.astype(F32)[:, None]
        scaled = lambda w, g: (w.astype(F32) * g).astype(BF)
        padded = lambda w: jnp.pad(w, ((0, 0), (0, pad)))
        down_rows = w_down.T
        a_one = jnp.concatenate([scaled(w_qkv[:, 0], gain_one), scaled(w_qkv[:, 1], gain_one)], axis=1)
        b_one = jnp.concatenate([scaled(w_qkv[:, 2], gain_one), w_out.T], axis=1)
        own_gate, own_up = scaled(w_in[:, 0], gain_two), scaled(w_in[:, 1], gain_two)

        seg = comm.turn_rows(comm.swap(segments[0]))
        cot = comm.to_relative(comm.swap(cotangent[0]))
        cot_all = comm.gather_rows(cot)
        tables = rope_tables(comm.positions(tokens.shape[1]))
        seg_col, seg_row = seg[:, None], seg[None, :]
        owned = (a_one, b_one, own_gate, own_up, down_rows)
        if paired:
            owned = [comm.swap(w) for w in owned[:2] + tuple(padded(w) for w in owned[2:])]
            x_half = comm.swap(tokens[0])
            q, k, v, o, lse, xh, w_qk, w_vo, resid, xn, w_gate, w_up, w_dn = forward_block(
                owned, x_half, tables, seg_col, seg_row
            )
            w_qk, w_vo, w_gate, w_up, w_dn = (
                w.reshape(-1, w.shape[-1]) for w in (w_qk, w_vo, w_gate, w_up, w_dn)
            )
        else:
            w_qk, w_vo, w_gate, w_up, w_dn = (
                lax.all_gather(w, "dp", axis=0, tiled=True) for w in owned
            )
            w_o = w_vo[:, cols:]
            x_in = tokens[0].astype(F32)
            xh_one, scale_one = normalize(x_in)
            xh = comm.gather_rows(xh_one.astype(BF))
            o, q, k, v, lse = attn_fwd(xh, w_qk, w_vo, tables, seg_col, seg_row)
            resid = x_in + comm.scatter_rows(dotf(o, w_o, NT))
            xh_two, scale_two = normalize(resid)
            xn = comm.gather_rows(xh_two.astype(BF))
        if paired:
            placed, resid_grad, attn_cot, d_gate, d_up, d_down = mlp_block(
                xn, cot_all, w_gate, w_up, w_dn, resid
            )
            result = comm.swap(placed)
        else:
            gate, up = dotf(xn, w_gate, NN), dotf(xn, w_up, NN)
            act, slope = gelu_parts(gate)
            hidden = (act * up).astype(BF)
            mlp = comm.scatter_rows(dotf(hidden, w_dn, NT))
            result = comm.swap(comm.from_relative((resid + mlp).astype(BF)))
            hidden_grad = dotf(cot_all, w_dn, NN).astype(BF).astype(F32)
            gate_grad = (hidden_grad * up * slope).astype(BF)
            up_grad = (hidden_grad * act).astype(BF)
            f_two = comm.scatter_rows(dotf(gate_grad, w_gate, NT) + dotf(up_grad, w_up, NT))
            resid_grad = cot.astype(F32) + normalize_back(f_two, xh_two, scale_two)
            attn_cot = comm.gather_rows(resid_grad.astype(BF))
            d_down = dotf(cot_all, hidden, TN)
            d_gate, d_up = dotf(xn, gate_grad, TN), dotf(xn, up_grad, TN)

        if paired:
            placed, *sums = backward_block(
                (d_gate, d_up, d_down), (q, k, v, o), lse, attn_cot, w_qk, w_vo, xh, x_half,
                resid_grad, tables, seg_col, seg_row,
            )
            token_grad = comm.swap(placed).astype(F32)
            s_gate, s_up, s_low, s_high, one_a, one_b = (w.astype(F32) for w in sums)
            in_raw = jnp.stack([s_gate[:, :units], s_up[:, :units]], axis=1)
            down_sum = jnp.concatenate([s_low[:, :units], s_high[:, :units]], axis=0).T
        else:
            wide = lambda g, d: jnp.concatenate([padded(g), d], axis=1)
            two_a, two_b = comm.reduce(wide(d_gate, d_down[:, :low]), wide(d_up, d_down[:, low:]))

            heads_grad = dotf(attn_cot, w_o, NN).astype(BF)
            pg = attn_bwd(q, k, v, o, heads_grad, lse, tables, seg_col, seg_row)
            d_out = dotf(attn_cot, o, TN)
            d_q, d_k, d_v = (dotf(xh, pg[i], TN) for i in range(3))
            one_a, one_b = comm.reduce(
                jnp.concatenate([d_q, d_k], axis=1), jnp.concatenate([d_v, d_out], axis=1)
            )
            f_one = comm.scatter_rows(
                dotf(pg[0], w_qk[:, :cols], NT)
                + dotf(pg[1], w_qk[:, cols:], NT)
                + dotf(pg[2], w_vo[:, :cols], NT)
            )
            token_grad = resid_grad + normalize_back(f_one, xh_one, scale_one)
            in_raw = jnp.stack([two_a[:, :units], two_b[:, :units]], axis=1)
            down_sum = jnp.concatenate([two_a[:, units + pad :], two_b[:, units + pad :]], axis=1).T

        qkv_raw = jnp.stack([one_a[:, :cols], one_a[:, cols:], one_b[:, :cols]], axis=1)
        gains = jnp.stack(
            [
                jnp.sum(qkv_raw * w_qkv.astype(F32), axis=(1, 2)),
                jnp.sum(in_raw * w_in.astype(F32), axis=(1, 2)),
            ]
        )
        gains = comm.sum_tensor(gains)
        return (
            result[None],
            token_grad[None],
            gains[0],
            gains[1],
            qkv_raw * gain_one[:, :, None],
            one_b[:, cols:].T,
            in_raw * gain_two[:, :, None],
            down_sum,
        )

    return local


def solution(mesh):
    paired = mesh.shape["dp"] == 16 and mesh.shape["tensor"] == 2
    return jax.shard_map(
        make_local(Chips if paired else Axes),
        mesh=mesh,
        in_specs=(
            P("dp", "tensor", None),
            P("dp", None),
            P("dp", None, "tensor"),
            P("tensor", "dp"),
            P("dp", None, "tensor"),
            P("tensor", "dp"),
            P("dp"),
            P("dp"),
            P("dp", "tensor", None),
        ),
        out_specs=(
            P("dp", "tensor", None),
            P("dp", "tensor", None),
            P("dp"),
            P("dp"),
            P("dp", None, "tensor"),
            P("tensor", "dp"),
            P("dp", None, "tensor"),
            P("tensor", "dp"),
        ),
        check_vma=False,
    )
```

```python
import math

import jax
import jax.numpy as jnp
from jax import lax
from jax.experimental import pallas as pl
from jax.experimental.pallas import tpu as pltpu
from jax.sharding import PartitionSpec as P

HD = 64
EPS = 1e-05
ROTARY_BASE = 160000.0
BF = jnp.bfloat16
F32 = jnp.float32


def dotf(a, b, dims):
    return lax.dot_general(a, b, (dims, ((), ())), preferred_element_type=F32)


NN = ((1,), (0,))
NT = ((1,), (1,))
TN = ((0,), (0,))


def rope_rates():
    return 1.0 / ROTARY_BASE ** (jnp.arange(HD // 2).astype(F32) * (2.0 / HD))


def rope_tables(positions):
    angles = positions.astype(F32)[:, None] * rope_rates()[None, :]
    cos, sin = jnp.cos(angles), jnp.sin(angles)
    zero = jnp.zeros_like(sin)
    cosine = jnp.concatenate([cos] * 4, axis=-1)
    upper = jnp.concatenate([-sin, zero] * 2, axis=-1)
    lower = jnp.concatenate([zero, sin] * 2, axis=-1)
    return cosine, upper, lower


def turn(u, upper, lower):
    return pltpu.roll(u, 128 - HD // 2, 1) * upper + pltpu.roll(u, HD // 2, 1) * lower


def attn_fwd_kernel(xh, wq, wk, wv, cos, upper, lower, seg_col, seg_row, o, q, k, v, lse, kh):
    length = xh.shape[0]
    rows = min(256, length)
    lane = lax.broadcasted_iota(jnp.int32, (length, 128), 1)
    first = lane < HD
    tokens = xh[...]
    qf = dotf(tokens, wq[...], NN)
    qf = qf * cos[...] + turn(qf, upper[...], lower[...])
    q[...] = (qf * (1.0 / math.sqrt(HD))).astype(BF)
    kf = dotf(tokens, wk[...], NN)
    kf = (kf * cos[...] + turn(kf, upper[...], lower[...])).astype(BF)
    k[...] = kf
    kh[0] = jnp.where(first, kf, jnp.zeros_like(kf))
    kh[1] = jnp.where(first, jnp.zeros_like(kf), kf)
    v[...] = dotf(tokens, wv[...], NN).astype(BF)

    def block(i, carry):
        at = pl.multiple_of(i * rows, rows)
        q_rows = q[pl.ds(at, rows), :]
        same = seg_col[pl.ds(at, rows), :] == seg_row[...]
        outs = []
        for head in range(2):
            scores = dotf(q_rows, kh[head], NT)
            scores = jnp.where(same, scores, -1e30)
            top = jnp.max(scores, axis=-1, keepdims=True)
            expv = jnp.exp(scores - top)
            total = jnp.sum(expv, axis=-1, keepdims=True)
            low = (expv * (1.0 / total)).astype(BF)
            outs.append(dotf(low, v[...], NN))
            level = top + jnp.log(total)
            flat = jnp.transpose(jnp.broadcast_to(level, (rows, 128)))
            lse[0, pl.ds(head, 1), pl.ds(at, rows)] = flat[0:1, :]
        o[pl.ds(at, rows), :] = jnp.where(first[:rows], outs[0], outs[1]).astype(BF)
        return carry

    lax.fori_loop(0, length // rows, block, 0)


def attn_fwd(xh, w_qk, w_vo, tables, seg_col, seg_row):
    length, width = xh.shape
    pairs = w_qk.shape[1] // 256
    whole = lambda a: pl.BlockSpec(a.shape, lambda h: (0,) * a.ndim)
    col = lambda off: pl.BlockSpec((width, 128), lambda h: (0, h + off))
    out = pl.BlockSpec((length, 128), lambda h: (0, h))
    shape = jax.ShapeDtypeStruct((length, pairs * 128), BF)
    flops = 2 * length * width * pairs * 384 + 4 * pairs * 2 * length * length * 128
    return pl.pallas_call(
        attn_fwd_kernel,
        grid=(pairs,),
        in_specs=[whole(xh), col(0), col(pairs), col(0)]
        + [whole(t) for t in tables]
        + [whole(seg_col), whole(seg_row)],
        out_specs=[out] * 4 + [pl.BlockSpec((1, 2, length), lambda h: (h, 0, 0))],
        out_shape=[shape] * 4 + [jax.ShapeDtypeStruct((pairs, 2, length), F32)],
        scratch_shapes=[pltpu.VMEM((2, length, 128), BF)],
        cost_estimate=pl.CostEstimate(
            flops=flops, bytes_accessed=length * width * 8, transcendentals=pairs * 2 * length * length
        ),
        name="attn_fwd",
    )(xh, w_qk, w_qk, w_vo, *tables, seg_col, seg_row)


def attn_bwd_kernel(
    q, k, v, o, do, lse, cos, upper, lower, seg_col, seg_row, pg, kh, dk, dv
):
    length = q.shape[0]
    rows = min(256, length)
    lane = lax.broadcasted_iota(jnp.int32, (length, 128), 1)
    first = lane < HD
    kf = k[...]
    none = jnp.zeros_like(kf)
    kh[0] = jnp.where(first, kf, none)
    kh[1] = jnp.where(first, none, kf)
    dk[...] = jnp.zeros_like(dk)
    dv[...] = jnp.zeros_like(dv)

    def block(i, carry):
        at = pl.multiple_of(i * rows, rows)
        here = pl.ds(at, rows)
        q_rows = q[here, :]
        g_rows = do[here, :]
        seg_here = seg_row[:, here]
        same = seg_col[...] == seg_here
        prod = g_rows.astype(F32) * o[here, :].astype(F32)
        f = first[:rows]
        blank = jnp.zeros_like(q_rows)
        dq = jnp.zeros((rows, 128), F32)
        for head in range(2):
            mine = f if head == 0 else jnp.logical_not(f)
            q_head = jnp.where(mine, q_rows, blank)
            g_head = jnp.where(mine, g_rows, blank)
            delta = lax.dot_general(
                jnp.ones((8, 128), F32),
                jnp.where(mine, prod, 0.0),
                (NT, ((), ())),
                precision=lax.Precision.HIGHEST,
                preferred_element_type=F32,
            )[0:1, :]
            scores = dotf(k[...], q_head, NT)
            level = lse[0, pl.ds(head, 1), here]
            probs = jnp.where(same, jnp.exp(scores - level), 0.0)
            dv[...] += dotf(probs.astype(BF), g_head, NN)
            dp = dotf(v[...], g_head, NT)
            ds = (probs * (dp - delta)).astype(BF)
            dk[...] += dotf(ds, q_head, NN)
            dq = dq + dotf(ds, kh[head], TN)
        dq = dq * (1.0 / math.sqrt(HD))
        c, a, b = cos[here, :], upper[here, :], lower[here, :]
        pg[0, here, :] = (dq * c - turn(dq, a, b)).astype(BF)
        return carry

    lax.fori_loop(0, length // rows, block, 0)
    dkf = dk[...]
    pg[1] = (dkf * cos[...] - turn(dkf, upper[...], lower[...])).astype(BF)
    pg[2] = dv[...].astype(BF)


def attn_bwd(q, k, v, o, do, lse, tables, seg_col, seg_row):
    length, width = q.shape
    pairs = width // 128
    whole = lambda a: pl.BlockSpec(a.shape, lambda h: (0,) * a.ndim)
    col = pl.BlockSpec((length, 128), lambda h: (0, h))
    return pl.pallas_call(
        attn_bwd_kernel,
        grid=(pairs,),
        in_specs=[col] * 5
        + [pl.BlockSpec((1, 2, length), lambda h: (h, 0, 0))]
        + [whole(t) for t in tables]
        + [whole(seg_col), whole(seg_row)],
        out_specs=pl.BlockSpec((3, length, 128), lambda h: (0, 0, h)),
        out_shape=jax.ShapeDtypeStruct((3, length, width), BF),
        scratch_shapes=[
            pltpu.VMEM((2, length, 128), BF),
            pltpu.VMEM((length, 128), F32),
            pltpu.VMEM((length, 128), F32),
        ],
        cost_estimate=pl.CostEstimate(
            flops=10 * pairs * 2 * length * length * 128,
            bytes_accessed=length * width * 20,
            transcendentals=pairs * 2 * length * length,
        ),
        name="attn_bwd",
    )(q, k, v, o, do, lse, *tables, seg_col, seg_row)


def in_chunks(total, size, body):
    def step(j, carry):
        body(pl.ds(pl.multiple_of(j * size, size), size))
        return carry

    lax.fori_loop(0, total // size, step, 0)
    if total % size:
        body(pl.ds(total - total % size, total % size))


SHARD = (4, 2, 2)


def place():
    dp = lax.axis_index("dp")
    return dp // 4, (dp // 2) % 2, dp % 2, lax.axis_index("tensor")


def partners():
    z, x, c, y = place()
    at = lambda z, x, c, y: ((z * 2 + x) * 2 + c, y)
    return {
        "z1": at(z + 1 - 2 * (z % 2), x, c, y),
        "z2": at(z + 2 - 4 * (z // 2), x, c, y),
        "z3": at(3 - z, x, c, y),
        "x": at(z, 1 - x, c, y),
        "y": at(z, x, c, 1 - y),
        "c": at(z, x, 1 - c, y),
    }


def meet(peers, other=None):
    barrier = pltpu.get_barrier_semaphore()
    greet = lambda peer: pl.semaphore_signal(
        barrier, inc=1, device_id=peer, device_id_type=pl.DeviceIdType.MESH
    )
    for peer in peers.values():
        greet(peer)
    if other is None:
        pl.semaphore_wait(barrier, len(peers))
    else:
        moved, peer = other

        @pl.when(moved)
        def _():
            greet(peer)

        pl.semaphore_wait(barrier, len(peers) + jnp.where(moved, 1, 0))


def exchanged():
    z, x, c, y = place()
    return c != y, ((z * 2 + x) * 2 + y, c)


def remote(src, dst, send_sem, recv_sem, peer):
    return pltpu.make_async_remote_copy(
        src_ref=src,
        dst_ref=dst,
        send_sem=send_sem,
        recv_sem=recv_sem,
        device_id=peer,
        device_id_type=pl.DeviceIdType.MESH,
    )


class Move:
    def __init__(self, src, dst, sems, i):
        send_sem, recv_sem, near_sem = sems
        self.moved, peer = exchanged()
        self.far = remote(src, dst, send_sem.at[i], recv_sem.at[i], peer)
        self.near = pltpu.make_async_copy(src, dst, near_sem.at[i])

    def start(self):
        @pl.when(self.moved)
        def _():
            self.far.start()

        @pl.when(jnp.logical_not(self.moved))
        def _():
            self.near.start()

    def wait(self):
        @pl.when(self.moved)
        def _():
            self.far.wait()

        @pl.when(jnp.logical_not(self.moved))
        def _():
            self.near.wait()


def move_sems(n):
    return [pltpu.SemaphoreType.DMA((n,))] * 3


def to_place(values):
    z, x, _, y = place()
    tiles = [values[:, j * 128 : (j + 1) * 128] for j in range(8)]
    tiles = [jnp.where(y == 1, pltpu.roll(t, 64, 1), t) for t in tiles]
    for bit, step in ((x, 1), (z % 2, 2), (z // 2, 4)):
        tiles = [jnp.where(bit == 1, tiles[j ^ step], tiles[j]) for j in range(8)]
    return jnp.concatenate(tiles, axis=1)


class Gather:
    MESSAGES = 15

    def __init__(self, own, buf, rows, axes, peers, sems, base):
        self.buf, self.rows, self.axes, self.peers = buf, rows, axes, peers
        self.own = own.at[rows]
        self.send_sem, self.recv_sem = sems
        self.base = base

    def slot(self, z, first, second):
        x, y = (first, second) if self.axes[0] == "x" else (second, first)
        return self.buf.at[z, x, y, self.rows]

    def copy(self, i):
        if i < 3:
            src, dst, peer = self.own, self.slot(i + 1, 0, 0), "z%d" % (i + 1)
        elif i < 7:
            src, dst, peer = self.slot(i - 3, 0, 0), self.slot(i - 3, 1, 0), self.axes[0]
        else:
            f, z = divmod(i - 7, 4)
            src, dst, peer = self.slot(z, f, 0), self.slot(z, f, 1), self.axes[1]
        if i in (3, 7):
            src = self.own
        n = self.base + i
        return remote(src, dst, self.send_sem.at[n], self.recv_sem.at[n], self.peers[peer])

    def start_z(self):
        for i in range(3):
            self.copy(i).start()

    def relay_z(self, z):
        if z:
            self.copy(z - 1).wait_recv()
        self.copy(3 + z).start()
        self.copy(7 + z).start()

    def relay_first(self, z):
        self.copy(3 + z).wait_recv()
        self.copy(11 + z).start()

    def finish(self):
        for i in range(7, 15):
            self.copy(i).wait_recv()
        for i in range(15):
            self.copy(i).wait_send()


def forward_kernel(
    a_in, b_in, g_in, u_in, d_in, x_in, c_in, seg_in, inverse,
    q, k, v, o, lse, xh, w_qk, w_vo, resid, xn, x_half, cot, cos, upper, lower, seg_col, seg_row,
    w_gate, w_up, w_down,
    a_own, b_own, g_own, u_own, d_own, c_own, seg_own,
    kh, x_rel, part, sent, got, send_sem, recv_sem, pair_send, pair_recv, own_sem, *moving,
):
    length = xh.shape[0]
    half = length // 2
    width = xh.shape[1]
    pairs = q.shape[1] // 128
    rows = 256
    core = place()[2]
    peers = partners()
    sems = (send_sem, recv_sem)
    n = Gather.MESSAGES
    whole, low, high = pl.ds(0, 64), pl.ds(0, 32), pl.ds(32, 32)
    one = [
        Gather(a_own, w_qk, whole, "xy", peers, sems, 0),
        Gather(b_own, w_vo, whole, "yx", peers, sems, n),
    ]
    two = [
        Gather(g_own, w_gate, whole, "xy", peers, sems, 2 * n),
        Gather(u_own, w_up, whole, "yx", peers, sems, 3 * n),
    ]
    three = [
        Gather(d_own, w_down, low, "xy", peers, sems, 4 * n),
        Gather(d_own, w_down, high, "yx", peers, sems, 5 * n),
    ]
    owns = [
        pltpu.make_async_copy(src, dst.at[0, 0, 0], own_sem.at[i])
        for i, (src, dst) in enumerate(
            ((a_own, w_qk), (b_own, w_vo), (g_own, w_gate), (u_own, w_up), (d_own, w_down))
        )
    ]
    move_a, move_b, move_x, move_seg, move_g, move_u, move_d, move_c = (
        Move(src, dst, moving, i)
        for i, (src, dst) in enumerate(
            (
                (a_in, a_own),
                (b_in, b_own),
                (x_in, x_half),
                (seg_in, seg_own),
                (g_in, g_own),
                (u_in, u_own),
                (d_in, d_own),
                (c_in, c_own),
            )
        )
    )
    meet(peers, exchanged())
    for move in (move_a, move_b, move_seg, move_x, move_g, move_u, move_d):
        move.start()

    def tables(here):
        shape = (here.size, 128)
        row = here.start + lax.broadcasted_iota(jnp.int32, shape, 0) + core * half
        row = jnp.where(row >= length, row - length, row)
        angle = row.astype(F32) * inverse[0:1, :]
        front = lax.broadcasted_iota(jnp.int32, shape, 1) % HD < HD // 2
        sin = jnp.sin(angle)
        cos[here, :] = jnp.cos(angle)
        upper[here, :] = jnp.where(front, -sin, 0.0)
        lower[here, :] = jnp.where(front, 0.0, sin)

    move_a.wait()
    move_b.wait()
    for gather in one:
        gather.start_z()
    for gather in one:
        gather.relay_z(0)
    for copy in owns[:2]:
        copy.start()
    in_chunks(length, 64, tables)
    move_seg.wait()
    ids = seg_own[...]
    ids = jnp.where(core == 0, ids, jnp.concatenate([ids[:, half:], ids[:, :half]], axis=1))
    seg_row[...] = ids
    seg_col[...] = jnp.transpose(jnp.broadcast_to(ids[0:1, :], (128, length)))
    move_x.wait()

    def first_norm(i, carry):
        here = pl.ds(pl.multiple_of(i * 128, 128), 128)
        values = to_place(x_half[here, :].astype(F32))
        x_rel[here, :] = values.astype(BF)
        xh[here, :] = normalize(values)[0].astype(BF)
        return carry

    lax.fori_loop(0, half // 128, first_norm, 0)
    for z in (1, 2, 3):
        for gather in one:
            gather.relay_z(z)
    swap_xh = remote(
        xh.at[pl.ds(0, half)], xh.at[pl.ds(half, half)], pair_send.at[0], pair_recv.at[0], peers["c"]
    )
    swap_xh.start()
    move_g.wait()
    move_u.wait()
    for gather in two:
        gather.start_z()
    for z in range(4):
        for gather in one:
            gather.relay_first(z)
    move_d.wait()
    for gather in three:
        gather.start_z()
    for copy in owns[2:]:
        copy.start()
    swap_xh.wait()
    for gather in one:
        gather.finish()
    for copy in owns[:2]:
        copy.wait()

    events = {}
    for z in range(4):
        events.setdefault(1 + z, []).extend((g.relay_z, z) for g in two)
        events.setdefault(6 + z, []).extend((g.relay_first, z) for g in two)
        events.setdefault(9 + z, []).extend((g.relay_z, z) for g in three)
    events.setdefault(5, []).append((lambda _: move_c.start(), 0))
    first = lax.broadcasted_iota(jnp.int32, (length, 128), 1) < HD

    def pair(h, carry):
        lanes = pl.ds(pl.multiple_of(h * 128, 128), 128)
        lanes_k = pl.ds(pl.multiple_of((h + pairs) * 128, 128), 128)
        weight = lambda ref, cols: ref[:, :, :, :, cols].reshape(width, 128)
        tokens = xh[...]
        qf = dotf(tokens, weight(w_qk, lanes), NN)
        qf = qf * cos[...] + turn(qf, upper[...], lower[...])
        q[:, lanes] = (qf * (1.0 / math.sqrt(HD))).astype(BF)
        kf = dotf(tokens, weight(w_qk, lanes_k), NN)
        kf = (kf * cos[...] + turn(kf, upper[...], lower[...])).astype(BF)
        k[:, lanes] = kf
        kh[0] = jnp.where(first, kf, jnp.zeros_like(kf))
        kh[1] = jnp.where(first, jnp.zeros_like(kf), kf)
        v[:, lanes] = dotf(tokens, weight(w_vo, lanes), NN).astype(BF)

        def block(i, carry):
            for step, calls in events.items():

                @pl.when(h * (length // rows) + i == step)
                def _():
                    for call, z in calls:
                        call(z)

            at = pl.multiple_of(i * rows, rows)
            q_rows = q[pl.ds(at, rows), lanes]
            same = seg_col[pl.ds(at, rows), 0:1] == seg_row[0:1, :]
            outs = []
            for head in range(2):
                scores = dotf(q_rows, kh[head], NT)
                scores = jnp.where(same, scores, -1e30)
                top = jnp.max(scores, axis=-1, keepdims=True)
                expv = jnp.exp(scores - top)
                total = jnp.sum(expv, axis=-1, keepdims=True)
                low_probs = (expv * (1.0 / total)).astype(BF)
                outs.append(dotf(low_probs, v[:, lanes], NN))
                level = top + jnp.log(total)
                flat = jnp.transpose(jnp.broadcast_to(level, (rows, 128)))
                lse[h, pl.ds(head, 1), pl.ds(at, rows)] = flat[0:1, :]
            o[pl.ds(at, rows), lanes] = jnp.where(first[:rows], outs[0], outs[1]).astype(BF)
            return carry

        return lax.fori_loop(0, length // rows, block, carry)

    lax.fori_loop(0, pairs, pair, 0)
    w_o = w_vo[:, :, :, :, pairs * 128 :].reshape(width, pairs * 128)

    def project(i, carry):
        at = pl.multiple_of(half + i * rows, rows)
        sent[pl.ds(pl.multiple_of(i * rows, rows), rows), :] = dotf(
            o[pl.ds(at, rows), :], w_o, NT
        ).astype(BF)
        return carry

    lax.fori_loop(0, half // rows, project, 0)

    def project_own(i, carry):
        here = pl.ds(pl.multiple_of(i * rows, rows), rows)
        part[here, :] = dotf(o[here, :], w_o, NT)
        return carry

    give = remote(sent, got, pair_send.at[1], pair_recv.at[1], peers["c"])
    lax.fori_loop(0, half // rows, project_own, 0)
    give.start()
    move_c.wait()

    def turn_cot(here):
        cot[here, :] = to_place(c_own[here, :].astype(F32)).astype(BF)

    in_chunks(half, 128, turn_cot)
    swap_cot = remote(
        cot.at[pl.ds(0, half)], cot.at[pl.ds(half, half)], pair_send.at[3], pair_recv.at[3], peers["c"]
    )
    swap_cot.start()
    for gather in three:
        for z in range(4):
            gather.relay_first(z)
    give.wait()

    def second_norm(i, carry):
        here = pl.ds(pl.multiple_of(i * 128, 128), 128)
        values = x_rel[here, :].astype(F32) + (part[here, :] + got[here, :].astype(F32))
        resid[here, :] = values
        xn[here, :] = normalize(values)[0].astype(BF)
        return carry

    lax.fori_loop(0, half // 128, second_norm, 0)
    swap_xn = remote(
        xn.at[pl.ds(0, half)], xn.at[pl.ds(half, half)], pair_send.at[2], pair_recv.at[2], peers["c"]
    )
    swap_xn.start()
    for gather in two + three:
        gather.finish()
    for copy in owns[2:]:
        copy.wait()
    swap_cot.wait()
    swap_xn.wait()


def forward_block(owned, x_half, cot_half, seg, inverse):
    half, width = x_half.shape
    length = 2 * half
    cols = owned[0].shape[1] // 2
    pairs = cols // 128
    units = owned[2].shape[1]
    shard = width // 16
    vmem = pl.BlockSpec(memory_space=pltpu.VMEM)
    any_ = pl.BlockSpec(memory_space=pl.ANY)
    gathered = lambda n: jax.ShapeDtypeStruct(SHARD + (shard, n), BF)
    heads = jax.ShapeDtypeStruct((length, cols), BF)
    flat = jax.ShapeDtypeStruct((length, width), BF)
    table = jax.ShapeDtypeStruct((length, 128), F32)
    return pl.pallas_call(
        forward_kernel,
        in_specs=[any_] * 8 + [vmem],
        out_specs=[vmem] * 17 + [any_] * 3,
        out_shape=[heads] * 4
        + [
            jax.ShapeDtypeStruct((pairs, 2, length), F32),
            flat,
            gathered(2 * cols),
            gathered(2 * cols),
            jax.ShapeDtypeStruct((half, width), F32),
            flat,
            jax.ShapeDtypeStruct((half, width), BF),
            flat,
        ]
        + [table] * 4
        + [jax.ShapeDtypeStruct((8, length), F32)]
        + [gathered(units)] * 3,
        scratch_shapes=[pltpu.VMEM((shard, 2 * cols), BF)] * 2
        + [pltpu.VMEM((shard, units), BF)] * 3
        + [
            pltpu.VMEM((half, width), BF),
            pltpu.VMEM((8, length), F32),
            pltpu.VMEM((2, length, 128), BF),
            pltpu.VMEM((half, width), BF),
            pltpu.VMEM((half, width), F32),
            pltpu.VMEM((half, width), BF),
            pltpu.VMEM((half, width), BF),
            pltpu.SemaphoreType.DMA((6 * Gather.MESSAGES,)),
            pltpu.SemaphoreType.DMA((6 * Gather.MESSAGES,)),
            pltpu.SemaphoreType.DMA((4,)),
            pltpu.SemaphoreType.DMA((4,)),
            pltpu.SemaphoreType.DMA((5,)),
        ]
        + move_sems(8),
        compiler_params=pltpu.CompilerParams(
            collective_id=0, has_side_effects=True, vmem_limit_bytes=60 << 20
        ),
        name="forward_block",
    )(*owned, x_half, cot_half, seg, inverse)


def mlp_kernel(
    xn, cot, w_gate, w_up, w_down, resid,
    result, resid_grad, attn_cot, d_gate, d_up, d_down,
    hidden, gate_grad, up_grad, own, sent, got, placed, send_sem, recv_sem, *moving,
):
    length, width = xn.shape
    half = length // 2
    units = w_gate.shape[1]
    peer = partners()["c"]
    meet({"c": peer}, exchanged())
    move = Move(placed, result, moving, 0)

    def units_of(rows, cols):
        gate = dotf(xn[rows, :], w_gate[:, cols], NN)
        up = dotf(xn[rows, :], w_up[:, cols], NN)
        grad = dotf(cot[rows, :], w_down[:, cols], NN).astype(BF).astype(F32)
        act, slope = gelu_parts(gate)
        hidden[rows, cols] = (act * up).astype(BF)
        gate_grad[rows, cols] = (grad * up * slope).astype(BF)
        up_grad[rows, cols] = (grad * act).astype(BF)

    def phase(rows, put):
        in_chunks(units, 256, lambda cols: units_of(rows, cols))

        def sums(here):
            put[0, :, here] = dotf(hidden[rows, :], w_down[here, :], NT).astype(put.dtype)
            both = dotf(gate_grad[rows, :], w_gate[here, :], NT)
            both = both + dotf(up_grad[rows, :], w_up[here, :], NT)
            put[1, :, here] = both.astype(put.dtype)

        in_chunks(width, 256, sums)

    phase(pl.ds(half, half), sent)
    give = remote(sent, got, send_sem.at[0], recv_sem.at[0], peer)
    give.start()
    phase(pl.ds(0, half), own)
    give.wait()

    def finish(here):
        values = resid[here, :]
        mlp = own[0, here, :] + got[0, here, :].astype(F32)
        placed[here, :] = to_place(values + mlp).astype(BF)
        xhat, scale = normalize(values)
        back = normalize_back(own[1, here, :] + got[1, here, :].astype(F32), xhat, scale)
        grad = cot[here, :].astype(F32) + back
        resid_grad[here, :] = grad
        attn_cot[here, :] = grad.astype(BF)

    in_chunks(half, 64, finish)
    swap = remote(
        attn_cot.at[pl.ds(0, half)], attn_cot.at[pl.ds(half, half)], send_sem.at[1], recv_sem.at[1], peer
    )
    swap.start()
    move.start()

    def weights(here):
        left = jnp.transpose(cot[:, here])
        d_down[here, :] = dotf(left, hidden[...], NN).astype(BF)
        left = jnp.transpose(xn[:, here])
        d_gate[here, :] = dotf(left, gate_grad[...], NN).astype(BF)
        d_up[here, :] = dotf(left, up_grad[...], NN).astype(BF)

    in_chunks(width, 256, weights)
    swap.wait()
    move.wait()


def mlp_block(xn, cot, w_gate, w_up, w_down, resid):
    length, width = xn.shape
    half = length // 2
    units = w_gate.shape[1]
    vmem = pl.BlockSpec(memory_space=pltpu.VMEM)
    grads = jax.ShapeDtypeStruct((width, units), BF)
    return pl.pallas_call(
        mlp_kernel,
        in_specs=[vmem] * 6,
        out_specs=[vmem] * 6,
        out_shape=[
            jax.ShapeDtypeStruct((half, width), BF),
            jax.ShapeDtypeStruct((half, width), F32),
            jax.ShapeDtypeStruct((length, width), BF),
            grads,
            grads,
            grads,
        ],
        scratch_shapes=[pltpu.VMEM((length, units), BF)] * 3
        + [
            pltpu.VMEM((2, half, width), F32),
            pltpu.VMEM((2, half, width), BF),
            pltpu.VMEM((2, half, width), BF),
            pltpu.VMEM((half, width), BF),
            pltpu.SemaphoreType.DMA((2,)),
            pltpu.SemaphoreType.DMA((2,)),
        ]
        + move_sems(1),
        compiler_params=pltpu.CompilerParams(
            collective_id=1, has_side_effects=True, vmem_limit_bytes=60 << 20
        ),
        name="mlp_block",
    )(xn, cot, w_gate, w_up, w_down, resid)


class Reduce:
    MESSAGES = 12
    ORDER = (2, 3, 1, 0)

    def __init__(self, parts, near, rows, axes, peers, sems, base, bufs, out):
        self.parts, self.near, self.rows, self.axes, self.peers = parts, near, rows, axes, peers
        self.send_sem, self.recv_sem = sems
        self.base = base
        self.one, self.two, self.three, self.sum = bufs
        self.out = out

    def link(self, i, src, dst, peer):
        n = self.base + i
        return remote(src, dst, self.send_sem.at[n], self.recv_sem.at[n], peer)

    def first(self, z):
        if self.axes == "xy":
            src = self.parts.at[z, :, 1, self.rows]
        else:
            src = self.parts.at[z, 1, :, self.rows]
        return self.link(z, src, self.one.at[z], self.peers[self.axes[1]])

    def second(self, z):
        return self.link(4 + z, self.one.at[z, 1], self.two.at[z], self.peers[self.axes[0]])

    def third(self, z):
        return self.link(7 + z, self.two.at[z], self.three.at[z - 1], self.peers["z%d" % z])

    def start(self):
        for z in self.ORDER:
            self.first(z).start()

    def relay_first(self, z):
        self.first(z).wait_recv()
        self.one[z] = (self.one[z].astype(F32) + self.near(z).astype(F32)).astype(BF)
        self.second(z).start()

    def relay_second(self, z):
        self.second(z).wait_recv()
        self.two[z] = (self.two[z].astype(F32) + self.one[z, 0].astype(F32)).astype(BF)
        if z:
            self.third(z).start()

    def last(self):
        moved, peer = exchanged()
        return moved, self.link(11, self.sum, self.out, peer)

    def finish(self):
        total = self.two[0].astype(F32)
        for z in (1, 2, 3):
            self.third(z).wait_recv()
            total = total + self.three[z - 1].astype(F32)
        self.sum[...] = total.astype(BF)
        moved, copy = self.last()

        @pl.when(moved)
        def _():
            copy.start()

        @pl.when(jnp.logical_not(moved))
        def _():
            self.out[...] = self.sum[...]

    def close(self):
        for z in range(4):
            self.first(z).wait_send()
            self.second(z).wait_send()
            if z:
                self.third(z).wait_send()
        moved, copy = self.last()

        @pl.when(moved)
        def _():
            copy.wait()


def backward_kernel(
    d_gate, d_up, d_down, q, k, v, o, lse, attn_cot, w_qk, w_vo, xh, x_half, resid_grad,
    cos, upper, lower, seg_col, seg_row,
    token_grad, s_gate, s_up, s_down_low, s_down_high, s_qk, s_vo,
    d_qk, d_vo, pg, heads_grad, kh, dk, dv, own, sent, got, placed, near_gate, near_up, near_low, near_high,
    *rest,
):
    bufs = [rest[4 * i : 4 * i + 4] for i in range(6)]
    send_sem, recv_sem, pair_send, pair_recv, near_sem, *moving = rest[24:]
    length, width = xh.shape
    half = length // 2
    cols = q.shape[1]
    pairs = cols // 128
    rows = 256
    peers = partners()
    sems = (send_sem, recv_sem)
    n = Reduce.MESSAGES
    whole, low, high = pl.ds(0, 64), pl.ds(0, 32), pl.ds(32, 32)
    held = lambda ref: (lambda z: ref[z])
    gate = Reduce(d_gate, held(near_gate), whole, "xy", peers, sems, 0, bufs[0], s_gate)
    up = Reduce(d_up, held(near_up), whole, "yx", peers, sems, n, bufs[1], s_up)
    down = [
        Reduce(d_down, held(near_low), low, "xy", peers, sems, 2 * n, bufs[2], s_down_low),
        Reduce(d_down, held(near_high), high, "yx", peers, sems, 3 * n, bufs[3], s_down_high),
    ]
    one = [gate, up]
    last = [
        Reduce(d_qk, lambda z: d_qk[z, :, 0], whole, "xy", peers, sems, 4 * n, bufs[4], s_qk),
        Reduce(d_vo, lambda z: d_vo[z, 0], whole, "yx", peers, sems, 5 * n, bufs[5], s_vo),
    ]
    nears = [
        pltpu.make_async_copy(src, dst, near_sem.at[i])
        for i, (src, dst) in enumerate(
            (
                (d_gate.at[:, :, 0], near_gate),
                (d_up.at[:, 0], near_up),
                (d_down.at[:, :, 0, low], near_low),
                (d_down.at[:, 0, :, high], near_high),
            )
        )
    ]
    for copy in nears:
        copy.start()
    meet(peers, exchanged())
    for part in one:
        part.start()

    def heads(here):
        heads_grad[here, :] = dotf(attn_cot[here, :], w_vo[:, cols:], NN).astype(BF)

    in_chunks(length, 256, heads)

    def out_weights(z, carry):
        here = pl.ds(pl.multiple_of(z * 256, 256), 256)
        value = dotf(jnp.transpose(attn_cot[:, here]), o[...], NN).astype(BF)
        d_vo[z, :, :, :, cols:] = value.reshape(2, 2, 64, cols)
        return carry

    lax.fori_loop(0, width // 256, out_weights, 0)
    for copy in nears:
        copy.wait()

    events = {}
    for i, z in enumerate(Reduce.ORDER):
        events.setdefault(2 + 4 * i, []).extend((lambda r=r, z=z: r.relay_first(z)) for r in one)
    events.setdefault(11, []).extend(r.start for r in down)
    lane = lax.broadcasted_iota(jnp.int32, (length, 128), 1)
    first = lane < HD

    def pair(h, carry):
        lanes = pl.ds(pl.multiple_of(h * 128, 128), 128)
        kf = k[:, lanes]
        none = jnp.zeros_like(kf)
        kh[0] = jnp.where(first, kf, none)
        kh[1] = jnp.where(first, none, kf)
        dk[...] = jnp.zeros_like(dk)
        dv[...] = jnp.zeros_like(dv)

        def block(i, carry):
            for step, calls in events.items():

                @pl.when(h * (length // rows) + i == step)
                def _():
                    for call in calls:
                        call()

            at = pl.multiple_of(i * rows, rows)
            here = pl.ds(at, rows)
            q_rows = q[here, lanes]
            g_rows = heads_grad[here, lanes]
            same = seg_col[:, 0:1] == seg_row[0:1, here]
            prod = g_rows.astype(F32) * o[here, lanes].astype(F32)
            f = first[:rows]
            blank = jnp.zeros_like(q_rows)
            dq = jnp.zeros((rows, 128), F32)
            for head in range(2):
                mine = f if head == 0 else jnp.logical_not(f)
                q_head = jnp.where(mine, q_rows, blank)
                g_head = jnp.where(mine, g_rows, blank)
                delta = lax.dot_general(
                    jnp.ones((8, 128), F32),
                    jnp.where(mine, prod, 0.0),
                    (NT, ((), ())),
                    precision=lax.Precision.HIGHEST,
                    preferred_element_type=F32,
                )[0:1, :]
                scores = dotf(k[:, lanes], q_head, NT)
                level = lse[h, pl.ds(head, 1), here]
                probs = jnp.where(same, jnp.exp(scores - level), 0.0)
                dv[...] += dotf(probs.astype(BF), g_head, NN)
                dp = dotf(v[:, lanes], g_head, NT)
                ds = (probs * (dp - delta)).astype(BF)
                dk[...] += dotf(ds, q_head, NN)
                dq = dq + dotf(ds, kh[head], TN)
            dq = dq * (1.0 / math.sqrt(HD))
            c, a, b = cos[here, :], upper[here, :], lower[here, :]
            pg[0, here, lanes] = (dq * c - turn(dq, a, b)).astype(BF)
            return carry

        lax.fori_loop(0, length // rows, block, 0)
        dkf = dk[...]
        pg[1, :, lanes] = (dkf * cos[...] - turn(dkf, upper[...], lower[...])).astype(BF)
        pg[2, :, lanes] = dv[...].astype(BF)
        return carry

    lax.fori_loop(0, pairs, pair, 0)

    def weights(z, carry):
        left = jnp.transpose(xh[:, pl.ds(pl.multiple_of(z * 256, 256), 256)])
        for i, (ref, at) in enumerate(((d_qk, 0), (d_qk, cols), (d_vo, 0))):
            value = dotf(left, pg[i], NN).astype(BF)
            ref[z, :, :, :, at : at + cols] = value.reshape(2, 2, 64, cols)
        return carry

    lax.fori_loop(0, width // 256, weights, 0)

    def back(tokens, put):
        def step(here):
            total = dotf(pg[0, tokens, :], w_qk[here, :cols], NT)
            total = total + dotf(pg[1, tokens, :], w_qk[here, cols:], NT)
            put[:, here] = (total + dotf(pg[2, tokens, :], w_vo[here, :cols], NT)).astype(put.dtype)

        in_chunks(width, 256, step)

    back(pl.ds(half, half), sent)
    for part in last:
        part.start()
    give = remote(sent, got, pair_send.at[0], pair_recv.at[0], peers["c"])
    give.start()
    back(pl.ds(0, half), own)
    for z in Reduce.ORDER:
        for part in one:
            part.relay_second(z)
    give.wait()

    def finish(here):
        xhat, scale = normalize(to_place(x_half[here, :].astype(F32)))
        f = own[here, :] + got[here, :].astype(F32)
        value = resid_grad[here, :] + normalize_back(f, xhat, scale)
        placed[here, :] = to_place(value).astype(BF)

    in_chunks(half, 64, finish)
    move = Move(placed, token_grad, moving, 0)
    move.start()
    for z in Reduce.ORDER:
        for part in down:
            part.relay_first(z)
    for part in one:
        part.finish()
    for z in Reduce.ORDER:
        for part in down:
            part.relay_second(z)
        for part in last:
            part.relay_first(z)
    for part in down:
        part.finish()
    for z in Reduce.ORDER:
        for part in last:
            part.relay_second(z)
    for part in last:
        part.finish()
    for part in one + down + last:
        part.close()
    move.wait()


def backward_block(grads, heads, lse, attn_cot, w_qk, w_vo, xh, x_half, resid_grad, tables, seg_col, seg_row):
    length, width = xh.shape
    half = length // 2
    cols = heads[0].shape[1]
    units = grads[0].shape[1]
    shard = width // 16
    vmem = pl.BlockSpec(memory_space=pltpu.VMEM)
    any_ = pl.BlockSpec(memory_space=pl.ANY)
    sizes = [(shard, units), (shard, units), (shard // 2, units), (shard // 2, units)]
    sizes += [(shard, 2 * cols)] * 2
    bufs = []
    for size in sizes:
        bufs += [
            pltpu.VMEM((4, 2) + size, BF),
            pltpu.VMEM((4,) + size, BF),
            pltpu.VMEM((3,) + size, BF),
            pltpu.VMEM(size, BF),
        ]
    messages = 6 * Reduce.MESSAGES
    return pl.pallas_call(
        backward_kernel,
        in_specs=[any_] * 3 + [vmem] * 16,
        out_specs=[vmem] * 7,
        out_shape=[jax.ShapeDtypeStruct((half, width), BF)]
        + [jax.ShapeDtypeStruct(size, BF) for size in sizes],
        scratch_shapes=[pltpu.VMEM(SHARD + (shard, 2 * cols), BF)] * 2
        + [
            pltpu.VMEM((3, length, cols), BF),
            pltpu.VMEM((length, cols), BF),
            pltpu.VMEM((2, length, 128), BF),
            pltpu.VMEM((length, 128), F32),
            pltpu.VMEM((length, 128), F32),
            pltpu.VMEM((half, width), F32),
            pltpu.VMEM((half, width), BF),
            pltpu.VMEM((half, width), BF),
            pltpu.VMEM((half, width), BF),
        ]
        + [pltpu.VMEM((4, 2) + size, BF) for size in sizes[:4]]
        + bufs
        + [
            pltpu.SemaphoreType.DMA((messages,)),
            pltpu.SemaphoreType.DMA((messages,)),
            pltpu.SemaphoreType.DMA((1,)),
            pltpu.SemaphoreType.DMA((1,)),
            pltpu.SemaphoreType.DMA((4,)),
        ]
        + move_sems(1),
        compiler_params=pltpu.CompilerParams(
            collective_id=2, has_side_effects=True, vmem_limit_bytes=60 << 20
        ),
        name="backward_block",
    )(
        *(g.reshape(SHARD + (shard, units)) for g in grads),
        *heads, lse, attn_cot, w_qk, w_vo, xh, x_half, resid_grad, *tables, seg_col, seg_row,
    )


class Chips:
    def sum_tensor(self, value):
        pairs = [(2 * i + y, 2 * i + 1 - y) for i in range(16) for y in range(2)]
        return value + lax.ppermute(value, ("dp", "tensor"), pairs)


class Axes:
    def gather_rows(self, value):
        return lax.all_gather(value, "tensor", axis=0, tiled=True)

    def scatter_rows(self, value):
        return lax.psum_scatter(value.astype(BF), "tensor", scatter_dimension=0, tiled=True).astype(F32)

    def reduce(self, a, b):
        return tuple(
            lax.psum_scatter(w.astype(BF), "dp", scatter_dimension=0, tiled=True).astype(F32)
            for w in (a, b)
        )

    def sum_tensor(self, value):
        return lax.psum(value, "tensor")


def normalize(values):
    centred = values - jnp.mean(values, axis=-1, keepdims=True)
    scale = lax.rsqrt(jnp.mean(centred * centred, axis=-1, keepdims=True) + EPS)
    return centred * scale, scale


def normalize_back(f, xhat, scale):
    return scale * (
        f
        - jnp.mean(f, axis=-1, keepdims=True)
        - xhat * jnp.mean(f * xhat, axis=-1, keepdims=True)
    )


def gelu_parts(gate):
    half_erf = 0.5 * (1.0 + lax.erf(gate * (1.0 / math.sqrt(2.0))))
    density = jnp.exp(-0.5 * gate * gate) * (1.0 / math.sqrt(2.0 * math.pi))
    return gate * half_erf, half_erf + gate * density


def make_local(comm_type):
    def local(tokens, segments, w_qkv, w_out, w_in, w_down, g_attn, g_mlp, cotangent):
        comm = comm_type()
        paired = comm_type is Chips
        shard = w_qkv.shape[0]
        cols = w_qkv.shape[2]
        units = w_in.shape[2]
        low = 128 * (units // 256)
        pad = 128 * pl.cdiv(units, 128) - units
        gain_one = g_attn.astype(F32)[:, None]
        gain_two = g_mlp.astype(F32)[:, None]
        scaled = lambda w, g: (w.astype(F32) * g).astype(BF)
        padded = lambda w: jnp.pad(w, ((0, 0), (0, pad)))
        down_rows = w_down.T
        a_one = jnp.concatenate([scaled(w_qkv[:, 0], gain_one), scaled(w_qkv[:, 1], gain_one)], axis=1)
        b_one = jnp.concatenate([scaled(w_qkv[:, 2], gain_one), w_out.T], axis=1)
        own_gate, own_up = scaled(w_in[:, 0], gain_two), scaled(w_in[:, 1], gain_two)

        owned = (a_one, b_one, own_gate, own_up, down_rows)
        if paired:
            owned = owned[:2] + tuple(padded(w) for w in owned[2:])
            seg = jnp.broadcast_to(segments.astype(F32), (8, segments.shape[1]))
            inverse = jnp.broadcast_to(jnp.tile(rope_rates(), 4), (8, 128))
            (
                q, k, v, o, lse, xh, w_qk, w_vo, resid, xn, x_half, cot_all, *tables, seg_col, seg_row,
                w_gate, w_up, w_dn,
            ) = forward_block(owned, tokens[0], cotangent[0], seg, inverse)
            w_qk, w_vo, w_gate, w_up, w_dn = (
                w.reshape(-1, w.shape[-1]) for w in (w_qk, w_vo, w_gate, w_up, w_dn)
            )
        else:
            w_qk, w_vo, w_gate, w_up, w_dn = (
                lax.all_gather(w, "dp", axis=0, tiled=True) for w in owned
            )
            w_o = w_vo[:, cols:]
            seg_col, seg_row = segments[0][:, None], segments
            cot = cotangent[0]
            cot_all = comm.gather_rows(cot)
            tables = rope_tables(jnp.arange(segments.shape[1]))
            x_in = tokens[0].astype(F32)
            xh_one, scale_one = normalize(x_in)
            xh = comm.gather_rows(xh_one.astype(BF))
            o, q, k, v, lse = attn_fwd(xh, w_qk, w_vo, tables, seg_col, seg_row)
            resid = x_in + comm.scatter_rows(dotf(o, w_o, NT))
            xh_two, scale_two = normalize(resid)
            xn = comm.gather_rows(xh_two.astype(BF))
        if paired:
            result, resid_grad, attn_cot, d_gate, d_up, d_down = mlp_block(
                xn, cot_all, w_gate, w_up, w_dn, resid
            )
        else:
            gate, up = dotf(xn, w_gate, NN), dotf(xn, w_up, NN)
            act, slope = gelu_parts(gate)
            hidden = (act * up).astype(BF)
            mlp = comm.scatter_rows(dotf(hidden, w_dn, NT))
            result = (resid + mlp).astype(BF)
            hidden_grad = dotf(cot_all, w_dn, NN).astype(BF).astype(F32)
            gate_grad = (hidden_grad * up * slope).astype(BF)
            up_grad = (hidden_grad * act).astype(BF)
            f_two = comm.scatter_rows(dotf(gate_grad, w_gate, NT) + dotf(up_grad, w_up, NT))
            resid_grad = cot.astype(F32) + normalize_back(f_two, xh_two, scale_two)
            attn_cot = comm.gather_rows(resid_grad.astype(BF))
            d_down = dotf(cot_all, hidden, TN)
            d_gate, d_up = dotf(xn, gate_grad, TN), dotf(xn, up_grad, TN)

        if paired:
            token_grad, *sums = backward_block(
                (d_gate, d_up, d_down), (q, k, v, o), lse, attn_cot, w_qk, w_vo, xh, x_half,
                resid_grad, tables, seg_col, seg_row,
            )
            token_grad = token_grad.astype(F32)
            s_gate, s_up, s_low, s_high, one_a, one_b = (w.astype(F32) for w in sums)
            in_raw = jnp.stack([s_gate[:, :units], s_up[:, :units]], axis=1)
            down_sum = jnp.concatenate([s_low[:, :units], s_high[:, :units]], axis=0).T
        else:
            wide = lambda g, d: jnp.concatenate([padded(g), d], axis=1)
            two_a, two_b = comm.reduce(wide(d_gate, d_down[:, :low]), wide(d_up, d_down[:, low:]))

            heads_grad = dotf(attn_cot, w_o, NN).astype(BF)
            pg = attn_bwd(q, k, v, o, heads_grad, lse, tables, seg_col, seg_row)
            d_out = dotf(attn_cot, o, TN)
            d_q, d_k, d_v = (dotf(xh, pg[i], TN) for i in range(3))
            one_a, one_b = comm.reduce(
                jnp.concatenate([d_q, d_k], axis=1), jnp.concatenate([d_v, d_out], axis=1)
            )
            f_one = comm.scatter_rows(
                dotf(pg[0], w_qk[:, :cols], NT)
                + dotf(pg[1], w_qk[:, cols:], NT)
                + dotf(pg[2], w_vo[:, :cols], NT)
            )
            token_grad = resid_grad + normalize_back(f_one, xh_one, scale_one)
            in_raw = jnp.stack([two_a[:, :units], two_b[:, :units]], axis=1)
            down_sum = jnp.concatenate([two_a[:, units + pad :], two_b[:, units + pad :]], axis=1).T

        qkv_raw = jnp.stack([one_a[:, :cols], one_a[:, cols:], one_b[:, :cols]], axis=1)
        gains = jnp.stack(
            [
                jnp.sum(qkv_raw * w_qkv.astype(F32), axis=(1, 2)),
                jnp.sum(in_raw * w_in.astype(F32), axis=(1, 2)),
            ]
        )
        gains = comm.sum_tensor(gains)
        return (
            result[None],
            token_grad[None],
            gains[0],
            gains[1],
            qkv_raw * gain_one[:, :, None],
            one_b[:, cols:].T,
            in_raw * gain_two[:, :, None],
            down_sum,
        )

    return local


def solution(mesh):
    paired = mesh.shape["dp"] == 16 and mesh.shape["tensor"] == 2
    return jax.shard_map(
        make_local(Chips if paired else Axes),
        mesh=mesh,
        in_specs=(
            P("dp", "tensor", None),
            P("dp", None),
            P("dp", None, "tensor"),
            P("tensor", "dp"),
            P("dp", None, "tensor"),
            P("tensor", "dp"),
            P("dp"),
            P("dp"),
            P("dp", "tensor", None),
        ),
        out_specs=(
            P("dp", "tensor", None),
            P("dp", "tensor", None),
            P("dp"),
            P("dp"),
            P("dp", None, "tensor"),
            P("tensor", "dp"),
            P("dp", None, "tensor"),
            P("tensor", "dp"),
        ),
        check_vma=False,
    )
```

```python
import math

import jax
import jax.numpy as jnp
from jax import lax
from jax.experimental import pallas as pl
from jax.experimental.pallas import tpu as pltpu
from jax.sharding import PartitionSpec as P

HD = 64
EPS = 1e-05
ROTARY_BASE = 160000.0
BF = jnp.bfloat16
F32 = jnp.float32


def dotf(a, b, dims):
    return lax.dot_general(a, b, (dims, ((), ())), preferred_element_type=F32)


NN = ((1,), (0,))
NT = ((1,), (1,))
TN = ((0,), (0,))


def rope_rates():
    return 1.0 / ROTARY_BASE ** (jnp.arange(HD // 2).astype(F32) * (2.0 / HD))


def rope_tables(positions):
    angles = positions.astype(F32)[:, None] * rope_rates()[None, :]
    cos, sin = jnp.cos(angles), jnp.sin(angles)
    zero = jnp.zeros_like(sin)
    cosine = jnp.concatenate([cos] * 4, axis=-1)
    upper = jnp.concatenate([-sin, zero] * 2, axis=-1)
    lower = jnp.concatenate([zero, sin] * 2, axis=-1)
    return cosine, upper, lower


def turn(u, upper, lower):
    return pltpu.roll(u, 128 - HD // 2, 1) * upper + pltpu.roll(u, HD // 2, 1) * lower


def attn_fwd_kernel(xh, wq, wk, wv, cos, upper, lower, seg_col, seg_row, o, q, k, v, lse, kh):
    length = xh.shape[0]
    rows = min(256, length)
    lane = lax.broadcasted_iota(jnp.int32, (length, 128), 1)
    first = lane < HD
    tokens = xh[...]
    qf = dotf(tokens, wq[...], NN)
    qf = qf * cos[...] + turn(qf, upper[...], lower[...])
    q[...] = (qf * (1.0 / math.sqrt(HD))).astype(BF)
    kf = dotf(tokens, wk[...], NN)
    kf = (kf * cos[...] + turn(kf, upper[...], lower[...])).astype(BF)
    k[...] = kf
    kh[0] = jnp.where(first, kf, jnp.zeros_like(kf))
    kh[1] = jnp.where(first, jnp.zeros_like(kf), kf)
    v[...] = dotf(tokens, wv[...], NN).astype(BF)

    def block(i, carry):
        at = pl.multiple_of(i * rows, rows)
        q_rows = q[pl.ds(at, rows), :]
        same = seg_col[pl.ds(at, rows), :] == seg_row[...]
        outs = []
        for head in range(2):
            scores = dotf(q_rows, kh[head], NT)
            scores = jnp.where(same, scores, -1e30)
            top = jnp.max(scores, axis=-1, keepdims=True)
            expv = jnp.exp(scores - top)
            total = jnp.sum(expv, axis=-1, keepdims=True)
            low = (expv * (1.0 / total)).astype(BF)
            outs.append(dotf(low, v[...], NN))
            level = top + jnp.log(total)
            flat = jnp.transpose(jnp.broadcast_to(level, (rows, 128)))
            lse[0, pl.ds(head, 1), pl.ds(at, rows)] = flat[0:1, :]
        o[pl.ds(at, rows), :] = jnp.where(first[:rows], outs[0], outs[1]).astype(BF)
        return carry

    lax.fori_loop(0, length // rows, block, 0)


def attn_fwd(xh, w_qk, w_vo, tables, seg_col, seg_row):
    length, width = xh.shape
    pairs = w_qk.shape[1] // 256
    whole = lambda a: pl.BlockSpec(a.shape, lambda h: (0,) * a.ndim)
    col = lambda off: pl.BlockSpec((width, 128), lambda h: (0, h + off))
    out = pl.BlockSpec((length, 128), lambda h: (0, h))
    shape = jax.ShapeDtypeStruct((length, pairs * 128), BF)
    flops = 2 * length * width * pairs * 384 + 4 * pairs * 2 * length * length * 128
    return pl.pallas_call(
        attn_fwd_kernel,
        grid=(pairs,),
        in_specs=[whole(xh), col(0), col(pairs), col(0)]
        + [whole(t) for t in tables]
        + [whole(seg_col), whole(seg_row)],
        out_specs=[out] * 4 + [pl.BlockSpec((1, 2, length), lambda h: (h, 0, 0))],
        out_shape=[shape] * 4 + [jax.ShapeDtypeStruct((pairs, 2, length), F32)],
        scratch_shapes=[pltpu.VMEM((2, length, 128), BF)],
        cost_estimate=pl.CostEstimate(
            flops=flops, bytes_accessed=length * width * 8, transcendentals=pairs * 2 * length * length
        ),
        name="attn_fwd",
    )(xh, w_qk, w_qk, w_vo, *tables, seg_col, seg_row)


def attn_bwd_kernel(
    q, k, v, o, do, lse, cos, upper, lower, seg_col, seg_row, pg, kh, dk, dv
):
    length = q.shape[0]
    rows = min(256, length)
    lane = lax.broadcasted_iota(jnp.int32, (length, 128), 1)
    first = lane < HD
    kf = k[...]
    none = jnp.zeros_like(kf)
    kh[0] = jnp.where(first, kf, none)
    kh[1] = jnp.where(first, none, kf)
    dk[...] = jnp.zeros_like(dk)
    dv[...] = jnp.zeros_like(dv)

    def block(i, carry):
        at = pl.multiple_of(i * rows, rows)
        here = pl.ds(at, rows)
        q_rows = q[here, :]
        g_rows = do[here, :]
        seg_here = seg_row[:, here]
        same = seg_col[...] == seg_here
        prod = g_rows.astype(F32) * o[here, :].astype(F32)
        f = first[:rows]
        blank = jnp.zeros_like(q_rows)
        dq = jnp.zeros((rows, 128), F32)
        for head in range(2):
            mine = f if head == 0 else jnp.logical_not(f)
            q_head = jnp.where(mine, q_rows, blank)
            g_head = jnp.where(mine, g_rows, blank)
            delta = lax.dot_general(
                jnp.ones((8, 128), F32),
                jnp.where(mine, prod, 0.0),
                (NT, ((), ())),
                precision=lax.Precision.HIGHEST,
                preferred_element_type=F32,
            )[0:1, :]
            scores = dotf(k[...], q_head, NT)
            level = lse[0, pl.ds(head, 1), here]
            probs = jnp.where(same, jnp.exp(scores - level), 0.0)
            dv[...] += dotf(probs.astype(BF), g_head, NN)
            dp = dotf(v[...], g_head, NT)
            ds = (probs * (dp - delta)).astype(BF)
            dk[...] += dotf(ds, q_head, NN)
            dq = dq + dotf(ds, kh[head], TN)
        dq = dq * (1.0 / math.sqrt(HD))
        c, a, b = cos[here, :], upper[here, :], lower[here, :]
        pg[0, here, :] = (dq * c - turn(dq, a, b)).astype(BF)
        return carry

    lax.fori_loop(0, length // rows, block, 0)
    dkf = dk[...]
    pg[1] = (dkf * cos[...] - turn(dkf, upper[...], lower[...])).astype(BF)
    pg[2] = dv[...].astype(BF)


def attn_bwd(q, k, v, o, do, lse, tables, seg_col, seg_row):
    length, width = q.shape
    pairs = width // 128
    whole = lambda a: pl.BlockSpec(a.shape, lambda h: (0,) * a.ndim)
    col = pl.BlockSpec((length, 128), lambda h: (0, h))
    return pl.pallas_call(
        attn_bwd_kernel,
        grid=(pairs,),
        in_specs=[col] * 5
        + [pl.BlockSpec((1, 2, length), lambda h: (h, 0, 0))]
        + [whole(t) for t in tables]
        + [whole(seg_col), whole(seg_row)],
        out_specs=pl.BlockSpec((3, length, 128), lambda h: (0, 0, h)),
        out_shape=jax.ShapeDtypeStruct((3, length, width), BF),
        scratch_shapes=[
            pltpu.VMEM((2, length, 128), BF),
            pltpu.VMEM((length, 128), F32),
            pltpu.VMEM((length, 128), F32),
        ],
        cost_estimate=pl.CostEstimate(
            flops=10 * pairs * 2 * length * length * 128,
            bytes_accessed=length * width * 20,
            transcendentals=pairs * 2 * length * length,
        ),
        name="attn_bwd",
    )(q, k, v, o, do, lse, *tables, seg_col, seg_row)


def in_chunks(total, size, body):
    def step(j, carry):
        body(pl.ds(pl.multiple_of(j * size, size), size))
        return carry

    lax.fori_loop(0, total // size, step, 0)
    if total % size:
        body(pl.ds(total - total % size, total % size))


SHARD = (4, 2, 2)


def place():
    dp = lax.axis_index("dp")
    return dp // 4, (dp // 2) % 2, dp % 2, lax.axis_index("tensor")


def partners():
    z, x, c, y = place()
    at = lambda z, x, c, y: ((z * 2 + x) * 2 + c, y)
    return {
        "z1": at(z + 1 - 2 * (z % 2), x, c, y),
        "z2": at(z + 2 - 4 * (z // 2), x, c, y),
        "z3": at(3 - z, x, c, y),
        "x": at(z, 1 - x, c, y),
        "y": at(z, x, c, 1 - y),
        "c": at(z, x, 1 - c, y),
    }


def meet(peers, other=None):
    barrier = pltpu.get_barrier_semaphore()
    greet = lambda peer: pl.semaphore_signal(
        barrier, inc=1, device_id=peer, device_id_type=pl.DeviceIdType.MESH
    )
    for peer in peers.values():
        greet(peer)
    if other is None:
        pl.semaphore_wait(barrier, len(peers))
    else:
        moved, peer = other

        @pl.when(moved)
        def _():
            greet(peer)

        pl.semaphore_wait(barrier, len(peers) + jnp.where(moved, 1, 0))


def exchanged():
    z, x, c, y = place()
    return c != y, ((z * 2 + x) * 2 + y, c)


def remote(src, dst, send_sem, recv_sem, peer):
    return pltpu.make_async_remote_copy(
        src_ref=src,
        dst_ref=dst,
        send_sem=send_sem,
        recv_sem=recv_sem,
        device_id=peer,
        device_id_type=pl.DeviceIdType.MESH,
    )


class Move:
    def __init__(self, src, dst, sems, i):
        send_sem, recv_sem, near_sem = sems
        self.moved, peer = exchanged()
        self.far = remote(src, dst, send_sem.at[i], recv_sem.at[i], peer)
        self.near = pltpu.make_async_copy(src, dst, near_sem.at[i])

    def start(self):
        @pl.when(self.moved)
        def _():
            self.far.start()

        @pl.when(jnp.logical_not(self.moved))
        def _():
            self.near.start()

    def wait(self):
        @pl.when(self.moved)
        def _():
            self.far.wait()

        @pl.when(jnp.logical_not(self.moved))
        def _():
            self.near.wait()


def move_sems(n):
    return [pltpu.SemaphoreType.DMA((n,))] * 3


def to_place(values):
    z, x, _, y = place()
    tiles = [values[:, j * 128 : (j + 1) * 128] for j in range(8)]
    tiles = [jnp.where(y == 1, pltpu.roll(t, 64, 1), t) for t in tiles]
    for bit, step in ((x, 1), (z % 2, 2), (z // 2, 4)):
        tiles = [jnp.where(bit == 1, tiles[j ^ step], tiles[j]) for j in range(8)]
    return jnp.concatenate(tiles, axis=1)


AXIS = {"z": 4, "x": 2, "y": 2}


def partner(peers, axis, step):
    return peers["z%d" % step if axis == "z" else axis]


class Gather:
    MESSAGES = 15

    def __init__(self, own, buf, rows, order, peers, sems, base):
        self.buf, self.rows, self.order, self.peers = buf, rows, order, peers
        self.own = own.at[rows]
        self.send_sem, self.recv_sem = sems
        self.base = base
        n, m, p = (AXIS[axis] for axis in order)
        self.outer, self.middle = range(n), range(1, m)
        self.stages = [
            [(i, 0, 0) for i in range(1, n)],
            [(i, j, 0) for i in range(n) for j in range(1, m)],
            [(i, j, k) for i in range(n) for j in range(m) for k in range(1, p)],
        ]
        self.numbers = {at: n for n, at in enumerate(sum(self.stages, []))}

    def slot(self, at):
        where = dict(zip(self.order, at))
        return self.buf.at[where["z"], where["x"], where["y"], self.rows]

    def copy(self, at):
        hop = max(i for i in range(3) if at[i])
        source = at[:hop] + (0,) * (3 - hop)
        src = self.slot(source) if any(source) else self.own
        n = self.base + self.numbers[at]
        peer = partner(self.peers, self.order[hop], at[hop])
        return remote(src, self.slot(at), self.send_sem.at[n], self.recv_sem.at[n], peer)

    def send(self, stage, *prefix):
        for at in self.stages[stage]:
            if at[: len(prefix)] == prefix:
                self.copy(at).start()

    def start(self):
        self.send(0)

    def relay(self, i):
        if i:
            self.copy((i, 0, 0)).wait_recv()
        self.send(1, i)
        self.send(2, i, 0)

    def relay_again(self, i):
        for j in self.middle:
            self.copy((i, j, 0)).wait_recv()
            self.send(2, i, j)

    def finish(self):
        for at in self.stages[2]:
            self.copy(at).wait_recv()
        for at in self.numbers:
            self.copy(at).wait_send()


def forward_kernel(
    a_in, b_in, g_in, u_in, d_in, x_in, c_in, seg_in, inverse,
    q, k, v, o, lse, xh, w_qk, w_vo, resid, xn, x_half, cot, cos, upper, lower, seg_col, seg_row,
    w_gate, w_up, w_down,
    a_own, b_own, g_own, u_own, d_own, c_own, seg_own,
    kh, x_rel, part, sent, got, send_sem, recv_sem, pair_send, pair_recv, own_sem, *moving,
):
    length = xh.shape[0]
    half = length // 2
    width = xh.shape[1]
    pairs = q.shape[1] // 128
    rows = 256
    core = place()[2]
    peers = partners()
    sems = (send_sem, recv_sem)
    n = Gather.MESSAGES
    whole, low, high = pl.ds(0, 64), pl.ds(0, 32), pl.ds(32, 32)
    plan = (
        (a_own, w_qk, whole, "zyx"),
        (b_own, w_vo, low, "zyx"),
        (b_own, w_vo, high, "xyz"),
        (g_own, w_gate, whole, "zyx"),
        (u_own, w_up, low, "zyx"),
        (u_own, w_up, high, "zxy"),
        (d_own, w_down, low, "zyx"),
        (d_own, w_down, high, "xyz"),
    )
    gathers = [Gather(*piece, peers, sems, i * n) for i, piece in enumerate(plan)]
    one, early, two, three, late = gathers[:2], gathers[2], gathers[3:6], gathers[6], gathers[7]
    owns = [
        pltpu.make_async_copy(src, dst.at[0, 0, 0], own_sem.at[i])
        for i, (src, dst) in enumerate(
            ((a_own, w_qk), (b_own, w_vo), (g_own, w_gate), (u_own, w_up), (d_own, w_down))
        )
    ]
    move_a, move_b, move_x, move_seg, move_g, move_u, move_d, move_c = (
        Move(src, dst, moving, i)
        for i, (src, dst) in enumerate(
            (
                (a_in, a_own),
                (b_in, b_own),
                (x_in, x_half),
                (seg_in, seg_own),
                (g_in, g_own),
                (u_in, u_own),
                (d_in, d_own),
                (c_in, c_own),
            )
        )
    )
    meet(peers, exchanged())
    for move in (move_a, move_b, move_seg, move_x, move_g, move_u, move_d):
        move.start()

    def tables(here):
        shape = (here.size, 128)
        row = here.start + lax.broadcasted_iota(jnp.int32, shape, 0) + core * half
        row = jnp.where(row >= length, row - length, row)
        angle = row.astype(F32) * inverse[0:1, :]
        front = lax.broadcasted_iota(jnp.int32, shape, 1) % HD < HD // 2
        sin = jnp.sin(angle)
        cos[here, :] = jnp.cos(angle)
        upper[here, :] = jnp.where(front, -sin, 0.0)
        lower[here, :] = jnp.where(front, 0.0, sin)

    move_a.wait()
    move_b.wait()
    early.start()
    for gather in one:
        gather.start()
    for gather in [early] + one:
        gather.relay(0)
    for copy in owns[:2]:
        copy.start()
    in_chunks(length, 64, tables)
    early.relay(1)
    move_seg.wait()
    ids = seg_own[...]
    ids = jnp.where(core == 0, ids, jnp.concatenate([ids[:, half:], ids[:, :half]], axis=1))
    seg_row[...] = ids
    seg_col[...] = jnp.transpose(jnp.broadcast_to(ids[0:1, :], (128, length)))
    early.relay_again(0)
    for gather in one:
        gather.relay(1)
    early.relay_again(1)
    move_x.wait()

    def first_norm(i, carry):
        here = pl.ds(pl.multiple_of(i * 128, 128), 128)
        values = to_place(x_half[here, :].astype(F32))
        x_rel[here, :] = values.astype(BF)
        xh[here, :] = normalize(values)[0].astype(BF)
        return carry

    lax.fori_loop(0, half // 128, first_norm, 0)
    for z in (2, 3):
        for gather in one:
            gather.relay(z)
    swap_xh = remote(
        xh.at[pl.ds(0, half)], xh.at[pl.ds(half, half)], pair_send.at[0], pair_recv.at[0], peers["c"]
    )
    swap_xh.start()
    move_g.wait()
    move_u.wait()
    for gather in two:
        gather.start()
    for z in range(4):
        for gather in one:
            gather.relay_again(z)
    for gather in two:
        gather.relay(0)
    move_d.wait()
    late.start()
    three.start()
    for copy in owns[2:]:
        copy.start()
    swap_xh.wait()
    for gather in one + [early]:
        gather.finish()
    for copy in owns[:2]:
        copy.wait()

    events = {}
    at_step = lambda step, call, *args: events.setdefault(step, []).append((call, args))
    for z in range(4):
        for gather in two:
            if z:
                at_step(1 + z, gather.relay, z)
            at_step(6 + z, gather.relay_again, z)
        at_step(9 + z, three.relay, z)
    at_step(1, late.relay, 0)
    at_step(5, late.relay, 1)
    at_step(5, move_c.start)
    at_step(9, late.relay_again, 0)
    at_step(12, late.relay_again, 1)
    first = lax.broadcasted_iota(jnp.int32, (length, 128), 1) < HD

    def pair(h, carry):
        lanes = pl.ds(pl.multiple_of(h * 128, 128), 128)
        lanes_k = pl.ds(pl.multiple_of((h + pairs) * 128, 128), 128)
        weight = lambda ref, cols: ref[:, :, :, :, cols].reshape(width, 128)
        tokens = xh[...]
        qf = dotf(tokens, weight(w_qk, lanes), NN)
        qf = qf * cos[...] + turn(qf, upper[...], lower[...])
        q[:, lanes] = (qf * (1.0 / math.sqrt(HD))).astype(BF)
        kf = dotf(tokens, weight(w_qk, lanes_k), NN)
        kf = (kf * cos[...] + turn(kf, upper[...], lower[...])).astype(BF)
        k[:, lanes] = kf
        kh[0] = jnp.where(first, kf, jnp.zeros_like(kf))
        kh[1] = jnp.where(first, jnp.zeros_like(kf), kf)
        v[:, lanes] = dotf(tokens, weight(w_vo, lanes), NN).astype(BF)

        def block(i, carry):
            for step, calls in events.items():

                @pl.when(h * (length // rows) + i == step)
                def _():
                    for call, args in calls:
                        call(*args)

            at = pl.multiple_of(i * rows, rows)
            q_rows = q[pl.ds(at, rows), lanes]
            same = seg_col[pl.ds(at, rows), 0:1] == seg_row[0:1, :]
            outs = []
            for head in range(2):
                scores = dotf(q_rows, kh[head], NT)
                scores = jnp.where(same, scores, -1e30)
                top = jnp.max(scores, axis=-1, keepdims=True)
                expv = jnp.exp(scores - top)
                total = jnp.sum(expv, axis=-1, keepdims=True)
                low_probs = (expv * (1.0 / total)).astype(BF)
                outs.append(dotf(low_probs, v[:, lanes], NN))
                level = top + jnp.log(total)
                flat = jnp.transpose(jnp.broadcast_to(level, (rows, 128)))
                lse[h, pl.ds(head, 1), pl.ds(at, rows)] = flat[0:1, :]
            o[pl.ds(at, rows), lanes] = jnp.where(first[:rows], outs[0], outs[1]).astype(BF)
            return carry

        return lax.fori_loop(0, length // rows, block, carry)

    lax.fori_loop(0, pairs, pair, 0)
    w_o = w_vo[:, :, :, :, pairs * 128 :].reshape(width, pairs * 128)

    def project(i, carry):
        at = pl.multiple_of(half + i * rows, rows)
        sent[pl.ds(pl.multiple_of(i * rows, rows), rows), :] = dotf(
            o[pl.ds(at, rows), :], w_o, NT
        ).astype(BF)
        return carry

    lax.fori_loop(0, half // rows, project, 0)

    def project_own(i, carry):
        here = pl.ds(pl.multiple_of(i * rows, rows), rows)
        part[here, :] = dotf(o[here, :], w_o, NT)
        return carry

    give = remote(sent, got, pair_send.at[1], pair_recv.at[1], peers["c"])
    lax.fori_loop(0, half // rows, project_own, 0)
    give.start()
    move_c.wait()

    def turn_cot(here):
        cot[here, :] = to_place(c_own[here, :].astype(F32)).astype(BF)

    in_chunks(half, 128, turn_cot)
    swap_cot = remote(
        cot.at[pl.ds(0, half)], cot.at[pl.ds(half, half)], pair_send.at[3], pair_recv.at[3], peers["c"]
    )
    swap_cot.start()
    for z in range(4):
        three.relay_again(z)
    give.wait()

    def second_norm(i, carry):
        here = pl.ds(pl.multiple_of(i * 128, 128), 128)
        values = x_rel[here, :].astype(F32) + (part[here, :] + got[here, :].astype(F32))
        resid[here, :] = values
        xn[here, :] = normalize(values)[0].astype(BF)
        return carry

    lax.fori_loop(0, half // 128, second_norm, 0)
    swap_xn = remote(
        xn.at[pl.ds(0, half)], xn.at[pl.ds(half, half)], pair_send.at[2], pair_recv.at[2], peers["c"]
    )
    swap_xn.start()
    for gather in two + [three, late]:
        gather.finish()
    for copy in owns[2:]:
        copy.wait()
    swap_cot.wait()
    swap_xn.wait()


def forward_block(owned, x_half, cot_half, seg, inverse):
    half, width = x_half.shape
    length = 2 * half
    cols = owned[0].shape[1] // 2
    pairs = cols // 128
    units = owned[2].shape[1]
    shard = width // 16
    vmem = pl.BlockSpec(memory_space=pltpu.VMEM)
    any_ = pl.BlockSpec(memory_space=pl.ANY)
    gathered = lambda n: jax.ShapeDtypeStruct(SHARD + (shard, n), BF)
    heads = jax.ShapeDtypeStruct((length, cols), BF)
    flat = jax.ShapeDtypeStruct((length, width), BF)
    table = jax.ShapeDtypeStruct((length, 128), F32)
    return pl.pallas_call(
        forward_kernel,
        in_specs=[any_] * 8 + [vmem],
        out_specs=[vmem] * 17 + [any_] * 3,
        out_shape=[heads] * 4
        + [
            jax.ShapeDtypeStruct((pairs, 2, length), F32),
            flat,
            gathered(2 * cols),
            gathered(2 * cols),
            jax.ShapeDtypeStruct((half, width), F32),
            flat,
            jax.ShapeDtypeStruct((half, width), BF),
            flat,
        ]
        + [table] * 4
        + [jax.ShapeDtypeStruct((8, length), F32)]
        + [gathered(units)] * 3,
        scratch_shapes=[pltpu.VMEM((shard, 2 * cols), BF)] * 2
        + [pltpu.VMEM((shard, units), BF)] * 3
        + [
            pltpu.VMEM((half, width), BF),
            pltpu.VMEM((8, length), F32),
            pltpu.VMEM((2, length, 128), BF),
            pltpu.VMEM((half, width), BF),
            pltpu.VMEM((half, width), F32),
            pltpu.VMEM((half, width), BF),
            pltpu.VMEM((half, width), BF),
            pltpu.SemaphoreType.DMA((8 * Gather.MESSAGES,)),
            pltpu.SemaphoreType.DMA((8 * Gather.MESSAGES,)),
            pltpu.SemaphoreType.DMA((4,)),
            pltpu.SemaphoreType.DMA((4,)),
            pltpu.SemaphoreType.DMA((5,)),
        ]
        + move_sems(8),
        compiler_params=pltpu.CompilerParams(
            collective_id=0, has_side_effects=True, vmem_limit_bytes=60 << 20
        ),
        name="forward_block",
    )(*owned, x_half, cot_half, seg, inverse)


def mlp_kernel(
    xn, cot, w_gate, w_up, w_down, resid,
    result, resid_grad, attn_cot, d_gate, d_up, d_down,
    hidden, gate_grad, up_grad, own, sent, got, placed, send_sem, recv_sem, *moving,
):
    length, width = xn.shape
    half = length // 2
    units = w_gate.shape[1]
    peer = partners()["c"]
    meet({"c": peer}, exchanged())
    move = Move(placed, result, moving, 0)

    def units_of(rows, cols):
        gate = dotf(xn[rows, :], w_gate[:, cols], NN)
        up = dotf(xn[rows, :], w_up[:, cols], NN)
        grad = dotf(cot[rows, :], w_down[:, cols], NN).astype(BF).astype(F32)
        act, slope = gelu_parts(gate)
        hidden[rows, cols] = (act * up).astype(BF)
        gate_grad[rows, cols] = (grad * up * slope).astype(BF)
        up_grad[rows, cols] = (grad * act).astype(BF)

    def phase(rows, put):
        in_chunks(units, 256, lambda cols: units_of(rows, cols))

        def sums(here):
            put[0, :, here] = dotf(hidden[rows, :], w_down[here, :], NT).astype(put.dtype)
            both = dotf(gate_grad[rows, :], w_gate[here, :], NT)
            both = both + dotf(up_grad[rows, :], w_up[here, :], NT)
            put[1, :, here] = both.astype(put.dtype)

        in_chunks(width, 256, sums)

    phase(pl.ds(half, half), sent)
    give = remote(sent, got, send_sem.at[0], recv_sem.at[0], peer)
    give.start()
    phase(pl.ds(0, half), own)
    give.wait()

    def finish(here):
        values = resid[here, :]
        mlp = own[0, here, :] + got[0, here, :].astype(F32)
        placed[here, :] = to_place(values + mlp).astype(BF)
        xhat, scale = normalize(values)
        back = normalize_back(own[1, here, :] + got[1, here, :].astype(F32), xhat, scale)
        grad = cot[here, :].astype(F32) + back
        resid_grad[here, :] = grad
        attn_cot[here, :] = grad.astype(BF)

    in_chunks(half, 64, finish)
    swap = remote(
        attn_cot.at[pl.ds(0, half)], attn_cot.at[pl.ds(half, half)], send_sem.at[1], recv_sem.at[1], peer
    )
    swap.start()
    move.start()

    def weights(here):
        left = jnp.transpose(cot[:, here])
        d_down[here, :] = dotf(left, hidden[...], NN).astype(BF)
        left = jnp.transpose(xn[:, here])
        d_gate[here, :] = dotf(left, gate_grad[...], NN).astype(BF)
        d_up[here, :] = dotf(left, up_grad[...], NN).astype(BF)

    in_chunks(width, 256, weights)
    swap.wait()
    move.wait()


def mlp_block(xn, cot, w_gate, w_up, w_down, resid):
    length, width = xn.shape
    half = length // 2
    units = w_gate.shape[1]
    vmem = pl.BlockSpec(memory_space=pltpu.VMEM)
    grads = jax.ShapeDtypeStruct((width, units), BF)
    return pl.pallas_call(
        mlp_kernel,
        in_specs=[vmem] * 6,
        out_specs=[vmem] * 6,
        out_shape=[
            jax.ShapeDtypeStruct((half, width), BF),
            jax.ShapeDtypeStruct((half, width), F32),
            jax.ShapeDtypeStruct((length, width), BF),
            grads,
            grads,
            grads,
        ],
        scratch_shapes=[pltpu.VMEM((length, units), BF)] * 3
        + [
            pltpu.VMEM((2, half, width), F32),
            pltpu.VMEM((2, half, width), BF),
            pltpu.VMEM((2, half, width), BF),
            pltpu.VMEM((half, width), BF),
            pltpu.SemaphoreType.DMA((2,)),
            pltpu.SemaphoreType.DMA((2,)),
        ]
        + move_sems(1),
        compiler_params=pltpu.CompilerParams(
            collective_id=1, has_side_effects=True, vmem_limit_bytes=60 << 20
        ),
        name="mlp_block",
    )(xn, cot, w_gate, w_up, w_down, resid)


class Reduce:
    MESSAGES = 12
    ORDER = (2, 3, 1, 0)

    def __init__(self, parts, near, rows, axes, peers, sems, base, bufs, out):
        self.parts, self.near, self.rows, self.axes, self.peers = parts, near, rows, axes, peers
        self.send_sem, self.recv_sem = sems
        self.base = base
        self.one, self.two, self.three, self.sum = bufs
        self.out = out

    def link(self, i, src, dst, peer):
        n = self.base + i
        return remote(src, dst, self.send_sem.at[n], self.recv_sem.at[n], peer)

    def first(self, z):
        if self.axes == "xy":
            src = self.parts.at[z, :, 1, self.rows]
        else:
            src = self.parts.at[z, 1, :, self.rows]
        return self.link(z, src, self.one.at[z], self.peers[self.axes[1]])

    def second(self, z):
        return self.link(4 + z, self.one.at[z, 1], self.two.at[z], self.peers[self.axes[0]])

    def third(self, z):
        return self.link(7 + z, self.two.at[z], self.three.at[z - 1], self.peers["z%d" % z])

    def start(self):
        for z in self.ORDER:
            self.first(z).start()

    def relay_first(self, z):
        self.first(z).wait_recv()
        self.one[z] = (self.one[z].astype(F32) + self.near(z).astype(F32)).astype(BF)
        self.second(z).start()

    def relay_second(self, z):
        self.second(z).wait_recv()
        self.two[z] = (self.two[z].astype(F32) + self.one[z, 0].astype(F32)).astype(BF)
        if z:
            self.third(z).start()

    def last(self):
        moved, peer = exchanged()
        return moved, self.link(11, self.sum, self.out, peer)

    def total(self):
        total = self.two[0].astype(F32)
        for z in (1, 2, 3):
            self.third(z).wait_recv()
            total = total + self.three[z - 1].astype(F32)
        return total

    def finish(self):
        self.sum[...] = self.total().astype(BF)
        moved, copy = self.last()

        @pl.when(moved)
        def _():
            copy.start()

        @pl.when(jnp.logical_not(moved))
        def _():
            self.out[...] = self.sum[...]

    def sent(self):
        thirds = [self.third(z) for z in (1, 2, 3)]
        return [hop(z) for z in range(4) for hop in (self.first, self.second)] + thirds

    def close(self):
        for copy in self.sent():
            copy.wait_send()
        moved, copy = self.last()

        @pl.when(moved)
        def _():
            copy.wait()


class ReduceAlongZ(Reduce):
    def first(self, z):
        src = self.parts.at[z, :, :, self.rows]
        return self.link(z - 1, src, self.one.at[z - 1], self.peers["z%d" % z])

    def second(self):
        return self.link(3, self.two.at[:, 1], self.three.at[0:2], self.peers["y"])

    def third(self):
        return self.link(4, self.three.at[1], self.three.at[2], self.peers["x"])

    def start(self):
        for z in (2, 3, 1):
            self.first(z).start()

    def relay_first(self):
        total = self.near().astype(F32)
        for z in (1, 2, 3):
            self.first(z).wait_recv()
            total = total + self.one[z - 1].astype(F32)
        self.two[...] = total.astype(BF)
        self.second().start()

    def relay_second(self):
        self.second().wait_recv()
        for x in (0, 1):
            self.three[x] = (self.three[x].astype(F32) + self.two[x, 0].astype(F32)).astype(BF)
        self.third().start()

    def total(self):
        self.third().wait_recv()
        return self.three[0].astype(F32) + self.three[2].astype(F32)

    def sent(self):
        return [self.first(z) for z in (1, 2, 3)] + [self.second(), self.third()]


def backward_kernel(
    d_gate, d_up, d_down, q, k, v, o, lse, attn_cot, w_qk, w_vo, xh, x_half, resid_grad,
    cos, upper, lower, seg_col, seg_row,
    token_grad, s_gate, s_up_low, s_up_high, s_down_low, s_down_high, s_qk, s_vo_low, s_vo_high,
    d_qk, d_vo, pg, heads_grad, kh, dk, dv, own, sent, got, placed,
    near_gate, near_up_low, near_up_high, near_low, near_high,
    *rest,
):
    bufs = [rest[4 * i : 4 * i + 4] for i in range(8)]
    send_sem, recv_sem, pair_send, pair_recv, near_sem, *moving = rest[32:]
    length, width = xh.shape
    half = length // 2
    cols = q.shape[1]
    pairs = cols // 128
    rows = 256
    peers = partners()
    sems = (send_sem, recv_sem)
    n = Reduce.MESSAGES
    whole, low, high = pl.ds(0, 64), pl.ds(0, 32), pl.ds(32, 32)
    most, few = pl.ds(0, 48), pl.ds(48, 16)
    held = lambda ref: (lambda z: ref[z])
    plan = (
        (Reduce, d_gate, held(near_gate), whole, "yx", s_gate),
        (Reduce, d_up, held(near_up_low), low, "yx", s_up_low),
        (Reduce, d_up, held(near_up_high), high, "xy", s_up_high),
        (Reduce, d_down, held(near_low), low, "yx", s_down_low),
        (ReduceAlongZ, d_down, lambda: near_high[...], high, None, s_down_high),
        (Reduce, d_qk, lambda z: d_qk[z, 0], whole, "yx", s_qk),
        (Reduce, d_vo, lambda z: d_vo[z, :, 0, 0:48], most, "xy", s_vo_low),
        (ReduceAlongZ, d_vo, lambda: d_vo[0, :, :, 48:64], few, None, s_vo_high),
    )
    parts = [
        kind(src, near, rows_, axes, peers, sems, i * n, bufs[i], out)
        for i, (kind, src, near, rows_, axes, out) in enumerate(plan)
    ]
    gate, up_low, up_high, down_low, down_high, qk, vo_low, vo_high = parts
    nears = [
        pltpu.make_async_copy(src, dst, near_sem.at[i])
        for i, (src, dst) in enumerate(
            (
                (d_gate.at[:, 0], near_gate),
                (d_up.at[:, 0, :, low], near_up_low),
                (d_up.at[:, :, 0, high], near_up_high),
                (d_down.at[:, 0, :, low], near_low),
                (d_down.at[0, :, :, high], near_high),
            )
        )
    ]
    for copy in nears:
        copy.start()
    meet(peers, exchanged())
    for part in (down_high, up_high, gate, up_low):
        part.start()

    def heads(here):
        heads_grad[here, :] = dotf(attn_cot[here, :], w_vo[:, cols:], NN).astype(BF)

    in_chunks(length, 256, heads)

    def out_weights(z, carry):
        here = pl.ds(pl.multiple_of(z * 256, 256), 256)
        value = dotf(jnp.transpose(attn_cot[:, here]), o[...], NN).astype(BF)
        d_vo[z, :, :, :, cols:] = value.reshape(2, 2, 64, cols)
        return carry

    lax.fori_loop(0, width // 256, out_weights, 0)
    for copy in nears:
        copy.wait()

    events = {}
    for i, z in enumerate(Reduce.ORDER):
        events.setdefault(2 + 4 * i, []).append(lambda z=z: gate.relay_first(z))
        events.setdefault(3 + 2 * i, []).append(lambda z=z: up_high.relay_first(z))
    events.setdefault(11, []).append(down_low.start)
    events.setdefault(12, []).append(down_high.relay_first)
    lane = lax.broadcasted_iota(jnp.int32, (length, 128), 1)
    first = lane < HD

    def pair(h, carry):
        lanes = pl.ds(pl.multiple_of(h * 128, 128), 128)
        kf = k[:, lanes]
        none = jnp.zeros_like(kf)
        kh[0] = jnp.where(first, kf, none)
        kh[1] = jnp.where(first, none, kf)
        dk[...] = jnp.zeros_like(dk)
        dv[...] = jnp.zeros_like(dv)

        def block(i, carry):
            for step, calls in events.items():

                @pl.when(h * (length // rows) + i == step)
                def _():
                    for call in calls:
                        call()

            at = pl.multiple_of(i * rows, rows)
            here = pl.ds(at, rows)
            q_rows = q[here, lanes]
            g_rows = heads_grad[here, lanes]
            same = seg_col[:, 0:1] == seg_row[0:1, here]
            prod = g_rows.astype(F32) * o[here, lanes].astype(F32)
            f = first[:rows]
            blank = jnp.zeros_like(q_rows)
            dq = jnp.zeros((rows, 128), F32)
            for head in range(2):
                mine = f if head == 0 else jnp.logical_not(f)
                q_head = jnp.where(mine, q_rows, blank)
                g_head = jnp.where(mine, g_rows, blank)
                delta = lax.dot_general(
                    jnp.ones((8, 128), F32),
                    jnp.where(mine, prod, 0.0),
                    (NT, ((), ())),
                    precision=lax.Precision.HIGHEST,
                    preferred_element_type=F32,
                )[0:1, :]
                scores = dotf(k[:, lanes], q_head, NT)
                level = lse[h, pl.ds(head, 1), here]
                probs = jnp.where(same, jnp.exp(scores - level), 0.0)
                dv[...] += dotf(probs.astype(BF), g_head, NN)
                dp = dotf(v[:, lanes], g_head, NT)
                ds = (probs * (dp - delta)).astype(BF)
                dk[...] += dotf(ds, q_head, NN)
                dq = dq + dotf(ds, kh[head], TN)
            dq = dq * (1.0 / math.sqrt(HD))
            c, a, b = cos[here, :], upper[here, :], lower[here, :]
            pg[0, here, lanes] = (dq * c - turn(dq, a, b)).astype(BF)
            return carry

        lax.fori_loop(0, length // rows, block, 0)
        dkf = dk[...]
        pg[1, :, lanes] = (dkf * cos[...] - turn(dkf, upper[...], lower[...])).astype(BF)
        pg[2, :, lanes] = dv[...].astype(BF)
        return carry

    lax.fori_loop(0, pairs, pair, 0)

    def weights(z, carry):
        left = jnp.transpose(xh[:, pl.ds(pl.multiple_of(z * 256, 256), 256)])
        for i, (ref, at) in enumerate(((d_qk, 0), (d_qk, cols), (d_vo, 0))):
            value = dotf(left, pg[i], NN).astype(BF)
            ref[z, :, :, :, at : at + cols] = value.reshape(2, 2, 64, cols)
        return carry

    lax.fori_loop(0, width // 256, weights, 0)

    def back(tokens, put):
        def step(here):
            total = dotf(pg[0, tokens, :], w_qk[here, :cols], NT)
            total = total + dotf(pg[1, tokens, :], w_qk[here, cols:], NT)
            put[:, here] = (total + dotf(pg[2, tokens, :], w_vo[here, :cols], NT)).astype(put.dtype)

        in_chunks(width, 256, step)

    for part in (qk, vo_low, vo_high):
        part.start()
    back(pl.ds(half, half), sent)
    give = remote(sent, got, pair_send.at[0], pair_recv.at[0], peers["c"])
    give.start()
    back(pl.ds(0, half), own)
    for z in Reduce.ORDER:
        gate.relay_second(z)
    down_high.relay_second()
    give.wait()

    def finish(here):
        xhat, scale = normalize(to_place(x_half[here, :].astype(F32)))
        f = own[here, :] + got[here, :].astype(F32)
        value = resid_grad[here, :] + normalize_back(f, xhat, scale)
        placed[here, :] = to_place(value).astype(BF)

    in_chunks(half, 64, finish)
    move = Move(placed, token_grad, moving, 0)
    move.start()
    for z in Reduce.ORDER:
        up_low.relay_first(z)
        up_high.relay_second(z)
    gate.finish()
    for z in Reduce.ORDER:
        down_low.relay_first(z)
        vo_low.relay_first(z)
    up_high.finish()
    vo_high.relay_first()
    for z in Reduce.ORDER:
        up_low.relay_second(z)
    down_high.finish()
    for z in Reduce.ORDER:
        qk.relay_first(z)
        down_low.relay_second(z)
    up_low.finish()
    vo_high.relay_second()
    for z in Reduce.ORDER:
        vo_low.relay_second(z)
    down_low.finish()
    for z in Reduce.ORDER:
        qk.relay_second(z)
    vo_high.finish()
    vo_low.finish()
    qk.finish()
    for part in parts:
        part.close()
    move.wait()


def backward_block(grads, heads, lse, attn_cot, w_qk, w_vo, xh, x_half, resid_grad, tables, seg_col, seg_row):
    length, width = xh.shape
    half = length // 2
    cols = heads[0].shape[1]
    units = grads[0].shape[1]
    shard = width // 16
    vmem = pl.BlockSpec(memory_space=pltpu.VMEM)
    any_ = pl.BlockSpec(memory_space=pl.ANY)
    sizes = [(shard, units)] + [(shard // 2, units)] * 4
    sizes += [(shard, 2 * cols), (shard * 3 // 4, 2 * cols), (shard // 4, 2 * cols)]
    along_z = (4, 7)
    bufs = []
    for i, size in enumerate(sizes):
        if i in along_z:
            lead = (3, 2, 2), (2, 2), (3,)
        else:
            lead = (4, 2), (4,), (3,)
        bufs += [pltpu.VMEM(n + size, BF) for n in lead + ((),)]
    nears = [pltpu.VMEM(((2, 2) if i in along_z else (4, 2)) + size, BF) for i, size in enumerate(sizes[:5])]
    messages = 8 * Reduce.MESSAGES
    return pl.pallas_call(
        backward_kernel,
        in_specs=[any_] * 3 + [vmem] * 16,
        out_specs=[vmem] * 9,
        out_shape=[jax.ShapeDtypeStruct((half, width), BF)]
        + [jax.ShapeDtypeStruct(size, BF) for size in sizes],
        scratch_shapes=[pltpu.VMEM(SHARD + (shard, 2 * cols), BF)] * 2
        + [
            pltpu.VMEM((3, length, cols), BF),
            pltpu.VMEM((length, cols), BF),
            pltpu.VMEM((2, length, 128), BF),
            pltpu.VMEM((length, 128), F32),
            pltpu.VMEM((length, 128), F32),
            pltpu.VMEM((half, width), F32),
            pltpu.VMEM((half, width), BF),
            pltpu.VMEM((half, width), BF),
            pltpu.VMEM((half, width), BF),
        ]
        + nears
        + bufs
        + [
            pltpu.SemaphoreType.DMA((messages,)),
            pltpu.SemaphoreType.DMA((messages,)),
            pltpu.SemaphoreType.DMA((1,)),
            pltpu.SemaphoreType.DMA((1,)),
            pltpu.SemaphoreType.DMA((5,)),
        ]
        + move_sems(1),
        compiler_params=pltpu.CompilerParams(
            collective_id=2, has_side_effects=True, vmem_limit_bytes=60 << 20
        ),
        name="backward_block",
    )(
        *(g.reshape(SHARD + (shard, units)) for g in grads),
        *heads, lse, attn_cot, w_qk, w_vo, xh, x_half, resid_grad, *tables, seg_col, seg_row,
    )


class Chips:
    def sum_tensor(self, value):
        pairs = [(2 * i + y, 2 * i + 1 - y) for i in range(16) for y in range(2)]
        return value + lax.ppermute(value, ("dp", "tensor"), pairs)


class Axes:
    def gather_rows(self, value):
        return lax.all_gather(value, "tensor", axis=0, tiled=True)

    def scatter_rows(self, value):
        return lax.psum_scatter(value.astype(BF), "tensor", scatter_dimension=0, tiled=True).astype(F32)

    def reduce(self, a, b):
        return tuple(
            lax.psum_scatter(w.astype(BF), "dp", scatter_dimension=0, tiled=True).astype(F32)
            for w in (a, b)
        )

    def sum_tensor(self, value):
        return lax.psum(value, "tensor")


def normalize(values):
    centred = values - jnp.mean(values, axis=-1, keepdims=True)
    scale = lax.rsqrt(jnp.mean(centred * centred, axis=-1, keepdims=True) + EPS)
    return centred * scale, scale


def normalize_back(f, xhat, scale):
    return scale * (
        f
        - jnp.mean(f, axis=-1, keepdims=True)
        - xhat * jnp.mean(f * xhat, axis=-1, keepdims=True)
    )


def gelu_parts(gate):
    half_erf = 0.5 * (1.0 + lax.erf(gate * (1.0 / math.sqrt(2.0))))
    density = jnp.exp(-0.5 * gate * gate) * (1.0 / math.sqrt(2.0 * math.pi))
    return gate * half_erf, half_erf + gate * density


def make_local(comm_type):
    def local(tokens, segments, w_qkv, w_out, w_in, w_down, g_attn, g_mlp, cotangent):
        comm = comm_type()
        paired = comm_type is Chips
        shard = w_qkv.shape[0]
        cols = w_qkv.shape[2]
        units = w_in.shape[2]
        low = 128 * (units // 256)
        pad = 128 * pl.cdiv(units, 128) - units
        gain_one = g_attn.astype(F32)[:, None]
        gain_two = g_mlp.astype(F32)[:, None]
        scaled = lambda w, g: (w.astype(F32) * g).astype(BF)
        padded = lambda w: jnp.pad(w, ((0, 0), (0, pad)))
        down_rows = w_down.T
        a_one = jnp.concatenate([scaled(w_qkv[:, 0], gain_one), scaled(w_qkv[:, 1], gain_one)], axis=1)
        b_one = jnp.concatenate([scaled(w_qkv[:, 2], gain_one), w_out.T], axis=1)
        own_gate, own_up = scaled(w_in[:, 0], gain_two), scaled(w_in[:, 1], gain_two)

        owned = (a_one, b_one, own_gate, own_up, down_rows)
        if paired:
            owned = owned[:2] + tuple(padded(w) for w in owned[2:])
            seg = jnp.broadcast_to(segments.astype(F32), (8, segments.shape[1]))
            inverse = jnp.broadcast_to(jnp.tile(rope_rates(), 4), (8, 128))
            (
                q, k, v, o, lse, xh, w_qk, w_vo, resid, xn, x_half, cot_all, *tables, seg_col, seg_row,
                w_gate, w_up, w_dn,
            ) = forward_block(owned, tokens[0], cotangent[0], seg, inverse)
            w_qk, w_vo, w_gate, w_up, w_dn = (
                w.reshape(-1, w.shape[-1]) for w in (w_qk, w_vo, w_gate, w_up, w_dn)
            )
        else:
            w_qk, w_vo, w_gate, w_up, w_dn = (
                lax.all_gather(w, "dp", axis=0, tiled=True) for w in owned
            )
            w_o = w_vo[:, cols:]
            seg_col, seg_row = segments[0][:, None], segments
            cot = cotangent[0]
            cot_all = comm.gather_rows(cot)
            tables = rope_tables(jnp.arange(segments.shape[1]))
            x_in = tokens[0].astype(F32)
            xh_one, scale_one = normalize(x_in)
            xh = comm.gather_rows(xh_one.astype(BF))
            o, q, k, v, lse = attn_fwd(xh, w_qk, w_vo, tables, seg_col, seg_row)
            resid = x_in + comm.scatter_rows(dotf(o, w_o, NT))
            xh_two, scale_two = normalize(resid)
            xn = comm.gather_rows(xh_two.astype(BF))
        if paired:
            result, resid_grad, attn_cot, d_gate, d_up, d_down = mlp_block(
                xn, cot_all, w_gate, w_up, w_dn, resid
            )
        else:
            gate, up = dotf(xn, w_gate, NN), dotf(xn, w_up, NN)
            act, slope = gelu_parts(gate)
            hidden = (act * up).astype(BF)
            mlp = comm.scatter_rows(dotf(hidden, w_dn, NT))
            result = (resid + mlp).astype(BF)
            hidden_grad = dotf(cot_all, w_dn, NN).astype(BF).astype(F32)
            gate_grad = (hidden_grad * up * slope).astype(BF)
            up_grad = (hidden_grad * act).astype(BF)
            f_two = comm.scatter_rows(dotf(gate_grad, w_gate, NT) + dotf(up_grad, w_up, NT))
            resid_grad = cot.astype(F32) + normalize_back(f_two, xh_two, scale_two)
            attn_cot = comm.gather_rows(resid_grad.astype(BF))
            d_down = dotf(cot_all, hidden, TN)
            d_gate, d_up = dotf(xn, gate_grad, TN), dotf(xn, up_grad, TN)

        if paired:
            token_grad, *sums = backward_block(
                (d_gate, d_up, d_down), (q, k, v, o), lse, attn_cot, w_qk, w_vo, xh, x_half,
                resid_grad, tables, seg_col, seg_row,
            )
            token_grad = token_grad.astype(F32)
            s_gate, up_low, up_high, s_low, s_high, one_a, vo_low, vo_high = (w.astype(F32) for w in sums)
            s_up = jnp.concatenate([up_low, up_high], axis=0)
            one_b = jnp.concatenate([vo_low, vo_high], axis=0)
            in_raw = jnp.stack([s_gate[:, :units], s_up[:, :units]], axis=1)
            down_sum = jnp.concatenate([s_low[:, :units], s_high[:, :units]], axis=0).T
        else:
            wide = lambda g, d: jnp.concatenate([padded(g), d], axis=1)
            two_a, two_b = comm.reduce(wide(d_gate, d_down[:, :low]), wide(d_up, d_down[:, low:]))

            heads_grad = dotf(attn_cot, w_o, NN).astype(BF)
            pg = attn_bwd(q, k, v, o, heads_grad, lse, tables, seg_col, seg_row)
            d_out = dotf(attn_cot, o, TN)
            d_q, d_k, d_v = (dotf(xh, pg[i], TN) for i in range(3))
            one_a, one_b = comm.reduce(
                jnp.concatenate([d_q, d_k], axis=1), jnp.concatenate([d_v, d_out], axis=1)
            )
            f_one = comm.scatter_rows(
                dotf(pg[0], w_qk[:, :cols], NT)
                + dotf(pg[1], w_qk[:, cols:], NT)
                + dotf(pg[2], w_vo[:, :cols], NT)
            )
            token_grad = resid_grad + normalize_back(f_one, xh_one, scale_one)
            in_raw = jnp.stack([two_a[:, :units], two_b[:, :units]], axis=1)
            down_sum = jnp.concatenate([two_a[:, units + pad :], two_b[:, units + pad :]], axis=1).T

        qkv_raw = jnp.stack([one_a[:, :cols], one_a[:, cols:], one_b[:, :cols]], axis=1)
        gains = jnp.stack(
            [
                jnp.sum(qkv_raw * w_qkv.astype(F32), axis=(1, 2)),
                jnp.sum(in_raw * w_in.astype(F32), axis=(1, 2)),
            ]
        )
        gains = comm.sum_tensor(gains)
        return (
            result[None],
            token_grad[None],
            gains[0],
            gains[1],
            qkv_raw * gain_one[:, :, None],
            one_b[:, cols:].T,
            in_raw * gain_two[:, :, None],
            down_sum,
        )

    return local


def solution(mesh):
    paired = mesh.shape["dp"] == 16 and mesh.shape["tensor"] == 2
    return jax.shard_map(
        make_local(Chips if paired else Axes),
        mesh=mesh,
        in_specs=(
            P("dp", "tensor", None),
            P("dp", None),
            P("dp", None, "tensor"),
            P("tensor", "dp"),
            P("dp", None, "tensor"),
            P("tensor", "dp"),
            P("dp"),
            P("dp"),
            P("dp", "tensor", None),
        ),
        out_specs=(
            P("dp", "tensor", None),
            P("dp", "tensor", None),
            P("dp"),
            P("dp"),
            P("dp", None, "tensor"),
            P("tensor", "dp"),
            P("dp", None, "tensor"),
            P("tensor", "dp"),
        ),
        check_vma=False,
    )
```

```python
import math

import jax
import jax.numpy as jnp
from jax import lax
from jax.experimental import pallas as pl
from jax.experimental.pallas import tpu as pltpu
from jax.sharding import PartitionSpec as P

HD = 64
EPS = 1e-05
ROTARY_BASE = 160000.0
BF = jnp.bfloat16
F32 = jnp.float32


def dotf(a, b, dims):
    return lax.dot_general(a, b, (dims, ((), ())), preferred_element_type=F32)


NN = ((1,), (0,))
NT = ((1,), (1,))
TN = ((0,), (0,))


def rope_rates():
    return 1.0 / ROTARY_BASE ** (jnp.arange(HD // 2).astype(F32) * (2.0 / HD))


def rope_tables(positions):
    angles = positions.astype(F32)[:, None] * rope_rates()[None, :]
    cos, sin = jnp.cos(angles), jnp.sin(angles)
    zero = jnp.zeros_like(sin)
    cosine = jnp.concatenate([cos] * 4, axis=-1)
    upper = jnp.concatenate([-sin, zero] * 2, axis=-1)
    lower = jnp.concatenate([zero, sin] * 2, axis=-1)
    return cosine, upper, lower


def turn(u, upper, lower):
    return pltpu.roll(u, 128 - HD // 2, 1) * upper + pltpu.roll(u, HD // 2, 1) * lower


def attn_fwd_kernel(xh, wq, wk, wv, cos, upper, lower, seg_col, seg_row, o, q, k, v, lse, kh):
    length = xh.shape[0]
    rows = min(256, length)
    lane = lax.broadcasted_iota(jnp.int32, (length, 128), 1)
    first = lane < HD
    tokens = xh[...]
    qf = dotf(tokens, wq[...], NN)
    qf = qf * cos[...] + turn(qf, upper[...], lower[...])
    q[...] = (qf * (1.0 / math.sqrt(HD))).astype(BF)
    kf = dotf(tokens, wk[...], NN)
    kf = (kf * cos[...] + turn(kf, upper[...], lower[...])).astype(BF)
    k[...] = kf
    kh[0] = jnp.where(first, kf, jnp.zeros_like(kf))
    kh[1] = jnp.where(first, jnp.zeros_like(kf), kf)
    v[...] = dotf(tokens, wv[...], NN).astype(BF)

    def block(i, carry):
        at = pl.multiple_of(i * rows, rows)
        q_rows = q[pl.ds(at, rows), :]
        same = seg_col[pl.ds(at, rows), :] == seg_row[...]
        outs = []
        for head in range(2):
            scores = dotf(q_rows, kh[head], NT)
            scores = jnp.where(same, scores, -1e30)
            top = jnp.max(scores, axis=-1, keepdims=True)
            expv = jnp.exp(scores - top)
            total = jnp.sum(expv, axis=-1, keepdims=True)
            low = (expv * (1.0 / total)).astype(BF)
            outs.append(dotf(low, v[...], NN))
            level = top + jnp.log(total)
            flat = jnp.transpose(jnp.broadcast_to(level, (rows, 128)))
            lse[0, pl.ds(head, 1), pl.ds(at, rows)] = flat[0:1, :]
        o[pl.ds(at, rows), :] = jnp.where(first[:rows], outs[0], outs[1]).astype(BF)
        return carry

    lax.fori_loop(0, length // rows, block, 0)


def attn_fwd(xh, w_qk, w_vo, tables, seg_col, seg_row):
    length, width = xh.shape
    pairs = w_qk.shape[1] // 256
    whole = lambda a: pl.BlockSpec(a.shape, lambda h: (0,) * a.ndim)
    col = lambda off: pl.BlockSpec((width, 128), lambda h: (0, h + off))
    out = pl.BlockSpec((length, 128), lambda h: (0, h))
    shape = jax.ShapeDtypeStruct((length, pairs * 128), BF)
    flops = 2 * length * width * pairs * 384 + 4 * pairs * 2 * length * length * 128
    return pl.pallas_call(
        attn_fwd_kernel,
        grid=(pairs,),
        in_specs=[whole(xh), col(0), col(pairs), col(0)]
        + [whole(t) for t in tables]
        + [whole(seg_col), whole(seg_row)],
        out_specs=[out] * 4 + [pl.BlockSpec((1, 2, length), lambda h: (h, 0, 0))],
        out_shape=[shape] * 4 + [jax.ShapeDtypeStruct((pairs, 2, length), F32)],
        scratch_shapes=[pltpu.VMEM((2, length, 128), BF)],
        cost_estimate=pl.CostEstimate(
            flops=flops, bytes_accessed=length * width * 8, transcendentals=pairs * 2 * length * length
        ),
        name="attn_fwd",
    )(xh, w_qk, w_qk, w_vo, *tables, seg_col, seg_row)


def attn_bwd_kernel(
    q, k, v, o, do, lse, cos, upper, lower, seg_col, seg_row, pg, kh, dk, dv
):
    length = q.shape[0]
    rows = min(256, length)
    lane = lax.broadcasted_iota(jnp.int32, (length, 128), 1)
    first = lane < HD
    kf = k[...]
    none = jnp.zeros_like(kf)
    kh[0] = jnp.where(first, kf, none)
    kh[1] = jnp.where(first, none, kf)
    dk[...] = jnp.zeros_like(dk)
    dv[...] = jnp.zeros_like(dv)

    def block(i, carry):
        at = pl.multiple_of(i * rows, rows)
        here = pl.ds(at, rows)
        q_rows = q[here, :]
        g_rows = do[here, :]
        seg_here = seg_row[:, here]
        same = seg_col[...] == seg_here
        prod = g_rows.astype(F32) * o[here, :].astype(F32)
        f = first[:rows]
        blank = jnp.zeros_like(q_rows)
        dq = jnp.zeros((rows, 128), F32)
        for head in range(2):
            mine = f if head == 0 else jnp.logical_not(f)
            q_head = jnp.where(mine, q_rows, blank)
            g_head = jnp.where(mine, g_rows, blank)
            delta = lax.dot_general(
                jnp.ones((8, 128), F32),
                jnp.where(mine, prod, 0.0),
                (NT, ((), ())),
                precision=lax.Precision.HIGHEST,
                preferred_element_type=F32,
            )[0:1, :]
            scores = dotf(k[...], q_head, NT)
            level = lse[0, pl.ds(head, 1), here]
            probs = jnp.where(same, jnp.exp(scores - level), 0.0)
            dv[...] += dotf(probs.astype(BF), g_head, NN)
            dp = dotf(v[...], g_head, NT)
            ds = (probs * (dp - delta)).astype(BF)
            dk[...] += dotf(ds, q_head, NN)
            dq = dq + dotf(ds, kh[head], TN)
        dq = dq * (1.0 / math.sqrt(HD))
        c, a, b = cos[here, :], upper[here, :], lower[here, :]
        pg[0, here, :] = (dq * c - turn(dq, a, b)).astype(BF)
        return carry

    lax.fori_loop(0, length // rows, block, 0)
    dkf = dk[...]
    pg[1] = (dkf * cos[...] - turn(dkf, upper[...], lower[...])).astype(BF)
    pg[2] = dv[...].astype(BF)


def attn_bwd(q, k, v, o, do, lse, tables, seg_col, seg_row):
    length, width = q.shape
    pairs = width // 128
    whole = lambda a: pl.BlockSpec(a.shape, lambda h: (0,) * a.ndim)
    col = pl.BlockSpec((length, 128), lambda h: (0, h))
    return pl.pallas_call(
        attn_bwd_kernel,
        grid=(pairs,),
        in_specs=[col] * 5
        + [pl.BlockSpec((1, 2, length), lambda h: (h, 0, 0))]
        + [whole(t) for t in tables]
        + [whole(seg_col), whole(seg_row)],
        out_specs=pl.BlockSpec((3, length, 128), lambda h: (0, 0, h)),
        out_shape=jax.ShapeDtypeStruct((3, length, width), BF),
        scratch_shapes=[
            pltpu.VMEM((2, length, 128), BF),
            pltpu.VMEM((length, 128), F32),
            pltpu.VMEM((length, 128), F32),
        ],
        cost_estimate=pl.CostEstimate(
            flops=10 * pairs * 2 * length * length * 128,
            bytes_accessed=length * width * 20,
            transcendentals=pairs * 2 * length * length,
        ),
        name="attn_bwd",
    )(q, k, v, o, do, lse, *tables, seg_col, seg_row)


def in_chunks(total, size, body):
    def step(j, carry):
        body(pl.ds(pl.multiple_of(j * size, size), size))
        return carry

    lax.fori_loop(0, total // size, step, 0)
    if total % size:
        body(pl.ds(total - total % size, total % size))


SHARD = (4, 2, 2)


def place():
    dp = lax.axis_index("dp")
    return dp // 4, (dp // 2) % 2, dp % 2, lax.axis_index("tensor")


def partners():
    z, x, c, y = place()
    at = lambda z, x, c, y: ((z * 2 + x) * 2 + c, y)
    return {
        "z1": at(z + 1 - 2 * (z % 2), x, c, y),
        "z2": at(z + 2 - 4 * (z // 2), x, c, y),
        "z3": at(3 - z, x, c, y),
        "x": at(z, 1 - x, c, y),
        "y": at(z, x, c, 1 - y),
        "c": at(z, x, 1 - c, y),
    }


def meet(peers, other=None):
    barrier = pltpu.get_barrier_semaphore()
    greet = lambda peer: pl.semaphore_signal(
        barrier, inc=1, device_id=peer, device_id_type=pl.DeviceIdType.MESH
    )
    for peer in peers.values():
        greet(peer)
    if other is None:
        pl.semaphore_wait(barrier, len(peers))
    else:
        moved, peer = other

        @pl.when(moved)
        def _():
            greet(peer)

        pl.semaphore_wait(barrier, len(peers) + jnp.where(moved, 1, 0))


def exchanged():
    z, x, c, y = place()
    return c != y, ((z * 2 + x) * 2 + y, c)


def remote(src, dst, send_sem, recv_sem, peer):
    return pltpu.make_async_remote_copy(
        src_ref=src,
        dst_ref=dst,
        send_sem=send_sem,
        recv_sem=recv_sem,
        device_id=peer,
        device_id_type=pl.DeviceIdType.MESH,
    )


class Move:
    def __init__(self, src, dst, sems, i):
        send_sem, recv_sem, near_sem = sems
        self.moved, peer = exchanged()
        self.far = remote(src, dst, send_sem.at[i], recv_sem.at[i], peer)
        self.near = pltpu.make_async_copy(src, dst, near_sem.at[i])

    def start(self):
        @pl.when(self.moved)
        def _():
            self.far.start()

        @pl.when(jnp.logical_not(self.moved))
        def _():
            self.near.start()

    def wait(self):
        @pl.when(self.moved)
        def _():
            self.far.wait()

        @pl.when(jnp.logical_not(self.moved))
        def _():
            self.near.wait()


def move_sems(n):
    return [pltpu.SemaphoreType.DMA((n,))] * 3


def to_place(values):
    z, x, _, y = place()
    tiles = [values[:, j * 128 : (j + 1) * 128] for j in range(8)]
    tiles = [jnp.where(y == 1, pltpu.roll(t, 64, 1), t) for t in tiles]
    for bit, step in ((x, 1), (z % 2, 2), (z // 2, 4)):
        tiles = [jnp.where(bit == 1, tiles[j ^ step], tiles[j]) for j in range(8)]
    return jnp.concatenate(tiles, axis=1)


AXIS = {"z": 4, "x": 2, "y": 2}


def partner(peers, axis, step):
    return peers["z%d" % step if axis == "z" else axis]


class Gather:
    MESSAGES = 15

    def __init__(self, own, buf, rows, order, hops, peers, sems, base):
        self.buf, self.rows, self.order, self.hops, self.peers = buf, rows, order, hops, peers
        self.own = own.at[rows]
        self.send_sem, self.recv_sem = sems
        self.base = base
        n, m, p = (AXIS[axis] for axis in order)
        self.outer, self.middle = range(n), range(1, m)
        self.stages = [
            [(i, 0, 0) for i in range(1, n)],
            [(i, j, 0) for i in range(n) for j in range(1, m)],
            [(i, j, k) for i in range(n) for j in range(m) for k in range(1, p)],
        ]
        self.stages = self.stages[:hops]
        self.numbers = {at: n for n, at in enumerate(sum(self.stages, []))}

    def slot(self, at):
        where = dict(zip(self.order, at))
        return self.buf.at[where["z"], where["x"], where["y"], self.rows]

    def copy(self, at):
        hop = max(i for i in range(3) if at[i])
        source = at[:hop] + (0,) * (3 - hop)
        src = self.slot(source) if any(source) else self.own
        n = self.base + self.numbers[at]
        peer = partner(self.peers, self.order[hop], at[hop])
        return remote(src, self.slot(at), self.send_sem.at[n], self.recv_sem.at[n], peer)

    def send(self, stage, *prefix):
        for at in self.stages[stage]:
            if at[: len(prefix)] == prefix:
                self.copy(at).start()

    def start(self):
        self.send(0)

    def relay(self, i):
        if i:
            self.copy((i, 0, 0)).wait_recv()
        self.send(1, i)
        if self.hops == 3:
            self.send(2, i, 0)

    def relay_again(self, i):
        for j in self.middle:
            self.copy((i, j, 0)).wait_recv()
            self.send(2, i, j)

    def finish(self):
        for at in self.stages[-1]:
            self.copy(at).wait_recv()
        for at in self.numbers:
            self.copy(at).wait_send()


def forward_kernel(
    a_in, b_in, g_in, u_in, d_in, x_in, c_in, seg_in, inverse,
    q, k, v, o, lse, xh, w_qk, w_vo, resid, xn, x_half, cot, cos, upper, lower, seg_col, seg_row,
    w_gate, w_up, w_down,
    a_own, b_own, g_own, u_own, d_own, c_own, seg_own,
    kh, x_rel, part, sent, got, send_sem, recv_sem, pair_send, pair_recv, own_sem, *moving,
):
    length = xh.shape[0]
    half = length // 2
    width = xh.shape[1]
    pairs = q.shape[1] // 128
    rows = 256
    core = place()[2]
    peers = partners()
    sems = (send_sem, recv_sem)
    n = Gather.MESSAGES
    whole, low, high = pl.ds(0, 64), pl.ds(0, 32), pl.ds(32, 32)
    third, fourth = pl.ds(32, 16), pl.ds(48, 16)
    plan = (
        (a_own, w_qk, whole, "zyx", 3),
        (b_own, w_vo, low, "zyx", 3),
        (b_own, w_vo, high, "xyz", 3),
        (g_own, w_gate, whole, "zyx", 3),
        (u_own, w_up, low, "zyx", 3),
        (u_own, w_up, third, "zxy", 3),
        (u_own, w_up, fourth, "xyz", 3),
        (d_own, w_down, low, "zyx", 2),
        (d_own, w_down, high, "zxy", 2),
    )
    gathers = [Gather(*piece, peers, sems, i * n) for i, piece in enumerate(plan)]
    one, early, two, late, three = gathers[:2], gathers[2], gathers[3:6], gathers[6], gathers[7:]
    owns = [
        pltpu.make_async_copy(src, dst.at[0, 0, 0], own_sem.at[i])
        for i, (src, dst) in enumerate(
            ((a_own, w_qk), (b_own, w_vo), (g_own, w_gate), (u_own, w_up), (d_own, w_down))
        )
    ]
    move_a, move_b, move_x, move_seg, move_g, move_u, move_d, move_c = (
        Move(src, dst, moving, i)
        for i, (src, dst) in enumerate(
            (
                (a_in, a_own),
                (b_in, b_own),
                (x_in, x_half),
                (seg_in, seg_own),
                (g_in, g_own),
                (u_in, u_own),
                (d_in, d_own),
                (c_in, c_own),
            )
        )
    )
    meet(peers, exchanged())
    for move in (move_a, move_b, move_seg, move_x, move_g, move_u, move_d):
        move.start()

    def tables(here):
        shape = (here.size, 128)
        row = here.start + lax.broadcasted_iota(jnp.int32, shape, 0) + core * half
        row = jnp.where(row >= length, row - length, row)
        angle = row.astype(F32) * inverse[0:1, :]
        front = lax.broadcasted_iota(jnp.int32, shape, 1) % HD < HD // 2
        sin = jnp.sin(angle)
        cos[here, :] = jnp.cos(angle)
        upper[here, :] = jnp.where(front, -sin, 0.0)
        lower[here, :] = jnp.where(front, 0.0, sin)

    move_a.wait()
    move_b.wait()
    early.start()
    for gather in one:
        gather.start()
    for gather in [early] + one:
        gather.relay(0)
    for copy in owns[:2]:
        copy.start()
    in_chunks(length, 64, tables)
    early.relay(1)
    move_seg.wait()
    ids = seg_own[...]
    ids = jnp.where(core == 0, ids, jnp.concatenate([ids[:, half:], ids[:, :half]], axis=1))
    seg_row[...] = ids
    seg_col[...] = jnp.transpose(jnp.broadcast_to(ids[0:1, :], (128, length)))
    early.relay_again(0)
    for gather in one:
        gather.relay(1)
    early.relay_again(1)
    move_x.wait()

    def first_norm(i, carry):
        here = pl.ds(pl.multiple_of(i * 128, 128), 128)
        values = to_place(x_half[here, :].astype(F32))
        x_rel[here, :] = values.astype(BF)
        xh[here, :] = normalize(values)[0].astype(BF)
        return carry

    lax.fori_loop(0, half // 128, first_norm, 0)
    for z in (2, 3):
        for gather in one:
            gather.relay(z)
    swap_xh = remote(
        xh.at[pl.ds(0, half)], xh.at[pl.ds(half, half)], pair_send.at[0], pair_recv.at[0], peers["c"]
    )
    swap_xh.start()
    move_g.wait()
    move_u.wait()
    for gather in two:
        gather.start()
    for z in range(4):
        for gather in one:
            gather.relay_again(z)
    for gather in two:
        gather.relay(0)
    late.start()
    move_d.wait()
    for gather in three:
        gather.start()
    for copy in owns[2:]:
        copy.start()
    swap_xh.wait()
    for gather in one + [early]:
        gather.finish()
    for copy in owns[:2]:
        copy.wait()

    events = {}
    at_step = lambda step, call, *args: events.setdefault(step, []).append((call, args))
    for z in range(4):
        for gather in two:
            if z:
                at_step(1 + z, gather.relay, z)
            at_step(6 + z, gather.relay_again, z)
        for gather in three:
            at_step(9 + z, gather.relay, z)
    at_step(1, late.relay, 0)
    at_step(5, late.relay, 1)
    at_step(5, move_c.start)
    at_step(9, late.relay_again, 0)
    at_step(12, late.relay_again, 1)
    first = lax.broadcasted_iota(jnp.int32, (length, 128), 1) < HD

    def pair(h, carry):
        lanes = pl.ds(pl.multiple_of(h * 128, 128), 128)
        lanes_k = pl.ds(pl.multiple_of((h + pairs) * 128, 128), 128)
        weight = lambda ref, cols: ref[:, :, :, :, cols].reshape(width, 128)
        tokens = xh[...]
        qf = dotf(tokens, weight(w_qk, lanes), NN)
        qf = qf * cos[...] + turn(qf, upper[...], lower[...])
        q[:, lanes] = (qf * (1.0 / math.sqrt(HD))).astype(BF)
        kf = dotf(tokens, weight(w_qk, lanes_k), NN)
        kf = (kf * cos[...] + turn(kf, upper[...], lower[...])).astype(BF)
        k[:, lanes] = kf
        kh[0] = jnp.where(first, kf, jnp.zeros_like(kf))
        kh[1] = jnp.where(first, jnp.zeros_like(kf), kf)
        v[:, lanes] = dotf(tokens, weight(w_vo, lanes), NN).astype(BF)

        def block(i, carry):
            for step, calls in events.items():

                @pl.when(h * (length // rows) + i == step)
                def _():
                    for call, args in calls:
                        call(*args)

            at = pl.multiple_of(i * rows, rows)
            q_rows = q[pl.ds(at, rows), lanes]
            same = seg_col[pl.ds(at, rows), 0:1] == seg_row[0:1, :]
            outs = []
            for head in range(2):
                scores = dotf(q_rows, kh[head], NT)
                scores = jnp.where(same, scores, -1e30)
                top = jnp.max(scores, axis=-1, keepdims=True)
                expv = jnp.exp(scores - top)
                total = jnp.sum(expv, axis=-1, keepdims=True)
                low_probs = (expv * (1.0 / total)).astype(BF)
                outs.append(dotf(low_probs, v[:, lanes], NN))
                level = top + jnp.log(total)
                flat = jnp.transpose(jnp.broadcast_to(level, (rows, 128)))
                lse[h, pl.ds(head, 1), pl.ds(at, rows)] = flat[0:1, :]
            o[pl.ds(at, rows), lanes] = jnp.where(first[:rows], outs[0], outs[1]).astype(BF)
            return carry

        return lax.fori_loop(0, length // rows, block, carry)

    lax.fori_loop(0, pairs, pair, 0)
    w_o = w_vo[:, :, :, :, pairs * 128 :].reshape(width, pairs * 128)

    def project(i, carry):
        at = pl.multiple_of(half + i * rows, rows)
        sent[pl.ds(pl.multiple_of(i * rows, rows), rows), :] = dotf(
            o[pl.ds(at, rows), :], w_o, NT
        ).astype(BF)
        return carry

    lax.fori_loop(0, half // rows, project, 0)

    def project_own(i, carry):
        here = pl.ds(pl.multiple_of(i * rows, rows), rows)
        part[here, :] = dotf(o[here, :], w_o, NT)
        return carry

    give = remote(sent, got, pair_send.at[1], pair_recv.at[1], peers["c"])
    lax.fori_loop(0, half // rows, project_own, 0)
    give.start()
    move_c.wait()

    def turn_cot(here):
        cot[here, :] = to_place(c_own[here, :].astype(F32)).astype(BF)

    in_chunks(half, 128, turn_cot)
    swap_cot = remote(
        cot.at[pl.ds(0, half)], cot.at[pl.ds(half, half)], pair_send.at[3], pair_recv.at[3], peers["c"]
    )
    swap_cot.start()
    give.wait()

    def second_norm(i, carry):
        here = pl.ds(pl.multiple_of(i * 128, 128), 128)
        values = x_rel[here, :].astype(F32) + (part[here, :] + got[here, :].astype(F32))
        resid[here, :] = values
        xn[here, :] = normalize(values)[0].astype(BF)
        return carry

    lax.fori_loop(0, half // 128, second_norm, 0)
    swap_xn = remote(
        xn.at[pl.ds(0, half)], xn.at[pl.ds(half, half)], pair_send.at[2], pair_recv.at[2], peers["c"]
    )
    swap_xn.start()
    for gather in two + three + [late]:
        gather.finish()
    for copy in owns[2:]:
        copy.wait()
    swap_cot.wait()
    swap_xn.wait()


def forward_block(owned, x_half, cot_half, seg, inverse):
    half, width = x_half.shape
    length = 2 * half
    cols = owned[0].shape[1] // 2
    pairs = cols // 128
    units = owned[2].shape[1]
    shard = width // 16
    vmem = pl.BlockSpec(memory_space=pltpu.VMEM)
    any_ = pl.BlockSpec(memory_space=pl.ANY)
    gathered = lambda n: jax.ShapeDtypeStruct(SHARD + (shard, n), BF)
    heads = jax.ShapeDtypeStruct((length, cols), BF)
    flat = jax.ShapeDtypeStruct((length, width), BF)
    table = jax.ShapeDtypeStruct((length, 128), F32)
    return pl.pallas_call(
        forward_kernel,
        in_specs=[any_] * 8 + [vmem],
        out_specs=[vmem] * 17 + [any_] * 3,
        out_shape=[heads] * 4
        + [
            jax.ShapeDtypeStruct((pairs, 2, length), F32),
            flat,
            gathered(2 * cols),
            gathered(2 * cols),
            jax.ShapeDtypeStruct((half, width), F32),
            flat,
            jax.ShapeDtypeStruct((half, width), BF),
            flat,
        ]
        + [table] * 4
        + [jax.ShapeDtypeStruct((8, length), F32)]
        + [gathered(units)] * 3,
        scratch_shapes=[pltpu.VMEM((shard, 2 * cols), BF)] * 2
        + [pltpu.VMEM((shard, units), BF)] * 3
        + [
            pltpu.VMEM((half, width), BF),
            pltpu.VMEM((8, length), F32),
            pltpu.VMEM((2, length, 128), BF),
            pltpu.VMEM((half, width), BF),
            pltpu.VMEM((half, width), F32),
            pltpu.VMEM((half, width), BF),
            pltpu.VMEM((half, width), BF),
            pltpu.SemaphoreType.DMA((9 * Gather.MESSAGES,)),
            pltpu.SemaphoreType.DMA((9 * Gather.MESSAGES,)),
            pltpu.SemaphoreType.DMA((4,)),
            pltpu.SemaphoreType.DMA((4,)),
            pltpu.SemaphoreType.DMA((5,)),
        ]
        + move_sems(8),
        compiler_params=pltpu.CompilerParams(
            collective_id=0, has_side_effects=True, vmem_limit_bytes=60 << 20
        ),
        name="forward_block",
    )(*owned, x_half, cot_half, seg, inverse)


class Reduce:
    MESSAGES = 12
    ORDER = (2, 3, 1, 0)

    def __init__(self, parts, near, rows, axes, peers, sems, base, bufs, out):
        self.parts, self.near, self.rows, self.axes, self.peers = parts, near, rows, axes, peers
        self.send_sem, self.recv_sem = sems
        self.base = base
        self.one, self.two, self.three, self.sum = bufs
        self.out = out

    def link(self, i, src, dst, peer):
        n = self.base + i
        return remote(src, dst, self.send_sem.at[n], self.recv_sem.at[n], peer)

    def first(self, z):
        if self.axes == "xy":
            src = self.parts.at[z, :, 1, self.rows]
        else:
            src = self.parts.at[z, 1, :, self.rows]
        return self.link(z, src, self.one.at[z], self.peers[self.axes[1]])

    def second(self, z):
        return self.link(4 + z, self.one.at[z, 1], self.two.at[z], self.peers[self.axes[0]])

    def third(self, z):
        return self.link(7 + z, self.two.at[z], self.three.at[z - 1], self.peers["z%d" % z])

    def start(self):
        for z in self.ORDER:
            self.first(z).start()

    def add_first(self, z):
        self.first(z).wait_recv()
        self.one[z] = (self.one[z].astype(F32) + self.near(z).astype(F32)).astype(BF)

    def relay_first(self, z):
        self.add_first(z)
        self.second(z).start()

    def resume(self):
        for z in self.ORDER:
            self.second(z).start()

    def relay_second(self, z):
        self.second(z).wait_recv()
        self.two[z] = (self.two[z].astype(F32) + self.one[z, 0].astype(F32)).astype(BF)
        if z:
            self.third(z).start()

    def last(self):
        moved, peer = exchanged()
        return moved, self.link(11, self.sum, self.out, peer)

    def total(self):
        total = self.two[0].astype(F32)
        for z in (1, 2, 3):
            self.third(z).wait_recv()
            total = total + self.three[z - 1].astype(F32)
        return total

    def finish(self):
        self.sum[...] = self.total().astype(BF)
        moved, copy = self.last()

        @pl.when(moved)
        def _():
            copy.start()

        @pl.when(jnp.logical_not(moved))
        def _():
            self.out[...] = self.sum[...]

    def sent(self):
        hops = (self.second,) if self.parts is None else (self.first, self.second)
        thirds = [self.third(z) for z in (1, 2, 3)]
        return [hop(z) for z in range(4) for hop in hops] + thirds

    def close(self):
        for copy in self.sent():
            copy.wait_send()
        moved, copy = self.last()

        @pl.when(moved)
        def _():
            copy.wait()


class ReduceAlongZ(Reduce):
    def first(self, z):
        src = self.parts.at[z, :, :, self.rows]
        return self.link(z - 1, src, self.one.at[z - 1], self.peers["z%d" % z])

    def second(self):
        return self.link(3, self.two.at[:, 1], self.three.at[0:2], self.peers["y"])

    def third(self):
        return self.link(4, self.three.at[1], self.three.at[2], self.peers["x"])

    def start(self):
        for z in (2, 3, 1):
            self.first(z).start()

    def relay_first(self):
        total = self.near().astype(F32)
        for z in (1, 2, 3):
            self.first(z).wait_recv()
            total = total + self.one[z - 1].astype(F32)
        self.two[...] = total.astype(BF)
        self.second().start()

    def relay_second(self):
        self.second().wait_recv()
        for x in (0, 1):
            self.three[x] = (self.three[x].astype(F32) + self.two[x, 0].astype(F32)).astype(BF)
        self.third().start()

    def total(self):
        self.third().wait_recv()
        return self.three[0].astype(F32) + self.three[2].astype(F32)

    def sent(self):
        return [self.first(z) for z in (1, 2, 3)] + [self.second(), self.third()]


def mlp_kernel(
    down_in, xn, cot, w_gate, w_up, resid,
    result, resid_grad, attn_cot, d_gate, d_up, d_low, d_high,
    w_down, d_down, hidden, act, slope_up, gate_grad, up_grad, own, sent, got, placed,
    send_sem, recv_sem, last_send, last_recv, first_send, first_recv, own_sem, *moving,
):
    length, width = xn.shape
    half = length // 2
    units = w_gate.shape[1]
    peers = {axis: partners()[axis] for axis in "xyc"}
    move = Move(placed, result, moving, 0)
    low, high = pl.ds(0, 32), pl.ds(32, 32)
    most, few = pl.ds(0, 48), pl.ds(48, 16)
    at_low = lambda ref, z, x: ref.at[z, x, :, low]
    at_high = lambda ref, z, y: ref.at[z, :, y, high]
    last = []
    for z in range(4):
        for i, (part, axis) in enumerate(((at_low, "x"), (at_high, "y"))):
            n = 2 * z + i
            last.append(
                remote(
                    part(down_in, z, 0), part(w_down, z, 1), last_send.at[n], last_recv.at[n], peers[axis]
                )
            )
    every = pl.ds(0, 4)
    owns = [
        pltpu.make_async_copy(part(down_in, every, 0), part(w_down, every, 0), own_sem.at[i])
        for i, part in enumerate((at_low, at_high))
    ]
    sems = (first_send, first_recv)
    n = Reduce.MESSAGES
    reduce_low = Reduce(
        d_down, lambda z: d_down[z, 0, :, 0:48], most, "yx", peers, sems, 0, (d_low, None, None, None), None
    )
    reduce_high = Reduce(
        d_down, lambda z: d_down[z, :, 0, 48:64], few, "xy", peers, sems, n, (d_high, None, None, None), None
    )
    meet(peers, exchanged())
    for copy in last + owns:
        copy.start()
    back, front = pl.ds(half, half), pl.ds(0, half)

    def gate_and_up(rows):
        def step(cols):
            gate = dotf(xn[rows, :], w_gate[:, cols], NN)
            up = dotf(xn[rows, :], w_up[:, cols], NN)
            value, slope = gelu_parts(gate)
            hidden[rows, cols] = (value * up).astype(BF)
            act[rows, cols] = value
            slope_up[rows, cols] = up * slope

        in_chunks(units, 256, step)

    def units_back(rows):
        def step(cols):
            down = w_down[:, :, :, :, cols].reshape(width, cols.size)
            grad = dotf(cot[rows, :], down, NN).astype(BF).astype(F32)
            gate_grad[rows, cols] = (grad * slope_up[rows, cols]).astype(BF)
            up_grad[rows, cols] = (grad * act[rows, cols]).astype(BF)

        in_chunks(units, 256, step)

    def sums(rows, put):
        def step(z, carry):
            here = pl.ds(pl.multiple_of(z * 256, 256), 256)
            down = w_down[z].reshape(256, units)
            put[0, :, here] = dotf(hidden[rows, :], down, NT).astype(put.dtype)
            both = dotf(gate_grad[rows, :], w_gate[here, :], NT)
            both = both + dotf(up_grad[rows, :], w_up[here, :], NT)
            put[1, :, here] = both.astype(put.dtype)
            return carry

        lax.fori_loop(0, width // 256, step, 0)

    gate_and_up(back)
    gate_and_up(front)
    for z in Reduce.ORDER:
        left = jnp.transpose(cot[:, z * 256 : (z + 1) * 256])
        d_down[z] = dotf(left, hidden[...], NN).astype(BF).reshape(2, 2, 64, units)
        reduce_low.first(z).start()
        reduce_high.first(z).start()
    for copy in owns:
        copy.wait()
    for copy in last:
        copy.wait()
    units_back(back)
    sums(back, sent)
    give = remote(sent, got, send_sem.at[0], recv_sem.at[0], peers["c"])
    give.start()
    units_back(front)
    sums(front, own)
    give.wait()

    def finish(here):
        values = resid[here, :]
        mlp = own[0, here, :] + got[0, here, :].astype(F32)
        placed[here, :] = to_place(values + mlp).astype(BF)
        xhat, scale = normalize(values)
        back = normalize_back(own[1, here, :] + got[1, here, :].astype(F32), xhat, scale)
        grad = cot[here, :].astype(F32) + back
        resid_grad[here, :] = grad
        attn_cot[here, :] = grad.astype(BF)

    in_chunks(half, 64, finish)
    swap = remote(
        attn_cot.at[pl.ds(0, half)], attn_cot.at[pl.ds(half, half)], send_sem.at[1], recv_sem.at[1], peers["c"]
    )
    swap.start()
    move.start()

    def weights(here):
        left = jnp.transpose(xn[:, here])
        d_gate[here, :] = dotf(left, gate_grad[...], NN).astype(BF)
        d_up[here, :] = dotf(left, up_grad[...], NN).astype(BF)

    in_chunks(width, 256, weights)
    for z in Reduce.ORDER:
        reduce_low.add_first(z)
        reduce_high.add_first(z)
    for z in range(4):
        reduce_low.first(z).wait_send()
        reduce_high.first(z).wait_send()
    swap.wait()
    move.wait()


def mlp_block(down_in, xn, cot, w_gate, w_up, resid):
    length, width = xn.shape
    half = length // 2
    units = w_gate.shape[1]
    shard = width // 16
    vmem = pl.BlockSpec(memory_space=pltpu.VMEM)
    any_ = pl.BlockSpec(memory_space=pl.ANY)
    grads = jax.ShapeDtypeStruct((width, units), BF)
    dma = lambda n: pltpu.SemaphoreType.DMA((n,))
    return pl.pallas_call(
        mlp_kernel,
        in_specs=[any_] + [vmem] * 5,
        out_specs=[any_] + [vmem] * 6,
        out_shape=[
            jax.ShapeDtypeStruct((half, width), BF),
            jax.ShapeDtypeStruct((half, width), F32),
            jax.ShapeDtypeStruct((length, width), BF),
            grads,
            grads,
            jax.ShapeDtypeStruct((4, 2, shard * 3 // 4, units), BF),
            jax.ShapeDtypeStruct((4, 2, shard // 4, units), BF),
        ],
        scratch_shapes=[pltpu.VMEM(SHARD + (shard, units), BF)] * 2
        + [
            pltpu.VMEM((length, units), BF),
            pltpu.VMEM((length, units), F32),
            pltpu.VMEM((length, units), F32),
            pltpu.VMEM((length, units), BF),
            pltpu.VMEM((length, units), BF),
            pltpu.VMEM((2, half, width), F32),
            pltpu.VMEM((2, half, width), BF),
            pltpu.VMEM((2, half, width), BF),
            pltpu.VMEM((half, width), BF),
        ]
        + [dma(2), dma(2), dma(8), dma(8), dma(2 * Reduce.MESSAGES), dma(2 * Reduce.MESSAGES), dma(2)]
        + move_sems(1),
        compiler_params=pltpu.CompilerParams(
            collective_id=1, has_side_effects=True, vmem_limit_bytes=63 << 20
        ),
        name="mlp_block",
    )(down_in, xn, cot, w_gate, w_up, resid)


def backward_kernel(
    d_gate, d_up, d_low, d_high, q, k, v, o, lse, attn_cot, w_qk, w_vo, xh, x_half, resid_grad,
    cos, upper, lower, seg_col, seg_row,
    token_grad, s_gate, s_up_low, s_up_high, s_down_low, s_down_high, s_qk, s_vo_low, s_vo_high,
    d_qk, d_vo, pg, heads_grad, kh, dk, dv, own, sent, got, placed,
    near_gate, near_up_low, near_up_high,
    *rest,
):
    bufs = [rest[4 * i : 4 * i + 4] for i in range(3)]
    bufs += [(first,) + rest[12 + 3 * i : 15 + 3 * i] for i, first in enumerate((d_low, d_high))]
    bufs += [rest[18 + 4 * i : 22 + 4 * i] for i in range(3)]
    send_sem, recv_sem, pair_send, pair_recv, near_sem, *moving = rest[30:]
    length, width = xh.shape
    half = length // 2
    cols = q.shape[1]
    pairs = cols // 128
    rows = 256
    peers = partners()
    sems = (send_sem, recv_sem)
    n = Reduce.MESSAGES
    whole, most, few = pl.ds(0, 64), pl.ds(0, 48), pl.ds(48, 16)
    held = lambda ref: (lambda z: ref[z])
    plan = (
        (Reduce, d_gate, held(near_gate), whole, "yx", s_gate),
        (Reduce, d_up, held(near_up_low), most, "yx", s_up_low),
        (ReduceAlongZ, d_up, lambda: near_up_high[...], few, None, s_up_high),
        (Reduce, None, None, most, "yx", s_down_low),
        (Reduce, None, None, few, "xy", s_down_high),
        (Reduce, d_qk, lambda z: d_qk[z, 0], whole, "yx", s_qk),
        (Reduce, d_vo, lambda z: d_vo[z, :, 0, 0:48], most, "xy", s_vo_low),
        (ReduceAlongZ, d_vo, lambda: d_vo[0, :, :, 48:64], few, None, s_vo_high),
    )
    parts = [
        kind(src, near, rows_, axes, peers, sems, i * n, bufs[i], out)
        for i, (kind, src, near, rows_, axes, out) in enumerate(plan)
    ]
    gate, up_low, up_high, down_low, down_high, qk, vo_low, vo_high = parts
    nears = [
        pltpu.make_async_copy(src, dst, near_sem.at[i])
        for i, (src, dst) in enumerate(
            (
                (d_gate.at[:, 0], near_gate),
                (d_up.at[:, 0, :, most], near_up_low),
                (d_up.at[0, :, :, few], near_up_high),
            )
        )
    ]
    for copy in nears:
        copy.start()
    meet(peers, exchanged())
    up_high.start()
    down_low.resume()
    down_high.resume()
    gate.start()
    up_low.start()

    def heads(here):
        heads_grad[here, :] = dotf(attn_cot[here, :], w_vo[:, cols:], NN).astype(BF)

    in_chunks(length, 256, heads)

    def out_weights(z, carry):
        here = pl.ds(pl.multiple_of(z * 256, 256), 256)
        value = dotf(jnp.transpose(attn_cot[:, here]), o[...], NN).astype(BF)
        d_vo[z, :, :, :, cols:] = value.reshape(2, 2, 64, cols)
        return carry

    lax.fori_loop(0, width // 256, out_weights, 0)
    for copy in nears:
        copy.wait()

    events = {}
    for i, z in enumerate(Reduce.ORDER):
        if i < 3:
            events.setdefault(4 + 4 * i, []).append(lambda z=z: gate.relay_first(z))
        events.setdefault(3 + 3 * i, []).append(lambda z=z: down_low.relay_second(z))
        events.setdefault(2 + 3 * i, []).append(lambda z=z: down_high.relay_second(z))
    events.setdefault(7, []).append(up_high.relay_first)
    events.setdefault(13, []).append(up_high.relay_second)
    lane = lax.broadcasted_iota(jnp.int32, (length, 128), 1)
    first = lane < HD

    def pair(h, carry):
        lanes = pl.ds(pl.multiple_of(h * 128, 128), 128)
        kf = k[:, lanes]
        none = jnp.zeros_like(kf)
        kh[0] = jnp.where(first, kf, none)
        kh[1] = jnp.where(first, none, kf)
        dk[...] = jnp.zeros_like(dk)
        dv[...] = jnp.zeros_like(dv)

        def block(i, carry):
            for step, calls in events.items():

                @pl.when(h * (length // rows) + i == step)
                def _():
                    for call in calls:
                        call()

            at = pl.multiple_of(i * rows, rows)
            here = pl.ds(at, rows)
            q_rows = q[here, lanes]
            g_rows = heads_grad[here, lanes]
            same = seg_col[:, 0:1] == seg_row[0:1, here]
            prod = g_rows.astype(F32) * o[here, lanes].astype(F32)
            f = first[:rows]
            blank = jnp.zeros_like(q_rows)
            dq = jnp.zeros((rows, 128), F32)
            for head in range(2):
                mine = f if head == 0 else jnp.logical_not(f)
                q_head = jnp.where(mine, q_rows, blank)
                g_head = jnp.where(mine, g_rows, blank)
                delta = lax.dot_general(
                    jnp.ones((8, 128), F32),
                    jnp.where(mine, prod, 0.0),
                    (NT, ((), ())),
                    precision=lax.Precision.HIGHEST,
                    preferred_element_type=F32,
                )[0:1, :]
                scores = dotf(k[:, lanes], q_head, NT)
                level = lse[h, pl.ds(head, 1), here]
                probs = jnp.where(same, jnp.exp(scores - level), 0.0)
                dv[...] += dotf(probs.astype(BF), g_head, NN)
                dp = dotf(v[:, lanes], g_head, NT)
                ds = (probs * (dp - delta)).astype(BF)
                dk[...] += dotf(ds, q_head, NN)
                dq = dq + dotf(ds, kh[head], TN)
            dq = dq * (1.0 / math.sqrt(HD))
            c, a, b = cos[here, :], upper[here, :], lower[here, :]
            pg[0, here, lanes] = (dq * c - turn(dq, a, b)).astype(BF)
            return carry

        lax.fori_loop(0, length // rows, block, 0)
        dkf = dk[...]
        pg[1, :, lanes] = (dkf * cos[...] - turn(dkf, upper[...], lower[...])).astype(BF)
        pg[2, :, lanes] = dv[...].astype(BF)
        return carry

    lax.fori_loop(0, pairs, pair, 0)
    gate.relay_first(Reduce.ORDER[3])

    def weights(z, carry):
        left = jnp.transpose(xh[:, pl.ds(pl.multiple_of(z * 256, 256), 256)])
        for i, (ref, at) in enumerate(((d_qk, 0), (d_qk, cols), (d_vo, 0))):
            value = dotf(left, pg[i], NN).astype(BF)
            ref[z, :, :, :, at : at + cols] = value.reshape(2, 2, 64, cols)
        return carry

    lax.fori_loop(0, width // 256, weights, 0)

    def back(tokens, put):
        def step(here):
            total = dotf(pg[0, tokens, :], w_qk[here, :cols], NT)
            total = total + dotf(pg[1, tokens, :], w_qk[here, cols:], NT)
            put[:, here] = (total + dotf(pg[2, tokens, :], w_vo[here, :cols], NT)).astype(put.dtype)

        in_chunks(width, 256, step)

    for part in (qk, vo_low, vo_high):
        part.start()
    back(pl.ds(half, half), sent)
    give = remote(sent, got, pair_send.at[0], pair_recv.at[0], peers["c"])
    give.start()
    back(pl.ds(0, half), own)
    down_low.finish()
    down_high.finish()
    give.wait()

    def finish(here):
        xhat, scale = normalize(to_place(x_half[here, :].astype(F32)))
        f = own[here, :] + got[here, :].astype(F32)
        value = resid_grad[here, :] + normalize_back(f, xhat, scale)
        placed[here, :] = to_place(value).astype(BF)

    in_chunks(half, 64, finish)
    move = Move(placed, token_grad, moving, 0)
    move.start()
    up_high.finish()
    for z in Reduce.ORDER:
        up_low.relay_first(z)
        gate.relay_second(z)
    vo_high.relay_first()
    for z in Reduce.ORDER:
        vo_low.relay_first(z)
    gate.finish()
    for z in Reduce.ORDER:
        qk.relay_first(z)
        up_low.relay_second(z)
    vo_high.relay_second()
    for z in Reduce.ORDER:
        vo_low.relay_second(z)
    up_low.finish()
    for z in Reduce.ORDER:
        qk.relay_second(z)
    vo_high.finish()
    vo_low.finish()
    qk.finish()
    for part in parts:
        part.close()
    move.wait()


def backward_block(grads, heads, lse, attn_cot, w_qk, w_vo, xh, x_half, resid_grad, tables, seg_col, seg_row):
    length, width = xh.shape
    half = length // 2
    cols = heads[0].shape[1]
    units = grads[0].shape[1]
    shard = width // 16
    vmem = pl.BlockSpec(memory_space=pltpu.VMEM)
    any_ = pl.BlockSpec(memory_space=pl.ANY)
    most, few = shard * 3 // 4, shard // 4
    sizes = [(shard, units)] + [(most, units), (few, units)] * 2
    sizes += [(shard, 2 * cols), (most, 2 * cols), (few, 2 * cols)]
    along_z, begun = (2, 7), (3, 4)
    bufs = []
    for i, size in enumerate(sizes):
        if i in along_z:
            lead = (3, 2, 2), (2, 2), (3,)
        else:
            lead = (4, 2), (4,), (3,)
        bufs += [pltpu.VMEM(n + size, BF) for n in lead[i in begun :] + ((),)]
    nears = [pltpu.VMEM(((2, 2) if i in along_z else (4, 2)) + size, BF) for i, size in enumerate(sizes[:3])]
    messages = 8 * Reduce.MESSAGES
    return pl.pallas_call(
        backward_kernel,
        in_specs=[any_] * 2 + [vmem] * 18,
        out_specs=[vmem] * 9,
        out_shape=[jax.ShapeDtypeStruct((half, width), BF)]
        + [jax.ShapeDtypeStruct(size, BF) for size in sizes],
        scratch_shapes=[pltpu.VMEM(SHARD + (shard, 2 * cols), BF)] * 2
        + [
            pltpu.VMEM((3, length, cols), BF),
            pltpu.VMEM((length, cols), BF),
            pltpu.VMEM((2, length, 128), BF),
            pltpu.VMEM((length, 128), F32),
            pltpu.VMEM((length, 128), F32),
            pltpu.VMEM((half, width), F32),
            pltpu.VMEM((half, width), BF),
            pltpu.VMEM((half, width), BF),
            pltpu.VMEM((half, width), BF),
        ]
        + nears
        + bufs
        + [
            pltpu.SemaphoreType.DMA((messages,)),
            pltpu.SemaphoreType.DMA((messages,)),
            pltpu.SemaphoreType.DMA((1,)),
            pltpu.SemaphoreType.DMA((1,)),
            pltpu.SemaphoreType.DMA((3,)),
        ]
        + move_sems(1),
        compiler_params=pltpu.CompilerParams(
            collective_id=2, has_side_effects=True, vmem_limit_bytes=60 << 20
        ),
        name="backward_block",
    )(
        *(g.reshape(SHARD + (shard, units)) for g in grads[:2]), *grads[2:],
        *heads, lse, attn_cot, w_qk, w_vo, xh, x_half, resid_grad, *tables, seg_col, seg_row,
    )


class Chips:
    def sum_tensor(self, value):
        pairs = [(2 * i + y, 2 * i + 1 - y) for i in range(16) for y in range(2)]
        return value + lax.ppermute(value, ("dp", "tensor"), pairs)


class Axes:
    def gather_rows(self, value):
        return lax.all_gather(value, "tensor", axis=0, tiled=True)

    def scatter_rows(self, value):
        return lax.psum_scatter(value.astype(BF), "tensor", scatter_dimension=0, tiled=True).astype(F32)

    def reduce(self, a, b):
        return tuple(
            lax.psum_scatter(w.astype(BF), "dp", scatter_dimension=0, tiled=True).astype(F32)
            for w in (a, b)
        )

    def sum_tensor(self, value):
        return lax.psum(value, "tensor")


def normalize(values):
    centred = values - jnp.mean(values, axis=-1, keepdims=True)
    scale = lax.rsqrt(jnp.mean(centred * centred, axis=-1, keepdims=True) + EPS)
    return centred * scale, scale


def normalize_back(f, xhat, scale):
    return scale * (
        f
        - jnp.mean(f, axis=-1, keepdims=True)
        - xhat * jnp.mean(f * xhat, axis=-1, keepdims=True)
    )


def gelu_parts(gate):
    half_erf = 0.5 * (1.0 + lax.erf(gate * (1.0 / math.sqrt(2.0))))
    density = jnp.exp(-0.5 * gate * gate) * (1.0 / math.sqrt(2.0 * math.pi))
    return gate * half_erf, half_erf + gate * density


def make_local(comm_type):
    def local(tokens, segments, w_qkv, w_out, w_in, w_down, g_attn, g_mlp, cotangent):
        comm = comm_type()
        paired = comm_type is Chips
        shard = w_qkv.shape[0]
        cols = w_qkv.shape[2]
        units = w_in.shape[2]
        low = 128 * (units // 256)
        pad = 128 * pl.cdiv(units, 128) - units
        gain_one = g_attn.astype(F32)[:, None]
        gain_two = g_mlp.astype(F32)[:, None]
        scaled = lambda w, g: (w.astype(F32) * g).astype(BF)
        padded = lambda w: jnp.pad(w, ((0, 0), (0, pad)))
        down_rows = w_down.T
        a_one = jnp.concatenate([scaled(w_qkv[:, 0], gain_one), scaled(w_qkv[:, 1], gain_one)], axis=1)
        b_one = jnp.concatenate([scaled(w_qkv[:, 2], gain_one), w_out.T], axis=1)
        own_gate, own_up = scaled(w_in[:, 0], gain_two), scaled(w_in[:, 1], gain_two)

        owned = (a_one, b_one, own_gate, own_up, down_rows)
        if paired:
            owned = owned[:2] + tuple(padded(w) for w in owned[2:])
            seg = jnp.broadcast_to(segments.astype(F32), (8, segments.shape[1]))
            inverse = jnp.broadcast_to(jnp.tile(rope_rates(), 4), (8, 128))
            (
                q, k, v, o, lse, xh, w_qk, w_vo, resid, xn, x_half, cot_all, *tables, seg_col, seg_row,
                w_gate, w_up, w_dn,
            ) = forward_block(owned, tokens[0], cotangent[0], seg, inverse)
            w_qk, w_vo, w_gate, w_up = (
                w.reshape(-1, w.shape[-1]) for w in (w_qk, w_vo, w_gate, w_up)
            )
        else:
            w_qk, w_vo, w_gate, w_up, w_dn = (
                lax.all_gather(w, "dp", axis=0, tiled=True) for w in owned
            )
            w_o = w_vo[:, cols:]
            seg_col, seg_row = segments[0][:, None], segments
            cot = cotangent[0]
            cot_all = comm.gather_rows(cot)
            tables = rope_tables(jnp.arange(segments.shape[1]))
            x_in = tokens[0].astype(F32)
            xh_one, scale_one = normalize(x_in)
            xh = comm.gather_rows(xh_one.astype(BF))
            o, q, k, v, lse = attn_fwd(xh, w_qk, w_vo, tables, seg_col, seg_row)
            resid = x_in + comm.scatter_rows(dotf(o, w_o, NT))
            xh_two, scale_two = normalize(resid)
            xn = comm.gather_rows(xh_two.astype(BF))
        if paired:
            result, resid_grad, attn_cot, *grads = mlp_block(w_dn, xn, cot_all, w_gate, w_up, resid)
        else:
            gate, up = dotf(xn, w_gate, NN), dotf(xn, w_up, NN)
            act, slope = gelu_parts(gate)
            hidden = (act * up).astype(BF)
            mlp = comm.scatter_rows(dotf(hidden, w_dn, NT))
            result = (resid + mlp).astype(BF)
            hidden_grad = dotf(cot_all, w_dn, NN).astype(BF).astype(F32)
            gate_grad = (hidden_grad * up * slope).astype(BF)
            up_grad = (hidden_grad * act).astype(BF)
            f_two = comm.scatter_rows(dotf(gate_grad, w_gate, NT) + dotf(up_grad, w_up, NT))
            resid_grad = cot.astype(F32) + normalize_back(f_two, xh_two, scale_two)
            attn_cot = comm.gather_rows(resid_grad.astype(BF))
            d_down = dotf(cot_all, hidden, TN)
            d_gate, d_up = dotf(xn, gate_grad, TN), dotf(xn, up_grad, TN)

        if paired:
            token_grad, *sums = backward_block(
                grads, (q, k, v, o), lse, attn_cot, w_qk, w_vo, xh, x_half,
                resid_grad, tables, seg_col, seg_row,
            )
            token_grad = token_grad.astype(F32)
            s_gate, up_low, up_high, s_low, s_high, one_a, vo_low, vo_high = (w.astype(F32) for w in sums)
            s_up = jnp.concatenate([up_low, up_high], axis=0)
            one_b = jnp.concatenate([vo_low, vo_high], axis=0)
            in_raw = jnp.stack([s_gate[:, :units], s_up[:, :units]], axis=1)
            down_sum = jnp.concatenate([s_low[:, :units], s_high[:, :units]], axis=0).T
        else:
            wide = lambda g, d: jnp.concatenate([padded(g), d], axis=1)
            two_a, two_b = comm.reduce(wide(d_gate, d_down[:, :low]), wide(d_up, d_down[:, low:]))

            heads_grad = dotf(attn_cot, w_o, NN).astype(BF)
            pg = attn_bwd(q, k, v, o, heads_grad, lse, tables, seg_col, seg_row)
            d_out = dotf(attn_cot, o, TN)
            d_q, d_k, d_v = (dotf(xh, pg[i], TN) for i in range(3))
            one_a, one_b = comm.reduce(
                jnp.concatenate([d_q, d_k], axis=1), jnp.concatenate([d_v, d_out], axis=1)
            )
            f_one = comm.scatter_rows(
                dotf(pg[0], w_qk[:, :cols], NT)
                + dotf(pg[1], w_qk[:, cols:], NT)
                + dotf(pg[2], w_vo[:, :cols], NT)
            )
            token_grad = resid_grad + normalize_back(f_one, xh_one, scale_one)
            in_raw = jnp.stack([two_a[:, :units], two_b[:, :units]], axis=1)
            down_sum = jnp.concatenate([two_a[:, units + pad :], two_b[:, units + pad :]], axis=1).T

        qkv_raw = jnp.stack([one_a[:, :cols], one_a[:, cols:], one_b[:, :cols]], axis=1)
        gains = jnp.stack(
            [
                jnp.sum(qkv_raw * w_qkv.astype(F32), axis=(1, 2)),
                jnp.sum(in_raw * w_in.astype(F32), axis=(1, 2)),
            ]
        )
        gains = comm.sum_tensor(gains)
        return (
            result[None],
            token_grad[None],
            gains[0],
            gains[1],
            qkv_raw * gain_one[:, :, None],
            one_b[:, cols:].T,
            in_raw * gain_two[:, :, None],
            down_sum,
        )

    return local


def solution(mesh):
    paired = mesh.shape["dp"] == 16 and mesh.shape["tensor"] == 2
    return jax.shard_map(
        make_local(Chips if paired else Axes),
        mesh=mesh,
        in_specs=(
            P("dp", "tensor", None),
            P("dp", None),
            P("dp", None, "tensor"),
            P("tensor", "dp"),
            P("dp", None, "tensor"),
            P("tensor", "dp"),
            P("dp"),
            P("dp"),
            P("dp", "tensor", None),
        ),
        out_specs=(
            P("dp", "tensor", None),
            P("dp", "tensor", None),
            P("dp"),
            P("dp"),
            P("dp", None, "tensor"),
            P("tensor", "dp"),
            P("dp", None, "tensor"),
            P("tensor", "dp"),
        ),
        check_vma=False,
    )
```

```python
import math

import jax
import jax.numpy as jnp
from jax import lax
from jax.experimental import pallas as pl
from jax.experimental.pallas import tpu as pltpu
from jax.sharding import PartitionSpec as P

HD = 64
EPS = 1e-05
ROTARY_BASE = 160000.0
BF = jnp.bfloat16
F32 = jnp.float32


def dotf(a, b, dims):
    return lax.dot_general(a, b, (dims, ((), ())), preferred_element_type=F32)


NN = ((1,), (0,))
NT = ((1,), (1,))
TN = ((0,), (0,))


def rope_rates():
    return 1.0 / ROTARY_BASE ** (jnp.arange(HD // 2).astype(F32) * (2.0 / HD))


def rope_tables(positions):
    angles = positions.astype(F32)[:, None] * rope_rates()[None, :]
    cos, sin = jnp.cos(angles), jnp.sin(angles)
    zero = jnp.zeros_like(sin)
    cosine = jnp.concatenate([cos] * 4, axis=-1)
    upper = jnp.concatenate([-sin, zero] * 2, axis=-1)
    lower = jnp.concatenate([zero, sin] * 2, axis=-1)
    return cosine, upper, lower


def turn(u, upper, lower):
    return pltpu.roll(u, 128 - HD // 2, 1) * upper + pltpu.roll(u, HD // 2, 1) * lower


def attn_fwd_kernel(xh, wq, wk, wv, cos, upper, lower, seg_col, seg_row, o, q, k, v, lse, kh):
    length = xh.shape[0]
    rows = min(256, length)
    lane = lax.broadcasted_iota(jnp.int32, (length, 128), 1)
    first = lane < HD
    tokens = xh[...]
    qf = dotf(tokens, wq[...], NN)
    qf = qf * cos[...] + turn(qf, upper[...], lower[...])
    q[...] = (qf * (1.0 / math.sqrt(HD))).astype(BF)
    kf = dotf(tokens, wk[...], NN)
    kf = (kf * cos[...] + turn(kf, upper[...], lower[...])).astype(BF)
    k[...] = kf
    kh[0] = jnp.where(first, kf, jnp.zeros_like(kf))
    kh[1] = jnp.where(first, jnp.zeros_like(kf), kf)
    v[...] = dotf(tokens, wv[...], NN).astype(BF)

    def block(i, carry):
        at = pl.multiple_of(i * rows, rows)
        q_rows = q[pl.ds(at, rows), :]
        same = seg_col[pl.ds(at, rows), :] == seg_row[...]
        outs = []
        for head in range(2):
            scores = dotf(q_rows, kh[head], NT)
            scores = jnp.where(same, scores, -1e30)
            top = jnp.max(scores, axis=-1, keepdims=True)
            expv = jnp.exp(scores - top)
            total = jnp.sum(expv, axis=-1, keepdims=True)
            low = (expv * (1.0 / total)).astype(BF)
            outs.append(dotf(low, v[...], NN))
            level = top + jnp.log(total)
            flat = jnp.transpose(jnp.broadcast_to(level, (rows, 128)))
            lse[0, pl.ds(head, 1), pl.ds(at, rows)] = flat[0:1, :]
        o[pl.ds(at, rows), :] = jnp.where(first[:rows], outs[0], outs[1]).astype(BF)
        return carry

    lax.fori_loop(0, length // rows, block, 0)


def attn_fwd(xh, w_qk, w_vo, tables, seg_col, seg_row):
    length, width = xh.shape
    pairs = w_qk.shape[1] // 256
    whole = lambda a: pl.BlockSpec(a.shape, lambda h: (0,) * a.ndim)
    col = lambda off: pl.BlockSpec((width, 128), lambda h: (0, h + off))
    out = pl.BlockSpec((length, 128), lambda h: (0, h))
    shape = jax.ShapeDtypeStruct((length, pairs * 128), BF)
    flops = 2 * length * width * pairs * 384 + 4 * pairs * 2 * length * length * 128
    return pl.pallas_call(
        attn_fwd_kernel,
        grid=(pairs,),
        in_specs=[whole(xh), col(0), col(pairs), col(0)]
        + [whole(t) for t in tables]
        + [whole(seg_col), whole(seg_row)],
        out_specs=[out] * 4 + [pl.BlockSpec((1, 2, length), lambda h: (h, 0, 0))],
        out_shape=[shape] * 4 + [jax.ShapeDtypeStruct((pairs, 2, length), F32)],
        scratch_shapes=[pltpu.VMEM((2, length, 128), BF)],
        cost_estimate=pl.CostEstimate(
            flops=flops, bytes_accessed=length * width * 8, transcendentals=pairs * 2 * length * length
        ),
        name="attn_fwd",
    )(xh, w_qk, w_qk, w_vo, *tables, seg_col, seg_row)


def attn_bwd_kernel(
    q, k, v, o, do, lse, cos, upper, lower, seg_col, seg_row, pg, kh, dk, dv
):
    length = q.shape[0]
    rows = min(256, length)
    lane = lax.broadcasted_iota(jnp.int32, (length, 128), 1)
    first = lane < HD
    kf = k[...]
    none = jnp.zeros_like(kf)
    kh[0] = jnp.where(first, kf, none)
    kh[1] = jnp.where(first, none, kf)
    dk[...] = jnp.zeros_like(dk)
    dv[...] = jnp.zeros_like(dv)

    def block(i, carry):
        at = pl.multiple_of(i * rows, rows)
        here = pl.ds(at, rows)
        q_rows = q[here, :]
        g_rows = do[here, :]
        seg_here = seg_row[:, here]
        same = seg_col[...] == seg_here
        prod = g_rows.astype(F32) * o[here, :].astype(F32)
        f = first[:rows]
        blank = jnp.zeros_like(q_rows)
        dq = jnp.zeros((rows, 128), F32)
        for head in range(2):
            mine = f if head == 0 else jnp.logical_not(f)
            q_head = jnp.where(mine, q_rows, blank)
            g_head = jnp.where(mine, g_rows, blank)
            delta = lax.dot_general(
                jnp.ones((8, 128), F32),
                jnp.where(mine, prod, 0.0),
                (NT, ((), ())),
                precision=lax.Precision.HIGHEST,
                preferred_element_type=F32,
            )[0:1, :]
            scores = dotf(k[...], q_head, NT)
            level = lse[0, pl.ds(head, 1), here]
            probs = jnp.where(same, jnp.exp(scores - level), 0.0)
            dv[...] += dotf(probs.astype(BF), g_head, NN)
            dp = dotf(v[...], g_head, NT)
            ds = (probs * (dp - delta)).astype(BF)
            dk[...] += dotf(ds, q_head, NN)
            dq = dq + dotf(ds, kh[head], TN)
        dq = dq * (1.0 / math.sqrt(HD))
        c, a, b = cos[here, :], upper[here, :], lower[here, :]
        pg[0, here, :] = (dq * c - turn(dq, a, b)).astype(BF)
        return carry

    lax.fori_loop(0, length // rows, block, 0)
    dkf = dk[...]
    pg[1] = (dkf * cos[...] - turn(dkf, upper[...], lower[...])).astype(BF)
    pg[2] = dv[...].astype(BF)


def attn_bwd(q, k, v, o, do, lse, tables, seg_col, seg_row):
    length, width = q.shape
    pairs = width // 128
    whole = lambda a: pl.BlockSpec(a.shape, lambda h: (0,) * a.ndim)
    col = pl.BlockSpec((length, 128), lambda h: (0, h))
    return pl.pallas_call(
        attn_bwd_kernel,
        grid=(pairs,),
        in_specs=[col] * 5
        + [pl.BlockSpec((1, 2, length), lambda h: (h, 0, 0))]
        + [whole(t) for t in tables]
        + [whole(seg_col), whole(seg_row)],
        out_specs=pl.BlockSpec((3, length, 128), lambda h: (0, 0, h)),
        out_shape=jax.ShapeDtypeStruct((3, length, width), BF),
        scratch_shapes=[
            pltpu.VMEM((2, length, 128), BF),
            pltpu.VMEM((length, 128), F32),
            pltpu.VMEM((length, 128), F32),
        ],
        cost_estimate=pl.CostEstimate(
            flops=10 * pairs * 2 * length * length * 128,
            bytes_accessed=length * width * 20,
            transcendentals=pairs * 2 * length * length,
        ),
        name="attn_bwd",
    )(q, k, v, o, do, lse, *tables, seg_col, seg_row)


def in_chunks(total, size, body):
    def step(j, carry):
        body(pl.ds(pl.multiple_of(j * size, size), size))
        return carry

    lax.fori_loop(0, total // size, step, 0)
    if total % size:
        body(pl.ds(total - total % size, total % size))


SHARD = (4, 2, 2)


def place():
    dp = lax.axis_index("dp")
    return dp // 4, (dp // 2) % 2, dp % 2, lax.axis_index("tensor")


def partners():
    z, x, c, y = place()
    at = lambda z, x, c, y: ((z * 2 + x) * 2 + c, y)
    return {
        "z1": at(z + 1 - 2 * (z % 2), x, c, y),
        "z2": at(z + 2 - 4 * (z // 2), x, c, y),
        "z3": at(3 - z, x, c, y),
        "x": at(z, 1 - x, c, y),
        "y": at(z, x, c, 1 - y),
        "c": at(z, x, 1 - c, y),
    }


def meet(peers, other=None):
    barrier = pltpu.get_barrier_semaphore()
    greet = lambda peer: pl.semaphore_signal(
        barrier, inc=1, device_id=peer, device_id_type=pl.DeviceIdType.MESH
    )
    for peer in peers.values():
        greet(peer)
    if other is None:
        pl.semaphore_wait(barrier, len(peers))
    else:
        moved, peer = other

        @pl.when(moved)
        def _():
            greet(peer)

        pl.semaphore_wait(barrier, len(peers) + jnp.where(moved, 1, 0))


def exchanged():
    z, x, c, y = place()
    return c != y, ((z * 2 + x) * 2 + y, c)


def remote(src, dst, send_sem, recv_sem, peer):
    return pltpu.make_async_remote_copy(
        src_ref=src,
        dst_ref=dst,
        send_sem=send_sem,
        recv_sem=recv_sem,
        device_id=peer,
        device_id_type=pl.DeviceIdType.MESH,
    )


class Move:
    def __init__(self, src, dst, sems, i):
        send_sem, recv_sem, near_sem = sems
        self.moved, peer = exchanged()
        self.far = remote(src, dst, send_sem.at[i], recv_sem.at[i], peer)
        self.near = pltpu.make_async_copy(src, dst, near_sem.at[i])

    def start(self):
        @pl.when(self.moved)
        def _():
            self.far.start()

        @pl.when(jnp.logical_not(self.moved))
        def _():
            self.near.start()

    def wait(self):
        @pl.when(self.moved)
        def _():
            self.far.wait()

        @pl.when(jnp.logical_not(self.moved))
        def _():
            self.near.wait()


def move_sems(n):
    return [pltpu.SemaphoreType.DMA((n,))] * 3


def to_place(values):
    z, x, _, y = place()
    tiles = [values[:, j * 128 : (j + 1) * 128] for j in range(8)]
    tiles = [jnp.where(y == 1, pltpu.roll(t, 64, 1), t) for t in tiles]
    for bit, step in ((x, 1), (z % 2, 2), (z // 2, 4)):
        tiles = [jnp.where(bit == 1, tiles[j ^ step], tiles[j]) for j in range(8)]
    return jnp.concatenate(tiles, axis=1)


AXIS = {"z": 4, "x": 2, "y": 2}


def partner(peers, axis, step):
    return peers["z%d" % step if axis == "z" else axis]


class Gather:
    MESSAGES = 15

    def __init__(self, own, buf, rows, cols, order, hops, peers, sems, base):
        self.buf, self.order, self.hops, self.peers = buf, order, hops, peers
        self.part = (rows, cols)
        self.own = own.at[self.part]
        self.send_sem, self.recv_sem = sems
        self.base = base
        n, m, p = (AXIS[axis] for axis in order)
        self.outer, self.middle = range(n), range(1, m)
        self.stages = [
            [(i, 0, 0) for i in range(1, n)],
            [(i, j, 0) for i in range(n) for j in range(1, m)],
            [(i, j, k) for i in range(n) for j in range(m) for k in range(1, p)],
        ]
        self.stages = self.stages[:hops]
        self.numbers = {at: n for n, at in enumerate(sum(self.stages, []))}

    def slot(self, at):
        where = dict(zip(self.order, at))
        return self.buf.at[(where["z"], where["x"], where["y"]) + self.part]

    def copy(self, at):
        hop = max(i for i in range(3) if at[i])
        source = at[:hop] + (0,) * (3 - hop)
        src = self.slot(source) if any(source) else self.own
        n = self.base + self.numbers[at]
        peer = partner(self.peers, self.order[hop], at[hop])
        return remote(src, self.slot(at), self.send_sem.at[n], self.recv_sem.at[n], peer)

    def send(self, stage, *prefix):
        for at in self.stages[stage]:
            if at[: len(prefix)] == prefix:
                self.copy(at).start()

    def start(self):
        self.send(0)

    def relay(self, i):
        if i:
            self.copy((i, 0, 0)).wait_recv()
        self.send(1, i)
        if self.hops == 3:
            self.send(2, i, 0)

    def relay_again(self, i):
        for j in self.middle:
            self.copy((i, j, 0)).wait_recv()
            self.send(2, i, j)

    def finish(self):
        for at in self.stages[-1]:
            self.copy(at).wait_recv()
        for at in self.numbers:
            self.copy(at).wait_send()


def forward_kernel(
    a_in, b_in, g_in, u_in, d_in, x_in, c_in, seg_in, inverse,
    q, k, v, o, lse, xh, w_qkv, w_out, resid, xn, x_half, cot, cos, upper, lower, seg_col, seg_row,
    w_gate, w_up, w_down,
    a_own, b_own, g_own, u_own, d_own, c_own, seg_own,
    kh, x_rel, part, sent, got, send_sem, recv_sem, pair_send, pair_recv, own_sem, *moving,
):
    length = xh.shape[0]
    half = length // 2
    width = xh.shape[1]
    pairs = q.shape[1] // 128
    rows = 256
    core = place()[2]
    peers = partners()
    sems = (send_sem, recv_sem)
    n = Gather.MESSAGES
    whole, low, high = pl.ds(0, 64), pl.ds(0, 32), pl.ds(32, 32)
    wide = w_qkv.shape[4] // 2
    all_ = lambda ref: pl.ds(0, ref.shape[-1])
    plan = (
        (a_own, w_qkv, whole, pl.ds(0, wide), "zyx", 3),
        (a_own, w_qkv, whole, pl.ds(wide, wide), "zyx", 3),
        (b_own, w_out, whole, all_(w_out), "zxy", 3),
        (g_own, w_gate, whole, all_(w_gate), "zyx", 3),
        (u_own, w_up, low, all_(w_up), "zyx", 3),
        (u_own, w_up, high, all_(w_up), "xyz", 3),
        (d_own, w_down, low, all_(w_down), "zyx", 2),
        (d_own, w_down, high, all_(w_down), "zxy", 2),
    )
    gathers = [Gather(*piece, peers, sems, i * n) for i, piece in enumerate(plan)]
    near, far, out, two, late, three = *gathers[:3], gathers[3:5], gathers[5], gathers[6:]
    owns = [
        pltpu.make_async_copy(src, dst.at[0, 0, 0], own_sem.at[i])
        for i, (src, dst) in enumerate(
            ((a_own, w_qkv), (b_own, w_out), (g_own, w_gate), (u_own, w_up), (d_own, w_down))
        )
    ]
    move_a, move_b, move_x, move_seg, move_g, move_u, move_d, move_c = (
        Move(src, dst, moving, i)
        for i, (src, dst) in enumerate(
            (
                (a_in, a_own),
                (b_in, b_own),
                (x_in, x_half),
                (seg_in, seg_own),
                (g_in, g_own),
                (u_in, u_own),
                (d_in, d_own),
                (c_in, c_own),
            )
        )
    )
    meet(peers, exchanged())
    for move in (move_a, move_seg, move_x):
        move.start()

    def tables(here):
        shape = (here.size, 128)
        row = here.start + lax.broadcasted_iota(jnp.int32, shape, 0) + core * half
        row = jnp.where(row >= length, row - length, row)
        angle = row.astype(F32) * inverse[0:1, :]
        front = lax.broadcasted_iota(jnp.int32, shape, 1) % HD < HD // 2
        sin = jnp.sin(angle)
        cos[here, :] = jnp.cos(angle)
        upper[here, :] = jnp.where(front, -sin, 0.0)
        lower[here, :] = jnp.where(front, 0.0, sin)

    move_a.wait()
    near.start()
    far.start()
    near.relay(0)
    owns[0].start()
    in_chunks(length, 64, tables)
    for z in (1, 2, 3):
        near.relay(z)
    for move in (move_b, move_g, move_u, move_d):
        move.start()
    move_seg.wait()
    ids = seg_own[...]
    ids = jnp.where(core == 0, ids, jnp.concatenate([ids[:, half:], ids[:, :half]], axis=1))
    seg_row[...] = ids
    seg_col[...] = jnp.transpose(jnp.broadcast_to(ids[0:1, :], (128, length)))
    move_x.wait()

    def first_norm(i, carry):
        here = pl.ds(pl.multiple_of(i * 128, 128), 128)
        values = to_place(x_half[here, :].astype(F32))
        x_rel[here, :] = values.astype(BF)
        xh[here, :] = normalize(values)[0].astype(BF)
        return carry

    lax.fori_loop(0, half // 128, first_norm, 0)
    swap_xh = remote(
        xh.at[pl.ds(0, half)], xh.at[pl.ds(half, half)], pair_send.at[0], pair_recv.at[0], peers["c"]
    )
    swap_xh.start()
    for z in range(4):
        near.relay_again(z)
        far.relay(z)
    move_b.wait()
    out.start()
    move_g.wait()
    move_u.wait()
    late.start()
    for gather in two:
        gather.start()
    out.relay(0)
    late.relay(0)
    for gather in two:
        gather.relay(0)
    move_d.wait()
    for gather in three:
        gather.start()
    for copy in owns[1:]:
        copy.start()
    swap_xh.wait()
    near.finish()
    owns[0].wait()

    events = {}
    at_step = lambda step, call, *args: events.setdefault(step, []).append((call, args))
    for z in range(4):
        at_step(z, far.relay_again, z)
        if z:
            at_step(z, out.relay, z)
        at_step(5 + z, out.relay_again, z)
        for gather in two:
            if z:
                at_step(1 + 2 * z, gather.relay, z)
            at_step(9 + z, gather.relay_again, z)
        for gather in three:
            at_step(11 + z, gather.relay, z)
    at_step(4, late.relay, 1)
    at_step(5, move_c.start)
    at_step(6, late.relay_again, 0)
    at_step(8, late.relay_again, 1)
    at_step(length // rows * pairs // 2 - 1, far.finish)
    first = lax.broadcasted_iota(jnp.int32, (length, 128), 1) < HD

    def pair(h, carry):
        lanes = pl.ds(pl.multiple_of(h * 128, 128), 128)
        weight = lambda i: w_qkv[
            :, :, :, :, pl.ds(pl.multiple_of((3 * h + i) * 128, 128), 128)
        ].reshape(width, 128)
        tokens = xh[...]
        qf = dotf(tokens, weight(0), NN)
        qf = qf * cos[...] + turn(qf, upper[...], lower[...])
        q[:, lanes] = (qf * (1.0 / math.sqrt(HD))).astype(BF)
        kf = dotf(tokens, weight(1), NN)
        kf = (kf * cos[...] + turn(kf, upper[...], lower[...])).astype(BF)
        k[:, lanes] = kf
        kh[0] = jnp.where(first, kf, jnp.zeros_like(kf))
        kh[1] = jnp.where(first, jnp.zeros_like(kf), kf)
        v[:, lanes] = dotf(tokens, weight(2), NN).astype(BF)

        def block(i, carry):
            for step, calls in events.items():

                @pl.when(h * (length // rows) + i == step)
                def _():
                    for call, args in calls:
                        call(*args)

            at = pl.multiple_of(i * rows, rows)
            q_rows = q[pl.ds(at, rows), lanes]
            same = seg_col[pl.ds(at, rows), 0:1] == seg_row[0:1, :]
            outs = []
            for head in range(2):
                scores = dotf(q_rows, kh[head], NT)
                scores = jnp.where(same, scores, -1e30)
                top = jnp.max(scores, axis=-1, keepdims=True)
                expv = jnp.exp(scores - top)
                total = jnp.sum(expv, axis=-1, keepdims=True)
                low_probs = (expv * (1.0 / total)).astype(BF)
                outs.append(dotf(low_probs, v[:, lanes], NN))
                level = top + jnp.log(total)
                flat = jnp.transpose(jnp.broadcast_to(level, (rows, 128)))
                lse[h, pl.ds(head, 1), pl.ds(at, rows)] = flat[0:1, :]
            o[pl.ds(at, rows), lanes] = jnp.where(first[:rows], outs[0], outs[1]).astype(BF)
            return carry

        return lax.fori_loop(0, length // rows, block, carry)

    lax.fori_loop(0, pairs, pair, 0)
    out.finish()
    owns[1].wait()
    w_o = w_out[...].reshape(width, pairs * 128)

    def project(i, carry):
        at = pl.multiple_of(half + i * rows, rows)
        sent[pl.ds(pl.multiple_of(i * rows, rows), rows), :] = dotf(
            o[pl.ds(at, rows), :], w_o, NT
        ).astype(BF)
        return carry

    lax.fori_loop(0, half // rows, project, 0)

    def project_own(i, carry):
        here = pl.ds(pl.multiple_of(i * rows, rows), rows)
        part[here, :] = dotf(o[here, :], w_o, NT)
        return carry

    give = remote(sent, got, pair_send.at[1], pair_recv.at[1], peers["c"])
    lax.fori_loop(0, half // rows, project_own, 0)
    give.start()
    move_c.wait()

    def turn_cot(here):
        cot[here, :] = to_place(c_own[here, :].astype(F32)).astype(BF)

    in_chunks(half, 128, turn_cot)
    swap_cot = remote(
        cot.at[pl.ds(0, half)], cot.at[pl.ds(half, half)], pair_send.at[3], pair_recv.at[3], peers["c"]
    )
    swap_cot.start()
    give.wait()

    def second_norm(i, carry):
        here = pl.ds(pl.multiple_of(i * 128, 128), 128)
        values = x_rel[here, :].astype(F32) + (part[here, :] + got[here, :].astype(F32))
        resid[here, :] = values
        xn[here, :] = normalize(values)[0].astype(BF)
        return carry

    lax.fori_loop(0, half // 128, second_norm, 0)
    swap_xn = remote(
        xn.at[pl.ds(0, half)], xn.at[pl.ds(half, half)], pair_send.at[2], pair_recv.at[2], peers["c"]
    )
    swap_xn.start()
    for gather in two + three + [late]:
        gather.finish()
    for copy in owns[2:]:
        copy.wait()
    swap_cot.wait()
    swap_xn.wait()


def forward_block(owned, x_half, cot_half, seg, inverse):
    half, width = x_half.shape
    length = 2 * half
    cols = owned[1].shape[1]
    pairs = cols // 128
    units = owned[2].shape[1]
    shard = width // 16
    vmem = pl.BlockSpec(memory_space=pltpu.VMEM)
    any_ = pl.BlockSpec(memory_space=pl.ANY)
    gathered = lambda n: jax.ShapeDtypeStruct(SHARD + (shard, n), BF)
    heads = jax.ShapeDtypeStruct((length, cols), BF)
    flat = jax.ShapeDtypeStruct((length, width), BF)
    table = jax.ShapeDtypeStruct((length, 128), F32)
    return pl.pallas_call(
        forward_kernel,
        in_specs=[any_] * 8 + [vmem],
        out_specs=[vmem] * 17 + [any_] * 3,
        out_shape=[heads] * 4
        + [
            jax.ShapeDtypeStruct((pairs, 2, length), F32),
            flat,
            gathered(3 * cols),
            gathered(cols),
            jax.ShapeDtypeStruct((half, width), F32),
            flat,
            jax.ShapeDtypeStruct((half, width), BF),
            flat,
        ]
        + [table] * 4
        + [jax.ShapeDtypeStruct((8, length), F32)]
        + [gathered(units)] * 3,
        scratch_shapes=[pltpu.VMEM((shard, 3 * cols), BF), pltpu.VMEM((shard, cols), BF)]
        + [pltpu.VMEM((shard, units), BF)] * 3
        + [
            pltpu.VMEM((half, width), BF),
            pltpu.VMEM((8, length), F32),
            pltpu.VMEM((2, length, 128), BF),
            pltpu.VMEM((half, width), BF),
            pltpu.VMEM((half, width), F32),
            pltpu.VMEM((half, width), BF),
            pltpu.VMEM((half, width), BF),
            pltpu.SemaphoreType.DMA((8 * Gather.MESSAGES,)),
            pltpu.SemaphoreType.DMA((8 * Gather.MESSAGES,)),
            pltpu.SemaphoreType.DMA((4,)),
            pltpu.SemaphoreType.DMA((4,)),
            pltpu.SemaphoreType.DMA((5,)),
        ]
        + move_sems(8),
        compiler_params=pltpu.CompilerParams(
            collective_id=0, has_side_effects=True, vmem_limit_bytes=60 << 20
        ),
        name="forward_block",
    )(*owned, x_half, cot_half, seg, inverse)


class Reduce:
    MESSAGES = 12
    ORDER = (2, 3, 1, 0)

    def __init__(self, parts, near, rows, axes, peers, sems, base, bufs, out):
        self.parts, self.near, self.rows, self.axes, self.peers = parts, near, rows, axes, peers
        self.send_sem, self.recv_sem = sems
        self.base = base
        self.one, self.two, self.three, self.sum = bufs
        self.out = out

    def link(self, i, src, dst, peer):
        n = self.base + i
        return remote(src, dst, self.send_sem.at[n], self.recv_sem.at[n], peer)

    def first(self, z):
        if self.axes == "xy":
            src = self.parts.at[z, :, 1, self.rows]
        else:
            src = self.parts.at[z, 1, :, self.rows]
        return self.link(z, src, self.one.at[z], self.peers[self.axes[1]])

    def second(self, z):
        return self.link(4 + z, self.one.at[z, 1], self.two.at[z], self.peers[self.axes[0]])

    def third(self, z):
        return self.link(7 + z, self.two.at[z], self.three.at[z - 1], self.peers["z%d" % z])

    def start(self):
        for z in self.ORDER:
            self.first(z).start()

    def add_first(self, z):
        self.first(z).wait_recv()
        self.one[z] = (self.one[z].astype(F32) + self.near(z).astype(F32)).astype(BF)

    def relay_first(self, z):
        self.add_first(z)
        self.second(z).start()

    def resume(self):
        for z in self.ORDER:
            self.second(z).start()

    def relay_second(self, z):
        self.second(z).wait_recv()
        self.two[z] = (self.two[z].astype(F32) + self.one[z, 0].astype(F32)).astype(BF)
        if z:
            self.third(z).start()

    def last(self):
        moved, peer = exchanged()
        return moved, self.link(11, self.sum, self.out, peer)

    def total(self):
        total = self.two[0].astype(F32)
        for z in (1, 2, 3):
            self.third(z).wait_recv()
            total = total + self.three[z - 1].astype(F32)
        return total

    def finish(self):
        self.sum[...] = self.total().astype(BF)
        moved, copy = self.last()

        @pl.when(moved)
        def _():
            copy.start()

        @pl.when(jnp.logical_not(moved))
        def _():
            self.out[...] = self.sum[...]

    def sent(self):
        hops = (self.second,) if self.parts is None else (self.first, self.second)
        thirds = [self.third(z) for z in (1, 2, 3)]
        return [hop(z) for z in range(4) for hop in hops] + thirds

    def close(self):
        for copy in self.sent():
            copy.wait_send()
        moved, copy = self.last()

        @pl.when(moved)
        def _():
            copy.wait()


class ReduceAlongZ(Reduce):
    def first(self, z):
        src = self.parts.at[z, :, :, self.rows]
        return self.link(z - 1, src, self.one.at[z - 1], self.peers["z%d" % z])

    def second(self):
        return self.link(3, self.two.at[:, 1], self.three.at[0:2], self.peers["y"])

    def third(self):
        return self.link(4, self.three.at[1], self.three.at[2], self.peers["x"])

    def start(self):
        for z in (2, 3, 1):
            self.first(z).start()

    def relay_first(self):
        total = self.near().astype(F32)
        for z in (1, 2, 3):
            self.first(z).wait_recv()
            total = total + self.one[z - 1].astype(F32)
        self.two[...] = total.astype(BF)
        self.second().start()

    def relay_second(self):
        self.second().wait_recv()
        for x in (0, 1):
            self.three[x] = (self.three[x].astype(F32) + self.two[x, 0].astype(F32)).astype(BF)
        self.third().start()

    def total(self):
        self.third().wait_recv()
        return self.three[0].astype(F32) + self.three[2].astype(F32)

    def sent(self):
        return [self.first(z) for z in (1, 2, 3)] + [self.second(), self.third()]


def mlp_kernel(
    down_in, xn, cot, w_gate, w_up, resid,
    result, resid_grad, attn_cot, d_gate, d_up, d_low, d_high,
    w_down, d_down, hidden, act, slope_up, gate_grad, up_grad, own, sent, got, placed,
    send_sem, recv_sem, last_send, last_recv, first_send, first_recv, own_sem, *moving,
):
    length, width = xn.shape
    half = length // 2
    units = w_gate.shape[1]
    peers = {axis: partners()[axis] for axis in "xyc"}
    move = Move(placed, result, moving, 0)
    low, high = pl.ds(0, 32), pl.ds(32, 32)
    most, few = pl.ds(0, 48), pl.ds(48, 16)
    at_low = lambda ref, z, x: ref.at[z, x, :, low]
    at_high = lambda ref, z, y: ref.at[z, :, y, high]
    last = []
    for z in range(4):
        for i, (part, axis) in enumerate(((at_low, "x"), (at_high, "y"))):
            n = 2 * z + i
            last.append(
                remote(
                    part(down_in, z, 0), part(w_down, z, 1), last_send.at[n], last_recv.at[n], peers[axis]
                )
            )
    every = pl.ds(0, 4)
    owns = [
        pltpu.make_async_copy(part(down_in, every, 0), part(w_down, every, 0), own_sem.at[i])
        for i, part in enumerate((at_low, at_high))
    ]
    sems = (first_send, first_recv)
    n = Reduce.MESSAGES
    reduce_low = Reduce(
        d_down, lambda z: d_down[z, 0, :, 0:48], most, "yx", peers, sems, 0, (d_low, None, None, None), None
    )
    reduce_high = Reduce(
        d_down, lambda z: d_down[z, :, 0, 48:64], few, "xy", peers, sems, n, (d_high, None, None, None), None
    )
    meet(peers, exchanged())
    for copy in last + owns:
        copy.start()
    back, front = pl.ds(half, half), pl.ds(0, half)

    def gate_and_up(rows):
        def step(cols):
            gate = dotf(xn[rows, :], w_gate[:, cols], NN)
            up = dotf(xn[rows, :], w_up[:, cols], NN)
            value, slope = gelu_parts(gate)
            hidden[rows, cols] = (value * up).astype(BF)
            act[rows, cols] = value
            slope_up[rows, cols] = up * slope

        in_chunks(units, 256, step)

    def units_back(rows):
        def step(cols):
            down = w_down[:, :, :, :, cols].reshape(width, cols.size)
            grad = dotf(cot[rows, :], down, NN).astype(BF).astype(F32)
            gate_grad[rows, cols] = (grad * slope_up[rows, cols]).astype(BF)
            up_grad[rows, cols] = (grad * act[rows, cols]).astype(BF)

        in_chunks(units, 256, step)

    def sums(rows, put):
        def step(z, carry):
            here = pl.ds(pl.multiple_of(z * 256, 256), 256)
            down = w_down[z].reshape(256, units)
            put[0, :, here] = dotf(hidden[rows, :], down, NT).astype(put.dtype)
            both = dotf(gate_grad[rows, :], w_gate[here, :], NT)
            both = both + dotf(up_grad[rows, :], w_up[here, :], NT)
            put[1, :, here] = both.astype(put.dtype)
            return carry

        lax.fori_loop(0, width // 256, step, 0)

    gate_and_up(back)
    gate_and_up(front)
    for z in Reduce.ORDER:
        left = jnp.transpose(cot[:, z * 256 : (z + 1) * 256])
        d_down[z] = dotf(left, hidden[...], NN).astype(BF).reshape(2, 2, 64, units)
        reduce_low.first(z).start()
        reduce_high.first(z).start()
    for copy in owns:
        copy.wait()
    for copy in last:
        copy.wait()
    units_back(back)
    sums(back, sent)
    give = remote(sent, got, send_sem.at[0], recv_sem.at[0], peers["c"])
    give.start()
    units_back(front)
    sums(front, own)
    give.wait()

    def finish(here):
        values = resid[here, :]
        mlp = own[0, here, :] + got[0, here, :].astype(F32)
        placed[here, :] = to_place(values + mlp).astype(BF)
        xhat, scale = normalize(values)
        back = normalize_back(own[1, here, :] + got[1, here, :].astype(F32), xhat, scale)
        grad = cot[here, :].astype(F32) + back
        resid_grad[here, :] = grad
        attn_cot[here, :] = grad.astype(BF)

    in_chunks(half, 64, finish)
    swap = remote(
        attn_cot.at[pl.ds(0, half)], attn_cot.at[pl.ds(half, half)], send_sem.at[1], recv_sem.at[1], peers["c"]
    )
    swap.start()
    move.start()

    def weights(here):
        left = jnp.transpose(xn[:, here])
        d_gate[here, :] = dotf(left, gate_grad[...], NN).astype(BF)
        d_up[here, :] = dotf(left, up_grad[...], NN).astype(BF)

    in_chunks(width, 256, weights)
    for z in Reduce.ORDER:
        reduce_low.add_first(z)
        reduce_high.add_first(z)
    for z in range(4):
        reduce_low.first(z).wait_send()
        reduce_high.first(z).wait_send()
    swap.wait()
    move.wait()


def mlp_block(down_in, xn, cot, w_gate, w_up, resid):
    length, width = xn.shape
    half = length // 2
    units = w_gate.shape[1]
    shard = width // 16
    vmem = pl.BlockSpec(memory_space=pltpu.VMEM)
    any_ = pl.BlockSpec(memory_space=pl.ANY)
    grads = jax.ShapeDtypeStruct((width, units), BF)
    dma = lambda n: pltpu.SemaphoreType.DMA((n,))
    return pl.pallas_call(
        mlp_kernel,
        in_specs=[any_] + [vmem] * 5,
        out_specs=[any_] + [vmem] * 6,
        out_shape=[
            jax.ShapeDtypeStruct((half, width), BF),
            jax.ShapeDtypeStruct((half, width), F32),
            jax.ShapeDtypeStruct((length, width), BF),
            grads,
            grads,
            jax.ShapeDtypeStruct((4, 2, shard * 3 // 4, units), BF),
            jax.ShapeDtypeStruct((4, 2, shard // 4, units), BF),
        ],
        scratch_shapes=[pltpu.VMEM(SHARD + (shard, units), BF)] * 2
        + [
            pltpu.VMEM((length, units), BF),
            pltpu.VMEM((length, units), F32),
            pltpu.VMEM((length, units), F32),
            pltpu.VMEM((length, units), BF),
            pltpu.VMEM((length, units), BF),
            pltpu.VMEM((2, half, width), F32),
            pltpu.VMEM((2, half, width), BF),
            pltpu.VMEM((2, half, width), BF),
            pltpu.VMEM((half, width), BF),
        ]
        + [dma(2), dma(2), dma(8), dma(8), dma(2 * Reduce.MESSAGES), dma(2 * Reduce.MESSAGES), dma(2)]
        + move_sems(1),
        compiler_params=pltpu.CompilerParams(
            collective_id=1, has_side_effects=True, vmem_limit_bytes=63 << 20
        ),
        name="mlp_block",
    )(down_in, xn, cot, w_gate, w_up, resid)


def backward_kernel(
    d_gate, d_up, d_low, d_high, q, k, v, o, lse, attn_cot, w_qkv, w_out, xh, x_half, resid_grad,
    cos, upper, lower, seg_col, seg_row,
    token_grad, s_gate, s_up_low, s_up_high, s_down_low, s_down_high, s_out, s_near, s_far,
    d_out, d_near, d_far, pg, heads_grad, kh, dk, dv, own, sent, got, placed,
    near_gate, near_up_low, near_up_high,
    *rest,
):
    bufs = [rest[4 * i : 4 * i + 4] for i in range(3)]
    bufs += [(first,) + rest[12 + 3 * i : 15 + 3 * i] for i, first in enumerate((d_low, d_high))]
    bufs += [rest[18 + 4 * i : 22 + 4 * i] for i in range(3)]
    send_sem, recv_sem, pair_send, pair_recv, near_sem, *moving = rest[30:]
    length, width = xh.shape
    half = length // 2
    cols = q.shape[1]
    pairs = cols // 128
    rows = 256
    peers = partners()
    sems = (send_sem, recv_sem)
    n = Reduce.MESSAGES
    whole, low, high = pl.ds(0, 64), pl.ds(0, 32), pl.ds(32, 32)
    held = lambda ref: (lambda z: ref[z])
    plan = (
        (Reduce, d_gate, held(near_gate), whole, "yx", s_gate),
        (Reduce, d_up, held(near_up_low), low, "yx", s_up_low),
        (ReduceAlongZ, d_up, lambda: near_up_high[...], high, None, s_up_high),
        (Reduce, None, None, None, "yx", s_down_low),
        (Reduce, None, None, None, "xy", s_down_high),
        (Reduce, d_out, lambda z: d_out[z, 0], whole, "yx", s_out),
        (Reduce, d_near, lambda z: d_near[z, 0], whole, "yx", s_near),
        (Reduce, d_far, lambda z: d_far[z, :, 0], whole, "xy", s_far),
    )
    parts = [
        kind(src, near, rows_, axes, peers, sems, i * n, bufs[i], out)
        for i, (kind, src, near, rows_, axes, out) in enumerate(plan)
    ]
    gate, up_low, up_high, down_low, down_high, out, near, far = parts
    nears = [
        pltpu.make_async_copy(src, dst, near_sem.at[i])
        for i, (src, dst) in enumerate(
            (
                (d_gate.at[:, 0], near_gate),
                (d_up.at[:, 0, :, low], near_up_low),
                (d_up.at[0, :, :, high], near_up_high),
            )
        )
    ]
    for copy in nears:
        copy.start()
    meet(peers, exchanged())
    up_high.start()
    down_low.resume()
    down_high.resume()
    gate.start()

    def heads(here):
        heads_grad[here, :] = dotf(attn_cot[here, :], w_out[...], NN).astype(BF)

    in_chunks(length, 256, heads)

    def out_weights(z, carry):
        here = pl.ds(pl.multiple_of(z * 256, 256), 256)
        value = dotf(jnp.transpose(attn_cot[:, here]), o[...], NN).astype(BF)
        d_out[z] = value.reshape(2, 2, 64, cols)
        return carry

    lax.fori_loop(0, width // 256, out_weights, 0)
    out.start()
    up_low.start()
    for copy in nears:
        copy.wait()
    for z in Reduce.ORDER:
        down_low.relay_second(z)
        down_high.relay_second(z)

    events = {}
    for i, z in enumerate(Reduce.ORDER):
        events.setdefault((1, 4, 7, 11)[i], []).append(lambda z=z: gate.relay_first(z))
        events.setdefault((3, 6, 9, 13)[i], []).append(lambda z=z: gate.relay_second(z))
        events.setdefault(12 + i, []).append(lambda z=z: out.relay_first(z))
    events.setdefault(6, []).append(up_high.relay_first)
    events.setdefault(9, []).append(up_high.relay_second)

    def weights(ref, at):
        def step(z, carry):
            left = jnp.transpose(xh[:, pl.ds(pl.multiple_of(z * 256, 256), 256)])
            value = dotf(left, pg[:, at : at + ref.shape[-1]], NN).astype(BF)
            ref[z] = value.reshape(2, 2, 64, ref.shape[-1])
            return carry

        lax.fori_loop(0, width // 256, step, 0)

    lane = lax.broadcasted_iota(jnp.int32, (length, 128), 1)
    first = lane < HD

    def pair(h, carry):
        lanes = pl.ds(pl.multiple_of(h * 128, 128), 128)
        third = lambda i: pl.ds(pl.multiple_of((3 * h + i) * 128, 128), 128)
        kf = k[:, lanes]
        none = jnp.zeros_like(kf)
        kh[0] = jnp.where(first, kf, none)
        kh[1] = jnp.where(first, none, kf)
        dk[...] = jnp.zeros_like(dk)
        dv[...] = jnp.zeros_like(dv)

        def block(i, carry):
            for step, calls in events.items():

                @pl.when(h * (length // rows) + i == step)
                def _():
                    for call in calls:
                        call()

            at = pl.multiple_of(i * rows, rows)
            here = pl.ds(at, rows)
            q_rows = q[here, lanes]
            g_rows = heads_grad[here, lanes]
            same = seg_col[:, 0:1] == seg_row[0:1, here]
            prod = g_rows.astype(F32) * o[here, lanes].astype(F32)
            f = first[:rows]
            blank = jnp.zeros_like(q_rows)
            dq = jnp.zeros((rows, 128), F32)
            for head in range(2):
                mine = f if head == 0 else jnp.logical_not(f)
                q_head = jnp.where(mine, q_rows, blank)
                g_head = jnp.where(mine, g_rows, blank)
                delta = lax.dot_general(
                    jnp.ones((8, 128), F32),
                    jnp.where(mine, prod, 0.0),
                    (NT, ((), ())),
                    precision=lax.Precision.HIGHEST,
                    preferred_element_type=F32,
                )[0:1, :]
                scores = dotf(k[:, lanes], q_head, NT)
                level = lse[h, pl.ds(head, 1), here]
                probs = jnp.where(same, jnp.exp(scores - level), 0.0)
                dv[...] += dotf(probs.astype(BF), g_head, NN)
                dp = dotf(v[:, lanes], g_head, NT)
                ds = (probs * (dp - delta)).astype(BF)
                dk[...] += dotf(ds, q_head, NN)
                dq = dq + dotf(ds, kh[head], TN)
            dq = dq * (1.0 / math.sqrt(HD))
            c, a, b = cos[here, :], upper[here, :], lower[here, :]
            pg[here, third(0)] = (dq * c - turn(dq, a, b)).astype(BF)
            return carry

        lax.fori_loop(0, length // rows, block, 0)
        dkf = dk[...]
        pg[:, third(1)] = (dkf * cos[...] - turn(dkf, upper[...], lower[...])).astype(BF)
        pg[:, third(2)] = dv[...].astype(BF)

        @pl.when(h == pairs // 2 - 1)
        def _():
            weights(d_near, 0)
            near.start()

        return carry

    lax.fori_loop(0, pairs, pair, 0)
    weights(d_far, d_near.shape[-1])
    far.start()

    def back(tokens, put):
        def step(here):
            put[:, here] = dotf(pg[tokens, :], w_qkv[here, :], NT).astype(put.dtype)

        in_chunks(width, 256, step)

    back(pl.ds(half, half), sent)
    give = remote(sent, got, pair_send.at[0], pair_recv.at[0], peers["c"])
    give.start()
    back(pl.ds(0, half), own)
    for z in Reduce.ORDER:
        up_low.relay_first(z)
    give.wait()

    def finish(here):
        xhat, scale = normalize(to_place(x_half[here, :].astype(F32)))
        f = own[here, :] + got[here, :].astype(F32)
        value = resid_grad[here, :] + normalize_back(f, xhat, scale)
        placed[here, :] = to_place(value).astype(BF)

    in_chunks(half, 64, finish)
    move = Move(placed, token_grad, moving, 0)
    move.start()
    for z in Reduce.ORDER:
        out.relay_second(z)
        near.relay_first(z)
        far.relay_first(z)
    for part in (down_low, down_high, gate, up_high):
        part.finish()
    for z in Reduce.ORDER:
        up_low.relay_second(z)
    out.finish()
    for z in Reduce.ORDER:
        far.relay_second(z)
        near.relay_second(z)
    up_low.finish()
    far.finish()
    near.finish()
    for part in parts:
        part.close()
    move.wait()


def backward_block(grads, heads, lse, attn_cot, w_qkv, w_out, xh, x_half, resid_grad, tables, seg_col, seg_row):
    length, width = xh.shape
    half = length // 2
    cols = heads[0].shape[1]
    units = grads[0].shape[1]
    shard = width // 16
    vmem = pl.BlockSpec(memory_space=pltpu.VMEM)
    any_ = pl.BlockSpec(memory_space=pl.ANY)
    wide = 3 * cols // 2
    sizes = [(shard, units), (shard // 2, units), (shard // 2, units)]
    sizes += [g.shape[2:] for g in grads[2:]]
    sizes += [(shard, cols), (shard, wide), (shard, wide)]
    along_z, begun = (2,), (3, 4)
    bufs = []
    for i, size in enumerate(sizes):
        if i in along_z:
            lead = (3, 2, 2), (2, 2), (3,)
        else:
            lead = (4, 2), (4,), (3,)
        bufs += [pltpu.VMEM(n + size, BF) for n in lead[i in begun :] + ((),)]
    nears = [pltpu.VMEM(((2, 2) if i in along_z else (4, 2)) + size, BF) for i, size in enumerate(sizes[:3])]
    messages = 8 * Reduce.MESSAGES
    return pl.pallas_call(
        backward_kernel,
        in_specs=[any_] * 2 + [vmem] * 18,
        out_specs=[vmem] * 9,
        out_shape=[jax.ShapeDtypeStruct((half, width), BF)]
        + [jax.ShapeDtypeStruct(size, BF) for size in sizes],
        scratch_shapes=[pltpu.VMEM(SHARD + (shard, n), BF) for n in (cols, wide, wide)]
        + [
            pltpu.VMEM((length, 3 * cols), BF),
            pltpu.VMEM((length, cols), BF),
            pltpu.VMEM((2, length, 128), BF),
            pltpu.VMEM((length, 128), F32),
            pltpu.VMEM((length, 128), F32),
            pltpu.VMEM((half, width), F32),
            pltpu.VMEM((half, width), BF),
            pltpu.VMEM((half, width), BF),
            pltpu.VMEM((half, width), BF),
        ]
        + nears
        + bufs
        + [
            pltpu.SemaphoreType.DMA((messages,)),
            pltpu.SemaphoreType.DMA((messages,)),
            pltpu.SemaphoreType.DMA((1,)),
            pltpu.SemaphoreType.DMA((1,)),
            pltpu.SemaphoreType.DMA((3,)),
        ]
        + move_sems(1),
        compiler_params=pltpu.CompilerParams(
            collective_id=2, has_side_effects=True, vmem_limit_bytes=60 << 20
        ),
        name="backward_block",
    )(
        *(g.reshape(SHARD + (shard, units)) for g in grads[:2]), *grads[2:],
        *heads, lse, attn_cot, w_qkv, w_out, xh, x_half, resid_grad, *tables, seg_col, seg_row,
    )


class Chips:
    def sum_tensor(self, value):
        pairs = [(2 * i + y, 2 * i + 1 - y) for i in range(16) for y in range(2)]
        return value + lax.ppermute(value, ("dp", "tensor"), pairs)


class Axes:
    def gather_rows(self, value):
        return lax.all_gather(value, "tensor", axis=0, tiled=True)

    def scatter_rows(self, value):
        return lax.psum_scatter(value.astype(BF), "tensor", scatter_dimension=0, tiled=True).astype(F32)

    def reduce(self, a, b):
        return tuple(
            lax.psum_scatter(w.astype(BF), "dp", scatter_dimension=0, tiled=True).astype(F32)
            for w in (a, b)
        )

    def sum_tensor(self, value):
        return lax.psum(value, "tensor")


def normalize(values):
    centred = values - jnp.mean(values, axis=-1, keepdims=True)
    scale = lax.rsqrt(jnp.mean(centred * centred, axis=-1, keepdims=True) + EPS)
    return centred * scale, scale


def normalize_back(f, xhat, scale):
    return scale * (
        f
        - jnp.mean(f, axis=-1, keepdims=True)
        - xhat * jnp.mean(f * xhat, axis=-1, keepdims=True)
    )


def gelu_parts(gate):
    half_erf = 0.5 * (1.0 + lax.erf(gate * (1.0 / math.sqrt(2.0))))
    density = jnp.exp(-0.5 * gate * gate) * (1.0 / math.sqrt(2.0 * math.pi))
    return gate * half_erf, half_erf + gate * density


def make_local(comm_type):
    def local(tokens, segments, w_qkv, w_out, w_in, w_down, g_attn, g_mlp, cotangent):
        comm = comm_type()
        paired = comm_type is Chips
        shard = w_qkv.shape[0]
        cols = w_qkv.shape[2]
        units = w_in.shape[2]
        low = 128 * (units // 256)
        pad = 128 * pl.cdiv(units, 128) - units
        gain_one = g_attn.astype(F32)[:, None]
        gain_two = g_mlp.astype(F32)[:, None]
        scaled = lambda w, g: (w.astype(F32) * g).astype(BF)
        padded = lambda w: jnp.pad(w, ((0, 0), (0, pad)))
        down_rows = w_down.T
        a_one = jnp.concatenate([scaled(w_qkv[:, 0], gain_one), scaled(w_qkv[:, 1], gain_one)], axis=1)
        b_one = jnp.concatenate([scaled(w_qkv[:, 2], gain_one), w_out.T], axis=1)
        own_gate, own_up = scaled(w_in[:, 0], gain_two), scaled(w_in[:, 1], gain_two)

        owned = (a_one, b_one, own_gate, own_up, down_rows)
        if paired:
            by_pair = scaled(w_qkv, gain_one[:, None]).reshape(shard, 3, cols // 128, 128).swapaxes(1, 2)
            owned = (by_pair.reshape(shard, 3 * cols), w_out.T) + tuple(padded(w) for w in owned[2:])
            seg = jnp.broadcast_to(segments.astype(F32), (8, segments.shape[1]))
            inverse = jnp.broadcast_to(jnp.tile(rope_rates(), 4), (8, 128))
            (
                q, k, v, o, lse, xh, qkv_all, out_all, resid, xn, x_half, cot_all, *tables, seg_col, seg_row,
                w_gate, w_up, w_dn,
            ) = forward_block(owned, tokens[0], cotangent[0], seg, inverse)
            qkv_all, out_all, w_gate, w_up = (
                w.reshape(-1, w.shape[-1]) for w in (qkv_all, out_all, w_gate, w_up)
            )
        else:
            w_qk, w_vo, w_gate, w_up, w_dn = (
                lax.all_gather(w, "dp", axis=0, tiled=True) for w in owned
            )
            w_o = w_vo[:, cols:]
            seg_col, seg_row = segments[0][:, None], segments
            cot = cotangent[0]
            cot_all = comm.gather_rows(cot)
            tables = rope_tables(jnp.arange(segments.shape[1]))
            x_in = tokens[0].astype(F32)
            xh_one, scale_one = normalize(x_in)
            xh = comm.gather_rows(xh_one.astype(BF))
            o, q, k, v, lse = attn_fwd(xh, w_qk, w_vo, tables, seg_col, seg_row)
            resid = x_in + comm.scatter_rows(dotf(o, w_o, NT))
            xh_two, scale_two = normalize(resid)
            xn = comm.gather_rows(xh_two.astype(BF))
        if paired:
            result, resid_grad, attn_cot, *grads = mlp_block(w_dn, xn, cot_all, w_gate, w_up, resid)
        else:
            gate, up = dotf(xn, w_gate, NN), dotf(xn, w_up, NN)
            act, slope = gelu_parts(gate)
            hidden = (act * up).astype(BF)
            mlp = comm.scatter_rows(dotf(hidden, w_dn, NT))
            result = (resid + mlp).astype(BF)
            hidden_grad = dotf(cot_all, w_dn, NN).astype(BF).astype(F32)
            gate_grad = (hidden_grad * up * slope).astype(BF)
            up_grad = (hidden_grad * act).astype(BF)
            f_two = comm.scatter_rows(dotf(gate_grad, w_gate, NT) + dotf(up_grad, w_up, NT))
            resid_grad = cot.astype(F32) + normalize_back(f_two, xh_two, scale_two)
            attn_cot = comm.gather_rows(resid_grad.astype(BF))
            d_down = dotf(cot_all, hidden, TN)
            d_gate, d_up = dotf(xn, gate_grad, TN), dotf(xn, up_grad, TN)

        if paired:
            token_grad, *sums = backward_block(
                grads, (q, k, v, o), lse, attn_cot, qkv_all, out_all, xh, x_half,
                resid_grad, tables, seg_col, seg_row,
            )
            token_grad = token_grad.astype(F32)
            s_gate, up_low, up_high, s_low, s_high, s_out, near, far = (w.astype(F32) for w in sums)
            s_up = jnp.concatenate([up_low, up_high], axis=0)
            qkv_raw = jnp.concatenate([near, far], axis=1).reshape(shard, cols // 128, 3, 128)
            qkv_raw = qkv_raw.swapaxes(1, 2).reshape(shard, 3, cols)
            in_raw = jnp.stack([s_gate[:, :units], s_up[:, :units]], axis=1)
            down_sum = jnp.concatenate([s_low[:, :units], s_high[:, :units]], axis=0).T
        else:
            wide = lambda g, d: jnp.concatenate([padded(g), d], axis=1)
            two_a, two_b = comm.reduce(wide(d_gate, d_down[:, :low]), wide(d_up, d_down[:, low:]))

            heads_grad = dotf(attn_cot, w_o, NN).astype(BF)
            pg = attn_bwd(q, k, v, o, heads_grad, lse, tables, seg_col, seg_row)
            d_out = dotf(attn_cot, o, TN)
            d_q, d_k, d_v = (dotf(xh, pg[i], TN) for i in range(3))
            one_a, one_b = comm.reduce(
                jnp.concatenate([d_q, d_k], axis=1), jnp.concatenate([d_v, d_out], axis=1)
            )
            f_one = comm.scatter_rows(
                dotf(pg[0], w_qk[:, :cols], NT)
                + dotf(pg[1], w_qk[:, cols:], NT)
                + dotf(pg[2], w_vo[:, :cols], NT)
            )
            token_grad = resid_grad + normalize_back(f_one, xh_one, scale_one)
            in_raw = jnp.stack([two_a[:, :units], two_b[:, :units]], axis=1)
            down_sum = jnp.concatenate([two_a[:, units + pad :], two_b[:, units + pad :]], axis=1).T
            s_out = one_b[:, cols:]
            qkv_raw = jnp.stack([one_a[:, :cols], one_a[:, cols:], one_b[:, :cols]], axis=1)

        gains = jnp.stack(
            [
                jnp.sum(qkv_raw * w_qkv.astype(F32), axis=(1, 2)),
                jnp.sum(in_raw * w_in.astype(F32), axis=(1, 2)),
            ]
        )
        gains = comm.sum_tensor(gains)
        return (
            result[None],
            token_grad[None],
            gains[0],
            gains[1],
            qkv_raw * gain_one[:, :, None],
            s_out.T,
            in_raw * gain_two[:, :, None],
            down_sum,
        )

    return local


def solution(mesh):
    paired = mesh.shape["dp"] == 16 and mesh.shape["tensor"] == 2
    return jax.shard_map(
        make_local(Chips if paired else Axes),
        mesh=mesh,
        in_specs=(
            P("dp", "tensor", None),
            P("dp", None),
            P("dp", None, "tensor"),
            P("tensor", "dp"),
            P("dp", None, "tensor"),
            P("tensor", "dp"),
            P("dp"),
            P("dp"),
            P("dp", "tensor", None),
        ),
        out_specs=(
            P("dp", "tensor", None),
            P("dp", "tensor", None),
            P("dp"),
            P("dp"),
            P("dp", None, "tensor"),
            P("tensor", "dp"),
            P("dp", None, "tensor"),
            P("tensor", "dp"),
        ),
        check_vma=False,
    )
```

```python
import math

import jax
import jax.numpy as jnp
from jax import lax
from jax.experimental import pallas as pl
from jax.experimental.pallas import tpu as pltpu
from jax.sharding import PartitionSpec as P

HD = 64
EPS = 1e-05
ROTARY_BASE = 160000.0
BF = jnp.bfloat16
F32 = jnp.float32


def dotf(a, b, dims):
    return lax.dot_general(a, b, (dims, ((), ())), preferred_element_type=F32)


NN = ((1,), (0,))
NT = ((1,), (1,))
TN = ((0,), (0,))


def rope_rates():
    return 1.0 / ROTARY_BASE ** (jnp.arange(HD // 2).astype(F32) * (2.0 / HD))


def rope_tables(positions):
    angles = positions.astype(F32)[:, None] * rope_rates()[None, :]
    cos, sin = jnp.cos(angles), jnp.sin(angles)
    zero = jnp.zeros_like(sin)
    cosine = jnp.concatenate([cos] * 4, axis=-1)
    upper = jnp.concatenate([-sin, zero] * 2, axis=-1)
    lower = jnp.concatenate([zero, sin] * 2, axis=-1)
    return cosine, upper, lower


def turn(u, upper, lower):
    return pltpu.roll(u, 128 - HD // 2, 1) * upper + pltpu.roll(u, HD // 2, 1) * lower


def attn_fwd_kernel(xh, wq, wk, wv, cos, upper, lower, seg_col, seg_row, o, q, k, v, lse, kh):
    length = xh.shape[0]
    rows = min(256, length)
    lane = lax.broadcasted_iota(jnp.int32, (length, 128), 1)
    first = lane < HD
    tokens = xh[...]
    qf = dotf(tokens, wq[...], NN)
    qf = qf * cos[...] + turn(qf, upper[...], lower[...])
    q[...] = (qf * (1.0 / math.sqrt(HD))).astype(BF)
    kf = dotf(tokens, wk[...], NN)
    kf = (kf * cos[...] + turn(kf, upper[...], lower[...])).astype(BF)
    k[...] = kf
    kh[0] = jnp.where(first, kf, jnp.zeros_like(kf))
    kh[1] = jnp.where(first, jnp.zeros_like(kf), kf)
    v[...] = dotf(tokens, wv[...], NN).astype(BF)

    def block(i, carry):
        at = pl.multiple_of(i * rows, rows)
        q_rows = q[pl.ds(at, rows), :]
        same = seg_col[pl.ds(at, rows), :] == seg_row[...]
        outs = []
        for head in range(2):
            scores = dotf(q_rows, kh[head], NT)
            scores = jnp.where(same, scores, -1e30)
            top = jnp.max(scores, axis=-1, keepdims=True)
            expv = jnp.exp(scores - top)
            total = jnp.sum(expv, axis=-1, keepdims=True)
            low = (expv * (1.0 / total)).astype(BF)
            outs.append(dotf(low, v[...], NN))
            level = top + jnp.log(total)
            flat = jnp.transpose(jnp.broadcast_to(level, (rows, 128)))
            lse[0, pl.ds(head, 1), pl.ds(at, rows)] = flat[0:1, :]
        o[pl.ds(at, rows), :] = jnp.where(first[:rows], outs[0], outs[1]).astype(BF)
        return carry

    lax.fori_loop(0, length // rows, block, 0)


def attn_fwd(xh, w_qk, w_vo, tables, seg_col, seg_row):
    length, width = xh.shape
    pairs = w_qk.shape[1] // 256
    whole = lambda a: pl.BlockSpec(a.shape, lambda h: (0,) * a.ndim)
    col = lambda off: pl.BlockSpec((width, 128), lambda h: (0, h + off))
    out = pl.BlockSpec((length, 128), lambda h: (0, h))
    shape = jax.ShapeDtypeStruct((length, pairs * 128), BF)
    flops = 2 * length * width * pairs * 384 + 4 * pairs * 2 * length * length * 128
    return pl.pallas_call(
        attn_fwd_kernel,
        grid=(pairs,),
        in_specs=[whole(xh), col(0), col(pairs), col(0)]
        + [whole(t) for t in tables]
        + [whole(seg_col), whole(seg_row)],
        out_specs=[out] * 4 + [pl.BlockSpec((1, 2, length), lambda h: (h, 0, 0))],
        out_shape=[shape] * 4 + [jax.ShapeDtypeStruct((pairs, 2, length), F32)],
        scratch_shapes=[pltpu.VMEM((2, length, 128), BF)],
        cost_estimate=pl.CostEstimate(
            flops=flops, bytes_accessed=length * width * 8, transcendentals=pairs * 2 * length * length
        ),
        name="attn_fwd",
    )(xh, w_qk, w_qk, w_vo, *tables, seg_col, seg_row)


def attn_bwd_kernel(
    q, k, v, o, do, lse, cos, upper, lower, seg_col, seg_row, pg, kh, dk, dv
):
    length = q.shape[0]
    rows = min(256, length)
    lane = lax.broadcasted_iota(jnp.int32, (length, 128), 1)
    first = lane < HD
    kf = k[...]
    none = jnp.zeros_like(kf)
    kh[0] = jnp.where(first, kf, none)
    kh[1] = jnp.where(first, none, kf)
    dk[...] = jnp.zeros_like(dk)
    dv[...] = jnp.zeros_like(dv)

    def block(i, carry):
        at = pl.multiple_of(i * rows, rows)
        here = pl.ds(at, rows)
        q_rows = q[here, :]
        g_rows = do[here, :]
        seg_here = seg_row[:, here]
        same = seg_col[...] == seg_here
        prod = g_rows.astype(F32) * o[here, :].astype(F32)
        f = first[:rows]
        blank = jnp.zeros_like(q_rows)
        dq = jnp.zeros((rows, 128), F32)
        for head in range(2):
            mine = f if head == 0 else jnp.logical_not(f)
            q_head = jnp.where(mine, q_rows, blank)
            g_head = jnp.where(mine, g_rows, blank)
            delta = lax.dot_general(
                jnp.ones((8, 128), F32),
                jnp.where(mine, prod, 0.0),
                (NT, ((), ())),
                precision=lax.Precision.HIGHEST,
                preferred_element_type=F32,
            )[0:1, :]
            scores = dotf(k[...], q_head, NT)
            level = lse[0, pl.ds(head, 1), here]
            probs = jnp.where(same, jnp.exp(scores - level), 0.0)
            dv[...] += dotf(probs.astype(BF), g_head, NN)
            dp = dotf(v[...], g_head, NT)
            ds = (probs * (dp - delta)).astype(BF)
            dk[...] += dotf(ds, q_head, NN)
            dq = dq + dotf(ds, kh[head], TN)
        dq = dq * (1.0 / math.sqrt(HD))
        c, a, b = cos[here, :], upper[here, :], lower[here, :]
        pg[0, here, :] = (dq * c - turn(dq, a, b)).astype(BF)
        return carry

    lax.fori_loop(0, length // rows, block, 0)
    dkf = dk[...]
    pg[1] = (dkf * cos[...] - turn(dkf, upper[...], lower[...])).astype(BF)
    pg[2] = dv[...].astype(BF)


def attn_bwd(q, k, v, o, do, lse, tables, seg_col, seg_row):
    length, width = q.shape
    pairs = width // 128
    whole = lambda a: pl.BlockSpec(a.shape, lambda h: (0,) * a.ndim)
    col = pl.BlockSpec((length, 128), lambda h: (0, h))
    return pl.pallas_call(
        attn_bwd_kernel,
        grid=(pairs,),
        in_specs=[col] * 5
        + [pl.BlockSpec((1, 2, length), lambda h: (h, 0, 0))]
        + [whole(t) for t in tables]
        + [whole(seg_col), whole(seg_row)],
        out_specs=pl.BlockSpec((3, length, 128), lambda h: (0, 0, h)),
        out_shape=jax.ShapeDtypeStruct((3, length, width), BF),
        scratch_shapes=[
            pltpu.VMEM((2, length, 128), BF),
            pltpu.VMEM((length, 128), F32),
            pltpu.VMEM((length, 128), F32),
        ],
        cost_estimate=pl.CostEstimate(
            flops=10 * pairs * 2 * length * length * 128,
            bytes_accessed=length * width * 20,
            transcendentals=pairs * 2 * length * length,
        ),
        name="attn_bwd",
    )(q, k, v, o, do, lse, *tables, seg_col, seg_row)


def in_chunks(total, size, body):
    def step(j, carry):
        body(pl.ds(pl.multiple_of(j * size, size), size))
        return carry

    lax.fori_loop(0, total // size, step, 0)
    if total % size:
        body(pl.ds(total - total % size, total % size))


SHARD = (4, 2, 2)


def place():
    dp = lax.axis_index("dp")
    return dp // 4, (dp // 2) % 2, dp % 2, lax.axis_index("tensor")


def partners():
    z, x, c, y = place()
    at = lambda z, x, c, y: ((z * 2 + x) * 2 + c, y)
    return {
        "z1": at(z + 1 - 2 * (z % 2), x, c, y),
        "z2": at(z + 2 - 4 * (z // 2), x, c, y),
        "z3": at(3 - z, x, c, y),
        "x": at(z, 1 - x, c, y),
        "y": at(z, x, c, 1 - y),
        "c": at(z, x, 1 - c, y),
    }


def meet(peers, other=None):
    barrier = pltpu.get_barrier_semaphore()
    greet = lambda peer: pl.semaphore_signal(
        barrier, inc=1, device_id=peer, device_id_type=pl.DeviceIdType.MESH
    )
    for peer in peers.values():
        greet(peer)
    if other is None:
        pl.semaphore_wait(barrier, len(peers))
    else:
        moved, peer = other

        @pl.when(moved)
        def _():
            greet(peer)

        pl.semaphore_wait(barrier, len(peers) + jnp.where(moved, 1, 0))


def exchanged():
    z, x, c, y = place()
    return c != y, ((z * 2 + x) * 2 + y, c)


def remote(src, dst, send_sem, recv_sem, peer):
    return pltpu.make_async_remote_copy(
        src_ref=src,
        dst_ref=dst,
        send_sem=send_sem,
        recv_sem=recv_sem,
        device_id=peer,
        device_id_type=pl.DeviceIdType.MESH,
    )


class Move:
    def __init__(self, src, dst, sems, i):
        send_sem, recv_sem, near_sem = sems
        self.moved, peer = exchanged()
        self.far = remote(src, dst, send_sem.at[i], recv_sem.at[i], peer)
        self.near = pltpu.make_async_copy(src, dst, near_sem.at[i])

    def start(self):
        @pl.when(self.moved)
        def _():
            self.far.start()

        @pl.when(jnp.logical_not(self.moved))
        def _():
            self.near.start()

    def wait(self):
        @pl.when(self.moved)
        def _():
            self.far.wait()

        @pl.when(jnp.logical_not(self.moved))
        def _():
            self.near.wait()


def move_sems(n):
    return [pltpu.SemaphoreType.DMA((n,))] * 3


def to_place(values):
    z, x, _, y = place()
    tiles = [values[:, j * 128 : (j + 1) * 128] for j in range(8)]
    tiles = [jnp.where(y == 1, pltpu.roll(t, 64, 1), t) for t in tiles]
    for bit, step in ((x, 1), (z % 2, 2), (z // 2, 4)):
        tiles = [jnp.where(bit == 1, tiles[j ^ step], tiles[j]) for j in range(8)]
    return jnp.concatenate(tiles, axis=1)


AXIS = {"z": 4, "x": 2, "y": 2}


def partner(peers, axis, step):
    return peers["z%d" % step if axis == "z" else axis]


class Gather:
    MESSAGES = 15

    def __init__(self, own, buf, rows, cols, order, hops, peers, sems, base):
        self.buf, self.order, self.hops, self.peers = buf, order, hops, peers
        self.part = (rows, cols)
        self.own = own.at[self.part]
        self.send_sem, self.recv_sem = sems
        self.base = base
        n, m, p = (AXIS[axis] for axis in order)
        self.outer, self.middle = range(n), range(1, m)
        self.stages = [
            [(i, 0, 0) for i in range(1, n)],
            [(i, j, 0) for i in range(n) for j in range(1, m)],
            [(i, j, k) for i in range(n) for j in range(m) for k in range(1, p)],
        ]
        self.stages = self.stages[:hops]
        self.numbers = {at: n for n, at in enumerate(sum(self.stages, []))}

    def slot(self, at):
        where = dict(zip(self.order, at))
        return self.buf.at[(where["z"], where["x"], where["y"]) + self.part]

    def copy(self, at):
        hop = max(i for i in range(3) if at[i])
        source = at[:hop] + (0,) * (3 - hop)
        src = self.slot(source) if any(source) else self.own
        n = self.base + self.numbers[at]
        peer = partner(self.peers, self.order[hop], at[hop])
        return remote(src, self.slot(at), self.send_sem.at[n], self.recv_sem.at[n], peer)

    def send(self, stage, *prefix):
        for at in self.stages[stage]:
            if at[: len(prefix)] == prefix:
                self.copy(at).start()

    def start(self):
        self.send(0)

    def relay(self, i):
        if i:
            self.copy((i, 0, 0)).wait_recv()
        self.send(1, i)
        if self.hops == 3:
            self.send(2, i, 0)

    def relay_again(self, i):
        for j in self.middle:
            self.copy((i, j, 0)).wait_recv()
            self.send(2, i, j)

    def finish(self):
        for at in self.stages[-1]:
            self.copy(at).wait_recv()
        for at in self.numbers:
            self.copy(at).wait_send()


def forward_kernel(
    a_in, b_in, g_in, u_in, d_in, x_in, c_in, seg_in, inverse,
    q, k, v, o, lse, xh, w_qkv, w_out, resid, xn, x_half, cot, cos, upper, lower, seg_col, seg_row,
    w_gate, w_up, w_down,
    a_own, b_own, g_own, u_own, d_own, c_own, seg_own,
    kh, x_rel, part, sent, got, send_sem, recv_sem, pair_send, pair_recv, own_sem, *moving,
):
    length = xh.shape[0]
    half = length // 2
    width = xh.shape[1]
    pairs = q.shape[1] // 128
    rows = 256
    core = place()[2]
    peers = partners()
    sems = (send_sem, recv_sem)
    n = Gather.MESSAGES
    whole, low, high = pl.ds(0, 64), pl.ds(0, 32), pl.ds(32, 32)
    wide = w_qkv.shape[4] // 2
    all_ = lambda ref: pl.ds(0, ref.shape[-1])
    plan = (
        (a_own, w_qkv, whole, pl.ds(0, wide), "zyx", 3),
        (a_own, w_qkv, whole, pl.ds(wide, wide), "zyx", 3),
        (b_own, w_out, whole, all_(w_out), "zxy", 3),
        (g_own, w_gate, whole, all_(w_gate), "zyx", 3),
        (u_own, w_up, low, all_(w_up), "zyx", 3),
        (u_own, w_up, high, all_(w_up), "xyz", 3),
        (d_own, w_down, low, all_(w_down), "zyx", 2),
        (d_own, w_down, high, all_(w_down), "zxy", 2),
    )
    gathers = [Gather(*piece, peers, sems, i * n) for i, piece in enumerate(plan)]
    near, far, out, two, late, three = *gathers[:3], gathers[3:5], gathers[5], gathers[6:]
    owns = [
        pltpu.make_async_copy(src, dst.at[0, 0, 0], own_sem.at[i])
        for i, (src, dst) in enumerate(
            ((a_own, w_qkv), (b_own, w_out), (g_own, w_gate), (u_own, w_up), (d_own, w_down))
        )
    ]
    move_a, move_b, move_x, move_seg, move_g, move_u, move_d, move_c = (
        Move(src, dst, moving, i)
        for i, (src, dst) in enumerate(
            (
                (a_in, a_own),
                (b_in, b_own),
                (x_in, x_half),
                (seg_in, seg_own),
                (g_in, g_own),
                (u_in, u_own),
                (d_in, d_own),
                (c_in, c_own),
            )
        )
    )
    meet(peers, exchanged())
    for move in (move_a, move_seg, move_x):
        move.start()

    def tables(here):
        shape = (here.size, 128)
        row = here.start + lax.broadcasted_iota(jnp.int32, shape, 0) + core * half
        row = jnp.where(row >= length, row - length, row)
        angle = row.astype(F32) * inverse[0:1, :]
        front = lax.broadcasted_iota(jnp.int32, shape, 1) % HD < HD // 2
        sin = jnp.sin(angle)
        cos[here, :] = jnp.cos(angle)
        upper[here, :] = jnp.where(front, -sin, 0.0)
        lower[here, :] = jnp.where(front, 0.0, sin)

    move_a.wait()
    near.start()
    far.start()
    near.relay(0)
    owns[0].start()
    in_chunks(length, 64, tables)
    for z in (1, 2, 3):
        near.relay(z)
    for move in (move_b, move_g, move_u, move_d):
        move.start()
    move_seg.wait()
    ids = seg_own[...]
    ids = jnp.where(core == 0, ids, jnp.concatenate([ids[:, half:], ids[:, :half]], axis=1))
    seg_row[...] = ids
    seg_col[...] = jnp.transpose(jnp.broadcast_to(ids[0:1, :], (128, length)))
    move_x.wait()

    def first_norm(i, carry):
        here = pl.ds(pl.multiple_of(i * 128, 128), 128)
        values = to_place(x_half[here, :].astype(F32))
        x_rel[here, :] = values.astype(BF)
        xh[here, :] = normalize(values)[0].astype(BF)
        return carry

    lax.fori_loop(0, half // 128, first_norm, 0)
    swap_xh = remote(
        xh.at[pl.ds(0, half)], xh.at[pl.ds(half, half)], pair_send.at[0], pair_recv.at[0], peers["c"]
    )
    swap_xh.start()
    for z in range(4):
        near.relay_again(z)
        far.relay(z)
    move_b.wait()
    out.start()
    move_g.wait()
    move_u.wait()
    late.start()
    for gather in two:
        gather.start()
    out.relay(0)
    late.relay(0)
    for gather in two:
        gather.relay(0)
    move_d.wait()
    for gather in three:
        gather.start()
    for copy in owns[1:]:
        copy.start()
    swap_xh.wait()
    near.finish()
    owns[0].wait()

    events = {}
    at_step = lambda step, call, *args: events.setdefault(step, []).append((call, args))
    for z in range(4):
        at_step(z, far.relay_again, z)
        if z:
            at_step(z, out.relay, z)
        at_step(5 + z, out.relay_again, z)
        for gather in two:
            if z:
                at_step(1 + 2 * z, gather.relay, z)
            at_step(9 + z, gather.relay_again, z)
        for gather in three:
            at_step(11 + z, gather.relay, z)
    at_step(4, late.relay, 1)
    at_step(5, move_c.start)
    at_step(6, late.relay_again, 0)
    at_step(8, late.relay_again, 1)
    at_step(length // rows * pairs // 2 - 1, far.finish)
    first = lax.broadcasted_iota(jnp.int32, (length, 128), 1) < HD

    def pair(h, carry):
        lanes = pl.ds(pl.multiple_of(h * 128, 128), 128)
        weight = lambda i: w_qkv[
            :, :, :, :, pl.ds(pl.multiple_of((3 * h + i) * 128, 128), 128)
        ].reshape(width, 128)
        tokens = xh[...]
        qf = dotf(tokens, weight(0), NN)
        qf = qf * cos[...] + turn(qf, upper[...], lower[...])
        q[:, lanes] = (qf * (1.0 / math.sqrt(HD))).astype(BF)
        kf = dotf(tokens, weight(1), NN)
        kf = (kf * cos[...] + turn(kf, upper[...], lower[...])).astype(BF)
        k[:, lanes] = kf
        kh[0] = jnp.where(first, kf, jnp.zeros_like(kf))
        kh[1] = jnp.where(first, jnp.zeros_like(kf), kf)
        v[:, lanes] = dotf(tokens, weight(2), NN).astype(BF)

        def block(i, carry):
            for step, calls in events.items():

                @pl.when(h * (length // rows) + i == step)
                def _():
                    for call, args in calls:
                        call(*args)

            at = pl.multiple_of(i * rows, rows)
            q_rows = q[pl.ds(at, rows), lanes]
            same = seg_col[pl.ds(at, rows), 0:1] == seg_row[0:1, :]
            outs = []
            for head in range(2):
                scores = dotf(q_rows, kh[head], NT)
                scores = jnp.where(same, scores, -1e30)
                top = jnp.max(scores, axis=-1, keepdims=True)
                expv = jnp.exp(scores - top)
                total = jnp.sum(expv, axis=-1, keepdims=True)
                low_probs = (expv * (1.0 / total)).astype(BF)
                outs.append(dotf(low_probs, v[:, lanes], NN))
                level = top + jnp.log(total)
                flat = jnp.transpose(jnp.broadcast_to(level, (rows, 128)))
                lse[h, pl.ds(head, 1), pl.ds(at, rows)] = flat[0:1, :]
            o[pl.ds(at, rows), lanes] = jnp.where(first[:rows], outs[0], outs[1]).astype(BF)
            return carry

        return lax.fori_loop(0, length // rows, block, carry)

    lax.fori_loop(0, pairs, pair, 0)
    out.finish()
    owns[1].wait()
    w_o = w_out[...].reshape(width, pairs * 128)

    def project(i, carry):
        at = pl.multiple_of(half + i * rows, rows)
        sent[pl.ds(pl.multiple_of(i * rows, rows), rows), :] = dotf(
            o[pl.ds(at, rows), :], w_o, NT
        ).astype(BF)
        return carry

    lax.fori_loop(0, half // rows, project, 0)

    def project_own(i, carry):
        here = pl.ds(pl.multiple_of(i * rows, rows), rows)
        part[here, :] = dotf(o[here, :], w_o, NT)
        return carry

    give = remote(sent, got, pair_send.at[1], pair_recv.at[1], peers["c"])
    lax.fori_loop(0, half // rows, project_own, 0)
    give.start()
    move_c.wait()

    def turn_cot(here):
        cot[here, :] = to_place(c_own[here, :].astype(F32)).astype(BF)

    in_chunks(half, 128, turn_cot)
    swap_cot = remote(
        cot.at[pl.ds(0, half)], cot.at[pl.ds(half, half)], pair_send.at[3], pair_recv.at[3], peers["c"]
    )
    swap_cot.start()
    give.wait()

    def second_norm(i, carry):
        here = pl.ds(pl.multiple_of(i * 128, 128), 128)
        values = x_rel[here, :].astype(F32) + (part[here, :] + got[here, :].astype(F32))
        resid[here, :] = values
        xn[here, :] = normalize(values)[0].astype(BF)
        return carry

    lax.fori_loop(0, half // 128, second_norm, 0)
    swap_xn = remote(
        xn.at[pl.ds(0, half)], xn.at[pl.ds(half, half)], pair_send.at[2], pair_recv.at[2], peers["c"]
    )
    swap_xn.start()
    for gather in two + three + [late]:
        gather.finish()
    for copy in owns[2:]:
        copy.wait()
    swap_cot.wait()
    swap_xn.wait()


def forward_block(owned, x_half, cot_half, seg, inverse):
    half, width = x_half.shape
    length = 2 * half
    cols = owned[1].shape[1]
    pairs = cols // 128
    units = owned[2].shape[1]
    shard = width // 16
    vmem = pl.BlockSpec(memory_space=pltpu.VMEM)
    any_ = pl.BlockSpec(memory_space=pl.ANY)
    gathered = lambda n: jax.ShapeDtypeStruct(SHARD + (shard, n), BF)
    heads = jax.ShapeDtypeStruct((length, cols), BF)
    flat = jax.ShapeDtypeStruct((length, width), BF)
    table = jax.ShapeDtypeStruct((length, 128), F32)
    return pl.pallas_call(
        forward_kernel,
        in_specs=[any_] * 8 + [vmem],
        out_specs=[vmem] * 17 + [any_] * 3,
        out_shape=[heads] * 4
        + [
            jax.ShapeDtypeStruct((pairs, 2, length), F32),
            flat,
            gathered(3 * cols),
            gathered(cols),
            jax.ShapeDtypeStruct((half, width), F32),
            flat,
            jax.ShapeDtypeStruct((half, width), BF),
            flat,
        ]
        + [table] * 4
        + [jax.ShapeDtypeStruct((8, length), F32)]
        + [gathered(units)] * 3,
        scratch_shapes=[pltpu.VMEM((shard, 3 * cols), BF), pltpu.VMEM((shard, cols), BF)]
        + [pltpu.VMEM((shard, units), BF)] * 3
        + [
            pltpu.VMEM((half, width), BF),
            pltpu.VMEM((8, length), F32),
            pltpu.VMEM((2, length, 128), BF),
            pltpu.VMEM((half, width), BF),
            pltpu.VMEM((half, width), F32),
            pltpu.VMEM((half, width), BF),
            pltpu.VMEM((half, width), BF),
            pltpu.SemaphoreType.DMA((8 * Gather.MESSAGES,)),
            pltpu.SemaphoreType.DMA((8 * Gather.MESSAGES,)),
            pltpu.SemaphoreType.DMA((4,)),
            pltpu.SemaphoreType.DMA((4,)),
            pltpu.SemaphoreType.DMA((5,)),
        ]
        + move_sems(8),
        compiler_params=pltpu.CompilerParams(
            collective_id=0, has_side_effects=True, vmem_limit_bytes=60 << 20
        ),
        name="forward_block",
    )(*owned, x_half, cot_half, seg, inverse)


class Reduce:
    MESSAGES = 12
    ORDER = (2, 3, 1, 0)

    def __init__(self, parts, near, rows, axes, peers, sems, base, bufs, out):
        self.parts, self.near, self.rows, self.axes, self.peers = parts, near, rows, axes, peers
        self.send_sem, self.recv_sem = sems
        self.base = base
        self.one, self.two, self.three, self.sum = bufs
        self.out = out

    def link(self, i, src, dst, peer):
        n = self.base + i
        return remote(src, dst, self.send_sem.at[n], self.recv_sem.at[n], peer)

    def first(self, z):
        if self.axes == "xy":
            src = self.parts.at[z, :, 1, self.rows]
        else:
            src = self.parts.at[z, 1, :, self.rows]
        return self.link(z, src, self.one.at[z], self.peers[self.axes[1]])

    def second(self, z):
        return self.link(4 + z, self.one.at[z, 1], self.two.at[z], self.peers[self.axes[0]])

    def third(self, z):
        return self.link(7 + z, self.two.at[z], self.three.at[z - 1], self.peers["z%d" % z])

    def start(self):
        for z in self.ORDER:
            self.first(z).start()

    def add_first(self, z):
        self.first(z).wait_recv()
        self.one[z] = (self.one[z].astype(F32) + self.near(z).astype(F32)).astype(BF)

    def relay_first(self, z):
        self.add_first(z)
        self.second(z).start()

    def resume(self):
        for z in self.ORDER:
            self.second(z).start()

    def relay_second(self, z):
        self.second(z).wait_recv()
        self.two[z] = (self.two[z].astype(F32) + self.one[z, 0].astype(F32)).astype(BF)
        if z:
            self.third(z).start()

    def last(self):
        moved, peer = exchanged()
        return moved, self.link(11, self.sum, self.out, peer)

    def total(self):
        total = self.two[0].astype(F32)
        for z in (1, 2, 3):
            self.third(z).wait_recv()
            total = total + self.three[z - 1].astype(F32)
        return total

    def finish(self):
        self.sum[...] = self.total().astype(BF)
        moved, copy = self.last()

        @pl.when(moved)
        def _():
            copy.start()

        @pl.when(jnp.logical_not(moved))
        def _():
            self.out[...] = self.sum[...]

    def sent(self):
        hops = (self.second,) if self.parts is None else (self.first, self.second)
        thirds = [self.third(z) for z in (1, 2, 3)]
        return [hop(z) for z in range(4) for hop in hops] + thirds

    def close(self):
        for copy in self.sent():
            copy.wait_send()
        moved, copy = self.last()

        @pl.when(moved)
        def _():
            copy.wait()


class ReduceAlongZ(Reduce):
    def first(self, z):
        src = self.parts.at[z, :, :, self.rows]
        return self.link(z - 1, src, self.one.at[z - 1], self.peers["z%d" % z])

    def second(self):
        return self.link(3, self.two.at[:, 1], self.three.at[0:2], self.peers["y"])

    def third(self):
        return self.link(4, self.three.at[1], self.three.at[2], self.peers["x"])

    def start(self):
        for z in (2, 3, 1):
            self.first(z).start()

    def relay_first(self):
        total = self.near().astype(F32)
        for z in (1, 2, 3):
            self.first(z).wait_recv()
            total = total + self.one[z - 1].astype(F32)
        self.two[...] = total.astype(BF)
        self.second().start()

    def relay_second(self):
        self.second().wait_recv()
        for x in (0, 1):
            self.three[x] = (self.three[x].astype(F32) + self.two[x, 0].astype(F32)).astype(BF)
        self.third().start()

    def total(self):
        self.third().wait_recv()
        return self.three[0].astype(F32) + self.three[2].astype(F32)

    def sent(self):
        return [self.first(z) for z in (1, 2, 3)] + [self.second(), self.third()]


def mlp_kernel(
    down_in, xn, cot, w_gate, w_up, resid,
    result, resid_grad, attn_cot, d_gate, d_up, d_low, d_high,
    w_down, d_down, hidden, act, slope_up, gate_grad, up_grad, own, sent, got, placed,
    send_sem, recv_sem, last_send, last_recv, first_send, first_recv, own_sem, *moving,
):
    length, width = xn.shape
    half = length // 2
    units = w_gate.shape[1]
    peers = {axis: partners()[axis] for axis in "xyc"}
    move = Move(placed, result, moving, 0)
    low, high = pl.ds(0, 32), pl.ds(32, 32)
    most, few = pl.ds(0, 48), pl.ds(48, 16)
    at_low = lambda ref, z, x: ref.at[z, x, :, low]
    at_high = lambda ref, z, y: ref.at[z, :, y, high]
    last = []
    for z in range(4):
        for i, (part, axis) in enumerate(((at_low, "x"), (at_high, "y"))):
            n = 2 * z + i
            last.append(
                remote(
                    part(down_in, z, 0), part(w_down, z, 1), last_send.at[n], last_recv.at[n], peers[axis]
                )
            )
    every = pl.ds(0, 4)
    owns = [
        pltpu.make_async_copy(part(down_in, every, 0), part(w_down, every, 0), own_sem.at[i])
        for i, part in enumerate((at_low, at_high))
    ]
    sems = (first_send, first_recv)
    n = Reduce.MESSAGES
    reduce_low = Reduce(
        d_down, lambda z: d_down[z, 0, :, 0:48], most, "yx", peers, sems, 0, (d_low, None, None, None), None
    )
    reduce_high = Reduce(
        d_down, lambda z: d_down[z, :, 0, 48:64], few, "xy", peers, sems, n, (d_high, None, None, None), None
    )
    meet(peers, exchanged())
    for copy in last + owns:
        copy.start()
    back, front = pl.ds(half, half), pl.ds(0, half)

    def gate_and_up(rows):
        def step(cols):
            gate = dotf(xn[rows, :], w_gate[:, cols], NN)
            up = dotf(xn[rows, :], w_up[:, cols], NN)
            value, slope = gelu_parts(gate)
            hidden[rows, cols] = (value * up).astype(BF)
            act[rows, cols] = value
            slope_up[rows, cols] = up * slope

        in_chunks(units, 256, step)

    def units_back(rows):
        def step(cols):
            down = w_down[:, :, :, :, cols].reshape(width, cols.size)
            grad = dotf(cot[rows, :], down, NN).astype(BF).astype(F32)
            gate_grad[rows, cols] = (grad * slope_up[rows, cols]).astype(BF)
            up_grad[rows, cols] = (grad * act[rows, cols]).astype(BF)

        in_chunks(units, 256, step)

    def sums(rows, put):
        def step(z, carry):
            here = pl.ds(pl.multiple_of(z * 256, 256), 256)
            down = w_down[z].reshape(256, units)
            put[0, :, here] = dotf(hidden[rows, :], down, NT).astype(put.dtype)
            both = dotf(gate_grad[rows, :], w_gate[here, :], NT)
            both = both + dotf(up_grad[rows, :], w_up[here, :], NT)
            put[1, :, here] = both.astype(put.dtype)
            return carry

        lax.fori_loop(0, width // 256, step, 0)

    gate_and_up(back)
    gate_and_up(front)
    for z in Reduce.ORDER:
        left = jnp.transpose(cot[:, z * 256 : (z + 1) * 256])
        d_down[z] = dotf(left, hidden[...], NN).astype(BF).reshape(2, 2, 64, units)
        reduce_low.first(z).start()
        reduce_high.first(z).start()
    for copy in owns:
        copy.wait()
    for copy in last:
        copy.wait()
    units_back(back)
    sums(back, sent)
    give = remote(sent, got, send_sem.at[0], recv_sem.at[0], peers["c"])
    give.start()
    units_back(front)
    sums(front, own)
    give.wait()

    def finish(here):
        values = resid[here, :]
        mlp = own[0, here, :] + got[0, here, :].astype(F32)
        placed[here, :] = to_place(values + mlp).astype(BF)
        xhat, scale = normalize(values)
        back = normalize_back(own[1, here, :] + got[1, here, :].astype(F32), xhat, scale)
        grad = cot[here, :].astype(F32) + back
        resid_grad[here, :] = grad
        attn_cot[here, :] = grad.astype(BF)

    in_chunks(half, 64, finish)
    swap = remote(
        attn_cot.at[pl.ds(0, half)], attn_cot.at[pl.ds(half, half)], send_sem.at[1], recv_sem.at[1], peers["c"]
    )
    swap.start()
    move.start()

    def weights(here):
        left = jnp.transpose(xn[:, here])
        d_gate[here, :] = dotf(left, gate_grad[...], NN).astype(BF)
        d_up[here, :] = dotf(left, up_grad[...], NN).astype(BF)

    in_chunks(width, 256, weights)
    for z in Reduce.ORDER:
        reduce_low.add_first(z)
        reduce_high.add_first(z)
    for z in range(4):
        reduce_low.first(z).wait_send()
        reduce_high.first(z).wait_send()
    swap.wait()
    move.wait()


def mlp_block(down_in, xn, cot, w_gate, w_up, resid):
    length, width = xn.shape
    half = length // 2
    units = w_gate.shape[1]
    shard = width // 16
    vmem = pl.BlockSpec(memory_space=pltpu.VMEM)
    any_ = pl.BlockSpec(memory_space=pl.ANY)
    grads = jax.ShapeDtypeStruct((width, units), BF)
    dma = lambda n: pltpu.SemaphoreType.DMA((n,))
    return pl.pallas_call(
        mlp_kernel,
        in_specs=[any_] + [vmem] * 5,
        out_specs=[any_] + [vmem] * 6,
        out_shape=[
            jax.ShapeDtypeStruct((half, width), BF),
            jax.ShapeDtypeStruct((half, width), F32),
            jax.ShapeDtypeStruct((length, width), BF),
            grads,
            grads,
            jax.ShapeDtypeStruct((4, 2, shard * 3 // 4, units), BF),
            jax.ShapeDtypeStruct((4, 2, shard // 4, units), BF),
        ],
        scratch_shapes=[pltpu.VMEM(SHARD + (shard, units), BF)] * 2
        + [
            pltpu.VMEM((length, units), BF),
            pltpu.VMEM((length, units), F32),
            pltpu.VMEM((length, units), F32),
            pltpu.VMEM((length, units), BF),
            pltpu.VMEM((length, units), BF),
            pltpu.VMEM((2, half, width), F32),
            pltpu.VMEM((2, half, width), BF),
            pltpu.VMEM((2, half, width), BF),
            pltpu.VMEM((half, width), BF),
        ]
        + [dma(2), dma(2), dma(8), dma(8), dma(2 * Reduce.MESSAGES), dma(2 * Reduce.MESSAGES), dma(2)]
        + move_sems(1),
        compiler_params=pltpu.CompilerParams(
            collective_id=1, has_side_effects=True, vmem_limit_bytes=63 << 20
        ),
        name="mlp_block",
    )(down_in, xn, cot, w_gate, w_up, resid)


def backward_kernel(
    d_gate, d_up, d_low, d_high, q, k, v, o, lse, attn_cot, w_qkv, w_out, xh, x_half, resid_grad,
    cos, upper, lower, seg_col, seg_row,
    token_grad, s_gate, s_up_low, s_up_high, s_down_low, s_down_high, s_out, s_near, s_far,
    d_out, d_near, d_far, pg, heads_grad, kh, dk, dv, own, sent, got, placed,
    near_gate, near_up_low, near_up_high,
    *rest,
):
    bufs = [rest[4 * i : 4 * i + 4] for i in range(3)]
    bufs += [(first,) + rest[12 + 3 * i : 15 + 3 * i] for i, first in enumerate((d_low, d_high))]
    bufs += [rest[18 + 4 * i : 22 + 4 * i] for i in range(3)]
    send_sem, recv_sem, pair_send, pair_recv, near_sem, *moving = rest[30:]
    length, width = xh.shape
    half = length // 2
    cols = q.shape[1]
    pairs = cols // 128
    rows = 256
    peers = partners()
    sems = (send_sem, recv_sem)
    n = Reduce.MESSAGES
    whole, low, high = pl.ds(0, 64), pl.ds(0, 32), pl.ds(32, 32)
    held = lambda ref: (lambda z: ref[z])
    plan = (
        (Reduce, d_gate, held(near_gate), whole, "yx", s_gate),
        (Reduce, d_up, held(near_up_low), low, "xy", s_up_low),
        (ReduceAlongZ, d_up, lambda: near_up_high[...], high, None, s_up_high),
        (Reduce, None, None, None, "yx", s_down_low),
        (Reduce, None, None, None, "xy", s_down_high),
        (Reduce, d_out, lambda z: d_out[z, 0], whole, "yx", s_out),
        (Reduce, d_near, lambda z: d_near[z, 0], whole, "yx", s_near),
        (Reduce, d_far, lambda z: d_far[z, 0], whole, "yx", s_far),
    )
    parts = [
        kind(src, near, rows_, axes, peers, sems, i * n, bufs[i], out)
        for i, (kind, src, near, rows_, axes, out) in enumerate(plan)
    ]
    gate, up_low, up_high, down_low, down_high, out, near, far = parts
    nears = [
        pltpu.make_async_copy(src, dst, near_sem.at[i])
        for i, (src, dst) in enumerate(
            (
                (d_gate.at[:, 0], near_gate),
                (d_up.at[:, :, 0, low], near_up_low),
                (d_up.at[0, :, :, high], near_up_high),
            )
        )
    ]
    for copy in nears:
        copy.start()
    meet(peers, exchanged())
    up_high.start()
    down_low.resume()
    down_high.resume()
    gate.start()
    up_low.start()

    def heads(here):
        heads_grad[here, :] = dotf(attn_cot[here, :], w_out[...], NN).astype(BF)

    in_chunks(length, 256, heads)

    def out_weights(z, carry):
        here = pl.ds(pl.multiple_of(z * 256, 256), 256)
        value = dotf(jnp.transpose(attn_cot[:, here]), o[...], NN).astype(BF)
        d_out[z] = value.reshape(2, 2, 64, cols)
        return carry

    lax.fori_loop(0, width // 256, out_weights, 0)
    out.start()
    for copy in nears:
        copy.wait()
    for z in Reduce.ORDER:
        down_low.relay_second(z)
        down_high.relay_second(z)

    events = {}
    for i, z in enumerate(Reduce.ORDER):
        events.setdefault((3, 6, 10, 13)[i], []).append(lambda z=z: gate.relay_first(z))
        events.setdefault((5, 7, 8, 10)[i], []).append(lambda z=z: up_low.relay_first(z))
    for z in Reduce.ORDER[:2]:
        events.setdefault(14, []).append(lambda z=z: gate.relay_second(z))
    events.setdefault(9, []).append(up_high.relay_first)
    events.setdefault(13, []).append(up_high.relay_second)

    def weights(ref, at):
        def step(z, carry):
            left = jnp.transpose(xh[:, pl.ds(pl.multiple_of(z * 256, 256), 256)])
            value = dotf(left, pg[:, at : at + ref.shape[-1]], NN).astype(BF)
            ref[z] = value.reshape(2, 2, 64, ref.shape[-1])
            return carry

        lax.fori_loop(0, width // 256, step, 0)

    lane = lax.broadcasted_iota(jnp.int32, (length, 128), 1)
    first = lane < HD

    def pair(h, carry):
        lanes = pl.ds(pl.multiple_of(h * 128, 128), 128)
        third = lambda i: pl.ds(pl.multiple_of((3 * h + i) * 128, 128), 128)
        kf = k[:, lanes]
        none = jnp.zeros_like(kf)
        kh[0] = jnp.where(first, kf, none)
        kh[1] = jnp.where(first, none, kf)
        dk[...] = jnp.zeros_like(dk)
        dv[...] = jnp.zeros_like(dv)

        def block(i, carry):
            for step, calls in events.items():

                @pl.when(h * (length // rows) + i == step)
                def _():
                    for call in calls:
                        call()

            at = pl.multiple_of(i * rows, rows)
            here = pl.ds(at, rows)
            q_rows = q[here, lanes]
            g_rows = heads_grad[here, lanes]
            same = seg_col[:, 0:1] == seg_row[0:1, here]
            prod = g_rows.astype(F32) * o[here, lanes].astype(F32)
            f = first[:rows]
            blank = jnp.zeros_like(q_rows)
            dq = jnp.zeros((rows, 128), F32)
            for head in range(2):
                mine = f if head == 0 else jnp.logical_not(f)
                q_head = jnp.where(mine, q_rows, blank)
                g_head = jnp.where(mine, g_rows, blank)
                delta = lax.dot_general(
                    jnp.ones((8, 128), F32),
                    jnp.where(mine, prod, 0.0),
                    (NT, ((), ())),
                    precision=lax.Precision.HIGHEST,
                    preferred_element_type=F32,
                )[0:1, :]
                scores = dotf(k[:, lanes], q_head, NT)
                level = lse[h, pl.ds(head, 1), here]
                probs = jnp.where(same, jnp.exp(scores - level), 0.0)
                dv[...] += dotf(probs.astype(BF), g_head, NN)
                dp = dotf(v[:, lanes], g_head, NT)
                ds = (probs * (dp - delta)).astype(BF)
                dk[...] += dotf(ds, q_head, NN)
                dq = dq + dotf(ds, kh[head], TN)
            dq = dq * (1.0 / math.sqrt(HD))
            c, a, b = cos[here, :], upper[here, :], lower[here, :]
            pg[here, third(0)] = (dq * c - turn(dq, a, b)).astype(BF)
            return carry

        lax.fori_loop(0, length // rows, block, 0)
        dkf = dk[...]
        pg[:, third(1)] = (dkf * cos[...] - turn(dkf, upper[...], lower[...])).astype(BF)
        pg[:, third(2)] = dv[...].astype(BF)

        @pl.when(h == pairs // 2 - 1)
        def _():
            weights(d_near, 0)
            near.start()

        return carry

    lax.fori_loop(0, pairs, pair, 0)
    weights(d_far, d_near.shape[-1])
    far.start()

    def back(tokens, put):
        def step(here):
            put[:, here] = dotf(pg[tokens, :], w_qkv[here, :], NT).astype(put.dtype)

        in_chunks(width, 256, step)

    for z in Reduce.ORDER[2:]:
        gate.relay_second(z)
    for z in Reduce.ORDER:
        out.relay_first(z)
    back(pl.ds(half, half), sent)
    give = remote(sent, got, pair_send.at[0], pair_recv.at[0], peers["c"])
    give.start()
    for z in Reduce.ORDER:
        up_low.relay_second(z)
    back(pl.ds(0, half), own)
    for z in Reduce.ORDER:
        out.relay_second(z)
    for part in (down_low, down_high):
        part.finish()
    give.wait()

    def finish(here):
        xhat, scale = normalize(to_place(x_half[here, :].astype(F32)))
        f = own[here, :] + got[here, :].astype(F32)
        value = resid_grad[here, :] + normalize_back(f, xhat, scale)
        placed[here, :] = to_place(value).astype(BF)

    in_chunks(half, 64, finish)
    move = Move(placed, token_grad, moving, 0)
    move.start()
    for z in Reduce.ORDER:
        near.relay_first(z)
    for part in (gate, up_high, up_low):
        part.finish()
    for z in Reduce.ORDER:
        far.relay_first(z)
        near.relay_second(z)
    out.finish()
    for z in Reduce.ORDER:
        far.relay_second(z)
    near.finish()
    far.finish()
    for part in parts:
        part.close()
    move.wait()


def backward_block(grads, heads, lse, attn_cot, w_qkv, w_out, xh, x_half, resid_grad, tables, seg_col, seg_row):
    length, width = xh.shape
    half = length // 2
    cols = heads[0].shape[1]
    units = grads[0].shape[1]
    shard = width // 16
    vmem = pl.BlockSpec(memory_space=pltpu.VMEM)
    any_ = pl.BlockSpec(memory_space=pl.ANY)
    wide = 3 * cols // 2
    sizes = [(shard, units), (shard // 2, units), (shard // 2, units)]
    sizes += [g.shape[2:] for g in grads[2:]]
    sizes += [(shard, cols), (shard, wide), (shard, wide)]
    along_z, begun = (2,), (3, 4)
    bufs = []
    for i, size in enumerate(sizes):
        if i in along_z:
            lead = (3, 2, 2), (2, 2), (3,)
        else:
            lead = (4, 2), (4,), (3,)
        bufs += [pltpu.VMEM(n + size, BF) for n in lead[i in begun :] + ((),)]
    nears = [pltpu.VMEM(((2, 2) if i in along_z else (4, 2)) + size, BF) for i, size in enumerate(sizes[:3])]
    messages = 8 * Reduce.MESSAGES
    return pl.pallas_call(
        backward_kernel,
        in_specs=[any_] * 2 + [vmem] * 18,
        out_specs=[vmem] * 9,
        out_shape=[jax.ShapeDtypeStruct((half, width), BF)]
        + [jax.ShapeDtypeStruct(size, BF) for size in sizes],
        scratch_shapes=[pltpu.VMEM(SHARD + (shard, n), BF) for n in (cols, wide, wide)]
        + [
            pltpu.VMEM((length, 3 * cols), BF),
            pltpu.VMEM((length, cols), BF),
            pltpu.VMEM((2, length, 128), BF),
            pltpu.VMEM((length, 128), F32),
            pltpu.VMEM((length, 128), F32),
            pltpu.VMEM((half, width), F32),
            pltpu.VMEM((half, width), BF),
            pltpu.VMEM((half, width), BF),
            pltpu.VMEM((half, width), BF),
        ]
        + nears
        + bufs
        + [
            pltpu.SemaphoreType.DMA((messages,)),
            pltpu.SemaphoreType.DMA((messages,)),
            pltpu.SemaphoreType.DMA((1,)),
            pltpu.SemaphoreType.DMA((1,)),
            pltpu.SemaphoreType.DMA((3,)),
        ]
        + move_sems(1),
        compiler_params=pltpu.CompilerParams(
            collective_id=2, has_side_effects=True, vmem_limit_bytes=60 << 20
        ),
        name="backward_block",
    )(
        *(g.reshape(SHARD + (shard, units)) for g in grads[:2]), *grads[2:],
        *heads, lse, attn_cot, w_qkv, w_out, xh, x_half, resid_grad, *tables, seg_col, seg_row,
    )


class Chips:
    def sum_tensor(self, value):
        pairs = [(2 * i + y, 2 * i + 1 - y) for i in range(16) for y in range(2)]
        return value + lax.ppermute(value, ("dp", "tensor"), pairs)


class Axes:
    def gather_rows(self, value):
        return lax.all_gather(value, "tensor", axis=0, tiled=True)

    def scatter_rows(self, value):
        return lax.psum_scatter(value.astype(BF), "tensor", scatter_dimension=0, tiled=True).astype(F32)

    def reduce(self, a, b):
        return tuple(
            lax.psum_scatter(w.astype(BF), "dp", scatter_dimension=0, tiled=True).astype(F32)
            for w in (a, b)
        )

    def sum_tensor(self, value):
        return lax.psum(value, "tensor")


def normalize(values):
    centred = values - jnp.mean(values, axis=-1, keepdims=True)
    scale = lax.rsqrt(jnp.mean(centred * centred, axis=-1, keepdims=True) + EPS)
    return centred * scale, scale


def normalize_back(f, xhat, scale):
    return scale * (
        f
        - jnp.mean(f, axis=-1, keepdims=True)
        - xhat * jnp.mean(f * xhat, axis=-1, keepdims=True)
    )


def gelu_parts(gate):
    half_erf = 0.5 * (1.0 + lax.erf(gate * (1.0 / math.sqrt(2.0))))
    density = jnp.exp(-0.5 * gate * gate) * (1.0 / math.sqrt(2.0 * math.pi))
    return gate * half_erf, half_erf + gate * density


def make_local(comm_type):
    def local(tokens, segments, w_qkv, w_out, w_in, w_down, g_attn, g_mlp, cotangent):
        comm = comm_type()
        paired = comm_type is Chips
        shard = w_qkv.shape[0]
        cols = w_qkv.shape[2]
        units = w_in.shape[2]
        low = 128 * (units // 256)
        pad = 128 * pl.cdiv(units, 128) - units
        gain_one = g_attn.astype(F32)[:, None]
        gain_two = g_mlp.astype(F32)[:, None]
        scaled = lambda w, g: (w.astype(F32) * g).astype(BF)
        padded = lambda w: jnp.pad(w, ((0, 0), (0, pad)))
        down_rows = w_down.T
        a_one = jnp.concatenate([scaled(w_qkv[:, 0], gain_one), scaled(w_qkv[:, 1], gain_one)], axis=1)
        b_one = jnp.concatenate([scaled(w_qkv[:, 2], gain_one), w_out.T], axis=1)
        own_gate, own_up = scaled(w_in[:, 0], gain_two), scaled(w_in[:, 1], gain_two)

        owned = (a_one, b_one, own_gate, own_up, down_rows)
        if paired:
            by_pair = scaled(w_qkv, gain_one[:, None]).reshape(shard, 3, cols // 128, 128).swapaxes(1, 2)
            owned = (by_pair.reshape(shard, 3 * cols), w_out.T) + tuple(padded(w) for w in owned[2:])
            seg = jnp.broadcast_to(segments.astype(F32), (8, segments.shape[1]))
            inverse = jnp.broadcast_to(jnp.tile(rope_rates(), 4), (8, 128))
            (
                q, k, v, o, lse, xh, qkv_all, out_all, resid, xn, x_half, cot_all, *tables, seg_col, seg_row,
                w_gate, w_up, w_dn,
            ) = forward_block(owned, tokens[0], cotangent[0], seg, inverse)
            qkv_all, out_all, w_gate, w_up = (
                w.reshape(-1, w.shape[-1]) for w in (qkv_all, out_all, w_gate, w_up)
            )
        else:
            w_qk, w_vo, w_gate, w_up, w_dn = (
                lax.all_gather(w, "dp", axis=0, tiled=True) for w in owned
            )
            w_o = w_vo[:, cols:]
            seg_col, seg_row = segments[0][:, None], segments
            cot = cotangent[0]
            cot_all = comm.gather_rows(cot)
            tables = rope_tables(jnp.arange(segments.shape[1]))
            x_in = tokens[0].astype(F32)
            xh_one, scale_one = normalize(x_in)
            xh = comm.gather_rows(xh_one.astype(BF))
            o, q, k, v, lse = attn_fwd(xh, w_qk, w_vo, tables, seg_col, seg_row)
            resid = x_in + comm.scatter_rows(dotf(o, w_o, NT))
            xh_two, scale_two = normalize(resid)
            xn = comm.gather_rows(xh_two.astype(BF))
        if paired:
            result, resid_grad, attn_cot, *grads = mlp_block(w_dn, xn, cot_all, w_gate, w_up, resid)
        else:
            gate, up = dotf(xn, w_gate, NN), dotf(xn, w_up, NN)
            act, slope = gelu_parts(gate)
            hidden = (act * up).astype(BF)
            mlp = comm.scatter_rows(dotf(hidden, w_dn, NT))
            result = (resid + mlp).astype(BF)
            hidden_grad = dotf(cot_all, w_dn, NN).astype(BF).astype(F32)
            gate_grad = (hidden_grad * up * slope).astype(BF)
            up_grad = (hidden_grad * act).astype(BF)
            f_two = comm.scatter_rows(dotf(gate_grad, w_gate, NT) + dotf(up_grad, w_up, NT))
            resid_grad = cot.astype(F32) + normalize_back(f_two, xh_two, scale_two)
            attn_cot = comm.gather_rows(resid_grad.astype(BF))
            d_down = dotf(cot_all, hidden, TN)
            d_gate, d_up = dotf(xn, gate_grad, TN), dotf(xn, up_grad, TN)

        if paired:
            token_grad, *sums = backward_block(
                grads, (q, k, v, o), lse, attn_cot, qkv_all, out_all, xh, x_half,
                resid_grad, tables, seg_col, seg_row,
            )
            token_grad = token_grad.astype(F32)
            s_gate, up_low, up_high, s_low, s_high, s_out, near, far = (w.astype(F32) for w in sums)
            s_up = jnp.concatenate([up_low, up_high], axis=0)
            qkv_raw = jnp.concatenate([near, far], axis=1).reshape(shard, cols // 128, 3, 128)
            qkv_raw = qkv_raw.swapaxes(1, 2).reshape(shard, 3, cols)
            in_raw = jnp.stack([s_gate[:, :units], s_up[:, :units]], axis=1)
            down_sum = jnp.concatenate([s_low[:, :units], s_high[:, :units]], axis=0).T
        else:
            wide = lambda g, d: jnp.concatenate([padded(g), d], axis=1)
            two_a, two_b = comm.reduce(wide(d_gate, d_down[:, :low]), wide(d_up, d_down[:, low:]))

            heads_grad = dotf(attn_cot, w_o, NN).astype(BF)
            pg = attn_bwd(q, k, v, o, heads_grad, lse, tables, seg_col, seg_row)
            d_out = dotf(attn_cot, o, TN)
            d_q, d_k, d_v = (dotf(xh, pg[i], TN) for i in range(3))
            one_a, one_b = comm.reduce(
                jnp.concatenate([d_q, d_k], axis=1), jnp.concatenate([d_v, d_out], axis=1)
            )
            f_one = comm.scatter_rows(
                dotf(pg[0], w_qk[:, :cols], NT)
                + dotf(pg[1], w_qk[:, cols:], NT)
                + dotf(pg[2], w_vo[:, :cols], NT)
            )
            token_grad = resid_grad + normalize_back(f_one, xh_one, scale_one)
            in_raw = jnp.stack([two_a[:, :units], two_b[:, :units]], axis=1)
            down_sum = jnp.concatenate([two_a[:, units + pad :], two_b[:, units + pad :]], axis=1).T
            s_out = one_b[:, cols:]
            qkv_raw = jnp.stack([one_a[:, :cols], one_a[:, cols:], one_b[:, :cols]], axis=1)

        gains = jnp.stack(
            [
                jnp.sum(qkv_raw * w_qkv.astype(F32), axis=(1, 2)),
                jnp.sum(in_raw * w_in.astype(F32), axis=(1, 2)),
            ]
        )
        gains = comm.sum_tensor(gains)
        return (
            result[None],
            token_grad[None],
            gains[0],
            gains[1],
            qkv_raw * gain_one[:, :, None],
            s_out.T,
            in_raw * gain_two[:, :, None],
            down_sum,
        )

    return local


def solution(mesh):
    paired = mesh.shape["dp"] == 16 and mesh.shape["tensor"] == 2
    return jax.shard_map(
        make_local(Chips if paired else Axes),
        mesh=mesh,
        in_specs=(
            P("dp", "tensor", None),
            P("dp", None),
            P("dp", None, "tensor"),
            P("tensor", "dp"),
            P("dp", None, "tensor"),
            P("tensor", "dp"),
            P("dp"),
            P("dp"),
            P("dp", "tensor", None),
        ),
        out_specs=(
            P("dp", "tensor", None),
            P("dp", "tensor", None),
            P("dp"),
            P("dp"),
            P("dp", None, "tensor"),
            P("tensor", "dp"),
            P("dp", None, "tensor"),
            P("tensor", "dp"),
        ),
        check_vma=False,
    )
```

```python
import math

import jax
import jax.numpy as jnp
from jax import lax
from jax.experimental import pallas as pl
from jax.experimental.pallas import tpu as pltpu
from jax.sharding import PartitionSpec as P

HD = 64
EPS = 1e-05
ROTARY_BASE = 160000.0
BF = jnp.bfloat16
F32 = jnp.float32


def dotf(a, b, dims):
    return lax.dot_general(a, b, (dims, ((), ())), preferred_element_type=F32)


NN = ((1,), (0,))
NT = ((1,), (1,))
TN = ((0,), (0,))


def rope_rates():
    return 1.0 / ROTARY_BASE ** (jnp.arange(HD // 2).astype(F32) * (2.0 / HD))


def rope_tables(positions):
    angles = positions.astype(F32)[:, None] * rope_rates()[None, :]
    cos, sin = jnp.cos(angles), jnp.sin(angles)
    zero = jnp.zeros_like(sin)
    cosine = jnp.concatenate([cos] * 4, axis=-1)
    upper = jnp.concatenate([-sin, zero] * 2, axis=-1)
    lower = jnp.concatenate([zero, sin] * 2, axis=-1)
    return cosine, upper, lower


def turn(u, upper, lower):
    return pltpu.roll(u, 128 - HD // 2, 1) * upper + pltpu.roll(u, HD // 2, 1) * lower


def attn_fwd_kernel(xh, wq, wk, wv, cos, upper, lower, seg_col, seg_row, o, q, k, v, lse, kh):
    length = xh.shape[0]
    rows = min(256, length)
    lane = lax.broadcasted_iota(jnp.int32, (length, 128), 1)
    first = lane < HD
    tokens = xh[...]
    qf = dotf(tokens, wq[...], NN)
    qf = qf * cos[...] + turn(qf, upper[...], lower[...])
    q[...] = (qf * (1.0 / math.sqrt(HD))).astype(BF)
    kf = dotf(tokens, wk[...], NN)
    kf = (kf * cos[...] + turn(kf, upper[...], lower[...])).astype(BF)
    k[...] = kf
    kh[0] = jnp.where(first, kf, jnp.zeros_like(kf))
    kh[1] = jnp.where(first, jnp.zeros_like(kf), kf)
    v[...] = dotf(tokens, wv[...], NN).astype(BF)

    def block(i, carry):
        at = pl.multiple_of(i * rows, rows)
        q_rows = q[pl.ds(at, rows), :]
        same = seg_col[pl.ds(at, rows), :] == seg_row[...]
        outs = []
        for head in range(2):
            scores = dotf(q_rows, kh[head], NT)
            scores = jnp.where(same, scores, -1e30)
            top = jnp.max(scores, axis=-1, keepdims=True)
            expv = jnp.exp(scores - top)
            total = jnp.sum(expv, axis=-1, keepdims=True)
            low = (expv * (1.0 / total)).astype(BF)
            outs.append(dotf(low, v[...], NN))
            level = top + jnp.log(total)
            flat = jnp.transpose(jnp.broadcast_to(level, (rows, 128)))
            lse[0, pl.ds(head, 1), pl.ds(at, rows)] = flat[0:1, :]
        o[pl.ds(at, rows), :] = jnp.where(first[:rows], outs[0], outs[1]).astype(BF)
        return carry

    lax.fori_loop(0, length // rows, block, 0)


def attn_fwd(xh, w_qk, w_vo, tables, seg_col, seg_row):
    length, width = xh.shape
    pairs = w_qk.shape[1] // 256
    whole = lambda a: pl.BlockSpec(a.shape, lambda h: (0,) * a.ndim)
    col = lambda off: pl.BlockSpec((width, 128), lambda h: (0, h + off))
    out = pl.BlockSpec((length, 128), lambda h: (0, h))
    shape = jax.ShapeDtypeStruct((length, pairs * 128), BF)
    flops = 2 * length * width * pairs * 384 + 4 * pairs * 2 * length * length * 128
    return pl.pallas_call(
        attn_fwd_kernel,
        grid=(pairs,),
        in_specs=[whole(xh), col(0), col(pairs), col(0)]
        + [whole(t) for t in tables]
        + [whole(seg_col), whole(seg_row)],
        out_specs=[out] * 4 + [pl.BlockSpec((1, 2, length), lambda h: (h, 0, 0))],
        out_shape=[shape] * 4 + [jax.ShapeDtypeStruct((pairs, 2, length), F32)],
        scratch_shapes=[pltpu.VMEM((2, length, 128), BF)],
        cost_estimate=pl.CostEstimate(
            flops=flops, bytes_accessed=length * width * 8, transcendentals=pairs * 2 * length * length
        ),
        name="attn_fwd",
    )(xh, w_qk, w_qk, w_vo, *tables, seg_col, seg_row)


def attn_bwd_kernel(
    q, k, v, o, do, lse, cos, upper, lower, seg_col, seg_row, pg, kh, dk, dv
):
    length = q.shape[0]
    rows = min(256, length)
    lane = lax.broadcasted_iota(jnp.int32, (length, 128), 1)
    first = lane < HD
    kf = k[...]
    none = jnp.zeros_like(kf)
    kh[0] = jnp.where(first, kf, none)
    kh[1] = jnp.where(first, none, kf)
    dk[...] = jnp.zeros_like(dk)
    dv[...] = jnp.zeros_like(dv)

    def block(i, carry):
        at = pl.multiple_of(i * rows, rows)
        here = pl.ds(at, rows)
        q_rows = q[here, :]
        g_rows = do[here, :]
        seg_here = seg_row[:, here]
        same = seg_col[...] == seg_here
        prod = g_rows.astype(F32) * o[here, :].astype(F32)
        f = first[:rows]
        blank = jnp.zeros_like(q_rows)
        dq = jnp.zeros((rows, 128), F32)
        for head in range(2):
            mine = f if head == 0 else jnp.logical_not(f)
            q_head = jnp.where(mine, q_rows, blank)
            g_head = jnp.where(mine, g_rows, blank)
            delta = lax.dot_general(
                jnp.ones((8, 128), F32),
                jnp.where(mine, prod, 0.0),
                (NT, ((), ())),
                precision=lax.Precision.HIGHEST,
                preferred_element_type=F32,
            )[0:1, :]
            scores = dotf(k[...], q_head, NT)
            level = lse[0, pl.ds(head, 1), here]
            probs = jnp.where(same, jnp.exp(scores - level), 0.0)
            dv[...] += dotf(probs.astype(BF), g_head, NN)
            dp = dotf(v[...], g_head, NT)
            ds = (probs * (dp - delta)).astype(BF)
            dk[...] += dotf(ds, q_head, NN)
            dq = dq + dotf(ds, kh[head], TN)
        dq = dq * (1.0 / math.sqrt(HD))
        c, a, b = cos[here, :], upper[here, :], lower[here, :]
        pg[0, here, :] = (dq * c - turn(dq, a, b)).astype(BF)
        return carry

    lax.fori_loop(0, length // rows, block, 0)
    dkf = dk[...]
    pg[1] = (dkf * cos[...] - turn(dkf, upper[...], lower[...])).astype(BF)
    pg[2] = dv[...].astype(BF)


def attn_bwd(q, k, v, o, do, lse, tables, seg_col, seg_row):
    length, width = q.shape
    pairs = width // 128
    whole = lambda a: pl.BlockSpec(a.shape, lambda h: (0,) * a.ndim)
    col = pl.BlockSpec((length, 128), lambda h: (0, h))
    return pl.pallas_call(
        attn_bwd_kernel,
        grid=(pairs,),
        in_specs=[col] * 5
        + [pl.BlockSpec((1, 2, length), lambda h: (h, 0, 0))]
        + [whole(t) for t in tables]
        + [whole(seg_col), whole(seg_row)],
        out_specs=pl.BlockSpec((3, length, 128), lambda h: (0, 0, h)),
        out_shape=jax.ShapeDtypeStruct((3, length, width), BF),
        scratch_shapes=[
            pltpu.VMEM((2, length, 128), BF),
            pltpu.VMEM((length, 128), F32),
            pltpu.VMEM((length, 128), F32),
        ],
        cost_estimate=pl.CostEstimate(
            flops=10 * pairs * 2 * length * length * 128,
            bytes_accessed=length * width * 20,
            transcendentals=pairs * 2 * length * length,
        ),
        name="attn_bwd",
    )(q, k, v, o, do, lse, *tables, seg_col, seg_row)


def in_chunks(total, size, body):
    def step(j, carry):
        body(pl.ds(pl.multiple_of(j * size, size), size))
        return carry

    lax.fori_loop(0, total // size, step, 0)
    if total % size:
        body(pl.ds(total - total % size, total % size))


SHARD = (4, 2, 2)


def place():
    dp = lax.axis_index("dp")
    return dp // 4, (dp // 2) % 2, dp % 2, lax.axis_index("tensor")


def partners():
    z, x, c, y = place()
    at = lambda z, x, c, y: ((z * 2 + x) * 2 + c, y)
    return {
        "z1": at(z + 1 - 2 * (z % 2), x, c, y),
        "z2": at(z + 2 - 4 * (z // 2), x, c, y),
        "z3": at(3 - z, x, c, y),
        "x": at(z, 1 - x, c, y),
        "y": at(z, x, c, 1 - y),
        "c": at(z, x, 1 - c, y),
    }


def meet(peers, other=None):
    barrier = pltpu.get_barrier_semaphore()
    greet = lambda peer: pl.semaphore_signal(
        barrier, inc=1, device_id=peer, device_id_type=pl.DeviceIdType.MESH
    )
    for peer in peers.values():
        greet(peer)
    if other is None:
        pl.semaphore_wait(barrier, len(peers))
    else:
        moved, peer = other

        @pl.when(moved)
        def _():
            greet(peer)

        pl.semaphore_wait(barrier, len(peers) + jnp.where(moved, 1, 0))


def exchanged():
    z, x, c, y = place()
    return c != y, ((z * 2 + x) * 2 + y, c)


def remote(src, dst, send_sem, recv_sem, peer):
    return pltpu.make_async_remote_copy(
        src_ref=src,
        dst_ref=dst,
        send_sem=send_sem,
        recv_sem=recv_sem,
        device_id=peer,
        device_id_type=pl.DeviceIdType.MESH,
    )


class Move:
    def __init__(self, src, dst, sems, i):
        send_sem, recv_sem, near_sem = sems
        self.moved, peer = exchanged()
        self.far = remote(src, dst, send_sem.at[i], recv_sem.at[i], peer)
        self.near = pltpu.make_async_copy(src, dst, near_sem.at[i])

    def start(self):
        @pl.when(self.moved)
        def _():
            self.far.start()

        @pl.when(jnp.logical_not(self.moved))
        def _():
            self.near.start()

    def wait(self):
        @pl.when(self.moved)
        def _():
            self.far.wait()

        @pl.when(jnp.logical_not(self.moved))
        def _():
            self.near.wait()


def move_sems(n):
    return [pltpu.SemaphoreType.DMA((n,))] * 3


def to_place(values):
    z, x, _, y = place()
    tiles = [values[:, j * 128 : (j + 1) * 128] for j in range(8)]
    tiles = [jnp.where(y == 1, pltpu.roll(t, 64, 1), t) for t in tiles]
    for bit, step in ((x, 1), (z % 2, 2), (z // 2, 4)):
        tiles = [jnp.where(bit == 1, tiles[j ^ step], tiles[j]) for j in range(8)]
    return jnp.concatenate(tiles, axis=1)


AXIS = {"z": 4, "x": 2, "y": 2}


def partner(peers, axis, step):
    return peers["z%d" % step if axis == "z" else axis]


class Gather:
    MESSAGES = 15

    def __init__(self, own, buf, rows, cols, order, hops, peers, sems, base):
        self.buf, self.order, self.hops, self.peers = buf, order, hops, peers
        self.part = (rows, cols)
        self.own = own.at[self.part]
        self.send_sem, self.recv_sem = sems
        self.base = base
        n, m, p = (AXIS[axis] for axis in order)
        self.outer, self.middle = range(n), range(1, m)
        self.stages = [
            [(i, 0, 0) for i in range(1, n)],
            [(i, j, 0) for i in range(n) for j in range(1, m)],
            [(i, j, k) for i in range(n) for j in range(m) for k in range(1, p)],
        ]
        self.stages = self.stages[:hops]
        self.numbers = {at: n for n, at in enumerate(sum(self.stages, []))}

    def slot(self, at):
        where = dict(zip(self.order, at))
        return self.buf.at[(where["z"], where["x"], where["y"]) + self.part]

    def copy(self, at):
        hop = max(i for i in range(3) if at[i])
        source = at[:hop] + (0,) * (3 - hop)
        src = self.slot(source) if any(source) else self.own
        n = self.base + self.numbers[at]
        peer = partner(self.peers, self.order[hop], at[hop])
        return remote(src, self.slot(at), self.send_sem.at[n], self.recv_sem.at[n], peer)

    def send(self, stage, *prefix):
        for at in self.stages[stage]:
            if at[: len(prefix)] == prefix:
                self.copy(at).start()

    def start(self):
        self.send(0)

    def relay(self, i):
        if i:
            self.copy((i, 0, 0)).wait_recv()
        self.send(1, i)
        if self.hops == 3:
            self.send(2, i, 0)

    def relay_again(self, i):
        for j in self.middle:
            self.copy((i, j, 0)).wait_recv()
            self.send(2, i, j)

    def finish(self):
        for at in self.stages[-1]:
            self.copy(at).wait_recv()
        for at in self.numbers:
            self.copy(at).wait_send()


def forward_kernel(
    writes, a_in, b_in, g_in, u_in, d_in, x_in, c_in, seg_in, inverse,
    q, k, v, o, lse, xh, w_qkv, w_out, resid, xn, x_half, cot, cos, upper, lower, seg_col, seg_row,
    w_gate, w_up, w_down,
    a_own, b_own, g_own, u_own, d_own, c_own, seg_own,
    kh, x_rel, part, sent, got, send_sem, recv_sem, pair_send, pair_recv, own_sem, *moving,
):
    length = xh.shape[0]
    half = length // 2
    width = xh.shape[1]
    pairs = q.shape[1] // 128
    rows = 256
    core = place()[2]
    peers = partners()
    sems = (send_sem, recv_sem)
    n = Gather.MESSAGES
    whole, low, high = pl.ds(0, 64), pl.ds(0, 32), pl.ds(32, 32)
    wide = w_qkv.shape[4] // 2
    all_ = lambda ref: pl.ds(0, ref.shape[-1])
    plan = (
        (a_own, w_qkv, whole, pl.ds(0, wide), "zyx", 3),
        (a_own, w_qkv, whole, pl.ds(wide, wide), "zyx", 3),
        (b_own, w_out, whole, all_(w_out), "zxy", 3),
        (g_own, w_gate, whole, all_(w_gate), "zyx", 3),
        (u_own, w_up, low, all_(w_up), "zyx", 3),
        (u_own, w_up, high, all_(w_up), "xyz", 3),
        (d_own, w_down, low, all_(w_down), "zyx", 2),
        (d_own, w_down, high, all_(w_down), "zxy", 2),
    )
    gathers = [Gather(*piece, peers, sems, i * n) for i, piece in enumerate(plan)]
    near, far, out, two, late, three = *gathers[:3], gathers[3:5], gathers[5], gathers[6:]
    owns = [
        pltpu.make_async_copy(src, dst.at[0, 0, 0], own_sem.at[i])
        for i, (src, dst) in enumerate(
            ((a_own, w_qkv), (b_own, w_out), (g_own, w_gate), (u_own, w_up), (d_own, w_down))
        )
    ]
    move_a, move_b, move_x, move_seg, move_g, move_u, move_d, move_c = (
        Move(src, dst, moving, i)
        for i, (src, dst) in enumerate(
            (
                (a_in, a_own),
                (b_in, b_own),
                (x_in, x_half),
                (seg_in, seg_own),
                (g_in, g_own),
                (u_in, u_own),
                (d_in, d_own),
                (c_in, c_own),
            )
        )
    )
    meet(peers, exchanged())
    for move in (move_a, move_seg, move_x):
        move.start()

    def tables(here):
        shape = (here.size, 128)
        row = here.start + lax.broadcasted_iota(jnp.int32, shape, 0) + core * half
        row = jnp.where(row >= length, row - length, row)
        angle = row.astype(F32) * inverse[0:1, :]
        front = lax.broadcasted_iota(jnp.int32, shape, 1) % HD < HD // 2
        sin = jnp.sin(angle)
        cos[here, :] = jnp.cos(angle)
        upper[here, :] = jnp.where(front, -sin, 0.0)
        lower[here, :] = jnp.where(front, 0.0, sin)

    move_a.wait()
    near.start()
    far.start()
    near.relay(0)
    owns[0].start()
    in_chunks(length, 64, tables)
    for z in (1, 2, 3):
        near.relay(z)
    for move in (move_b, move_g, move_u, move_d):
        move.start()
    move_seg.wait()
    ids = seg_own[...]
    ids = jnp.where(core == 0, ids, jnp.concatenate([ids[:, half:], ids[:, :half]], axis=1))
    seg_row[...] = ids
    seg_col[...] = jnp.transpose(jnp.broadcast_to(ids[0:1, :], (128, length)))
    move_x.wait()

    def first_norm(i, carry):
        here = pl.ds(pl.multiple_of(i * 128, 128), 128)
        values = to_place(x_half[here, :].astype(F32))
        x_rel[here, :] = values.astype(BF)
        xh[here, :] = normalize(values)[0].astype(BF)
        return carry

    lax.fori_loop(0, half // 128, first_norm, 0)
    swap_xh = remote(
        xh.at[pl.ds(0, half)], xh.at[pl.ds(half, half)], pair_send.at[0], pair_recv.at[0], peers["c"]
    )
    swap_xh.start()
    for z in range(4):
        near.relay_again(z)
        far.relay(z)
    move_b.wait()
    out.start()
    move_g.wait()
    move_u.wait()
    late.start()
    for gather in two:
        gather.start()
    out.relay(0)
    late.relay(0)
    for gather in two:
        gather.relay(0)
    move_d.wait()
    for gather in three:
        gather.start()
    for copy in owns[1:]:
        copy.start()
    swap_xh.wait()
    near.finish()
    owns[0].wait()

    events = {}
    at_step = lambda step, call, *args: events.setdefault(step, []).append((call, args))
    for z in range(4):
        at_step(z, far.relay_again, z)
        if z:
            at_step(z, out.relay, z)
        at_step(5 + z, out.relay_again, z)
        for gather in two:
            if z:
                at_step(1 + 2 * z, gather.relay, z)
            at_step(9 + z, gather.relay_again, z)
        for gather in three:
            at_step(11 + z, gather.relay, z)
    at_step(4, late.relay, 1)
    at_step(5, move_c.start)
    at_step(6, late.relay_again, 0)
    at_step(8, late.relay_again, 1)
    at_step(length // rows * pairs // 2 - 1, far.finish)
    first = lax.broadcasted_iota(jnp.int32, (length, 128), 1) < HD

    def pair(h, carry):
        lanes = pl.ds(pl.multiple_of(h * 128, 128), 128)
        weight = lambda i: w_qkv[
            :, :, :, :, pl.ds(pl.multiple_of((3 * h + i) * 128, 128), 128)
        ].reshape(width, 128)
        tokens = xh[...]
        qf = dotf(tokens, weight(0), NN)
        qf = qf * cos[...] + turn(qf, upper[...], lower[...])
        q[:, lanes] = (qf * (1.0 / math.sqrt(HD))).astype(BF)
        kf = dotf(tokens, weight(1), NN)
        kf = (kf * cos[...] + turn(kf, upper[...], lower[...])).astype(BF)
        k[:, lanes] = kf
        kh[0] = jnp.where(first, kf, jnp.zeros_like(kf))
        kh[1] = jnp.where(first, jnp.zeros_like(kf), kf)
        v[:, lanes] = dotf(tokens, weight(2), NN).astype(BF)

        def block(i, carry):
            for step, calls in events.items():

                @pl.when(h * (length // rows) + i == step)
                def _():
                    for call, args in calls:
                        call(*args)

            at = pl.multiple_of(i * rows, rows)
            q_rows = q[pl.ds(at, rows), lanes]
            same = seg_col[pl.ds(at, rows), 0:1] == seg_row[0:1, :]
            outs = []
            for head in range(2):
                scores = dotf(q_rows, kh[head], NT)
                scores = jnp.where(same, scores, -1e30)
                top = jnp.max(scores, axis=-1, keepdims=True)
                expv = jnp.exp(scores - top)
                total = jnp.sum(expv, axis=-1, keepdims=True)
                low_probs = (expv * (1.0 / total)).astype(BF)
                outs.append(dotf(low_probs, v[:, lanes], NN))
                level = top + jnp.log(total)
                flat = jnp.transpose(jnp.broadcast_to(level, (rows, 128)))
                lse[h, pl.ds(head, 1), pl.ds(at, rows)] = flat[0:1, :]
            o[pl.ds(at, rows), lanes] = jnp.where(first[:rows], outs[0], outs[1]).astype(BF)
            return carry

        return lax.fori_loop(0, length // rows, block, carry)

    lax.fori_loop(0, pairs, pair, 0)
    out.finish()
    owns[1].wait()
    w_o = w_out[...].reshape(width, pairs * 128)

    def project(i, carry):
        at = pl.multiple_of(half + i * rows, rows)
        sent[pl.ds(pl.multiple_of(i * rows, rows), rows), :] = dotf(
            o[pl.ds(at, rows), :], w_o, NT
        ).astype(BF)
        return carry

    lax.fori_loop(0, half // rows, project, 0)

    def project_own(i, carry):
        here = pl.ds(pl.multiple_of(i * rows, rows), rows)
        part[here, :] = dotf(o[here, :], w_o, NT)
        return carry

    give = remote(sent, got, pair_send.at[1], pair_recv.at[1], peers["c"])
    lax.fori_loop(0, half // rows, project_own, 0)
    give.start()
    for copy in writes:
        copy.start()
    move_c.wait()

    def turn_cot(here):
        cot[here, :] = to_place(c_own[here, :].astype(F32)).astype(BF)

    in_chunks(half, 128, turn_cot)
    swap_cot = remote(
        cot.at[pl.ds(0, half)], cot.at[pl.ds(half, half)], pair_send.at[3], pair_recv.at[3], peers["c"]
    )
    swap_cot.start()
    give.wait()

    def second_norm(i, carry):
        here = pl.ds(pl.multiple_of(i * 128, 128), 128)
        values = x_rel[here, :].astype(F32) + (part[here, :] + got[here, :].astype(F32))
        resid[here, :] = values
        xn[here, :] = normalize(values)[0].astype(BF)
        return carry

    lax.fori_loop(0, half // 128, second_norm, 0)
    swap_xn = remote(
        xn.at[pl.ds(0, half)], xn.at[pl.ds(half, half)], pair_send.at[2], pair_recv.at[2], peers["c"]
    )
    swap_xn.start()
    for gather in two + three + [late]:
        gather.finish()
    for copy in owns[2:]:
        copy.wait()
    swap_cot.wait()
    swap_xn.wait()
    for copy in writes:
        copy.wait()


WRITTEN = (0, 1, 2, 3, 5, 6, 7, 10, 12, 13, 14, 15)


def forward_written(*refs):
    count = len(WRITTEN)
    ins, outs, scratch = refs[:9], list(refs[9:29]), refs[29 : -count - 1]
    held, sem = refs[-count - 1 : -1], refs[-1]
    writes = []
    for i, (n, ref) in enumerate(zip(WRITTEN, held)):
        writes.append(pltpu.make_async_copy(ref, outs[n], sem.at[i]))
        outs[n] = ref
    forward_kernel(writes, *ins, *outs, *scratch)


def forward_block(owned, x_half, cot_half, seg, inverse):
    half, width = x_half.shape
    length = 2 * half
    cols = owned[1].shape[1]
    pairs = cols // 128
    units = owned[2].shape[1]
    shard = width // 16
    vmem = pl.BlockSpec(memory_space=pltpu.VMEM)
    any_ = pl.BlockSpec(memory_space=pl.ANY)
    gathered = lambda n: jax.ShapeDtypeStruct(SHARD + (shard, n), BF)
    heads = jax.ShapeDtypeStruct((length, cols), BF)
    flat = jax.ShapeDtypeStruct((length, width), BF)
    table = jax.ShapeDtypeStruct((length, 128), F32)
    shapes = [heads] * 4 + [
        jax.ShapeDtypeStruct((pairs, 2, length), F32),
        flat,
        gathered(3 * cols),
        gathered(cols),
        jax.ShapeDtypeStruct((half, width), F32),
        flat,
        jax.ShapeDtypeStruct((half, width), BF),
        flat,
    ]
    shapes += [table] * 4 + [jax.ShapeDtypeStruct((8, length), F32)] + [gathered(units)] * 3
    return pl.pallas_call(
        forward_written,
        in_specs=[any_] * 8 + [vmem],
        out_specs=[any_ if i in WRITTEN + (17, 18, 19) else vmem for i in range(20)],
        out_shape=shapes,
        scratch_shapes=[pltpu.VMEM((shard, 3 * cols), BF), pltpu.VMEM((shard, cols), BF)]
        + [pltpu.VMEM((shard, units), BF)] * 3
        + [
            pltpu.VMEM((half, width), BF),
            pltpu.VMEM((8, length), F32),
            pltpu.VMEM((2, length, 128), BF),
            pltpu.VMEM((half, width), BF),
            pltpu.VMEM((half, width), F32),
            pltpu.VMEM((half, width), BF),
            pltpu.VMEM((half, width), BF),
            pltpu.SemaphoreType.DMA((8 * Gather.MESSAGES,)),
            pltpu.SemaphoreType.DMA((8 * Gather.MESSAGES,)),
            pltpu.SemaphoreType.DMA((4,)),
            pltpu.SemaphoreType.DMA((4,)),
            pltpu.SemaphoreType.DMA((5,)),
        ]
        + move_sems(8)
        + [pltpu.VMEM(shapes[i].shape, shapes[i].dtype) for i in WRITTEN]
        + [pltpu.SemaphoreType.DMA((len(WRITTEN),))],
        compiler_params=pltpu.CompilerParams(
            collective_id=0, has_side_effects=True, vmem_limit_bytes=60 << 20
        ),
        name="forward_block",
    )(*owned, x_half, cot_half, seg, inverse)


class Reduce:
    MESSAGES = 12
    ORDER = (2, 3, 1, 0)

    def __init__(self, parts, near, rows, axes, peers, sems, base, bufs, out):
        self.parts, self.near, self.rows, self.axes, self.peers = parts, near, rows, axes, peers
        self.send_sem, self.recv_sem = sems
        self.base = base
        self.one, self.two, self.three, self.sum = bufs
        self.out = out

    def link(self, i, src, dst, peer):
        n = self.base + i
        return remote(src, dst, self.send_sem.at[n], self.recv_sem.at[n], peer)

    def first(self, z):
        if self.axes == "xy":
            src = self.parts.at[z, :, 1, self.rows]
        else:
            src = self.parts.at[z, 1, :, self.rows]
        return self.link(z, src, self.one.at[z], self.peers[self.axes[1]])

    def second(self, z):
        return self.link(4 + z, self.one.at[z, 1], self.two.at[z], self.peers[self.axes[0]])

    def third(self, z):
        return self.link(7 + z, self.two.at[z], self.three.at[z - 1], self.peers["z%d" % z])

    def start(self):
        for z in self.ORDER:
            self.first(z).start()

    def add_first(self, z):
        self.first(z).wait_recv()
        self.one[z] = (self.one[z].astype(F32) + self.near(z).astype(F32)).astype(BF)

    def relay_first(self, z):
        self.add_first(z)
        self.second(z).start()

    def resume(self):
        for z in self.ORDER:
            self.second(z).start()

    def relay_second(self, z):
        self.second(z).wait_recv()
        self.two[z] = (self.two[z].astype(F32) + self.one[z, 0].astype(F32)).astype(BF)
        if z:
            self.third(z).start()

    def last(self):
        moved, peer = exchanged()
        return moved, self.link(11, self.sum, self.out, peer)

    def total(self):
        total = self.two[0].astype(F32)
        for z in (1, 2, 3):
            self.third(z).wait_recv()
            total = total + self.three[z - 1].astype(F32)
        return total

    def finish(self):
        self.sum[...] = self.total().astype(BF)
        moved, copy = self.last()

        @pl.when(moved)
        def _():
            copy.start()

        @pl.when(jnp.logical_not(moved))
        def _():
            self.out[...] = self.sum[...]

    def sent(self):
        hops = (self.second,) if self.parts is None else (self.first, self.second)
        thirds = [self.third(z) for z in (1, 2, 3)]
        return [hop(z) for z in range(4) for hop in hops] + thirds

    def close(self):
        for copy in self.sent():
            copy.wait_send()
        moved, copy = self.last()

        @pl.when(moved)
        def _():
            copy.wait()


class ReduceAlongZ(Reduce):
    def first(self, z):
        src = self.parts.at[z, :, :, self.rows]
        return self.link(z - 1, src, self.one.at[z - 1], self.peers["z%d" % z])

    def second(self):
        return self.link(3, self.two.at[:, 1], self.three.at[0:2], self.peers["y"])

    def third(self):
        return self.link(4, self.three.at[1], self.three.at[2], self.peers["x"])

    def start(self):
        for z in (2, 3, 1):
            self.first(z).start()

    def relay_first(self):
        total = self.near().astype(F32)
        for z in (1, 2, 3):
            self.first(z).wait_recv()
            total = total + self.one[z - 1].astype(F32)
        self.two[...] = total.astype(BF)
        self.second().start()

    def relay_second(self):
        self.second().wait_recv()
        for x in (0, 1):
            self.three[x] = (self.three[x].astype(F32) + self.two[x, 0].astype(F32)).astype(BF)
        self.third().start()

    def total(self):
        self.third().wait_recv()
        return self.three[0].astype(F32) + self.three[2].astype(F32)

    def sent(self):
        return [self.first(z) for z in (1, 2, 3)] + [self.second(), self.third()]


def mlp_kernel(
    reads, writes, down_in, xn, cot, w_gate, w_up, resid,
    result, resid_grad, attn_cot, d_gate, d_up, d_low, d_high,
    w_down, d_down, hidden, act, slope_up, gate_grad, up_grad, own, sent, got, placed,
    send_sem, recv_sem, last_send, last_recv, first_send, first_recv, own_sem, *moving,
):
    length, width = xn.shape
    half = length // 2
    units = w_gate.shape[1]
    peers = {axis: partners()[axis] for axis in "xyc"}
    move = Move(placed, result, moving, 0)
    low, high = pl.ds(0, 32), pl.ds(32, 32)
    most, few = pl.ds(0, 48), pl.ds(48, 16)
    at_low = lambda ref, z, x: ref.at[z, x, :, low]
    at_high = lambda ref, z, y: ref.at[z, :, y, high]
    last = []
    for z in range(4):
        for i, (part, axis) in enumerate(((at_low, "x"), (at_high, "y"))):
            n = 2 * z + i
            last.append(
                remote(
                    part(down_in, z, 0), part(w_down, z, 1), last_send.at[n], last_recv.at[n], peers[axis]
                )
            )
    every = pl.ds(0, 4)
    owns = [
        pltpu.make_async_copy(part(down_in, every, 0), part(w_down, every, 0), own_sem.at[i])
        for i, part in enumerate((at_low, at_high))
    ]
    sems = (first_send, first_recv)
    n = Reduce.MESSAGES
    reduce_low = Reduce(
        d_down, lambda z: d_down[z, 0, :, 0:48], most, "yx", peers, sems, 0, (d_low, None, None, None), None
    )
    reduce_high = Reduce(
        d_down, lambda z: d_down[z, :, 0, 48:64], few, "xy", peers, sems, n, (d_high, None, None, None), None
    )
    for copy in reads:
        copy.start()
    meet(peers, exchanged())
    for copy in last + owns:
        copy.start()
    for copy in reads:
        copy.wait()
    back, front = pl.ds(half, half), pl.ds(0, half)

    def gate_and_up(rows):
        def step(cols):
            gate = dotf(xn[rows, :], w_gate[:, cols], NN)
            up = dotf(xn[rows, :], w_up[:, cols], NN)
            value, slope = gelu_parts(gate)
            hidden[rows, cols] = (value * up).astype(BF)
            act[rows, cols] = value
            slope_up[rows, cols] = up * slope

        in_chunks(units, 256, step)

    def units_back(rows):
        def step(cols):
            down = w_down[:, :, :, :, cols].reshape(width, cols.size)
            grad = dotf(cot[rows, :], down, NN).astype(BF).astype(F32)
            gate_grad[rows, cols] = (grad * slope_up[rows, cols]).astype(BF)
            up_grad[rows, cols] = (grad * act[rows, cols]).astype(BF)

        in_chunks(units, 256, step)

    def sums(rows, put):
        def step(z, carry):
            here = pl.ds(pl.multiple_of(z * 256, 256), 256)
            down = w_down[z].reshape(256, units)
            put[0, :, here] = dotf(hidden[rows, :], down, NT).astype(put.dtype)
            both = dotf(gate_grad[rows, :], w_gate[here, :], NT)
            both = both + dotf(up_grad[rows, :], w_up[here, :], NT)
            put[1, :, here] = both.astype(put.dtype)
            return carry

        lax.fori_loop(0, width // 256, step, 0)

    gate_and_up(back)
    gate_and_up(front)
    for z in Reduce.ORDER:
        left = jnp.transpose(cot[:, z * 256 : (z + 1) * 256])
        d_down[z] = dotf(left, hidden[...], NN).astype(BF).reshape(2, 2, 64, units)
        reduce_low.first(z).start()
        reduce_high.first(z).start()
    for copy in owns:
        copy.wait()
    for copy in last:
        copy.wait()
    units_back(back)
    sums(back, sent)
    give = remote(sent, got, send_sem.at[0], recv_sem.at[0], peers["c"])
    give.start()
    units_back(front)
    sums(front, own)
    give.wait()

    def finish(here):
        values = resid[here, :]
        mlp = own[0, here, :] + got[0, here, :].astype(F32)
        placed[here, :] = to_place(values + mlp).astype(BF)
        xhat, scale = normalize(values)
        back = normalize_back(own[1, here, :] + got[1, here, :].astype(F32), xhat, scale)
        grad = cot[here, :].astype(F32) + back
        resid_grad[here, :] = grad
        attn_cot[here, :] = grad.astype(BF)

    in_chunks(half, 64, finish)
    swap = remote(
        attn_cot.at[pl.ds(0, half)], attn_cot.at[pl.ds(half, half)], send_sem.at[1], recv_sem.at[1], peers["c"]
    )
    swap.start()
    move.start()

    def weights(here):
        left = jnp.transpose(xn[:, here])
        d_gate[here, :] = dotf(left, gate_grad[...], NN).astype(BF)
        d_up[here, :] = dotf(left, up_grad[...], NN).astype(BF)

    in_chunks(width, 256, weights)
    writes[0].start()
    for z in Reduce.ORDER:
        reduce_low.add_first(z)
        reduce_high.add_first(z)
    for z in range(4):
        reduce_low.first(z).wait_send()
        reduce_high.first(z).wait_send()
    for copy in writes[1:]:
        copy.start()
    swap.wait()
    move.wait()
    for copy in writes:
        copy.wait()


def mlp_staged(*refs):
    ins, outs, scratch = refs[1:6], list(refs[6:13]), refs[13:-10]
    held, read_sem, write_sem = refs[-10:-2], refs[-2], refs[-1]
    reads = [pltpu.make_async_copy(a, b, read_sem.at[i]) for i, (a, b) in enumerate(zip(ins, held))]
    writes = []
    for i, (n, ref) in enumerate(zip((1, 3, 4), held[5:])):
        writes.append(pltpu.make_async_copy(ref, outs[n], write_sem.at[i]))
        outs[n] = ref
    mlp_kernel(reads, writes, refs[0], *held[:5], *outs, *scratch)


def mlp_block(down_in, xn, cot, w_gate, w_up, resid):
    length, width = xn.shape
    half = length // 2
    units = w_gate.shape[1]
    shard = width // 16
    vmem = pl.BlockSpec(memory_space=pltpu.VMEM)
    any_ = pl.BlockSpec(memory_space=pl.ANY)
    grads = jax.ShapeDtypeStruct((width, units), BF)
    dma = lambda n: pltpu.SemaphoreType.DMA((n,))
    return pl.pallas_call(
        mlp_staged,
        in_specs=[any_] * 6,
        out_specs=[any_, any_, vmem, any_, any_, vmem, vmem],
        out_shape=[
            jax.ShapeDtypeStruct((half, width), BF),
            jax.ShapeDtypeStruct((half, width), F32),
            jax.ShapeDtypeStruct((length, width), BF),
            grads,
            grads,
            jax.ShapeDtypeStruct((4, 2, shard * 3 // 4, units), BF),
            jax.ShapeDtypeStruct((4, 2, shard // 4, units), BF),
        ],
        scratch_shapes=[pltpu.VMEM(SHARD + (shard, units), BF)] * 2
        + [
            pltpu.VMEM((length, units), BF),
            pltpu.VMEM((length, units), F32),
            pltpu.VMEM((length, units), F32),
            pltpu.VMEM((length, units), BF),
            pltpu.VMEM((length, units), BF),
            pltpu.VMEM((2, half, width), F32),
            pltpu.VMEM((2, half, width), BF),
            pltpu.VMEM((2, half, width), BF),
            pltpu.VMEM((half, width), BF),
        ]
        + [dma(2), dma(2), dma(8), dma(8), dma(2 * Reduce.MESSAGES), dma(2 * Reduce.MESSAGES), dma(2)]
        + move_sems(1)
        + [pltpu.VMEM(a.shape, a.dtype) for a in (xn, cot, w_gate, w_up, resid)]
        + [pltpu.VMEM((half, width), F32)]
        + [pltpu.VMEM((width, units), BF)] * 2
        + [dma(5), dma(3)],
        compiler_params=pltpu.CompilerParams(
            collective_id=1, has_side_effects=True, vmem_limit_bytes=63 << 20
        ),
        name="mlp_block",
    )(down_in, xn, cot, w_gate, w_up, resid)


def backward_kernel(
    reads, d_gate, d_up, d_low, d_high, q, k, v, o, lse, attn_cot, w_qkv, w_out, xh, x_half, resid_grad,
    cos, upper, lower, seg_col, seg_row,
    token_grad, s_gate, s_up_low, s_up_high, s_down_low, s_down_high, s_out, s_near, s_far,
    d_out, d_near, d_far, pg, heads_grad, kh, dk, dv, own, sent, got, placed,
    near_gate, near_up_low, near_up_high,
    *rest,
):
    bufs = [rest[4 * i : 4 * i + 4] for i in range(3)]
    bufs += [(first,) + rest[12 + 3 * i : 15 + 3 * i] for i, first in enumerate((d_low, d_high))]
    bufs += [rest[18 + 4 * i : 22 + 4 * i] for i in range(3)]
    send_sem, recv_sem, pair_send, pair_recv, near_sem, *moving = rest[30:]
    length, width = xh.shape
    half = length // 2
    cols = q.shape[1]
    pairs = cols // 128
    rows = 256
    peers = partners()
    sems = (send_sem, recv_sem)
    n = Reduce.MESSAGES
    whole, low, high = pl.ds(0, 64), pl.ds(0, 32), pl.ds(32, 32)
    held = lambda ref: (lambda z: ref[z])
    plan = (
        (Reduce, d_gate, held(near_gate), whole, "yx", s_gate),
        (Reduce, d_up, held(near_up_low), low, "xy", s_up_low),
        (ReduceAlongZ, d_up, lambda: near_up_high[...], high, None, s_up_high),
        (Reduce, None, None, None, "yx", s_down_low),
        (Reduce, None, None, None, "xy", s_down_high),
        (Reduce, d_out, lambda z: d_out[z, 0], whole, "yx", s_out),
        (Reduce, d_near, lambda z: d_near[z, 0], whole, "yx", s_near),
        (Reduce, d_far, lambda z: d_far[z, 0], whole, "yx", s_far),
    )
    parts = [
        kind(src, near, rows_, axes, peers, sems, i * n, bufs[i], out)
        for i, (kind, src, near, rows_, axes, out) in enumerate(plan)
    ]
    gate, up_low, up_high, down_low, down_high, out, near, far = parts
    nears = [
        pltpu.make_async_copy(src, dst, near_sem.at[i])
        for i, (src, dst) in enumerate(
            (
                (d_gate.at[:, 0], near_gate),
                (d_up.at[:, :, 0, low], near_up_low),
                (d_up.at[0, :, :, high], near_up_high),
            )
        )
    ]
    for copy in nears + reads:
        copy.start()
    meet(peers, exchanged())
    up_high.start()
    down_low.resume()
    down_high.resume()
    gate.start()
    up_low.start()
    for copy in reads:
        copy.wait()

    def heads(here):
        heads_grad[here, :] = dotf(attn_cot[here, :], w_out[...], NN).astype(BF)

    in_chunks(length, 256, heads)

    def out_weights(z, carry):
        here = pl.ds(pl.multiple_of(z * 256, 256), 256)
        value = dotf(jnp.transpose(attn_cot[:, here]), o[...], NN).astype(BF)
        d_out[z] = value.reshape(2, 2, 64, cols)
        return carry

    lax.fori_loop(0, width // 256, out_weights, 0)
    out.start()
    for copy in nears:
        copy.wait()
    for z in Reduce.ORDER:
        down_low.relay_second(z)
        down_high.relay_second(z)

    events = {}
    for i, z in enumerate(Reduce.ORDER):
        events.setdefault((3, 6, 10, 13)[i], []).append(lambda z=z: gate.relay_first(z))
        events.setdefault((5, 7, 8, 10)[i], []).append(lambda z=z: up_low.relay_first(z))
    for z in Reduce.ORDER[:2]:
        events.setdefault(14, []).append(lambda z=z: gate.relay_second(z))
    events.setdefault(9, []).append(up_high.relay_first)
    events.setdefault(13, []).append(up_high.relay_second)

    def weights(ref, at):
        def step(z, carry):
            left = jnp.transpose(xh[:, pl.ds(pl.multiple_of(z * 256, 256), 256)])
            value = dotf(left, pg[:, at : at + ref.shape[-1]], NN).astype(BF)
            ref[z] = value.reshape(2, 2, 64, ref.shape[-1])
            return carry

        lax.fori_loop(0, width // 256, step, 0)

    lane = lax.broadcasted_iota(jnp.int32, (length, 128), 1)
    first = lane < HD

    def pair(h, carry):
        lanes = pl.ds(pl.multiple_of(h * 128, 128), 128)
        third = lambda i: pl.ds(pl.multiple_of((3 * h + i) * 128, 128), 128)
        kf = k[:, lanes]
        none = jnp.zeros_like(kf)
        kh[0] = jnp.where(first, kf, none)
        kh[1] = jnp.where(first, none, kf)
        dk[...] = jnp.zeros_like(dk)
        dv[...] = jnp.zeros_like(dv)

        def block(i, carry):
            for step, calls in events.items():

                @pl.when(h * (length // rows) + i == step)
                def _():
                    for call in calls:
                        call()

            at = pl.multiple_of(i * rows, rows)
            here = pl.ds(at, rows)
            q_rows = q[here, lanes]
            g_rows = heads_grad[here, lanes]
            same = seg_col[:, 0:1] == seg_row[0:1, here]
            prod = g_rows.astype(F32) * o[here, lanes].astype(F32)
            f = first[:rows]
            blank = jnp.zeros_like(q_rows)
            dq = jnp.zeros((rows, 128), F32)
            for head in range(2):
                mine = f if head == 0 else jnp.logical_not(f)
                q_head = jnp.where(mine, q_rows, blank)
                g_head = jnp.where(mine, g_rows, blank)
                delta = lax.dot_general(
                    jnp.ones((8, 128), F32),
                    jnp.where(mine, prod, 0.0),
                    (NT, ((), ())),
                    precision=lax.Precision.HIGHEST,
                    preferred_element_type=F32,
                )[0:1, :]
                scores = dotf(k[:, lanes], q_head, NT)
                level = lse[h, pl.ds(head, 1), here]
                probs = jnp.where(same, jnp.exp(scores - level), 0.0)
                dv[...] += dotf(probs.astype(BF), g_head, NN)
                dp = dotf(v[:, lanes], g_head, NT)
                ds = (probs * (dp - delta)).astype(BF)
                dk[...] += dotf(ds, q_head, NN)
                dq = dq + dotf(ds, kh[head], TN)
            dq = dq * (1.0 / math.sqrt(HD))
            c, a, b = cos[here, :], upper[here, :], lower[here, :]
            pg[here, third(0)] = (dq * c - turn(dq, a, b)).astype(BF)
            return carry

        lax.fori_loop(0, length // rows, block, 0)
        dkf = dk[...]
        pg[:, third(1)] = (dkf * cos[...] - turn(dkf, upper[...], lower[...])).astype(BF)
        pg[:, third(2)] = dv[...].astype(BF)

        @pl.when(h == pairs // 2 - 1)
        def _():
            weights(d_near, 0)
            near.start()

        return carry

    lax.fori_loop(0, pairs, pair, 0)
    weights(d_far, d_near.shape[-1])
    far.start()

    def back(tokens, put):
        def step(here):
            put[:, here] = dotf(pg[tokens, :], w_qkv[here, :], NT).astype(put.dtype)

        in_chunks(width, 256, step)

    for z in Reduce.ORDER[2:]:
        gate.relay_second(z)
    for z in Reduce.ORDER:
        out.relay_first(z)
    back(pl.ds(half, half), sent)
    give = remote(sent, got, pair_send.at[0], pair_recv.at[0], peers["c"])
    give.start()
    for z in Reduce.ORDER:
        up_low.relay_second(z)
    back(pl.ds(0, half), own)
    for z in Reduce.ORDER:
        out.relay_second(z)
    for part in (down_low, down_high):
        part.finish()
    give.wait()

    def finish(here):
        xhat, scale = normalize(to_place(x_half[here, :].astype(F32)))
        f = own[here, :] + got[here, :].astype(F32)
        value = resid_grad[here, :] + normalize_back(f, xhat, scale)
        placed[here, :] = to_place(value).astype(BF)

    in_chunks(half, 64, finish)
    move = Move(placed, token_grad, moving, 0)
    move.start()
    for z in Reduce.ORDER:
        near.relay_first(z)
    for part in (gate, up_high, up_low):
        part.finish()
    for z in Reduce.ORDER:
        far.relay_first(z)
        near.relay_second(z)
    out.finish()
    for z in Reduce.ORDER:
        far.relay_second(z)
    near.finish()
    far.finish()
    for part in parts:
        part.close()
    move.wait()


def backward_staged(*refs):
    held, sem = refs[-17:-1], refs[-1]
    reads = [pltpu.make_async_copy(a, b, sem.at[i]) for i, (a, b) in enumerate(zip(refs[4:20], held))]
    backward_kernel(reads, *refs[:4], *held, *refs[20:-17])


def backward_block(grads, heads, lse, attn_cot, w_qkv, w_out, xh, x_half, resid_grad, tables, seg_col, seg_row):
    length, width = xh.shape
    half = length // 2
    cols = heads[0].shape[1]
    units = grads[0].shape[1]
    shard = width // 16
    vmem = pl.BlockSpec(memory_space=pltpu.VMEM)
    any_ = pl.BlockSpec(memory_space=pl.ANY)
    wide = 3 * cols // 2
    sizes = [(shard, units), (shard // 2, units), (shard // 2, units)]
    sizes += [g.shape[2:] for g in grads[2:]]
    sizes += [(shard, cols), (shard, wide), (shard, wide)]
    along_z, begun = (2,), (3, 4)
    bufs = []
    for i, size in enumerate(sizes):
        if i in along_z:
            lead = (3, 2, 2), (2, 2), (3,)
        else:
            lead = (4, 2), (4,), (3,)
        bufs += [pltpu.VMEM(n + size, BF) for n in lead[i in begun :] + ((),)]
    nears = [pltpu.VMEM(((2, 2) if i in along_z else (4, 2)) + size, BF) for i, size in enumerate(sizes[:3])]
    messages = 8 * Reduce.MESSAGES
    operands = (*heads, lse, attn_cot, w_qkv, w_out, xh, x_half, resid_grad, *tables, seg_col, seg_row)
    return pl.pallas_call(
        backward_staged,
        in_specs=[any_] * 2 + [vmem] * 2 + [any_] * 16,
        out_specs=[vmem] * 9,
        out_shape=[jax.ShapeDtypeStruct((half, width), BF)]
        + [jax.ShapeDtypeStruct(size, BF) for size in sizes],
        scratch_shapes=[pltpu.VMEM(SHARD + (shard, n), BF) for n in (cols, wide, wide)]
        + [
            pltpu.VMEM((length, 3 * cols), BF),
            pltpu.VMEM((length, cols), BF),
            pltpu.VMEM((2, length, 128), BF),
            pltpu.VMEM((length, 128), F32),
            pltpu.VMEM((length, 128), F32),
            pltpu.VMEM((half, width), F32),
            pltpu.VMEM((half, width), BF),
            pltpu.VMEM((half, width), BF),
            pltpu.VMEM((half, width), BF),
        ]
        + nears
        + bufs
        + [
            pltpu.SemaphoreType.DMA((messages,)),
            pltpu.SemaphoreType.DMA((messages,)),
            pltpu.SemaphoreType.DMA((1,)),
            pltpu.SemaphoreType.DMA((1,)),
            pltpu.SemaphoreType.DMA((3,)),
        ]
        + move_sems(1)
        + [pltpu.VMEM(a.shape, a.dtype) for a in operands]
        + [pltpu.SemaphoreType.DMA((16,))],
        compiler_params=pltpu.CompilerParams(
            collective_id=2, has_side_effects=True, vmem_limit_bytes=60 << 20
        ),
        name="backward_block",
    )(
        *(g.reshape(SHARD + (shard, units)) for g in grads[:2]), *grads[2:],
        *operands,
    )


class Chips:
    def sum_tensor(self, value):
        pairs = [(2 * i + y, 2 * i + 1 - y) for i in range(16) for y in range(2)]
        return value + lax.ppermute(value, ("dp", "tensor"), pairs)


class Axes:
    def gather_rows(self, value):
        return lax.all_gather(value, "tensor", axis=0, tiled=True)

    def scatter_rows(self, value):
        return lax.psum_scatter(value.astype(BF), "tensor", scatter_dimension=0, tiled=True).astype(F32)

    def reduce(self, a, b):
        return tuple(
            lax.psum_scatter(w.astype(BF), "dp", scatter_dimension=0, tiled=True).astype(F32)
            for w in (a, b)
        )

    def sum_tensor(self, value):
        return lax.psum(value, "tensor")


def normalize(values):
    centred = values - jnp.mean(values, axis=-1, keepdims=True)
    scale = lax.rsqrt(jnp.mean(centred * centred, axis=-1, keepdims=True) + EPS)
    return centred * scale, scale


def normalize_back(f, xhat, scale):
    return scale * (
        f
        - jnp.mean(f, axis=-1, keepdims=True)
        - xhat * jnp.mean(f * xhat, axis=-1, keepdims=True)
    )


def gelu_parts(gate):
    half_erf = 0.5 * (1.0 + lax.erf(gate * (1.0 / math.sqrt(2.0))))
    density = jnp.exp(-0.5 * gate * gate) * (1.0 / math.sqrt(2.0 * math.pi))
    return gate * half_erf, half_erf + gate * density


def make_local(comm_type):
    def local(tokens, segments, w_qkv, w_out, w_in, w_down, g_attn, g_mlp, cotangent):
        comm = comm_type()
        paired = comm_type is Chips
        shard = w_qkv.shape[0]
        cols = w_qkv.shape[2]
        units = w_in.shape[2]
        low = 128 * (units // 256)
        pad = 128 * pl.cdiv(units, 128) - units
        gain_one = g_attn.astype(F32)[:, None]
        gain_two = g_mlp.astype(F32)[:, None]
        scaled = lambda w, g: (w.astype(F32) * g).astype(BF)
        padded = lambda w: jnp.pad(w, ((0, 0), (0, pad)))
        down_rows = w_down.T
        a_one = jnp.concatenate([scaled(w_qkv[:, 0], gain_one), scaled(w_qkv[:, 1], gain_one)], axis=1)
        b_one = jnp.concatenate([scaled(w_qkv[:, 2], gain_one), w_out.T], axis=1)
        own_gate, own_up = scaled(w_in[:, 0], gain_two), scaled(w_in[:, 1], gain_two)

        owned = (a_one, b_one, own_gate, own_up, down_rows)
        if paired:
            by_pair = scaled(w_qkv, gain_one[:, None]).reshape(shard, 3, cols // 128, 128).swapaxes(1, 2)
            owned = (by_pair.reshape(shard, 3 * cols), w_out.T) + tuple(padded(w) for w in owned[2:])
            seg = jnp.broadcast_to(segments.astype(F32), (8, segments.shape[1]))
            inverse = jnp.broadcast_to(jnp.tile(rope_rates(), 4), (8, 128))
            (
                q, k, v, o, lse, xh, qkv_all, out_all, resid, xn, x_half, cot_all, *tables, seg_col, seg_row,
                w_gate, w_up, w_dn,
            ) = forward_block(owned, tokens[0], cotangent[0], seg, inverse)
            qkv_all, out_all, w_gate, w_up = (
                w.reshape(-1, w.shape[-1]) for w in (qkv_all, out_all, w_gate, w_up)
            )
        else:
            w_qk, w_vo, w_gate, w_up, w_dn = (
                lax.all_gather(w, "dp", axis=0, tiled=True) for w in owned
            )
            w_o = w_vo[:, cols:]
            seg_col, seg_row = segments[0][:, None], segments
            cot = cotangent[0]
            cot_all = comm.gather_rows(cot)
            tables = rope_tables(jnp.arange(segments.shape[1]))
            x_in = tokens[0].astype(F32)
            xh_one, scale_one = normalize(x_in)
            xh = comm.gather_rows(xh_one.astype(BF))
            o, q, k, v, lse = attn_fwd(xh, w_qk, w_vo, tables, seg_col, seg_row)
            resid = x_in + comm.scatter_rows(dotf(o, w_o, NT))
            xh_two, scale_two = normalize(resid)
            xn = comm.gather_rows(xh_two.astype(BF))
        if paired:
            result, resid_grad, attn_cot, *grads = mlp_block(w_dn, xn, cot_all, w_gate, w_up, resid)
        else:
            gate, up = dotf(xn, w_gate, NN), dotf(xn, w_up, NN)
            act, slope = gelu_parts(gate)
            hidden = (act * up).astype(BF)
            mlp = comm.scatter_rows(dotf(hidden, w_dn, NT))
            result = (resid + mlp).astype(BF)
            hidden_grad = dotf(cot_all, w_dn, NN).astype(BF).astype(F32)
            gate_grad = (hidden_grad * up * slope).astype(BF)
            up_grad = (hidden_grad * act).astype(BF)
            f_two = comm.scatter_rows(dotf(gate_grad, w_gate, NT) + dotf(up_grad, w_up, NT))
            resid_grad = cot.astype(F32) + normalize_back(f_two, xh_two, scale_two)
            attn_cot = comm.gather_rows(resid_grad.astype(BF))
            d_down = dotf(cot_all, hidden, TN)
            d_gate, d_up = dotf(xn, gate_grad, TN), dotf(xn, up_grad, TN)

        if paired:
            token_grad, *sums = backward_block(
                grads, (q, k, v, o), lse, attn_cot, qkv_all, out_all, xh, x_half,
                resid_grad, tables, seg_col, seg_row,
            )
            token_grad = token_grad.astype(F32)
            s_gate, up_low, up_high, s_low, s_high, s_out, near, far = (w.astype(F32) for w in sums)
            s_up = jnp.concatenate([up_low, up_high], axis=0)
            qkv_raw = jnp.concatenate([near, far], axis=1).reshape(shard, cols // 128, 3, 128)
            qkv_raw = qkv_raw.swapaxes(1, 2).reshape(shard, 3, cols)
            in_raw = jnp.stack([s_gate[:, :units], s_up[:, :units]], axis=1)
            down_sum = jnp.concatenate([s_low[:, :units], s_high[:, :units]], axis=0).T
        else:
            wide = lambda g, d: jnp.concatenate([padded(g), d], axis=1)
            two_a, two_b = comm.reduce(wide(d_gate, d_down[:, :low]), wide(d_up, d_down[:, low:]))

            heads_grad = dotf(attn_cot, w_o, NN).astype(BF)
            pg = attn_bwd(q, k, v, o, heads_grad, lse, tables, seg_col, seg_row)
            d_out = dotf(attn_cot, o, TN)
            d_q, d_k, d_v = (dotf(xh, pg[i], TN) for i in range(3))
            one_a, one_b = comm.reduce(
                jnp.concatenate([d_q, d_k], axis=1), jnp.concatenate([d_v, d_out], axis=1)
            )
            f_one = comm.scatter_rows(
                dotf(pg[0], w_qk[:, :cols], NT)
                + dotf(pg[1], w_qk[:, cols:], NT)
                + dotf(pg[2], w_vo[:, :cols], NT)
            )
            token_grad = resid_grad + normalize_back(f_one, xh_one, scale_one)
            in_raw = jnp.stack([two_a[:, :units], two_b[:, :units]], axis=1)
            down_sum = jnp.concatenate([two_a[:, units + pad :], two_b[:, units + pad :]], axis=1).T
            s_out = one_b[:, cols:]
            qkv_raw = jnp.stack([one_a[:, :cols], one_a[:, cols:], one_b[:, :cols]], axis=1)

        gains = jnp.stack(
            [
                jnp.sum(qkv_raw * w_qkv.astype(F32), axis=(1, 2)),
                jnp.sum(in_raw * w_in.astype(F32), axis=(1, 2)),
            ]
        )
        gains = comm.sum_tensor(gains)
        return (
            result[None],
            token_grad[None],
            gains[0],
            gains[1],
            qkv_raw * gain_one[:, :, None],
            s_out.T,
            in_raw * gain_two[:, :, None],
            down_sum,
        )

    return local


def solution(mesh):
    paired = mesh.shape["dp"] == 16 and mesh.shape["tensor"] == 2
    return jax.shard_map(
        make_local(Chips if paired else Axes),
        mesh=mesh,
        in_specs=(
            P("dp", "tensor", None),
            P("dp", None),
            P("dp", None, "tensor"),
            P("tensor", "dp"),
            P("dp", None, "tensor"),
            P("tensor", "dp"),
            P("dp"),
            P("dp"),
            P("dp", "tensor", None),
        ),
        out_specs=(
            P("dp", "tensor", None),
            P("dp", "tensor", None),
            P("dp"),
            P("dp"),
            P("dp", None, "tensor"),
            P("tensor", "dp"),
            P("dp", None, "tensor"),
            P("tensor", "dp"),
        ),
        check_vma=False,
    )
```

```python
import math

import jax
import jax.numpy as jnp
from jax import lax
from jax.experimental import pallas as pl
from jax.experimental.pallas import tpu as pltpu
from jax.sharding import PartitionSpec as P

HD = 64
EPS = 1e-05
ROTARY_BASE = 160000.0
BF = jnp.bfloat16
F32 = jnp.float32


def dotf(a, b, dims):
    return lax.dot_general(a, b, (dims, ((), ())), preferred_element_type=F32)


NN = ((1,), (0,))
NT = ((1,), (1,))
TN = ((0,), (0,))


def rope_rates():
    return 1.0 / ROTARY_BASE ** (jnp.arange(HD // 2).astype(F32) * (2.0 / HD))


def rope_tables(positions):
    angles = positions.astype(F32)[:, None] * rope_rates()[None, :]
    cos, sin = jnp.cos(angles), jnp.sin(angles)
    zero = jnp.zeros_like(sin)
    cosine = jnp.concatenate([cos] * 4, axis=-1)
    upper = jnp.concatenate([-sin, zero] * 2, axis=-1)
    lower = jnp.concatenate([zero, sin] * 2, axis=-1)
    return cosine, upper, lower


def turn(u, upper, lower):
    return pltpu.roll(u, 128 - HD // 2, 1) * upper + pltpu.roll(u, HD // 2, 1) * lower


def attn_fwd_kernel(xh, wq, wk, wv, cos, upper, lower, seg_col, seg_row, o, q, k, v, lse, kh):
    length = xh.shape[0]
    rows = min(256, length)
    lane = lax.broadcasted_iota(jnp.int32, (length, 128), 1)
    first = lane < HD
    tokens = xh[...]
    qf = dotf(tokens, wq[...], NN)
    qf = qf * cos[...] + turn(qf, upper[...], lower[...])
    q[...] = (qf * (1.0 / math.sqrt(HD))).astype(BF)
    kf = dotf(tokens, wk[...], NN)
    kf = (kf * cos[...] + turn(kf, upper[...], lower[...])).astype(BF)
    k[...] = kf
    kh[0] = jnp.where(first, kf, jnp.zeros_like(kf))
    kh[1] = jnp.where(first, jnp.zeros_like(kf), kf)
    v[...] = dotf(tokens, wv[...], NN).astype(BF)

    def block(i, carry):
        at = pl.multiple_of(i * rows, rows)
        q_rows = q[pl.ds(at, rows), :]
        same = seg_col[pl.ds(at, rows), :] == seg_row[...]
        outs = []
        for head in range(2):
            scores = dotf(q_rows, kh[head], NT)
            scores = jnp.where(same, scores, -1e30)
            top = jnp.max(scores, axis=-1, keepdims=True)
            expv = jnp.exp(scores - top)
            total = jnp.sum(expv, axis=-1, keepdims=True)
            low = (expv * (1.0 / total)).astype(BF)
            outs.append(dotf(low, v[...], NN))
            level = top + jnp.log(total)
            flat = jnp.transpose(jnp.broadcast_to(level, (rows, 128)))
            lse[0, pl.ds(head, 1), pl.ds(at, rows)] = flat[0:1, :]
        o[pl.ds(at, rows), :] = jnp.where(first[:rows], outs[0], outs[1]).astype(BF)
        return carry

    lax.fori_loop(0, length // rows, block, 0)


def attn_fwd(xh, w_qk, w_vo, tables, seg_col, seg_row):
    length, width = xh.shape
    pairs = w_qk.shape[1] // 256
    whole = lambda a: pl.BlockSpec(a.shape, lambda h: (0,) * a.ndim)
    col = lambda off: pl.BlockSpec((width, 128), lambda h: (0, h + off))
    out = pl.BlockSpec((length, 128), lambda h: (0, h))
    shape = jax.ShapeDtypeStruct((length, pairs * 128), BF)
    flops = 2 * length * width * pairs * 384 + 4 * pairs * 2 * length * length * 128
    return pl.pallas_call(
        attn_fwd_kernel,
        grid=(pairs,),
        in_specs=[whole(xh), col(0), col(pairs), col(0)]
        + [whole(t) for t in tables]
        + [whole(seg_col), whole(seg_row)],
        out_specs=[out] * 4 + [pl.BlockSpec((1, 2, length), lambda h: (h, 0, 0))],
        out_shape=[shape] * 4 + [jax.ShapeDtypeStruct((pairs, 2, length), F32)],
        scratch_shapes=[pltpu.VMEM((2, length, 128), BF)],
        cost_estimate=pl.CostEstimate(
            flops=flops, bytes_accessed=length * width * 8, transcendentals=pairs * 2 * length * length
        ),
        name="attn_fwd",
    )(xh, w_qk, w_qk, w_vo, *tables, seg_col, seg_row)


def attn_bwd_kernel(
    q, k, v, o, do, lse, cos, upper, lower, seg_col, seg_row, pg, kh, dk, dv
):
    length = q.shape[0]
    rows = min(256, length)
    lane = lax.broadcasted_iota(jnp.int32, (length, 128), 1)
    first = lane < HD
    kf = k[...]
    none = jnp.zeros_like(kf)
    kh[0] = jnp.where(first, kf, none)
    kh[1] = jnp.where(first, none, kf)
    dk[...] = jnp.zeros_like(dk)
    dv[...] = jnp.zeros_like(dv)

    def block(i, carry):
        at = pl.multiple_of(i * rows, rows)
        here = pl.ds(at, rows)
        q_rows = q[here, :]
        g_rows = do[here, :]
        seg_here = seg_row[:, here]
        same = seg_col[...] == seg_here
        prod = g_rows.astype(F32) * o[here, :].astype(F32)
        f = first[:rows]
        blank = jnp.zeros_like(q_rows)
        dq = jnp.zeros((rows, 128), F32)
        for head in range(2):
            mine = f if head == 0 else jnp.logical_not(f)
            q_head = jnp.where(mine, q_rows, blank)
            g_head = jnp.where(mine, g_rows, blank)
            delta = lax.dot_general(
                jnp.ones((8, 128), F32),
                jnp.where(mine, prod, 0.0),
                (NT, ((), ())),
                precision=lax.Precision.HIGHEST,
                preferred_element_type=F32,
            )[0:1, :]
            scores = dotf(k[...], q_head, NT)
            level = lse[0, pl.ds(head, 1), here]
            probs = jnp.where(same, jnp.exp(scores - level), 0.0)
            dv[...] += dotf(probs.astype(BF), g_head, NN)
            dp = dotf(v[...], g_head, NT)
            ds = (probs * (dp - delta)).astype(BF)
            dk[...] += dotf(ds, q_head, NN)
            dq = dq + dotf(ds, kh[head], TN)
        dq = dq * (1.0 / math.sqrt(HD))
        c, a, b = cos[here, :], upper[here, :], lower[here, :]
        pg[0, here, :] = (dq * c - turn(dq, a, b)).astype(BF)
        return carry

    lax.fori_loop(0, length // rows, block, 0)
    dkf = dk[...]
    pg[1] = (dkf * cos[...] - turn(dkf, upper[...], lower[...])).astype(BF)
    pg[2] = dv[...].astype(BF)


def attn_bwd(q, k, v, o, do, lse, tables, seg_col, seg_row):
    length, width = q.shape
    pairs = width // 128
    whole = lambda a: pl.BlockSpec(a.shape, lambda h: (0,) * a.ndim)
    col = pl.BlockSpec((length, 128), lambda h: (0, h))
    return pl.pallas_call(
        attn_bwd_kernel,
        grid=(pairs,),
        in_specs=[col] * 5
        + [pl.BlockSpec((1, 2, length), lambda h: (h, 0, 0))]
        + [whole(t) for t in tables]
        + [whole(seg_col), whole(seg_row)],
        out_specs=pl.BlockSpec((3, length, 128), lambda h: (0, 0, h)),
        out_shape=jax.ShapeDtypeStruct((3, length, width), BF),
        scratch_shapes=[
            pltpu.VMEM((2, length, 128), BF),
            pltpu.VMEM((length, 128), F32),
            pltpu.VMEM((length, 128), F32),
        ],
        cost_estimate=pl.CostEstimate(
            flops=10 * pairs * 2 * length * length * 128,
            bytes_accessed=length * width * 20,
            transcendentals=pairs * 2 * length * length,
        ),
        name="attn_bwd",
    )(q, k, v, o, do, lse, *tables, seg_col, seg_row)


def in_chunks(total, size, body):
    def step(j, carry):
        body(pl.ds(pl.multiple_of(j * size, size), size))
        return carry

    lax.fori_loop(0, total // size, step, 0)
    if total % size:
        body(pl.ds(total - total % size, total % size))


SHARD = (4, 2, 2)


def place():
    dp = lax.axis_index("dp")
    return dp // 4, (dp // 2) % 2, dp % 2, lax.axis_index("tensor")


def partners():
    z, x, c, y = place()
    at = lambda z, x, c, y: ((z * 2 + x) * 2 + c, y)
    return {
        "z1": at(z + 1 - 2 * (z % 2), x, c, y),
        "z2": at(z + 2 - 4 * (z // 2), x, c, y),
        "z3": at(3 - z, x, c, y),
        "x": at(z, 1 - x, c, y),
        "y": at(z, x, c, 1 - y),
        "c": at(z, x, 1 - c, y),
    }


def meet(peers, other=None):
    barrier = pltpu.get_barrier_semaphore()
    greet = lambda peer: pl.semaphore_signal(
        barrier, inc=1, device_id=peer, device_id_type=pl.DeviceIdType.MESH
    )
    for peer in peers.values():
        greet(peer)
    if other is None:
        pl.semaphore_wait(barrier, len(peers))
    else:
        moved, peer = other

        @pl.when(moved)
        def _():
            greet(peer)

        pl.semaphore_wait(barrier, len(peers) + jnp.where(moved, 1, 0))


def exchanged():
    z, x, c, y = place()
    return c != y, ((z * 2 + x) * 2 + y, c)


def remote(src, dst, send_sem, recv_sem, peer):
    return pltpu.make_async_remote_copy(
        src_ref=src,
        dst_ref=dst,
        send_sem=send_sem,
        recv_sem=recv_sem,
        device_id=peer,
        device_id_type=pl.DeviceIdType.MESH,
    )


class Move:
    def __init__(self, src, dst, sems, i):
        send_sem, recv_sem, near_sem = sems
        self.moved, peer = exchanged()
        self.far = remote(src, dst, send_sem.at[i], recv_sem.at[i], peer)
        self.near = pltpu.make_async_copy(src, dst, near_sem.at[i])

    def start(self):
        @pl.when(self.moved)
        def _():
            self.far.start()

        @pl.when(jnp.logical_not(self.moved))
        def _():
            self.near.start()

    def wait(self):
        @pl.when(self.moved)
        def _():
            self.far.wait()

        @pl.when(jnp.logical_not(self.moved))
        def _():
            self.near.wait()


def move_sems(n):
    return [pltpu.SemaphoreType.DMA((n,))] * 3


def to_place(values):
    z, x, _, y = place()
    tiles = [values[:, j * 128 : (j + 1) * 128] for j in range(8)]
    tiles = [jnp.where(y == 1, pltpu.roll(t, 64, 1), t) for t in tiles]
    for bit, step in ((x, 1), (z % 2, 2), (z // 2, 4)):
        tiles = [jnp.where(bit == 1, tiles[j ^ step], tiles[j]) for j in range(8)]
    return jnp.concatenate(tiles, axis=1)


AXIS = {"z": 4, "x": 2, "y": 2}


def partner(peers, axis, step):
    return peers["z%d" % step if axis == "z" else axis]


class Gather:
    MESSAGES = 15

    def __init__(self, own, buf, rows, cols, order, hops, peers, sems, base):
        self.buf, self.order, self.hops, self.peers = buf, order, hops, peers
        self.part = (rows, cols)
        self.own = own.at[self.part]
        self.send_sem, self.recv_sem = sems
        self.base = base
        n, m, p = (AXIS[axis] for axis in order)
        self.outer, self.middle = range(n), range(1, m)
        self.stages = [
            [(i, 0, 0) for i in range(1, n)],
            [(i, j, 0) for i in range(n) for j in range(1, m)],
            [(i, j, k) for i in range(n) for j in range(m) for k in range(1, p)],
        ]
        self.stages = self.stages[:hops]
        self.numbers = {at: n for n, at in enumerate(sum(self.stages, []))}

    def slot(self, at):
        where = dict(zip(self.order, at))
        return self.buf.at[(where["z"], where["x"], where["y"]) + self.part]

    def copy(self, at):
        hop = max(i for i in range(3) if at[i])
        source = at[:hop] + (0,) * (3 - hop)
        src = self.slot(source) if any(source) else self.own
        n = self.base + self.numbers[at]
        peer = partner(self.peers, self.order[hop], at[hop])
        return remote(src, self.slot(at), self.send_sem.at[n], self.recv_sem.at[n], peer)

    def send(self, stage, *prefix):
        for at in self.stages[stage]:
            if at[: len(prefix)] == prefix:
                self.copy(at).start()

    def start(self):
        self.send(0)

    def relay(self, i):
        if i:
            self.copy((i, 0, 0)).wait_recv()
        self.send(1, i)
        if self.hops == 3:
            self.send(2, i, 0)

    def relay_again(self, i):
        for j in self.middle:
            self.copy((i, j, 0)).wait_recv()
            self.send(2, i, j)

    def finish(self):
        for at in self.stages[-1]:
            self.copy(at).wait_recv()
        for at in self.numbers:
            self.copy(at).wait_send()


def forward_kernel(
    writes, a_in, b_in, g_in, u_in, d_in, x_in, c_in, seg_in, inverse,
    q, k, v, o, lse, xh, w_qkv, w_out, resid, xn, x_half, cot, cos, upper, lower, seg_col, seg_row,
    w_gate, w_up, w_down,
    a_own, b_own, g_own, u_own, d_own, c_own, seg_own,
    kh, x_rel, part, sent, got, send_sem, recv_sem, pair_send, pair_recv, own_sem, *moving,
):
    length = xh.shape[0]
    half = length // 2
    width = xh.shape[1]
    pairs = q.shape[1] // 128
    rows = 256
    core = place()[2]
    peers = partners()
    sems = (send_sem, recv_sem)
    n = Gather.MESSAGES
    whole, low, high = pl.ds(0, 64), pl.ds(0, 32), pl.ds(32, 32)
    wide = w_qkv.shape[4] // 2
    all_ = lambda ref: pl.ds(0, ref.shape[-1])
    plan = (
        (a_own, w_qkv, whole, pl.ds(0, wide), "zyx", 3),
        (a_own, w_qkv, whole, pl.ds(wide, wide), "zyx", 3),
        (b_own, w_out, whole, all_(w_out), "zxy", 3),
        (g_own, w_gate, whole, all_(w_gate), "zyx", 3),
        (u_own, w_up, low, all_(w_up), "zyx", 3),
        (u_own, w_up, high, all_(w_up), "xyz", 3),
        (d_own, w_down, low, all_(w_down), "zyx", 2),
        (d_own, w_down, high, all_(w_down), "zxy", 2),
    )
    gathers = [Gather(*piece, peers, sems, i * n) for i, piece in enumerate(plan)]
    near, far, out, two, late, three = *gathers[:3], gathers[3:5], gathers[5], gathers[6:]
    owns = [
        pltpu.make_async_copy(src, dst.at[0, 0, 0], own_sem.at[i])
        for i, (src, dst) in enumerate(
            ((a_own, w_qkv), (b_own, w_out), (g_own, w_gate), (u_own, w_up), (d_own, w_down))
        )
    ]
    move_a, move_b, move_x, move_seg, move_g, move_u, move_d, move_c = (
        Move(src, dst, moving, i)
        for i, (src, dst) in enumerate(
            (
                (a_in, a_own),
                (b_in, b_own),
                (x_in, x_half),
                (seg_in, seg_own),
                (g_in, g_own),
                (u_in, u_own),
                (d_in, d_own),
                (c_in, c_own),
            )
        )
    )
    meet(peers, exchanged())
    for move in (move_a, move_seg, move_x):
        move.start()

    def tables(here):
        shape = (here.size, 128)
        row = here.start + lax.broadcasted_iota(jnp.int32, shape, 0) + core * half
        row = jnp.where(row >= length, row - length, row)
        angle = row.astype(F32) * inverse[0:1, :]
        front = lax.broadcasted_iota(jnp.int32, shape, 1) % HD < HD // 2
        sin = jnp.sin(angle)
        cos[here, :] = jnp.cos(angle)
        upper[here, :] = jnp.where(front, -sin, 0.0)
        lower[here, :] = jnp.where(front, 0.0, sin)

    move_a.wait()
    near.start()
    far.start()
    near.relay(0)
    owns[0].start()
    in_chunks(length, 64, tables)
    for z in (1, 2, 3):
        near.relay(z)
    for move in (move_b, move_g, move_u, move_d):
        move.start()
    move_seg.wait()
    ids = seg_own[...]
    ids = jnp.where(core == 0, ids, jnp.concatenate([ids[:, half:], ids[:, :half]], axis=1))
    seg_row[...] = ids
    seg_col[...] = jnp.transpose(jnp.broadcast_to(ids[0:1, :], (128, length)))
    move_x.wait()

    def first_norm(i, carry):
        here = pl.ds(pl.multiple_of(i * 128, 128), 128)
        values = to_place(x_half[here, :].astype(F32))
        x_rel[here, :] = values.astype(BF)
        xh[here, :] = normalize(values)[0].astype(BF)
        return carry

    lax.fori_loop(0, half // 128, first_norm, 0)
    swap_xh = remote(
        xh.at[pl.ds(0, half)], xh.at[pl.ds(half, half)], pair_send.at[0], pair_recv.at[0], peers["c"]
    )
    swap_xh.start()
    for z in range(4):
        near.relay_again(z)
        far.relay(z)
    move_b.wait()
    out.start()
    move_g.wait()
    move_u.wait()
    late.start()
    for gather in two:
        gather.start()
    out.relay(0)
    late.relay(0)
    for gather in two:
        gather.relay(0)
    move_d.wait()
    for gather in three:
        gather.start()
    for copy in owns[1:]:
        copy.start()
    swap_xh.wait()
    near.finish()
    owns[0].wait()

    events = {}
    at_step = lambda step, call, *args: events.setdefault(step, []).append((call, args))
    for z in range(4):
        at_step(z, far.relay_again, z)
        if z:
            at_step(z, out.relay, z)
        at_step(5 + z, out.relay_again, z)
        for gather in two:
            if z:
                at_step(1 + 2 * z, gather.relay, z)
            at_step(9 + z, gather.relay_again, z)
        for gather in three:
            at_step(11 + z, gather.relay, z)
    at_step(4, late.relay, 1)
    at_step(5, move_c.start)
    at_step(6, late.relay_again, 0)
    at_step(8, late.relay_again, 1)
    at_step(length // rows * pairs // 2 - 1, far.finish)
    first = lax.broadcasted_iota(jnp.int32, (length, 128), 1) < HD

    def pair(h, carry):
        lanes = pl.ds(pl.multiple_of(h * 128, 128), 128)
        weight = lambda i: w_qkv[
            :, :, :, :, pl.ds(pl.multiple_of((3 * h + i) * 128, 128), 128)
        ].reshape(width, 128)
        tokens = xh[...]
        qf = dotf(tokens, weight(0), NN)
        qf = qf * cos[...] + turn(qf, upper[...], lower[...])
        q[:, lanes] = (qf * (1.0 / math.sqrt(HD))).astype(BF)
        kf = dotf(tokens, weight(1), NN)
        kf = (kf * cos[...] + turn(kf, upper[...], lower[...])).astype(BF)
        k[:, lanes] = kf
        kh[0] = jnp.where(first, kf, jnp.zeros_like(kf))
        kh[1] = jnp.where(first, jnp.zeros_like(kf), kf)
        v[:, lanes] = dotf(tokens, weight(2), NN).astype(BF)

        def block(i, carry):
            for step, calls in events.items():

                @pl.when(h * (length // rows) + i == step)
                def _():
                    for call, args in calls:
                        call(*args)

            at = pl.multiple_of(i * rows, rows)
            q_rows = q[pl.ds(at, rows), lanes]
            same = seg_col[pl.ds(at, rows), 0:1] == seg_row[0:1, :]
            outs = []
            for head in range(2):
                scores = dotf(q_rows, kh[head], NT)
                scores = jnp.where(same, scores, -1e30)
                top = jnp.max(scores, axis=-1, keepdims=True)
                expv = jnp.exp(scores - top)
                total = jnp.sum(expv, axis=-1, keepdims=True)
                low_probs = (expv * (1.0 / total)).astype(BF)
                outs.append(dotf(low_probs, v[:, lanes], NN))
                level = top + jnp.log(total)
                flat = jnp.transpose(jnp.broadcast_to(level, (rows, 128)))
                lse[h, pl.ds(head, 1), pl.ds(at, rows)] = flat[0:1, :]
            o[pl.ds(at, rows), lanes] = jnp.where(first[:rows], outs[0], outs[1]).astype(BF)
            return carry

        return lax.fori_loop(0, length // rows, block, carry)

    lax.fori_loop(0, pairs, pair, 0)
    out.finish()
    owns[1].wait()
    w_o = w_out[...].reshape(width, pairs * 128)

    def project(i, carry):
        at = pl.multiple_of(half + i * rows, rows)
        sent[pl.ds(pl.multiple_of(i * rows, rows), rows), :] = dotf(
            o[pl.ds(at, rows), :], w_o, NT
        ).astype(BF)
        return carry

    lax.fori_loop(0, half // rows, project, 0)

    def project_own(i, carry):
        here = pl.ds(pl.multiple_of(i * rows, rows), rows)
        part[here, :] = dotf(o[here, :], w_o, NT)
        return carry

    give = remote(sent, got, pair_send.at[1], pair_recv.at[1], peers["c"])
    lax.fori_loop(0, half // rows, project_own, 0)
    give.start()
    for copy in writes:
        copy.start()
    move_c.wait()

    def turn_cot(here):
        cot[here, :] = to_place(c_own[here, :].astype(F32)).astype(BF)

    in_chunks(half, 128, turn_cot)
    swap_cot = remote(
        cot.at[pl.ds(0, half)], cot.at[pl.ds(half, half)], pair_send.at[3], pair_recv.at[3], peers["c"]
    )
    swap_cot.start()
    give.wait()

    def second_norm(i, carry):
        here = pl.ds(pl.multiple_of(i * 128, 128), 128)
        values = x_rel[here, :].astype(F32) + (part[here, :] + got[here, :].astype(F32))
        resid[here, :] = values
        xn[here, :] = normalize(values)[0].astype(BF)
        return carry

    lax.fori_loop(0, half // 128, second_norm, 0)
    swap_xn = remote(
        xn.at[pl.ds(0, half)], xn.at[pl.ds(half, half)], pair_send.at[2], pair_recv.at[2], peers["c"]
    )
    swap_xn.start()
    for gather in two + three + [late]:
        gather.finish()
    for copy in owns[2:]:
        copy.wait()
    swap_cot.wait()
    swap_xn.wait()
    for copy in writes:
        copy.wait()


WRITTEN = (0, 1, 2, 3, 5, 6, 7, 10, 12, 13, 14, 15)


def forward_written(*refs):
    count = len(WRITTEN)
    ins, outs, scratch = refs[:9], list(refs[9:29]), refs[29 : -count - 1]
    held, sem = refs[-count - 1 : -1], refs[-1]
    writes = []
    for i, (n, ref) in enumerate(zip(WRITTEN, held)):
        writes.append(pltpu.make_async_copy(ref, outs[n], sem.at[i]))
        outs[n] = ref
    forward_kernel(writes, *ins, *outs, *scratch)


def forward_block(owned, x_half, cot_half, seg, inverse):
    half, width = x_half.shape
    length = 2 * half
    cols = owned[1].shape[1]
    pairs = cols // 128
    units = owned[2].shape[1]
    shard = width // 16
    vmem = pl.BlockSpec(memory_space=pltpu.VMEM)
    any_ = pl.BlockSpec(memory_space=pl.ANY)
    gathered = lambda n: jax.ShapeDtypeStruct(SHARD + (shard, n), BF)
    heads = jax.ShapeDtypeStruct((length, cols), BF)
    flat = jax.ShapeDtypeStruct((length, width), BF)
    table = jax.ShapeDtypeStruct((length, 128), F32)
    shapes = [heads] * 4 + [
        jax.ShapeDtypeStruct((pairs, 2, length), F32),
        flat,
        gathered(3 * cols),
        gathered(cols),
        jax.ShapeDtypeStruct((half, width), F32),
        flat,
        jax.ShapeDtypeStruct((half, width), BF),
        flat,
    ]
    shapes += [table] * 4 + [jax.ShapeDtypeStruct((8, length), F32)] + [gathered(units)] * 3
    return pl.pallas_call(
        forward_written,
        in_specs=[any_] * 8 + [vmem],
        out_specs=[any_ if i in WRITTEN + (17, 18, 19) else vmem for i in range(20)],
        out_shape=shapes,
        scratch_shapes=[pltpu.VMEM((shard, 3 * cols), BF), pltpu.VMEM((shard, cols), BF)]
        + [pltpu.VMEM((shard, units), BF)] * 3
        + [
            pltpu.VMEM((half, width), BF),
            pltpu.VMEM((8, length), F32),
            pltpu.VMEM((2, length, 128), BF),
            pltpu.VMEM((half, width), BF),
            pltpu.VMEM((half, width), F32),
            pltpu.VMEM((half, width), BF),
            pltpu.VMEM((half, width), BF),
            pltpu.SemaphoreType.DMA((8 * Gather.MESSAGES,)),
            pltpu.SemaphoreType.DMA((8 * Gather.MESSAGES,)),
            pltpu.SemaphoreType.DMA((4,)),
            pltpu.SemaphoreType.DMA((4,)),
            pltpu.SemaphoreType.DMA((5,)),
        ]
        + move_sems(8)
        + [pltpu.VMEM(shapes[i].shape, shapes[i].dtype) for i in WRITTEN]
        + [pltpu.SemaphoreType.DMA((len(WRITTEN),))],
        compiler_params=pltpu.CompilerParams(
            collective_id=0, has_side_effects=True, vmem_limit_bytes=60 << 20
        ),
        name="forward_block",
    )(*owned, x_half, cot_half, seg, inverse)


class Reduce:
    MESSAGES = 12
    ORDER = (2, 3, 1, 0)

    def __init__(self, parts, near, rows, axes, peers, sems, base, bufs, out):
        self.parts, self.near, self.rows, self.axes, self.peers = parts, near, rows, axes, peers
        self.send_sem, self.recv_sem = sems
        self.base = base
        self.one, self.two, self.three, self.sum = bufs
        self.out = out

    def link(self, i, src, dst, peer):
        n = self.base + i
        return remote(src, dst, self.send_sem.at[n], self.recv_sem.at[n], peer)

    def first(self, z):
        if self.axes == "xy":
            src = self.parts.at[z, :, 1, self.rows]
        else:
            src = self.parts.at[z, 1, :, self.rows]
        return self.link(z, src, self.one.at[z], self.peers[self.axes[1]])

    def second(self, z):
        return self.link(4 + z, self.one.at[z, 1], self.two.at[z], self.peers[self.axes[0]])

    def third(self, z):
        return self.link(7 + z, self.two.at[z], self.three.at[z - 1], self.peers["z%d" % z])

    def start(self):
        for z in self.ORDER:
            self.first(z).start()

    def add_first(self, z):
        self.first(z).wait_recv()
        self.one[z] = (self.one[z].astype(F32) + self.near(z).astype(F32)).astype(BF)

    def relay_first(self, z):
        self.add_first(z)
        self.second(z).start()

    def resume(self):
        for z in self.ORDER:
            self.second(z).start()

    def relay_second(self, z):
        self.second(z).wait_recv()
        self.two[z] = (self.two[z].astype(F32) + self.one[z, 0].astype(F32)).astype(BF)
        if z:
            self.third(z).start()

    def last(self):
        moved, peer = exchanged()
        return moved, self.link(11, self.sum, self.out, peer)

    def total(self):
        total = self.two[0].astype(F32)
        for z in (1, 2, 3):
            self.third(z).wait_recv()
            total = total + self.three[z - 1].astype(F32)
        return total

    def finish(self):
        self.sum[...] = self.total().astype(BF)
        moved, copy = self.last()

        @pl.when(moved)
        def _():
            copy.start()

        @pl.when(jnp.logical_not(moved))
        def _():
            self.out[...] = self.sum[...]

    def sent(self):
        hops = (self.second,) if self.parts is None else (self.first, self.second)
        thirds = [self.third(z) for z in (1, 2, 3)]
        return [hop(z) for z in range(4) for hop in hops] + thirds

    def close(self):
        for copy in self.sent():
            copy.wait_send()
        moved, copy = self.last()

        @pl.when(moved)
        def _():
            copy.wait()


class ReduceAlongZ(Reduce):
    def first(self, z):
        src = self.parts.at[z, :, :, self.rows]
        return self.link(z - 1, src, self.one.at[z - 1], self.peers["z%d" % z])

    def second(self):
        return self.link(3, self.two.at[:, 1], self.three.at[0:2], self.peers["y"])

    def third(self):
        return self.link(4, self.three.at[1], self.three.at[2], self.peers["x"])

    def start(self):
        for z in (2, 3, 1):
            self.first(z).start()

    def relay_first(self):
        total = self.near().astype(F32)
        for z in (1, 2, 3):
            self.first(z).wait_recv()
            total = total + self.one[z - 1].astype(F32)
        self.two[...] = total.astype(BF)
        self.second().start()

    def relay_second(self):
        self.second().wait_recv()
        for x in (0, 1):
            self.three[x] = (self.three[x].astype(F32) + self.two[x, 0].astype(F32)).astype(BF)
        self.third().start()

    def total(self):
        self.third().wait_recv()
        return self.three[0].astype(F32) + self.three[2].astype(F32)

    def sent(self):
        return [self.first(z) for z in (1, 2, 3)] + [self.second(), self.third()]


def mlp_kernel(
    reads, writes, down_in, xn, cot, w_gate, w_up, resid,
    result, resid_grad, attn_cot, d_gate, d_up, d_low, d_high,
    w_down, d_down, hidden, act, slope_up, gate_grad, up_grad, own, sent, got, placed,
    send_sem, recv_sem, last_send, last_recv, first_send, first_recv, own_sem, *moving,
):
    length, width = xn.shape
    half = length // 2
    units = w_gate.shape[1]
    peers = {axis: partners()[axis] for axis in "xyc"}
    move = Move(placed, result, moving, 0)
    low, high = pl.ds(0, 32), pl.ds(32, 32)
    most, few = pl.ds(0, 48), pl.ds(48, 16)
    at_low = lambda ref, z, x: ref.at[z, x, :, low]
    at_high = lambda ref, z, y: ref.at[z, :, y, high]
    last = []
    for z in range(4):
        for i, (part, axis) in enumerate(((at_low, "x"), (at_high, "y"))):
            n = 2 * z + i
            last.append(
                remote(
                    part(down_in, z, 0), part(w_down, z, 1), last_send.at[n], last_recv.at[n], peers[axis]
                )
            )
    every = pl.ds(0, 4)
    owns = [
        pltpu.make_async_copy(part(down_in, every, 0), part(w_down, every, 0), own_sem.at[i])
        for i, part in enumerate((at_low, at_high))
    ]
    sems = (first_send, first_recv)
    n = Reduce.MESSAGES
    reduce_low = Reduce(
        d_down, lambda z: d_down[z, 0, :, 0:48], most, "yx", peers, sems, 0, (d_low, None, None, None), None
    )
    reduce_high = Reduce(
        d_down, lambda z: d_down[z, :, 0, 48:64], few, "xy", peers, sems, n, (d_high, None, None, None), None
    )
    for copy in reads:
        copy.start()
    meet(peers, exchanged())
    for copy in last + owns:
        copy.start()
    for copy in reads:
        copy.wait()
    back, front = pl.ds(half, half), pl.ds(0, half)

    def gate_and_up(rows):
        def step(cols):
            gate = dotf(xn[rows, :], w_gate[:, cols], NN)
            up = dotf(xn[rows, :], w_up[:, cols], NN)
            value, slope = gelu_parts(gate)
            hidden[rows, cols] = (value * up).astype(BF)
            act[rows, cols] = value
            slope_up[rows, cols] = up * slope

        in_chunks(units, 256, step)

    def units_back(rows):
        def step(cols):
            down = w_down[:, :, :, :, cols].reshape(width, cols.size)
            grad = dotf(cot[rows, :], down, NN).astype(BF).astype(F32)
            gate_grad[rows, cols] = (grad * slope_up[rows, cols]).astype(BF)
            up_grad[rows, cols] = (grad * act[rows, cols]).astype(BF)

        in_chunks(units, 256, step)

    def sums(rows, put):
        def step(z, carry):
            here = pl.ds(pl.multiple_of(z * 256, 256), 256)
            down = w_down[z].reshape(256, units)
            put[0, :, here] = dotf(hidden[rows, :], down, NT).astype(put.dtype)
            both = dotf(gate_grad[rows, :], w_gate[here, :], NT)
            both = both + dotf(up_grad[rows, :], w_up[here, :], NT)
            put[1, :, here] = both.astype(put.dtype)
            return carry

        lax.fori_loop(0, width // 256, step, 0)

    gate_and_up(back)
    gate_and_up(front)
    for z in Reduce.ORDER:
        left = jnp.transpose(cot[:, z * 256 : (z + 1) * 256])
        d_down[z] = dotf(left, hidden[...], NN).astype(BF).reshape(2, 2, 64, units)
        reduce_low.first(z).start()
        reduce_high.first(z).start()
    for copy in owns:
        copy.wait()
    for copy in last:
        copy.wait()
    units_back(back)
    sums(back, sent)
    give = remote(sent, got, send_sem.at[0], recv_sem.at[0], peers["c"])
    give.start()
    units_back(front)
    sums(front, own)
    give.wait()

    def finish(here):
        values = resid[here, :]
        mlp = own[0, here, :] + got[0, here, :].astype(F32)
        placed[here, :] = to_place(values + mlp).astype(BF)
        xhat, scale = normalize(values)
        back = normalize_back(own[1, here, :] + got[1, here, :].astype(F32), xhat, scale)
        grad = cot[here, :].astype(F32) + back
        resid_grad[here, :] = grad
        attn_cot[here, :] = grad.astype(BF)

    in_chunks(half, 64, finish)
    swap = remote(
        attn_cot.at[pl.ds(0, half)], attn_cot.at[pl.ds(half, half)], send_sem.at[1], recv_sem.at[1], peers["c"]
    )
    swap.start()
    move.start()

    def weights(here):
        left = jnp.transpose(xn[:, here])
        d_gate[here, :] = dotf(left, gate_grad[...], NN).astype(BF)
        d_up[here, :] = dotf(left, up_grad[...], NN).astype(BF)

    in_chunks(width, 256, weights)
    writes[0].start()
    for z in Reduce.ORDER:
        reduce_low.add_first(z)
        reduce_high.add_first(z)
    for z in range(4):
        reduce_low.first(z).wait_send()
        reduce_high.first(z).wait_send()
    for copy in writes[1:]:
        copy.start()
    swap.wait()
    move.wait()
    for copy in writes:
        copy.wait()


def mlp_staged(*refs):
    ins, outs, scratch = refs[1:6], list(refs[6:13]), refs[13:-10]
    held, read_sem, write_sem = refs[-10:-2], refs[-2], refs[-1]
    reads = [pltpu.make_async_copy(a, b, read_sem.at[i]) for i, (a, b) in enumerate(zip(ins, held))]
    writes = []
    for i, (n, ref) in enumerate(zip((1, 3, 4), held[5:])):
        writes.append(pltpu.make_async_copy(ref, outs[n], write_sem.at[i]))
        outs[n] = ref
    mlp_kernel(reads, writes, refs[0], *held[:5], *outs, *scratch)


def mlp_block(down_in, xn, cot, w_gate, w_up, resid):
    length, width = xn.shape
    half = length // 2
    units = w_gate.shape[1]
    shard = width // 16
    vmem = pl.BlockSpec(memory_space=pltpu.VMEM)
    any_ = pl.BlockSpec(memory_space=pl.ANY)
    grads = jax.ShapeDtypeStruct((width, units), BF)
    dma = lambda n: pltpu.SemaphoreType.DMA((n,))
    return pl.pallas_call(
        mlp_staged,
        in_specs=[any_] * 6,
        out_specs=[any_, any_, vmem, any_, any_, vmem, vmem],
        out_shape=[
            jax.ShapeDtypeStruct((half, width), BF),
            jax.ShapeDtypeStruct((half, width), F32),
            jax.ShapeDtypeStruct((length, width), BF),
            grads,
            grads,
            jax.ShapeDtypeStruct((4, 2, shard * 3 // 4, units), BF),
            jax.ShapeDtypeStruct((4, 2, shard // 4, units), BF),
        ],
        scratch_shapes=[pltpu.VMEM(SHARD + (shard, units), BF)] * 2
        + [
            pltpu.VMEM((length, units), BF),
            pltpu.VMEM((length, units), F32),
            pltpu.VMEM((length, units), F32),
            pltpu.VMEM((length, units), BF),
            pltpu.VMEM((length, units), BF),
            pltpu.VMEM((2, half, width), F32),
            pltpu.VMEM((2, half, width), BF),
            pltpu.VMEM((2, half, width), BF),
            pltpu.VMEM((half, width), BF),
        ]
        + [dma(2), dma(2), dma(8), dma(8), dma(2 * Reduce.MESSAGES), dma(2 * Reduce.MESSAGES), dma(2)]
        + move_sems(1)
        + [pltpu.VMEM(a.shape, a.dtype) for a in (xn, cot, w_gate, w_up, resid)]
        + [pltpu.VMEM((half, width), F32)]
        + [pltpu.VMEM((width, units), BF)] * 2
        + [dma(5), dma(3)],
        compiler_params=pltpu.CompilerParams(
            collective_id=1, has_side_effects=True, vmem_limit_bytes=63 << 20
        ),
        name="mlp_block",
    )(down_in, xn, cot, w_gate, w_up, resid)


def backward_kernel(
    reads, d_gate, d_up, d_low, d_high, q, k, v, o, lse, attn_cot, w_qkv, w_out, xh, x_half, resid_grad,
    cos, upper, lower, seg_col, seg_row,
    token_grad, s_gate, s_up_low, s_up_high, s_down_low, s_down_high, s_out, s_near, s_far_low, s_far_high,
    d_out, d_near, d_far, pg, heads_grad, kh, dk, dv, own, sent, got, placed,
    near_gate, near_up_low, near_up_high,
    *rest,
):
    bufs = [rest[4 * i : 4 * i + 4] for i in range(3)]
    bufs += [(first,) + rest[12 + 3 * i : 15 + 3 * i] for i, first in enumerate((d_low, d_high))]
    bufs += [rest[18 + 4 * i : 22 + 4 * i] for i in range(4)]
    send_sem, recv_sem, pair_send, pair_recv, near_sem, *moving = rest[34:]
    length, width = xh.shape
    half = length // 2
    cols = q.shape[1]
    pairs = cols // 128
    rows = 256
    peers = partners()
    sems = (send_sem, recv_sem)
    n = Reduce.MESSAGES
    whole, low, high = pl.ds(0, 64), pl.ds(0, 32), pl.ds(32, 32)
    held = lambda ref: (lambda z: ref[z])
    plan = (
        (Reduce, d_gate, held(near_gate), whole, "yx", s_gate),
        (Reduce, d_up, held(near_up_low), low, "xy", s_up_low),
        (ReduceAlongZ, d_up, lambda: near_up_high[...], high, None, s_up_high),
        (Reduce, None, None, None, "yx", s_down_low),
        (Reduce, None, None, None, "xy", s_down_high),
        (Reduce, d_out, lambda z: d_out[z, 0], whole, "yx", s_out),
        (Reduce, d_near, lambda z: d_near[z, 0], whole, "yx", s_near),
        (Reduce, d_far, lambda z: d_far[z, 0, :, 0:32], low, "yx", s_far_low),
        (Reduce, d_far, lambda z: d_far[z, :, 0, 32:64], high, "xy", s_far_high),
    )
    parts = [
        kind(src, near, rows_, axes, peers, sems, i * n, bufs[i], out)
        for i, (kind, src, near, rows_, axes, out) in enumerate(plan)
    ]
    gate, up_low, up_high, down_low, down_high, out, near, far_low, far_high = parts
    nears = [
        pltpu.make_async_copy(src, dst, near_sem.at[i])
        for i, (src, dst) in enumerate(
            (
                (d_gate.at[:, 0], near_gate),
                (d_up.at[:, :, 0, low], near_up_low),
                (d_up.at[0, :, :, high], near_up_high),
            )
        )
    ]
    for copy in nears + reads:
        copy.start()
    meet(peers, exchanged())
    up_high.start()
    down_low.resume()
    down_high.resume()
    gate.start()
    up_low.start()
    for copy in reads:
        copy.wait()

    def heads(here):
        heads_grad[here, :] = dotf(attn_cot[here, :], w_out[...], NN).astype(BF)

    in_chunks(length, 256, heads)

    def out_weights(z, carry):
        here = pl.ds(pl.multiple_of(z * 256, 256), 256)
        value = dotf(jnp.transpose(attn_cot[:, here]), o[...], NN).astype(BF)
        d_out[z] = value.reshape(2, 2, 64, cols)
        return carry

    lax.fori_loop(0, width // 256, out_weights, 0)
    out.start()
    for copy in nears:
        copy.wait()
    for z in Reduce.ORDER:
        down_low.relay_second(z)
        down_high.relay_second(z)

    events = {}
    for i, z in enumerate(Reduce.ORDER):
        events.setdefault((3, 6, 10, 13)[i], []).append(lambda z=z: gate.relay_first(z))
        events.setdefault((5, 7, 8, 10)[i], []).append(lambda z=z: up_low.relay_first(z))
    for z in Reduce.ORDER[:2]:
        events.setdefault(14, []).append(lambda z=z: gate.relay_second(z))
    events.setdefault(9, []).append(up_high.relay_first)
    events.setdefault(13, []).append(up_high.relay_second)

    def weights(ref, at):
        def step(z, carry):
            left = jnp.transpose(xh[:, pl.ds(pl.multiple_of(z * 256, 256), 256)])
            value = dotf(left, pg[:, at : at + ref.shape[-1]], NN).astype(BF)
            ref[z] = value.reshape(2, 2, 64, ref.shape[-1])
            return carry

        lax.fori_loop(0, width // 256, step, 0)

    lane = lax.broadcasted_iota(jnp.int32, (length, 128), 1)
    first = lane < HD

    def pair(h, carry):
        lanes = pl.ds(pl.multiple_of(h * 128, 128), 128)
        third = lambda i: pl.ds(pl.multiple_of((3 * h + i) * 128, 128), 128)
        kf = k[:, lanes]
        none = jnp.zeros_like(kf)
        kh[0] = jnp.where(first, kf, none)
        kh[1] = jnp.where(first, none, kf)
        dk[...] = jnp.zeros_like(dk)
        dv[...] = jnp.zeros_like(dv)

        def block(i, carry):
            for step, calls in events.items():

                @pl.when(h * (length // rows) + i == step)
                def _():
                    for call in calls:
                        call()

            at = pl.multiple_of(i * rows, rows)
            here = pl.ds(at, rows)
            q_rows = q[here, lanes]
            g_rows = heads_grad[here, lanes]
            same = seg_col[:, 0:1] == seg_row[0:1, here]
            prod = g_rows.astype(F32) * o[here, lanes].astype(F32)
            f = first[:rows]
            blank = jnp.zeros_like(q_rows)
            dq = jnp.zeros((rows, 128), F32)
            for head in range(2):
                mine = f if head == 0 else jnp.logical_not(f)
                q_head = jnp.where(mine, q_rows, blank)
                g_head = jnp.where(mine, g_rows, blank)
                delta = lax.dot_general(
                    jnp.ones((8, 128), F32),
                    jnp.where(mine, prod, 0.0),
                    (NT, ((), ())),
                    precision=lax.Precision.HIGHEST,
                    preferred_element_type=F32,
                )[0:1, :]
                scores = dotf(k[:, lanes], q_head, NT)
                level = lse[h, pl.ds(head, 1), here]
                probs = jnp.where(same, jnp.exp(scores - level), 0.0)
                dv[...] += dotf(probs.astype(BF), g_head, NN)
                dp = dotf(v[:, lanes], g_head, NT)
                ds = (probs * (dp - delta)).astype(BF)
                dk[...] += dotf(ds, q_head, NN)
                dq = dq + dotf(ds, kh[head], TN)
            dq = dq * (1.0 / math.sqrt(HD))
            c, a, b = cos[here, :], upper[here, :], lower[here, :]
            pg[here, third(0)] = (dq * c - turn(dq, a, b)).astype(BF)
            return carry

        lax.fori_loop(0, length // rows, block, 0)
        dkf = dk[...]
        pg[:, third(1)] = (dkf * cos[...] - turn(dkf, upper[...], lower[...])).astype(BF)
        pg[:, third(2)] = dv[...].astype(BF)

        @pl.when(h == pairs // 2 - 1)
        def _():
            weights(d_near, 0)
            near.start()

        return carry

    lax.fori_loop(0, pairs, pair, 0)
    weights(d_far, d_near.shape[-1])
    far_low.start()
    far_high.start()

    def back(tokens, put):
        def step(here):
            put[:, here] = dotf(pg[tokens, :], w_qkv[here, :], NT).astype(put.dtype)

        in_chunks(width, 256, step)

    for z in Reduce.ORDER[2:]:
        gate.relay_second(z)
    for z in Reduce.ORDER:
        out.relay_first(z)
    back(pl.ds(half, half), sent)
    give = remote(sent, got, pair_send.at[0], pair_recv.at[0], peers["c"])
    give.start()
    for z in Reduce.ORDER:
        up_low.relay_second(z)
    back(pl.ds(0, half), own)
    for z in Reduce.ORDER:
        out.relay_second(z)
    for part in (down_low, down_high):
        part.finish()
    give.wait()

    def finish(here):
        xhat, scale = normalize(to_place(x_half[here, :].astype(F32)))
        f = own[here, :] + got[here, :].astype(F32)
        value = resid_grad[here, :] + normalize_back(f, xhat, scale)
        placed[here, :] = to_place(value).astype(BF)

    in_chunks(half, 64, finish)
    move = Move(placed, token_grad, moving, 0)
    move.start()
    for z in Reduce.ORDER:
        near.relay_first(z)
    for part in (gate, up_high, up_low):
        part.finish()
    for z in Reduce.ORDER:
        far_high.relay_first(z)
    for z in Reduce.ORDER:
        far_low.relay_first(z)
        near.relay_second(z)
    out.finish()
    for z in Reduce.ORDER:
        far_high.relay_second(z)
        far_low.relay_second(z)
    near.finish()
    far_high.finish()
    far_low.finish()
    for part in parts:
        part.close()
    move.wait()


def backward_staged(*refs):
    held, sem = refs[-17:-1], refs[-1]
    reads = [pltpu.make_async_copy(a, b, sem.at[i]) for i, (a, b) in enumerate(zip(refs[4:20], held))]
    backward_kernel(reads, *refs[:4], *held, *refs[20:-17])


def backward_block(grads, heads, lse, attn_cot, w_qkv, w_out, xh, x_half, resid_grad, tables, seg_col, seg_row):
    length, width = xh.shape
    half = length // 2
    cols = heads[0].shape[1]
    units = grads[0].shape[1]
    shard = width // 16
    vmem = pl.BlockSpec(memory_space=pltpu.VMEM)
    any_ = pl.BlockSpec(memory_space=pl.ANY)
    wide = 3 * cols // 2
    sizes = [(shard, units), (shard // 2, units), (shard // 2, units)]
    sizes += [g.shape[2:] for g in grads[2:]]
    sizes += [(shard, cols), (shard, wide), (shard // 2, wide), (shard // 2, wide)]
    along_z, begun = (2,), (3, 4)
    bufs = []
    for i, size in enumerate(sizes):
        if i in along_z:
            lead = (3, 2, 2), (2, 2), (3,)
        else:
            lead = (4, 2), (4,), (3,)
        bufs += [pltpu.VMEM(n + size, BF) for n in lead[i in begun :] + ((),)]
    nears = [pltpu.VMEM(((2, 2) if i in along_z else (4, 2)) + size, BF) for i, size in enumerate(sizes[:3])]
    messages = 9 * Reduce.MESSAGES
    operands = (*heads, lse, attn_cot, w_qkv, w_out, xh, x_half, resid_grad, *tables, seg_col, seg_row)
    return pl.pallas_call(
        backward_staged,
        in_specs=[any_] * 2 + [vmem] * 2 + [any_] * 16,
        out_specs=[vmem] * 10,
        out_shape=[jax.ShapeDtypeStruct((half, width), BF)]
        + [jax.ShapeDtypeStruct(size, BF) for size in sizes],
        scratch_shapes=[pltpu.VMEM(SHARD + (shard, n), BF) for n in (cols, wide, wide)]
        + [
            pltpu.VMEM((length, 3 * cols), BF),
            pltpu.VMEM((length, cols), BF),
            pltpu.VMEM((2, length, 128), BF),
            pltpu.VMEM((length, 128), F32),
            pltpu.VMEM((length, 128), F32),
            pltpu.VMEM((half, width), F32),
            pltpu.VMEM((half, width), BF),
            pltpu.VMEM((half, width), BF),
            pltpu.VMEM((half, width), BF),
        ]
        + nears
        + bufs
        + [
            pltpu.SemaphoreType.DMA((messages,)),
            pltpu.SemaphoreType.DMA((messages,)),
            pltpu.SemaphoreType.DMA((1,)),
            pltpu.SemaphoreType.DMA((1,)),
            pltpu.SemaphoreType.DMA((3,)),
        ]
        + move_sems(1)
        + [pltpu.VMEM(a.shape, a.dtype) for a in operands]
        + [pltpu.SemaphoreType.DMA((16,))],
        compiler_params=pltpu.CompilerParams(
            collective_id=2, has_side_effects=True, vmem_limit_bytes=60 << 20
        ),
        name="backward_block",
    )(
        *(g.reshape(SHARD + (shard, units)) for g in grads[:2]), *grads[2:],
        *operands,
    )


class Chips:
    def sum_tensor(self, value):
        pairs = [(2 * i + y, 2 * i + 1 - y) for i in range(16) for y in range(2)]
        return value + lax.ppermute(value, ("dp", "tensor"), pairs)


class Axes:
    def gather_rows(self, value):
        return lax.all_gather(value, "tensor", axis=0, tiled=True)

    def scatter_rows(self, value):
        return lax.psum_scatter(value.astype(BF), "tensor", scatter_dimension=0, tiled=True).astype(F32)

    def reduce(self, a, b):
        return tuple(
            lax.psum_scatter(w.astype(BF), "dp", scatter_dimension=0, tiled=True).astype(F32)
            for w in (a, b)
        )

    def sum_tensor(self, value):
        return lax.psum(value, "tensor")


def normalize(values):
    centred = values - jnp.mean(values, axis=-1, keepdims=True)
    scale = lax.rsqrt(jnp.mean(centred * centred, axis=-1, keepdims=True) + EPS)
    return centred * scale, scale


def normalize_back(f, xhat, scale):
    return scale * (
        f
        - jnp.mean(f, axis=-1, keepdims=True)
        - xhat * jnp.mean(f * xhat, axis=-1, keepdims=True)
    )


def gelu_parts(gate):
    half_erf = 0.5 * (1.0 + lax.erf(gate * (1.0 / math.sqrt(2.0))))
    density = jnp.exp(-0.5 * gate * gate) * (1.0 / math.sqrt(2.0 * math.pi))
    return gate * half_erf, half_erf + gate * density


def make_local(comm_type):
    def local(tokens, segments, w_qkv, w_out, w_in, w_down, g_attn, g_mlp, cotangent):
        comm = comm_type()
        paired = comm_type is Chips
        shard = w_qkv.shape[0]
        cols = w_qkv.shape[2]
        units = w_in.shape[2]
        low = 128 * (units // 256)
        pad = 128 * pl.cdiv(units, 128) - units
        gain_one = g_attn.astype(F32)[:, None]
        gain_two = g_mlp.astype(F32)[:, None]
        scaled = lambda w, g: (w.astype(F32) * g).astype(BF)
        padded = lambda w: jnp.pad(w, ((0, 0), (0, pad)))
        down_rows = w_down.T
        a_one = jnp.concatenate([scaled(w_qkv[:, 0], gain_one), scaled(w_qkv[:, 1], gain_one)], axis=1)
        b_one = jnp.concatenate([scaled(w_qkv[:, 2], gain_one), w_out.T], axis=1)
        own_gate, own_up = scaled(w_in[:, 0], gain_two), scaled(w_in[:, 1], gain_two)

        owned = (a_one, b_one, own_gate, own_up, down_rows)
        if paired:
            by_pair = scaled(w_qkv, gain_one[:, None]).reshape(shard, 3, cols // 128, 128).swapaxes(1, 2)
            owned = (by_pair.reshape(shard, 3 * cols), w_out.T) + tuple(padded(w) for w in owned[2:])
            seg = jnp.broadcast_to(segments.astype(F32), (8, segments.shape[1]))
            inverse = jnp.broadcast_to(jnp.tile(rope_rates(), 4), (8, 128))
            (
                q, k, v, o, lse, xh, qkv_all, out_all, resid, xn, x_half, cot_all, *tables, seg_col, seg_row,
                w_gate, w_up, w_dn,
            ) = forward_block(owned, tokens[0], cotangent[0], seg, inverse)
            qkv_all, out_all, w_gate, w_up = (
                w.reshape(-1, w.shape[-1]) for w in (qkv_all, out_all, w_gate, w_up)
            )
        else:
            w_qk, w_vo, w_gate, w_up, w_dn = (
                lax.all_gather(w, "dp", axis=0, tiled=True) for w in owned
            )
            w_o = w_vo[:, cols:]
            seg_col, seg_row = segments[0][:, None], segments
            cot = cotangent[0]
            cot_all = comm.gather_rows(cot)
            tables = rope_tables(jnp.arange(segments.shape[1]))
            x_in = tokens[0].astype(F32)
            xh_one, scale_one = normalize(x_in)
            xh = comm.gather_rows(xh_one.astype(BF))
            o, q, k, v, lse = attn_fwd(xh, w_qk, w_vo, tables, seg_col, seg_row)
            resid = x_in + comm.scatter_rows(dotf(o, w_o, NT))
            xh_two, scale_two = normalize(resid)
            xn = comm.gather_rows(xh_two.astype(BF))
        if paired:
            result, resid_grad, attn_cot, *grads = mlp_block(w_dn, xn, cot_all, w_gate, w_up, resid)
        else:
            gate, up = dotf(xn, w_gate, NN), dotf(xn, w_up, NN)
            act, slope = gelu_parts(gate)
            hidden = (act * up).astype(BF)
            mlp = comm.scatter_rows(dotf(hidden, w_dn, NT))
            result = (resid + mlp).astype(BF)
            hidden_grad = dotf(cot_all, w_dn, NN).astype(BF).astype(F32)
            gate_grad = (hidden_grad * up * slope).astype(BF)
            up_grad = (hidden_grad * act).astype(BF)
            f_two = comm.scatter_rows(dotf(gate_grad, w_gate, NT) + dotf(up_grad, w_up, NT))
            resid_grad = cot.astype(F32) + normalize_back(f_two, xh_two, scale_two)
            attn_cot = comm.gather_rows(resid_grad.astype(BF))
            d_down = dotf(cot_all, hidden, TN)
            d_gate, d_up = dotf(xn, gate_grad, TN), dotf(xn, up_grad, TN)

        if paired:
            token_grad, *sums = backward_block(
                grads, (q, k, v, o), lse, attn_cot, qkv_all, out_all, xh, x_half,
                resid_grad, tables, seg_col, seg_row,
            )
            token_grad = token_grad.astype(F32)
            s_gate, up_low, up_high, s_low, s_high, s_out, near, *far = (w.astype(F32) for w in sums)
            s_up = jnp.concatenate([up_low, up_high], axis=0)
            qkv_raw = jnp.concatenate([near, jnp.concatenate(far, axis=0)], axis=1).reshape(shard, cols // 128, 3, 128)
            qkv_raw = qkv_raw.swapaxes(1, 2).reshape(shard, 3, cols)
            in_raw = jnp.stack([s_gate[:, :units], s_up[:, :units]], axis=1)
            down_sum = jnp.concatenate([s_low[:, :units], s_high[:, :units]], axis=0).T
        else:
            wide = lambda g, d: jnp.concatenate([padded(g), d], axis=1)
            two_a, two_b = comm.reduce(wide(d_gate, d_down[:, :low]), wide(d_up, d_down[:, low:]))

            heads_grad = dotf(attn_cot, w_o, NN).astype(BF)
            pg = attn_bwd(q, k, v, o, heads_grad, lse, tables, seg_col, seg_row)
            d_out = dotf(attn_cot, o, TN)
            d_q, d_k, d_v = (dotf(xh, pg[i], TN) for i in range(3))
            one_a, one_b = comm.reduce(
                jnp.concatenate([d_q, d_k], axis=1), jnp.concatenate([d_v, d_out], axis=1)
            )
            f_one = comm.scatter_rows(
                dotf(pg[0], w_qk[:, :cols], NT)
                + dotf(pg[1], w_qk[:, cols:], NT)
                + dotf(pg[2], w_vo[:, :cols], NT)
            )
            token_grad = resid_grad + normalize_back(f_one, xh_one, scale_one)
            in_raw = jnp.stack([two_a[:, :units], two_b[:, :units]], axis=1)
            down_sum = jnp.concatenate([two_a[:, units + pad :], two_b[:, units + pad :]], axis=1).T
            s_out = one_b[:, cols:]
            qkv_raw = jnp.stack([one_a[:, :cols], one_a[:, cols:], one_b[:, :cols]], axis=1)

        gains = jnp.stack(
            [
                jnp.sum(qkv_raw * w_qkv.astype(F32), axis=(1, 2)),
                jnp.sum(in_raw * w_in.astype(F32), axis=(1, 2)),
            ]
        )
        gains = comm.sum_tensor(gains)
        return (
            result[None],
            token_grad[None],
            gains[0],
            gains[1],
            qkv_raw * gain_one[:, :, None],
            s_out.T,
            in_raw * gain_two[:, :, None],
            down_sum,
        )

    return local


def solution(mesh):
    paired = mesh.shape["dp"] == 16 and mesh.shape["tensor"] == 2
    return jax.shard_map(
        make_local(Chips if paired else Axes),
        mesh=mesh,
        in_specs=(
            P("dp", "tensor", None),
            P("dp", None),
            P("dp", None, "tensor"),
            P("tensor", "dp"),
            P("dp", None, "tensor"),
            P("tensor", "dp"),
            P("dp"),
            P("dp"),
            P("dp", "tensor", None),
        ),
        out_specs=(
            P("dp", "tensor", None),
            P("dp", "tensor", None),
            P("dp"),
            P("dp"),
            P("dp", None, "tensor"),
            P("tensor", "dp"),
            P("dp", None, "tensor"),
            P("tensor", "dp"),
        ),
        check_vma=False,
    )
```

```python
import math

import jax
import jax.numpy as jnp
from jax import lax
from jax.experimental import pallas as pl
from jax.experimental.pallas import tpu as pltpu
from jax.sharding import PartitionSpec as P

HD = 64
EPS = 1e-05
ROTARY_BASE = 160000.0
BF = jnp.bfloat16
F32 = jnp.float32


def dotf(a, b, dims):
    return lax.dot_general(a, b, (dims, ((), ())), preferred_element_type=F32)


NN = ((1,), (0,))
NT = ((1,), (1,))
TN = ((0,), (0,))


def rope_rates():
    return 1.0 / ROTARY_BASE ** (jnp.arange(HD // 2).astype(F32) * (2.0 / HD))


def rope_tables(positions):
    angles = positions.astype(F32)[:, None] * rope_rates()[None, :]
    cos, sin = jnp.cos(angles), jnp.sin(angles)
    zero = jnp.zeros_like(sin)
    cosine = jnp.concatenate([cos] * 4, axis=-1)
    upper = jnp.concatenate([-sin, zero] * 2, axis=-1)
    lower = jnp.concatenate([zero, sin] * 2, axis=-1)
    return cosine, upper, lower


def turn(u, upper, lower):
    return pltpu.roll(u, 128 - HD // 2, 1) * upper + pltpu.roll(u, HD // 2, 1) * lower


def attn_fwd_kernel(xh, wq, wk, wv, cos, upper, lower, seg_col, seg_row, o, q, k, v, lse, kh):
    length = xh.shape[0]
    rows = min(256, length)
    lane = lax.broadcasted_iota(jnp.int32, (length, 128), 1)
    first = lane < HD
    tokens = xh[...]
    qf = dotf(tokens, wq[...], NN)
    qf = qf * cos[...] + turn(qf, upper[...], lower[...])
    q[...] = (qf * (1.0 / math.sqrt(HD))).astype(BF)
    kf = dotf(tokens, wk[...], NN)
    kf = (kf * cos[...] + turn(kf, upper[...], lower[...])).astype(BF)
    k[...] = kf
    kh[0] = jnp.where(first, kf, jnp.zeros_like(kf))
    kh[1] = jnp.where(first, jnp.zeros_like(kf), kf)
    v[...] = dotf(tokens, wv[...], NN).astype(BF)

    def block(i, carry):
        at = pl.multiple_of(i * rows, rows)
        q_rows = q[pl.ds(at, rows), :]
        same = seg_col[pl.ds(at, rows), :] == seg_row[...]
        outs = []
        for head in range(2):
            scores = dotf(q_rows, kh[head], NT)
            scores = jnp.where(same, scores, -1e30)
            top = jnp.max(scores, axis=-1, keepdims=True)
            expv = jnp.exp(scores - top)
            total = jnp.sum(expv, axis=-1, keepdims=True)
            low = (expv * (1.0 / total)).astype(BF)
            outs.append(dotf(low, v[...], NN))
            level = top + jnp.log(total)
            flat = jnp.transpose(jnp.broadcast_to(level, (rows, 128)))
            lse[0, pl.ds(head, 1), pl.ds(at, rows)] = flat[0:1, :]
        o[pl.ds(at, rows), :] = jnp.where(first[:rows], outs[0], outs[1]).astype(BF)
        return carry

    lax.fori_loop(0, length // rows, block, 0)


def attn_fwd(xh, w_qk, w_vo, tables, seg_col, seg_row):
    length, width = xh.shape
    pairs = w_qk.shape[1] // 256
    whole = lambda a: pl.BlockSpec(a.shape, lambda h: (0,) * a.ndim)
    col = lambda off: pl.BlockSpec((width, 128), lambda h: (0, h + off))
    out = pl.BlockSpec((length, 128), lambda h: (0, h))
    shape = jax.ShapeDtypeStruct((length, pairs * 128), BF)
    flops = 2 * length * width * pairs * 384 + 4 * pairs * 2 * length * length * 128
    return pl.pallas_call(
        attn_fwd_kernel,
        grid=(pairs,),
        in_specs=[whole(xh), col(0), col(pairs), col(0)]
        + [whole(t) for t in tables]
        + [whole(seg_col), whole(seg_row)],
        out_specs=[out] * 4 + [pl.BlockSpec((1, 2, length), lambda h: (h, 0, 0))],
        out_shape=[shape] * 4 + [jax.ShapeDtypeStruct((pairs, 2, length), F32)],
        scratch_shapes=[pltpu.VMEM((2, length, 128), BF)],
        cost_estimate=pl.CostEstimate(
            flops=flops, bytes_accessed=length * width * 8, transcendentals=pairs * 2 * length * length
        ),
        name="attn_fwd",
    )(xh, w_qk, w_qk, w_vo, *tables, seg_col, seg_row)


def attn_bwd_kernel(
    q, k, v, o, do, lse, cos, upper, lower, seg_col, seg_row, pg, kh, dk, dv
):
    length = q.shape[0]
    rows = min(256, length)
    lane = lax.broadcasted_iota(jnp.int32, (length, 128), 1)
    first = lane < HD
    kf = k[...]
    none = jnp.zeros_like(kf)
    kh[0] = jnp.where(first, kf, none)
    kh[1] = jnp.where(first, none, kf)
    dk[...] = jnp.zeros_like(dk)
    dv[...] = jnp.zeros_like(dv)

    def block(i, carry):
        at = pl.multiple_of(i * rows, rows)
        here = pl.ds(at, rows)
        q_rows = q[here, :]
        g_rows = do[here, :]
        seg_here = seg_row[:, here]
        same = seg_col[...] == seg_here
        prod = g_rows.astype(F32) * o[here, :].astype(F32)
        f = first[:rows]
        blank = jnp.zeros_like(q_rows)
        dq = jnp.zeros((rows, 128), F32)
        for head in range(2):
            mine = f if head == 0 else jnp.logical_not(f)
            q_head = jnp.where(mine, q_rows, blank)
            g_head = jnp.where(mine, g_rows, blank)
            delta = lax.dot_general(
                jnp.ones((8, 128), F32),
                jnp.where(mine, prod, 0.0),
                (NT, ((), ())),
                precision=lax.Precision.HIGHEST,
                preferred_element_type=F32,
            )[0:1, :]
            scores = dotf(k[...], q_head, NT)
            level = lse[0, pl.ds(head, 1), here]
            probs = jnp.where(same, jnp.exp(scores - level), 0.0)
            dv[...] += dotf(probs.astype(BF), g_head, NN)
            dp = dotf(v[...], g_head, NT)
            ds = (probs * (dp - delta)).astype(BF)
            dk[...] += dotf(ds, q_head, NN)
            dq = dq + dotf(ds, kh[head], TN)
        dq = dq * (1.0 / math.sqrt(HD))
        c, a, b = cos[here, :], upper[here, :], lower[here, :]
        pg[0, here, :] = (dq * c - turn(dq, a, b)).astype(BF)
        return carry

    lax.fori_loop(0, length // rows, block, 0)
    dkf = dk[...]
    pg[1] = (dkf * cos[...] - turn(dkf, upper[...], lower[...])).astype(BF)
    pg[2] = dv[...].astype(BF)


def attn_bwd(q, k, v, o, do, lse, tables, seg_col, seg_row):
    length, width = q.shape
    pairs = width // 128
    whole = lambda a: pl.BlockSpec(a.shape, lambda h: (0,) * a.ndim)
    col = pl.BlockSpec((length, 128), lambda h: (0, h))
    return pl.pallas_call(
        attn_bwd_kernel,
        grid=(pairs,),
        in_specs=[col] * 5
        + [pl.BlockSpec((1, 2, length), lambda h: (h, 0, 0))]
        + [whole(t) for t in tables]
        + [whole(seg_col), whole(seg_row)],
        out_specs=pl.BlockSpec((3, length, 128), lambda h: (0, 0, h)),
        out_shape=jax.ShapeDtypeStruct((3, length, width), BF),
        scratch_shapes=[
            pltpu.VMEM((2, length, 128), BF),
            pltpu.VMEM((length, 128), F32),
            pltpu.VMEM((length, 128), F32),
        ],
        cost_estimate=pl.CostEstimate(
            flops=10 * pairs * 2 * length * length * 128,
            bytes_accessed=length * width * 20,
            transcendentals=pairs * 2 * length * length,
        ),
        name="attn_bwd",
    )(q, k, v, o, do, lse, *tables, seg_col, seg_row)


def in_chunks(total, size, body):
    def step(j, carry):
        body(pl.ds(pl.multiple_of(j * size, size), size))
        return carry

    lax.fori_loop(0, total // size, step, 0)
    if total % size:
        body(pl.ds(total - total % size, total % size))


SHARD = (4, 2, 2)


def place():
    dp = lax.axis_index("dp")
    return dp // 4, (dp // 2) % 2, dp % 2, lax.axis_index("tensor")


def partners():
    z, x, c, y = place()
    at = lambda z, x, c, y: ((z * 2 + x) * 2 + c, y)
    return {
        "z1": at(z + 1 - 2 * (z % 2), x, c, y),
        "z2": at(z + 2 - 4 * (z // 2), x, c, y),
        "z3": at(3 - z, x, c, y),
        "x": at(z, 1 - x, c, y),
        "y": at(z, x, c, 1 - y),
        "c": at(z, x, 1 - c, y),
    }


def meet(peers, other=None):
    barrier = pltpu.get_barrier_semaphore()
    greet = lambda peer: pl.semaphore_signal(
        barrier, inc=1, device_id=peer, device_id_type=pl.DeviceIdType.MESH
    )
    for peer in peers.values():
        greet(peer)
    if other is None:
        pl.semaphore_wait(barrier, len(peers))
    else:
        moved, peer = other

        @pl.when(moved)
        def _():
            greet(peer)

        pl.semaphore_wait(barrier, len(peers) + jnp.where(moved, 1, 0))


def exchanged():
    z, x, c, y = place()
    return c != y, ((z * 2 + x) * 2 + y, c)


def remote(src, dst, send_sem, recv_sem, peer):
    return pltpu.make_async_remote_copy(
        src_ref=src,
        dst_ref=dst,
        send_sem=send_sem,
        recv_sem=recv_sem,
        device_id=peer,
        device_id_type=pl.DeviceIdType.MESH,
    )


class Move:
    def __init__(self, src, dst, sems, i):
        send_sem, recv_sem, near_sem = sems
        self.moved, peer = exchanged()
        self.far = remote(src, dst, send_sem.at[i], recv_sem.at[i], peer)
        self.near = pltpu.make_async_copy(src, dst, near_sem.at[i])

    def start(self):
        @pl.when(self.moved)
        def _():
            self.far.start()

        @pl.when(jnp.logical_not(self.moved))
        def _():
            self.near.start()

    def wait(self):
        @pl.when(self.moved)
        def _():
            self.far.wait()

        @pl.when(jnp.logical_not(self.moved))
        def _():
            self.near.wait()


def move_sems(n):
    return [pltpu.SemaphoreType.DMA((n,))] * 3


def to_place(values):
    z, x, _, y = place()
    tiles = [values[:, j * 128 : (j + 1) * 128] for j in range(8)]
    tiles = [jnp.where(y == 1, pltpu.roll(t, 64, 1), t) for t in tiles]
    for bit, step in ((x, 1), (z % 2, 2), (z // 2, 4)):
        tiles = [jnp.where(bit == 1, tiles[j ^ step], tiles[j]) for j in range(8)]
    return jnp.concatenate(tiles, axis=1)


AXIS = {"z": 4, "x": 2, "y": 2}


def partner(peers, axis, step):
    return peers["z%d" % step if axis == "z" else axis]


class Gather:
    MESSAGES = 15

    def __init__(self, own, buf, rows, cols, order, hops, peers, sems, base):
        self.buf, self.order, self.hops, self.peers = buf, order, hops, peers
        self.part = (rows, cols)
        self.own = own.at[self.part]
        self.send_sem, self.recv_sem = sems
        self.base = base
        n, m, p = (AXIS[axis] for axis in order)
        self.outer, self.middle = range(n), range(1, m)
        self.stages = [
            [(i, 0, 0) for i in range(1, n)],
            [(i, j, 0) for i in range(n) for j in range(1, m)],
            [(i, j, k) for i in range(n) for j in range(m) for k in range(1, p)],
        ]
        self.stages = self.stages[:hops]
        self.numbers = {at: n for n, at in enumerate(sum(self.stages, []))}

    def slot(self, at):
        where = dict(zip(self.order, at))
        return self.buf.at[(where["z"], where["x"], where["y"]) + self.part]

    def copy(self, at):
        hop = max(i for i in range(3) if at[i])
        source = at[:hop] + (0,) * (3 - hop)
        src = self.slot(source) if any(source) else self.own
        n = self.base + self.numbers[at]
        peer = partner(self.peers, self.order[hop], at[hop])
        return remote(src, self.slot(at), self.send_sem.at[n], self.recv_sem.at[n], peer)

    def send(self, stage, *prefix):
        for at in self.stages[stage]:
            if at[: len(prefix)] == prefix:
                self.copy(at).start()

    def start(self):
        self.send(0)

    def relay(self, i):
        if i:
            self.copy((i, 0, 0)).wait_recv()
        self.send(1, i)
        if self.hops == 3:
            self.send(2, i, 0)

    def relay_again(self, i):
        for j in self.middle:
            self.copy((i, j, 0)).wait_recv()
            self.send(2, i, j)

    def finish(self):
        for at in self.stages[-1]:
            self.copy(at).wait_recv()
        for at in self.numbers:
            self.copy(at).wait_send()


def forward_kernel(
    writes, a_in, b_in, g_in, u_in, d_in, x_in, c_in, seg_in, inverse,
    q, k, v, o, lse, xh, w_qkv, w_out, resid, xn, x_half, cot, cos, upper, lower, seg_col, seg_row,
    w_gate, w_up, w_down,
    a_own, b_own, g_own, u_own, d_own, c_own, seg_own,
    kh, x_rel, part, sent, got, send_sem, recv_sem, pair_send, pair_recv, own_sem, *moving,
):
    length = xh.shape[0]
    half = length // 2
    width = xh.shape[1]
    pairs = q.shape[1] // 128
    rows = 256
    core = place()[2]
    peers = partners()
    sems = (send_sem, recv_sem)
    n = Gather.MESSAGES
    whole, low, high = pl.ds(0, 64), pl.ds(0, 32), pl.ds(32, 32)
    wide = w_qkv.shape[4] // 2
    all_ = lambda ref: pl.ds(0, ref.shape[-1])
    plan = (
        (a_own, w_qkv, whole, pl.ds(0, wide), "zyx", 3),
        (a_own, w_qkv, whole, pl.ds(wide, wide), "zyx", 3),
        (b_own, w_out, whole, all_(w_out), "zxy", 3),
        (g_own, w_gate, whole, all_(w_gate), "zyx", 3),
        (u_own, w_up, low, all_(w_up), "zyx", 3),
        (u_own, w_up, high, all_(w_up), "xyz", 3),
        (d_own, w_down, low, all_(w_down), "zyx", 2),
        (d_own, w_down, high, all_(w_down), "zxy", 2),
    )
    gathers = [Gather(*piece, peers, sems, i * n) for i, piece in enumerate(plan)]
    near, far, out, two, late, three = *gathers[:3], gathers[3:5], gathers[5], gathers[6:]
    owns = [
        pltpu.make_async_copy(src, dst.at[0, 0, 0], own_sem.at[i])
        for i, (src, dst) in enumerate(
            ((a_own, w_qkv), (b_own, w_out), (g_own, w_gate), (u_own, w_up), (d_own, w_down))
        )
    ]
    move_a, move_b, move_x, move_seg, move_g, move_u, move_d, move_c = (
        Move(src, dst, moving, i)
        for i, (src, dst) in enumerate(
            (
                (a_in, a_own),
                (b_in, b_own),
                (x_in, x_half),
                (seg_in, seg_own),
                (g_in, g_own),
                (u_in, u_own),
                (d_in, d_own),
                (c_in, c_own),
            )
        )
    )
    meet(peers, exchanged())
    for move in (move_a, move_seg, move_x):
        move.start()

    def tables(here):
        shape = (here.size, 128)
        row = here.start + lax.broadcasted_iota(jnp.int32, shape, 0) + core * half
        row = jnp.where(row >= length, row - length, row)
        angle = row.astype(F32) * inverse[0:1, :]
        front = lax.broadcasted_iota(jnp.int32, shape, 1) % HD < HD // 2
        sin = jnp.sin(angle)
        cos[here, :] = jnp.cos(angle)
        upper[here, :] = jnp.where(front, -sin, 0.0)
        lower[here, :] = jnp.where(front, 0.0, sin)

    move_a.wait()
    near.start()
    far.start()
    near.relay(0)
    owns[0].start()
    in_chunks(length, 64, tables)
    for z in (1, 2, 3):
        near.relay(z)
    for move in (move_b, move_g, move_u, move_d):
        move.start()
    move_seg.wait()
    ids = seg_own[...]
    ids = jnp.where(core == 0, ids, jnp.concatenate([ids[:, half:], ids[:, :half]], axis=1))
    seg_row[...] = ids
    seg_col[...] = jnp.transpose(jnp.broadcast_to(ids[0:1, :], (128, length)))
    move_x.wait()

    def first_norm(i, carry):
        here = pl.ds(pl.multiple_of(i * 128, 128), 128)
        values = to_place(x_half[here, :].astype(F32))
        x_rel[here, :] = values.astype(BF)
        xh[here, :] = normalize(values)[0].astype(BF)
        return carry

    lax.fori_loop(0, half // 128, first_norm, 0)
    swap_xh = remote(
        xh.at[pl.ds(0, half)], xh.at[pl.ds(half, half)], pair_send.at[0], pair_recv.at[0], peers["c"]
    )
    swap_xh.start()
    for z in range(4):
        near.relay_again(z)
        far.relay(z)
    move_b.wait()
    out.start()
    move_g.wait()
    move_u.wait()
    late.start()
    for gather in two:
        gather.start()
    out.relay(0)
    late.relay(0)
    for gather in two:
        gather.relay(0)
    move_d.wait()
    for gather in three:
        gather.start()
    for copy in owns[1:]:
        copy.start()
    swap_xh.wait()
    near.finish()
    owns[0].wait()

    events = {}
    at_step = lambda step, call, *args: events.setdefault(step, []).append((call, args))
    for z in range(4):
        at_step(z, far.relay_again, z)
        if z:
            at_step(z, out.relay, z)
        at_step(5 + z, out.relay_again, z)
        for gather in two:
            if z:
                at_step(1 + 2 * z, gather.relay, z)
            at_step(9 + z, gather.relay_again, z)
        for gather in three:
            at_step(11 + z, gather.relay, z)
    at_step(4, late.relay, 1)
    at_step(5, move_c.start)
    at_step(6, late.relay_again, 0)
    at_step(8, late.relay_again, 1)
    at_step(length // rows * pairs // 2 - 1, far.finish)
    first = lax.broadcasted_iota(jnp.int32, (length, 128), 1) < HD

    def pair(h, carry):
        lanes = pl.ds(pl.multiple_of(h * 128, 128), 128)
        weight = lambda i: w_qkv[
            :, :, :, :, pl.ds(pl.multiple_of((3 * h + i) * 128, 128), 128)
        ].reshape(width, 128)
        tokens = xh[...]
        qf = dotf(tokens, weight(0), NN)
        qf = qf * cos[...] + turn(qf, upper[...], lower[...])
        q[:, lanes] = (qf * (1.0 / math.sqrt(HD))).astype(BF)
        kf = dotf(tokens, weight(1), NN)
        kf = (kf * cos[...] + turn(kf, upper[...], lower[...])).astype(BF)
        k[:, lanes] = kf
        kh[0] = jnp.where(first, kf, jnp.zeros_like(kf))
        kh[1] = jnp.where(first, jnp.zeros_like(kf), kf)
        v[:, lanes] = dotf(tokens, weight(2), NN).astype(BF)

        def block(i, carry):
            for step, calls in events.items():

                @pl.when(h * (length // rows) + i == step)
                def _():
                    for call, args in calls:
                        call(*args)

            at = pl.multiple_of(i * rows, rows)
            q_rows = q[pl.ds(at, rows), lanes]
            same = seg_col[pl.ds(at, rows), 0:1] == seg_row[0:1, :]
            outs = []
            for head in range(2):
                scores = dotf(q_rows, kh[head], NT)
                scores = jnp.where(same, scores, -1e30)
                top = jnp.max(scores, axis=-1, keepdims=True)
                expv = jnp.exp(scores - top)
                total = jnp.sum(expv, axis=-1, keepdims=True)
                low_probs = (expv * (1.0 / total)).astype(BF)
                outs.append(dotf(low_probs, v[:, lanes], NN))
                level = top + jnp.log(total)
                flat = jnp.transpose(jnp.broadcast_to(level, (rows, 128)))
                lse[h, pl.ds(head, 1), pl.ds(at, rows)] = flat[0:1, :]
            o[pl.ds(at, rows), lanes] = jnp.where(first[:rows], outs[0], outs[1]).astype(BF)
            return carry

        return lax.fori_loop(0, length // rows, block, carry)

    lax.fori_loop(0, pairs, pair, 0)
    out.finish()
    owns[1].wait()
    w_o = w_out[...].reshape(width, pairs * 128)

    def project(i, carry):
        at = pl.multiple_of(half + i * rows, rows)
        sent[pl.ds(pl.multiple_of(i * rows, rows), rows), :] = dotf(
            o[pl.ds(at, rows), :], w_o, NT
        ).astype(BF)
        return carry

    lax.fori_loop(0, half // rows, project, 0)

    def project_own(i, carry):
        here = pl.ds(pl.multiple_of(i * rows, rows), rows)
        part[here, :] = dotf(o[here, :], w_o, NT)
        return carry

    give = remote(sent, got, pair_send.at[1], pair_recv.at[1], peers["c"])
    lax.fori_loop(0, half // rows, project_own, 0)
    give.start()
    for copy in writes:
        copy.start()
    move_c.wait()

    def turn_cot(here):
        cot[here, :] = to_place(c_own[here, :].astype(F32)).astype(BF)

    in_chunks(half, 128, turn_cot)
    swap_cot = remote(
        cot.at[pl.ds(0, half)], cot.at[pl.ds(half, half)], pair_send.at[3], pair_recv.at[3], peers["c"]
    )
    swap_cot.start()
    give.wait()

    def second_norm(i, carry):
        here = pl.ds(pl.multiple_of(i * 128, 128), 128)
        values = x_rel[here, :].astype(F32) + (part[here, :] + got[here, :].astype(F32))
        resid[here, :] = values
        xn[here, :] = normalize(values)[0].astype(BF)
        return carry

    lax.fori_loop(0, half // 128, second_norm, 0)
    swap_xn = remote(
        xn.at[pl.ds(0, half)], xn.at[pl.ds(half, half)], pair_send.at[2], pair_recv.at[2], peers["c"]
    )
    swap_xn.start()
    for gather in two + three + [late]:
        gather.finish()
    for copy in owns[2:]:
        copy.wait()
    swap_cot.wait()
    swap_xn.wait()
    for copy in writes:
        copy.wait()


WRITTEN = (0, 1, 2, 3, 5, 6, 7, 10, 12, 13, 14, 15)


def forward_written(*refs):
    count = len(WRITTEN)
    ins, outs, scratch = refs[:9], list(refs[9:29]), refs[29 : -count - 1]
    held, sem = refs[-count - 1 : -1], refs[-1]
    writes = []
    for i, (n, ref) in enumerate(zip(WRITTEN, held)):
        writes.append(pltpu.make_async_copy(ref, outs[n], sem.at[i]))
        outs[n] = ref
    forward_kernel(writes, *ins, *outs, *scratch)


def forward_block(owned, x_half, cot_half, seg, inverse):
    half, width = x_half.shape
    length = 2 * half
    cols = owned[1].shape[1]
    pairs = cols // 128
    units = owned[2].shape[1]
    shard = width // 16
    vmem = pl.BlockSpec(memory_space=pltpu.VMEM)
    any_ = pl.BlockSpec(memory_space=pl.ANY)
    gathered = lambda n: jax.ShapeDtypeStruct(SHARD + (shard, n), BF)
    heads = jax.ShapeDtypeStruct((length, cols), BF)
    flat = jax.ShapeDtypeStruct((length, width), BF)
    table = jax.ShapeDtypeStruct((length, 128), F32)
    shapes = [heads] * 4 + [
        jax.ShapeDtypeStruct((pairs, 2, length), F32),
        flat,
        gathered(3 * cols),
        gathered(cols),
        jax.ShapeDtypeStruct((half, width), F32),
        flat,
        jax.ShapeDtypeStruct((half, width), BF),
        flat,
    ]
    shapes += [table] * 4 + [jax.ShapeDtypeStruct((8, length), F32)] + [gathered(units)] * 3
    return pl.pallas_call(
        forward_written,
        in_specs=[any_] * 8 + [vmem],
        out_specs=[any_ if i in WRITTEN + (17, 18, 19) else vmem for i in range(20)],
        out_shape=shapes,
        scratch_shapes=[pltpu.VMEM((shard, 3 * cols), BF), pltpu.VMEM((shard, cols), BF)]
        + [pltpu.VMEM((shard, units), BF)] * 3
        + [
            pltpu.VMEM((half, width), BF),
            pltpu.VMEM((8, length), F32),
            pltpu.VMEM((2, length, 128), BF),
            pltpu.VMEM((half, width), BF),
            pltpu.VMEM((half, width), F32),
            pltpu.VMEM((half, width), BF),
            pltpu.VMEM((half, width), BF),
            pltpu.SemaphoreType.DMA((8 * Gather.MESSAGES,)),
            pltpu.SemaphoreType.DMA((8 * Gather.MESSAGES,)),
            pltpu.SemaphoreType.DMA((4,)),
            pltpu.SemaphoreType.DMA((4,)),
            pltpu.SemaphoreType.DMA((5,)),
        ]
        + move_sems(8)
        + [pltpu.VMEM(shapes[i].shape, shapes[i].dtype) for i in WRITTEN]
        + [pltpu.SemaphoreType.DMA((len(WRITTEN),))],
        compiler_params=pltpu.CompilerParams(
            collective_id=0, has_side_effects=True, vmem_limit_bytes=60 << 20
        ),
        name="forward_block",
    )(*owned, x_half, cot_half, seg, inverse)


class Reduce:
    MESSAGES = 12
    ORDER = (2, 3, 1, 0)

    def __init__(self, parts, near, rows, axes, peers, sems, base, bufs, out):
        self.parts, self.near, self.rows, self.axes, self.peers = parts, near, rows, axes, peers
        self.send_sem, self.recv_sem = sems
        self.base = base
        self.one, self.two, self.three, self.sum = bufs
        self.out = out

    def link(self, i, src, dst, peer):
        n = self.base + i
        return remote(src, dst, self.send_sem.at[n], self.recv_sem.at[n], peer)

    def first(self, z):
        if self.axes == "xy":
            src = self.parts.at[z, :, 1, self.rows]
        else:
            src = self.parts.at[z, 1, :, self.rows]
        return self.link(z, src, self.one.at[z], self.peers[self.axes[1]])

    def second(self, z):
        return self.link(4 + z, self.one.at[z, 1], self.two.at[z], self.peers[self.axes[0]])

    def third(self, z):
        return self.link(7 + z, self.two.at[z], self.three.at[z - 1], self.peers["z%d" % z])

    def start(self):
        for z in self.ORDER:
            self.first(z).start()

    def add_first(self, z):
        self.first(z).wait_recv()
        self.one[z] = (self.one[z].astype(F32) + self.near(z).astype(F32)).astype(BF)

    def relay_first(self, z):
        self.add_first(z)
        self.second(z).start()

    def resume(self):
        for z in self.ORDER:
            self.second(z).start()

    def relay_second(self, z):
        self.second(z).wait_recv()
        self.two[z] = (self.two[z].astype(F32) + self.one[z, 0].astype(F32)).astype(BF)
        if z:
            self.third(z).start()

    def last(self):
        moved, peer = exchanged()
        return moved, self.link(11, self.sum, self.out, peer)

    def total(self):
        total = self.two[0].astype(F32)
        for z in (1, 2, 3):
            self.third(z).wait_recv()
            total = total + self.three[z - 1].astype(F32)
        return total

    def finish(self):
        self.sum[...] = self.total().astype(BF)
        moved, copy = self.last()

        @pl.when(moved)
        def _():
            copy.start()

        @pl.when(jnp.logical_not(moved))
        def _():
            self.out[...] = self.sum[...]

    def sent(self):
        hops = (self.second,) if self.parts is None else (self.first, self.second)
        thirds = [self.third(z) for z in (1, 2, 3)]
        return [hop(z) for z in range(4) for hop in hops] + thirds

    def close(self):
        for copy in self.sent():
            copy.wait_send()
        moved, copy = self.last()

        @pl.when(moved)
        def _():
            copy.wait()


class ReduceAlongZ(Reduce):
    def first(self, z):
        src = self.parts.at[z, :, :, self.rows]
        return self.link(z - 1, src, self.one.at[z - 1], self.peers["z%d" % z])

    def second(self):
        return self.link(3, self.two.at[:, 1], self.three.at[0:2], self.peers["y"])

    def third(self):
        return self.link(4, self.three.at[1], self.three.at[2], self.peers["x"])

    def start(self):
        for z in (2, 3, 1):
            self.first(z).start()

    def relay_first(self):
        total = self.near().astype(F32)
        for z in (1, 2, 3):
            self.first(z).wait_recv()
            total = total + self.one[z - 1].astype(F32)
        self.two[...] = total.astype(BF)
        self.second().start()

    def relay_second(self):
        self.second().wait_recv()
        for x in (0, 1):
            self.three[x] = (self.three[x].astype(F32) + self.two[x, 0].astype(F32)).astype(BF)
        self.third().start()

    def total(self):
        self.third().wait_recv()
        return self.three[0].astype(F32) + self.three[2].astype(F32)

    def sent(self):
        return [self.first(z) for z in (1, 2, 3)] + [self.second(), self.third()]


def mlp_kernel(
    reads, writes, down_in, xn, cot, w_gate, w_up, resid,
    result, resid_grad, attn_cot, d_gate, d_up, d_low, d_high,
    w_down, d_down, hidden, act, slope_up, gate_grad, up_grad, own, sent, got, placed,
    send_sem, recv_sem, last_send, last_recv, first_send, first_recv, own_sem, *moving,
):
    length, width = xn.shape
    half = length // 2
    units = w_gate.shape[1]
    peers = {axis: partners()[axis] for axis in "xyc"}
    move = Move(placed, result, moving, 0)
    low, high = pl.ds(0, 32), pl.ds(32, 32)
    most, few = pl.ds(0, 48), pl.ds(48, 16)
    at_low = lambda ref, z, x: ref.at[z, x, :, low]
    at_high = lambda ref, z, y: ref.at[z, :, y, high]
    last = []
    for z in range(4):
        for i, (part, axis) in enumerate(((at_low, "x"), (at_high, "y"))):
            n = 2 * z + i
            last.append(
                remote(
                    part(down_in, z, 0), part(w_down, z, 1), last_send.at[n], last_recv.at[n], peers[axis]
                )
            )
    every = pl.ds(0, 4)
    owns = [
        pltpu.make_async_copy(part(down_in, every, 0), part(w_down, every, 0), own_sem.at[i])
        for i, part in enumerate((at_low, at_high))
    ]
    sems = (first_send, first_recv)
    n = Reduce.MESSAGES
    reduce_low = Reduce(
        d_down, lambda z: d_down[z, 0, :, 0:48], most, "yx", peers, sems, 0, (d_low, None, None, None), None
    )
    reduce_high = Reduce(
        d_down, lambda z: d_down[z, :, 0, 48:64], few, "xy", peers, sems, n, (d_high, None, None, None), None
    )
    for copy in reads:
        copy.start()
    meet(peers, exchanged())
    for copy in last + owns:
        copy.start()
    for copy in reads:
        copy.wait()
    back, front = pl.ds(half, half), pl.ds(0, half)

    def gate_and_up(rows):
        def step(cols):
            gate = dotf(xn[rows, :], w_gate[:, cols], NN)
            up = dotf(xn[rows, :], w_up[:, cols], NN)
            value, slope = gelu_parts(gate)
            hidden[rows, cols] = (value * up).astype(BF)
            act[rows, cols] = value
            slope_up[rows, cols] = up * slope

        in_chunks(units, 256, step)

    def units_back(rows):
        def step(cols):
            down = w_down[:, :, :, :, cols].reshape(width, cols.size)
            grad = dotf(cot[rows, :], down, NN).astype(BF).astype(F32)
            gate_grad[rows, cols] = (grad * slope_up[rows, cols]).astype(BF)
            up_grad[rows, cols] = (grad * act[rows, cols]).astype(BF)

        in_chunks(units, 256, step)

    def sums(rows, put):
        def step(z, carry):
            here = pl.ds(pl.multiple_of(z * 256, 256), 256)
            down = w_down[z].reshape(256, units)
            put[0, :, here] = dotf(hidden[rows, :], down, NT).astype(put.dtype)
            both = dotf(gate_grad[rows, :], w_gate[here, :], NT)
            both = both + dotf(up_grad[rows, :], w_up[here, :], NT)
            put[1, :, here] = both.astype(put.dtype)
            return carry

        lax.fori_loop(0, width // 256, step, 0)

    gate_and_up(back)
    gate_and_up(front)
    for z in Reduce.ORDER:
        left = jnp.transpose(cot[:, z * 256 : (z + 1) * 256])
        d_down[z] = dotf(left, hidden[...], NN).astype(BF).reshape(2, 2, 64, units)
        reduce_low.first(z).start()
        reduce_high.first(z).start()
    for copy in owns:
        copy.wait()
    for copy in last:
        copy.wait()
    units_back(back)
    sums(back, sent)
    give = remote(sent, got, send_sem.at[0], recv_sem.at[0], peers["c"])
    give.start()
    units_back(front)
    sums(front, own)
    give.wait()

    def finish(here):
        values = resid[here, :]
        mlp = own[0, here, :] + got[0, here, :].astype(F32)
        placed[here, :] = to_place(values + mlp).astype(BF)
        xhat, scale = normalize(values)
        back = normalize_back(own[1, here, :] + got[1, here, :].astype(F32), xhat, scale)
        grad = cot[here, :].astype(F32) + back
        resid_grad[here, :] = grad
        attn_cot[here, :] = grad.astype(BF)

    in_chunks(half, 64, finish)
    swap = remote(
        attn_cot.at[pl.ds(0, half)], attn_cot.at[pl.ds(half, half)], send_sem.at[1], recv_sem.at[1], peers["c"]
    )
    swap.start()
    move.start()

    def weights(here):
        left = jnp.transpose(xn[:, here])
        d_gate[here, :] = dotf(left, gate_grad[...], NN).astype(BF)
        d_up[here, :] = dotf(left, up_grad[...], NN).astype(BF)

    in_chunks(width, 256, weights)
    writes[0].start()
    for z in Reduce.ORDER:
        reduce_low.add_first(z)
        reduce_high.add_first(z)
    for z in range(4):
        reduce_low.first(z).wait_send()
        reduce_high.first(z).wait_send()
    for copy in writes[1:]:
        copy.start()
    swap.wait()
    move.wait()
    for copy in writes:
        copy.wait()


def mlp_staged(*refs):
    ins, outs, scratch = refs[1:6], list(refs[6:13]), refs[13:-10]
    held, read_sem, write_sem = refs[-10:-2], refs[-2], refs[-1]
    reads = [pltpu.make_async_copy(a, b, read_sem.at[i]) for i, (a, b) in enumerate(zip(ins, held))]
    writes = []
    for i, (n, ref) in enumerate(zip((1, 3, 4), held[5:])):
        writes.append(pltpu.make_async_copy(ref, outs[n], write_sem.at[i]))
        outs[n] = ref
    mlp_kernel(reads, writes, refs[0], *held[:5], *outs, *scratch)


def mlp_block(down_in, xn, cot, w_gate, w_up, resid):
    length, width = xn.shape
    half = length // 2
    units = w_gate.shape[1]
    shard = width // 16
    vmem = pl.BlockSpec(memory_space=pltpu.VMEM)
    any_ = pl.BlockSpec(memory_space=pl.ANY)
    grads = jax.ShapeDtypeStruct((width, units), BF)
    dma = lambda n: pltpu.SemaphoreType.DMA((n,))
    return pl.pallas_call(
        mlp_staged,
        in_specs=[any_] * 6,
        out_specs=[any_, any_, vmem, any_, any_, vmem, vmem],
        out_shape=[
            jax.ShapeDtypeStruct((half, width), BF),
            jax.ShapeDtypeStruct((half, width), F32),
            jax.ShapeDtypeStruct((length, width), BF),
            grads,
            grads,
            jax.ShapeDtypeStruct((4, 2, shard * 3 // 4, units), BF),
            jax.ShapeDtypeStruct((4, 2, shard // 4, units), BF),
        ],
        scratch_shapes=[pltpu.VMEM(SHARD + (shard, units), BF)] * 2
        + [
            pltpu.VMEM((length, units), BF),
            pltpu.VMEM((length, units), F32),
            pltpu.VMEM((length, units), F32),
            pltpu.VMEM((length, units), BF),
            pltpu.VMEM((length, units), BF),
            pltpu.VMEM((2, half, width), F32),
            pltpu.VMEM((2, half, width), BF),
            pltpu.VMEM((2, half, width), BF),
            pltpu.VMEM((half, width), BF),
        ]
        + [dma(2), dma(2), dma(8), dma(8), dma(2 * Reduce.MESSAGES), dma(2 * Reduce.MESSAGES), dma(2)]
        + move_sems(1)
        + [pltpu.VMEM(a.shape, a.dtype) for a in (xn, cot, w_gate, w_up, resid)]
        + [pltpu.VMEM((half, width), F32)]
        + [pltpu.VMEM((width, units), BF)] * 2
        + [dma(5), dma(3)],
        compiler_params=pltpu.CompilerParams(
            collective_id=1, has_side_effects=True, vmem_limit_bytes=63 << 20
        ),
        name="mlp_block",
    )(down_in, xn, cot, w_gate, w_up, resid)


def backward_kernel(
    reads, d_gate, d_up, d_low, d_high, q, k, v, o, lse, attn_cot, w_qkv, w_out, xh, x_half, resid_grad,
    cos, upper, lower, seg_col, seg_row,
    token_grad, s_gate, s_up_low, s_up_high, s_down_low, s_down_high, s_out, s_near, s_far_low, s_far_high,
    d_out, d_near, d_far, pg, heads_grad, kh, dk, dv, own, sent, got, placed,
    near_gate, near_up_low, near_up_high,
    *rest,
):
    bufs = [rest[4 * i : 4 * i + 4] for i in range(3)]
    bufs += [(first,) + rest[12 + 3 * i : 15 + 3 * i] for i, first in enumerate((d_low, d_high))]
    bufs += [rest[18 + 4 * i : 22 + 4 * i] for i in range(4)]
    send_sem, recv_sem, pair_send, pair_recv, near_sem, *moving = rest[34:]
    length, width = xh.shape
    half = length // 2
    cols = q.shape[1]
    pairs = cols // 128
    rows = 256
    peers = partners()
    sems = (send_sem, recv_sem)
    n = Reduce.MESSAGES
    whole, low, high = pl.ds(0, 64), pl.ds(0, 32), pl.ds(32, 32)
    held = lambda ref: (lambda z: ref[z])
    plan = (
        (Reduce, d_gate, held(near_gate), whole, "yx", s_gate),
        (Reduce, d_up, held(near_up_low), low, "xy", s_up_low),
        (ReduceAlongZ, d_up, lambda: near_up_high[...], high, None, s_up_high),
        (Reduce, None, None, None, "yx", s_down_low),
        (Reduce, None, None, None, "xy", s_down_high),
        (Reduce, d_out, lambda z: d_out[z, 0], whole, "yx", s_out),
        (Reduce, d_near, lambda z: d_near[z, 0], whole, "yx", s_near),
        (Reduce, d_far, lambda z: d_far[z, 0, :, 0:32], low, "yx", s_far_low),
        (Reduce, d_far, lambda z: d_far[z, :, 0, 32:64], high, "xy", s_far_high),
    )
    parts = [
        kind(src, near, rows_, axes, peers, sems, i * n, bufs[i], out)
        for i, (kind, src, near, rows_, axes, out) in enumerate(plan)
    ]
    gate, up_low, up_high, down_low, down_high, out, near, far_low, far_high = parts
    nears = [
        pltpu.make_async_copy(src, dst, near_sem.at[i])
        for i, (src, dst) in enumerate(
            (
                (d_gate.at[:, 0], near_gate),
                (d_up.at[:, :, 0, low], near_up_low),
                (d_up.at[0, :, :, high], near_up_high),
            )
        )
    ]
    for copy in nears + reads:
        copy.start()
    meet(peers, exchanged())
    up_high.start()
    down_low.resume()
    down_high.resume()
    gate.start()
    up_low.start()
    for i in (3, 5, 7):
        reads[i].wait()

    def heads(here):
        heads_grad[here, :] = dotf(attn_cot[here, :], w_out[...], NN).astype(BF)

    in_chunks(length, 256, heads)

    def out_weights(z, carry):
        here = pl.ds(pl.multiple_of(z * 256, 256), 256)
        value = dotf(jnp.transpose(attn_cot[:, here]), o[...], NN).astype(BF)
        d_out[z] = value.reshape(2, 2, 64, cols)
        return carry

    lax.fori_loop(0, width // 256, out_weights, 0)
    out.start()
    for copy in nears + [copy for i, copy in enumerate(reads) if i not in (3, 5, 7)]:
        copy.wait()
    for z in Reduce.ORDER:
        down_low.relay_second(z)
        down_high.relay_second(z)

    events = {}
    for i, z in enumerate(Reduce.ORDER):
        events.setdefault((3, 6, 10, 13)[i], []).append(lambda z=z: gate.relay_first(z))
        events.setdefault((5, 7, 8, 10)[i], []).append(lambda z=z: up_low.relay_first(z))
    for z in Reduce.ORDER[:2]:
        events.setdefault(14, []).append(lambda z=z: gate.relay_second(z))
    events.setdefault(9, []).append(up_high.relay_first)
    events.setdefault(13, []).append(up_high.relay_second)

    def weights(ref, at):
        def step(z, carry):
            left = jnp.transpose(xh[:, pl.ds(pl.multiple_of(z * 256, 256), 256)])
            value = dotf(left, pg[:, at : at + ref.shape[-1]], NN).astype(BF)
            ref[z] = value.reshape(2, 2, 64, ref.shape[-1])
            return carry

        lax.fori_loop(0, width // 256, step, 0)

    lane = lax.broadcasted_iota(jnp.int32, (length, 128), 1)
    first = lane < HD

    def pair(h, carry):
        lanes = pl.ds(pl.multiple_of(h * 128, 128), 128)
        third = lambda i: pl.ds(pl.multiple_of((3 * h + i) * 128, 128), 128)
        kf = k[:, lanes]
        none = jnp.zeros_like(kf)
        kh[0] = jnp.where(first, kf, none)
        kh[1] = jnp.where(first, none, kf)
        dk[...] = jnp.zeros_like(dk)
        dv[...] = jnp.zeros_like(dv)

        def block(i, carry):
            for step, calls in events.items():

                @pl.when(h * (length // rows) + i == step)
                def _():
                    for call in calls:
                        call()

            at = pl.multiple_of(i * rows, rows)
            here = pl.ds(at, rows)
            q_rows = q[here, lanes]
            g_rows = heads_grad[here, lanes]
            same = seg_col[:, 0:1] == seg_row[0:1, here]
            prod = g_rows.astype(F32) * o[here, lanes].astype(F32)
            f = first[:rows]
            blank = jnp.zeros_like(q_rows)
            dq = jnp.zeros((rows, 128), F32)
            for head in range(2):
                mine = f if head == 0 else jnp.logical_not(f)
                q_head = jnp.where(mine, q_rows, blank)
                g_head = jnp.where(mine, g_rows, blank)
                delta = lax.dot_general(
                    jnp.ones((8, 128), F32),
                    jnp.where(mine, prod, 0.0),
                    (NT, ((), ())),
                    precision=lax.Precision.HIGHEST,
                    preferred_element_type=F32,
                )[0:1, :]
                scores = dotf(k[:, lanes], q_head, NT)
                level = lse[h, pl.ds(head, 1), here]
                probs = jnp.where(same, jnp.exp(scores - level), 0.0)
                dv[...] += dotf(probs.astype(BF), g_head, NN)
                dp = dotf(v[:, lanes], g_head, NT)
                ds = (probs * (dp - delta)).astype(BF)
                dk[...] += dotf(ds, q_head, NN)
                dq = dq + dotf(ds, kh[head], TN)
            dq = dq * (1.0 / math.sqrt(HD))
            c, a, b = cos[here, :], upper[here, :], lower[here, :]
            pg[here, third(0)] = (dq * c - turn(dq, a, b)).astype(BF)
            return carry

        lax.fori_loop(0, length // rows, block, 0)
        dkf = dk[...]
        pg[:, third(1)] = (dkf * cos[...] - turn(dkf, upper[...], lower[...])).astype(BF)
        pg[:, third(2)] = dv[...].astype(BF)

        @pl.when(h == pairs // 2 - 1)
        def _():
            weights(d_near, 0)
            near.start()

        return carry

    lax.fori_loop(0, pairs, pair, 0)
    weights(d_far, d_near.shape[-1])
    far_low.start()
    far_high.start()

    def back(tokens, put):
        def step(here):
            put[:, here] = dotf(pg[tokens, :], w_qkv[here, :], NT).astype(put.dtype)

        in_chunks(width, 256, step)

    for z in Reduce.ORDER[2:]:
        gate.relay_second(z)
    for z in Reduce.ORDER:
        out.relay_first(z)
    back(pl.ds(half, half), sent)
    give = remote(sent, got, pair_send.at[0], pair_recv.at[0], peers["c"])
    give.start()
    for z in Reduce.ORDER:
        up_low.relay_second(z)
    back(pl.ds(0, half), own)
    for z in Reduce.ORDER:
        out.relay_second(z)
    for part in (down_low, down_high):
        part.finish()
    give.wait()

    def finish(here):
        xhat, scale = normalize(to_place(x_half[here, :].astype(F32)))
        f = own[here, :] + got[here, :].astype(F32)
        value = resid_grad[here, :] + normalize_back(f, xhat, scale)
        placed[here, :] = to_place(value).astype(BF)

    in_chunks(half, 64, finish)
    move = Move(placed, token_grad, moving, 0)
    move.start()
    for z in Reduce.ORDER:
        near.relay_first(z)
    for z in Reduce.ORDER:
        far_high.relay_first(z)
    for z in Reduce.ORDER:
        far_low.relay_first(z)
        near.relay_second(z)
    for part in (gate, up_high, up_low):
        part.finish()
    out.finish()
    for z in Reduce.ORDER:
        far_high.relay_second(z)
        far_low.relay_second(z)
    near.finish()
    far_high.finish()
    far_low.finish()
    for part in parts:
        part.close()
    move.wait()


def backward_staged(*refs):
    held, sem = refs[-17:-1], refs[-1]
    reads = [pltpu.make_async_copy(a, b, sem.at[i]) for i, (a, b) in enumerate(zip(refs[4:20], held))]
    backward_kernel(reads, *refs[:4], *held, *refs[20:-17])


def backward_block(grads, heads, lse, attn_cot, w_qkv, w_out, xh, x_half, resid_grad, tables, seg_col, seg_row):
    length, width = xh.shape
    half = length // 2
    cols = heads[0].shape[1]
    units = grads[0].shape[1]
    shard = width // 16
    vmem = pl.BlockSpec(memory_space=pltpu.VMEM)
    any_ = pl.BlockSpec(memory_space=pl.ANY)
    wide = 3 * cols // 2
    sizes = [(shard, units), (shard // 2, units), (shard // 2, units)]
    sizes += [g.shape[2:] for g in grads[2:]]
    sizes += [(shard, cols), (shard, wide), (shard // 2, wide), (shard // 2, wide)]
    along_z, begun = (2,), (3, 4)
    bufs = []
    for i, size in enumerate(sizes):
        if i in along_z:
            lead = (3, 2, 2), (2, 2), (3,)
        else:
            lead = (4, 2), (4,), (3,)
        bufs += [pltpu.VMEM(n + size, BF) for n in lead[i in begun :] + ((),)]
    nears = [pltpu.VMEM(((2, 2) if i in along_z else (4, 2)) + size, BF) for i, size in enumerate(sizes[:3])]
    messages = 9 * Reduce.MESSAGES
    operands = (*heads, lse, attn_cot, w_qkv, w_out, xh, x_half, resid_grad, *tables, seg_col, seg_row)
    return pl.pallas_call(
        backward_staged,
        in_specs=[any_] * 2 + [vmem] * 2 + [any_] * 16,
        out_specs=[vmem] * 10,
        out_shape=[jax.ShapeDtypeStruct((half, width), BF)]
        + [jax.ShapeDtypeStruct(size, BF) for size in sizes],
        scratch_shapes=[pltpu.VMEM(SHARD + (shard, n), BF) for n in (cols, wide, wide)]
        + [
            pltpu.VMEM((length, 3 * cols), BF),
            pltpu.VMEM((length, cols), BF),
            pltpu.VMEM((2, length, 128), BF),
            pltpu.VMEM((length, 128), F32),
            pltpu.VMEM((length, 128), F32),
            pltpu.VMEM((half, width), F32),
            pltpu.VMEM((half, width), BF),
            pltpu.VMEM((half, width), BF),
            pltpu.VMEM((half, width), BF),
        ]
        + nears
        + bufs
        + [
            pltpu.SemaphoreType.DMA((messages,)),
            pltpu.SemaphoreType.DMA((messages,)),
            pltpu.SemaphoreType.DMA((1,)),
            pltpu.SemaphoreType.DMA((1,)),
            pltpu.SemaphoreType.DMA((3,)),
        ]
        + move_sems(1)
        + [pltpu.VMEM(a.shape, a.dtype) for a in operands]
        + [pltpu.SemaphoreType.DMA((16,))],
        compiler_params=pltpu.CompilerParams(
            collective_id=2, has_side_effects=True, vmem_limit_bytes=60 << 20
        ),
        name="backward_block",
    )(
        *(g.reshape(SHARD + (shard, units)) for g in grads[:2]), *grads[2:],
        *operands,
    )


class Chips:
    def sum_tensor(self, value):
        pairs = [(2 * i + y, 2 * i + 1 - y) for i in range(16) for y in range(2)]
        return value + lax.ppermute(value, ("dp", "tensor"), pairs)


class Axes:
    def gather_rows(self, value):
        return lax.all_gather(value, "tensor", axis=0, tiled=True)

    def scatter_rows(self, value):
        return lax.psum_scatter(value.astype(BF), "tensor", scatter_dimension=0, tiled=True).astype(F32)

    def reduce(self, a, b):
        return tuple(
            lax.psum_scatter(w.astype(BF), "dp", scatter_dimension=0, tiled=True).astype(F32)
            for w in (a, b)
        )

    def sum_tensor(self, value):
        return lax.psum(value, "tensor")


def normalize(values):
    centred = values - jnp.mean(values, axis=-1, keepdims=True)
    scale = lax.rsqrt(jnp.mean(centred * centred, axis=-1, keepdims=True) + EPS)
    return centred * scale, scale


def normalize_back(f, xhat, scale):
    return scale * (
        f
        - jnp.mean(f, axis=-1, keepdims=True)
        - xhat * jnp.mean(f * xhat, axis=-1, keepdims=True)
    )


def gelu_parts(gate):
    half_erf = 0.5 * (1.0 + lax.erf(gate * (1.0 / math.sqrt(2.0))))
    density = jnp.exp(-0.5 * gate * gate) * (1.0 / math.sqrt(2.0 * math.pi))
    return gate * half_erf, half_erf + gate * density


def make_local(comm_type):
    def local(tokens, segments, w_qkv, w_out, w_in, w_down, g_attn, g_mlp, cotangent):
        comm = comm_type()
        paired = comm_type is Chips
        shard = w_qkv.shape[0]
        cols = w_qkv.shape[2]
        units = w_in.shape[2]
        low = 128 * (units // 256)
        pad = 128 * pl.cdiv(units, 128) - units
        gain_one = g_attn.astype(F32)[:, None]
        gain_two = g_mlp.astype(F32)[:, None]
        scaled = lambda w, g: (w.astype(F32) * g).astype(BF)
        padded = lambda w: jnp.pad(w, ((0, 0), (0, pad)))
        down_rows = w_down.T
        a_one = jnp.concatenate([scaled(w_qkv[:, 0], gain_one), scaled(w_qkv[:, 1], gain_one)], axis=1)
        b_one = jnp.concatenate([scaled(w_qkv[:, 2], gain_one), w_out.T], axis=1)
        own_gate, own_up = scaled(w_in[:, 0], gain_two), scaled(w_in[:, 1], gain_two)

        owned = (a_one, b_one, own_gate, own_up, down_rows)
        if paired:
            by_pair = scaled(w_qkv, gain_one[:, None]).reshape(shard, 3, cols // 128, 128).swapaxes(1, 2)
            owned = (by_pair.reshape(shard, 3 * cols), w_out.T) + tuple(padded(w) for w in owned[2:])
            seg = jnp.broadcast_to(segments.astype(F32), (8, segments.shape[1]))
            inverse = jnp.broadcast_to(jnp.tile(rope_rates(), 4), (8, 128))
            (
                q, k, v, o, lse, xh, qkv_all, out_all, resid, xn, x_half, cot_all, *tables, seg_col, seg_row,
                w_gate, w_up, w_dn,
            ) = forward_block(owned, tokens[0], cotangent[0], seg, inverse)
            qkv_all, out_all, w_gate, w_up = (
                w.reshape(-1, w.shape[-1]) for w in (qkv_all, out_all, w_gate, w_up)
            )
        else:
            w_qk, w_vo, w_gate, w_up, w_dn = (
                lax.all_gather(w, "dp", axis=0, tiled=True) for w in owned
            )
            w_o = w_vo[:, cols:]
            seg_col, seg_row = segments[0][:, None], segments
            cot = cotangent[0]
            cot_all = comm.gather_rows(cot)
            tables = rope_tables(jnp.arange(segments.shape[1]))
            x_in = tokens[0].astype(F32)
            xh_one, scale_one = normalize(x_in)
            xh = comm.gather_rows(xh_one.astype(BF))
            o, q, k, v, lse = attn_fwd(xh, w_qk, w_vo, tables, seg_col, seg_row)
            resid = x_in + comm.scatter_rows(dotf(o, w_o, NT))
            xh_two, scale_two = normalize(resid)
            xn = comm.gather_rows(xh_two.astype(BF))
        if paired:
            result, resid_grad, attn_cot, *grads = mlp_block(w_dn, xn, cot_all, w_gate, w_up, resid)
        else:
            gate, up = dotf(xn, w_gate, NN), dotf(xn, w_up, NN)
            act, slope = gelu_parts(gate)
            hidden = (act * up).astype(BF)
            mlp = comm.scatter_rows(dotf(hidden, w_dn, NT))
            result = (resid + mlp).astype(BF)
            hidden_grad = dotf(cot_all, w_dn, NN).astype(BF).astype(F32)
            gate_grad = (hidden_grad * up * slope).astype(BF)
            up_grad = (hidden_grad * act).astype(BF)
            f_two = comm.scatter_rows(dotf(gate_grad, w_gate, NT) + dotf(up_grad, w_up, NT))
            resid_grad = cot.astype(F32) + normalize_back(f_two, xh_two, scale_two)
            attn_cot = comm.gather_rows(resid_grad.astype(BF))
            d_down = dotf(cot_all, hidden, TN)
            d_gate, d_up = dotf(xn, gate_grad, TN), dotf(xn, up_grad, TN)

        if paired:
            token_grad, *sums = backward_block(
                grads, (q, k, v, o), lse, attn_cot, qkv_all, out_all, xh, x_half,
                resid_grad, tables, seg_col, seg_row,
            )
            token_grad = token_grad.astype(F32)
            s_gate, up_low, up_high, s_low, s_high, s_out, near, *far = (w.astype(F32) for w in sums)
            s_up = jnp.concatenate([up_low, up_high], axis=0)
            qkv_raw = jnp.concatenate([near, jnp.concatenate(far, axis=0)], axis=1).reshape(shard, cols // 128, 3, 128)
            qkv_raw = qkv_raw.swapaxes(1, 2).reshape(shard, 3, cols)
            in_raw = jnp.stack([s_gate[:, :units], s_up[:, :units]], axis=1)
            down_sum = jnp.concatenate([s_low[:, :units], s_high[:, :units]], axis=0).T
        else:
            wide = lambda g, d: jnp.concatenate([padded(g), d], axis=1)
            two_a, two_b = comm.reduce(wide(d_gate, d_down[:, :low]), wide(d_up, d_down[:, low:]))

            heads_grad = dotf(attn_cot, w_o, NN).astype(BF)
            pg = attn_bwd(q, k, v, o, heads_grad, lse, tables, seg_col, seg_row)
            d_out = dotf(attn_cot, o, TN)
            d_q, d_k, d_v = (dotf(xh, pg[i], TN) for i in range(3))
            one_a, one_b = comm.reduce(
                jnp.concatenate([d_q, d_k], axis=1), jnp.concatenate([d_v, d_out], axis=1)
            )
            f_one = comm.scatter_rows(
                dotf(pg[0], w_qk[:, :cols], NT)
                + dotf(pg[1], w_qk[:, cols:], NT)
                + dotf(pg[2], w_vo[:, :cols], NT)
            )
            token_grad = resid_grad + normalize_back(f_one, xh_one, scale_one)
            in_raw = jnp.stack([two_a[:, :units], two_b[:, :units]], axis=1)
            down_sum = jnp.concatenate([two_a[:, units + pad :], two_b[:, units + pad :]], axis=1).T
            s_out = one_b[:, cols:]
            qkv_raw = jnp.stack([one_a[:, :cols], one_a[:, cols:], one_b[:, :cols]], axis=1)

        gains = jnp.stack(
            [
                jnp.sum(qkv_raw * w_qkv.astype(F32), axis=(1, 2)),
                jnp.sum(in_raw * w_in.astype(F32), axis=(1, 2)),
            ]
        )
        gains = comm.sum_tensor(gains)
        return (
            result[None],
            token_grad[None],
            gains[0],
            gains[1],
            qkv_raw * gain_one[:, :, None],
            s_out.T,
            in_raw * gain_two[:, :, None],
            down_sum,
        )

    return local


def solution(mesh):
    paired = mesh.shape["dp"] == 16 and mesh.shape["tensor"] == 2
    return jax.shard_map(
        make_local(Chips if paired else Axes),
        mesh=mesh,
        in_specs=(
            P("dp", "tensor", None),
            P("dp", None),
            P("dp", None, "tensor"),
            P("tensor", "dp"),
            P("dp", None, "tensor"),
            P("tensor", "dp"),
            P("dp"),
            P("dp"),
            P("dp", "tensor", None),
        ),
        out_specs=(
            P("dp", "tensor", None),
            P("dp", "tensor", None),
            P("dp"),
            P("dp"),
            P("dp", None, "tensor"),
            P("tensor", "dp"),
            P("dp", None, "tensor"),
            P("tensor", "dp"),
        ),
        check_vma=False,
    )
```
